32 devices in a mesh: dp: 8 (over z, y), row: 2 (over x), col: 2 (over core).
Axes of the slice: x: 2, y: 2, z: 4, core: 2. Of those that a mesh axis runs over, the one named last changes fastest.
Arguments:
- tokens: bfloat16 [16384, 1024], P('dp', 'row'), may hold values from -6 to 6
- seq_lengths: int32 [8, 2], P('dp'), may hold values from 0 to 2048, as said below
- query_weight: bfloat16 [1024, 1024], P('row', 'col'), may hold values from -0.1875 to 0.1875
- key_matrix: bfloat16 [1024, 512], P('row', 'col'), may hold values from -0.1875 to 0.1875
- value_matrix: bfloat16 [1024, 512], P('row', 'col'), may hold values from -0.1875 to 0.1875
- out_weight: bfloat16 [1024, 1024], P('col', 'row'), may hold values from -3 to 3
- gate_weight: bfloat16 [1024, 4608], P('row', 'col'), may hold values from -0.1875 to 0.1875
- up_weight: bfloat16 [1024, 4608], P('row', 'col'), may hold values from -0.1875 to 0.1875
- down_weight: bfloat16 [4608, 1024], P('col', 'row'), may hold values from -0.09375 to 0.09375
- attn_gain: float32 [1024], P('row'), may hold values from 0.5 to 2
- ffn_gain: float32 [1024], P('row'), may hold values from 0.5 to 2
- query_gain: float32 [64], replicated, may hold values from 0.5 to 2
- key_gain: float32 [64], replicated, may hold values from 0.5 to 2
- cotangent: bfloat16 [16384, 1024], P('dp', 'row'), may hold values from -6 to 6
Outputs:
- output: bfloat16 [16384, 1024], P('dp', 'row')
- grad_tokens: bfloat16 [16384, 1024], P('dp', 'row')
- grad_query_weight: float32 [1024, 1024], P('row', 'col')
- grad_key_weight: float32 [1024, 512], P('row', 'col')
- grad_value_weight: float32 [1024, 512], P('row', 'col')
- grad_out_weight: float32 [1024, 1024], P('col', 'row')
- grad_gate_weight: float32 [1024, 4608], P('row', 'col')
- grad_up_weight: float32 [1024, 4608], P('row', 'col')
- grad_down_weight: float32 [4608, 1024], P('col', 'row')
- grad_attn_gain: float32 [1024], P('row')
- grad_ffn_gain: float32 [1024], P('row')
- grad_query_gain: float32 [64], replicated
- grad_key_gain: float32 [64], replicated
The draws below stay inside these ranges and needn't reach their ends.
Inputs may be any that keep to these rules, and one draw needn't show every extreme that they name: `seq_lengths`: each row sums to 2048; a present sequence has 1024 tokens or more, a zero stands only after a sequence of 2048 tokens.
All inputs are finite; a program needn't handle non-finite values.
Results may differ from the reference program's by a relative error of at most 0.015.
The reference program's roundings to bfloat16 on the way count: a program that leaves them out, or rounds other values in their place, can miss the bound.
Values may be sent and summed in bfloat16 or wider, within the bound.
A program may use at most 256 MiB of HBM per device.

```python
import math
import jax
import jax.numpy as jnp
from jax import lax

MODEL_WIDTH = 1024
FF = 4608
QUERY_HEADS = 16
KEY_VALUE_HEADS = 8
HEAD_SIZE = 64
TOK_DEV = 2048
MIN_LEN = 1024
GROUPS = 8
TOKENS = 16384


def draw_seq_lengths(key, part):
    first_part = jax.random.randint(jax.random.fold_in(key, 11), (GROUPS,), MIN_LEN, TOK_DEV - MIN_LEN + 1)
    single = jax.random.randint(jax.random.fold_in(key, 12), (), 0, GROUPS)
    first_part = jnp.where(jnp.arange(GROUPS) == single, TOK_DEV, first_part)
    return jnp.stack([first_part, TOK_DEV - first_part], axis=1).astype(jnp.int32)


def levels(stream_key, shape, cuts, low, high):
    def one(dim, parts):
        draws = jax.random.uniform(jax.random.fold_in(jax.random.fold_in(stream_key, 6), dim), (parts,), jnp.float32, low / len(cuts), high / len(cuts))
        return jnp.repeat(jnp.exp(draws), shape[dim] // parts).reshape((-1,) + (1,) * (len(shape) - dim - 1))

    loudness = one(*cuts[0])
    for cut in cuts[1:]:
        loudness = loudness * one(*cut)
    return loudness


def normal_values(key, extent, width, bound, cuts=(), held_as=jnp.bfloat16):
    drawn = jax.random.normal(key, extent, jnp.float32) * width
    if len(cuts) > 0:
        drawn = levels(key, extent, cuts, -0.22, 0.18) * drawn
    return jnp.clip(drawn, min=-bound, max=bound).astype(held_as)


def setup_inputs(seed: int = 0) -> dict:
    streams_of = jax.random.split(jax.random.key(seed), 15)
    return {
        "tokens": normal_values(streams_of[0], (TOKENS, MODEL_WIDTH), 1.0, 6.0, ((0, 8), (1, 2))),
        "seq_lengths": draw_seq_lengths(jax.random.fold_in(streams_of[14], 71), 0),
        "query_weight": normal_values(streams_of[2], (MODEL_WIDTH, QUERY_HEADS * HEAD_SIZE), MODEL_WIDTH ** -0.5, 0.1875, ((0, 2), (1, 2))),
        "key_matrix": normal_values(streams_of[3], (MODEL_WIDTH, KEY_VALUE_HEADS * HEAD_SIZE), MODEL_WIDTH ** -0.5, 0.1875, ((0, 2), (1, 2))),
        "value_matrix": normal_values(streams_of[4], (MODEL_WIDTH, KEY_VALUE_HEADS * HEAD_SIZE), MODEL_WIDTH ** -0.5, 0.1875, ((0, 2), (1, 2))),
        "out_weight": normal_values(streams_of[5], (QUERY_HEADS * HEAD_SIZE, MODEL_WIDTH), 4 ** -0.5, 3.0, ((0, 2), (1, 2))),
        "gate_weight": normal_values(streams_of[6], (MODEL_WIDTH, FF), MODEL_WIDTH ** -0.5, 0.1875, ((0, 2), (1, 2))),
        "up_weight": normal_values(streams_of[7], (MODEL_WIDTH, FF), MODEL_WIDTH ** -0.5, 0.1875, ((0, 2), (1, 2))),
        "down_weight": normal_values(streams_of[8], (FF, MODEL_WIDTH), FF ** -0.5, 0.09375, ((0, 2), (1, 2))),
        "attn_gain": jnp.clip(jnp.exp(math.log(2.0) - 1.3862944 * jax.random.uniform(streams_of[9], (MODEL_WIDTH,), jnp.float32) ** levels(streams_of[9], (MODEL_WIDTH,), ((0, 2),), -0.2, 0.2)), 0.5, 2.0),
        "ffn_gain": jnp.clip(jnp.exp(math.log(2.0) - 1.3862944 * jax.random.uniform(streams_of[10], (MODEL_WIDTH,), jnp.float32) ** levels(streams_of[10], (MODEL_WIDTH,), ((0, 2),), -0.2, 0.2)), 0.5, 2.0),
        "query_gain": jnp.clip(jnp.exp(jax.random.uniform(streams_of[11], (HEAD_SIZE,), jnp.float32, math.log(0.5), math.log(2.0))), 0.5, 2.0),
        "key_gain": jnp.clip(jnp.exp(jax.random.uniform(streams_of[12], (HEAD_SIZE,), jnp.float32, math.log(0.5), math.log(2.0))), 0.5, 2.0),
        "cotangent": normal_values(streams_of[13], (TOKENS, MODEL_WIDTH), 1.0, 6.0, ((0, 8), (1, 2))),
    }


EPSILON = 1e-05
ROPE_BASE = 1000000.0
NEGATIVE = -1e+30

@jax.custom_vjp
def reduced_precision(v):
    return lax.optimization_barrier(v.astype(jnp.bfloat16)).astype(jnp.float32)

@jax.custom_vjp
def reduced_precision_backward(v):
    return v

def low_keep(v):
    return (reduced_precision(v), None)

def low_pass(kept, grad):
    return (grad,)

def back_keep(v):
    return (v, None)

def back_low(kept, grad):
    return (reduced_precision(grad),)
reduced_precision.defvjp(low_keep, low_pass)
reduced_precision_backward.defvjp(back_keep, back_low)

def matrix_multiply(left_side, right_side):
    return jnp.dot(left_side, right_side, precision=lax.Precision.HIGHEST, preferred_element_type=jnp.float32)

def rms_scale(operand, scale_gain):
    return operand * lax.rsqrt(lax.optimization_barrier(jnp.mean(operand * operand, axis=-1, keepdims=True)) + EPSILON) * scale_gain

def layout(lengths, packed_length):
    seq_ends = jnp.cumsum(lengths).astype(jnp.int32)
    starts = seq_ends - lengths
    places = jnp.arange(packed_length, dtype=jnp.int32)
    member = lax.optimization_barrier(jnp.sum((places[:, None] >= seq_ends[None, :]).astype(jnp.int32), axis=1))
    picked = member[:, None] == jnp.arange(lengths.shape[0], dtype=jnp.int32)[None, :]
    offset = lax.optimization_barrier(jnp.sum(jnp.where(picked, starts[None, :], 0), axis=1))
    return (member, places - offset)

def rotate(operand, position):
    half_width = operand.shape[-1] // 2
    freq_index = jnp.arange(half_width, dtype=jnp.float32)
    inverse = jnp.exp(freq_index * (-2.0 * math.log(ROPE_BASE) / operand.shape[-1]))
    angles = position.astype(jnp.float32)[:, None] * inverse[None, :]
    cosine = jnp.cos(angles)[:, None, :]
    sine_part = jnp.sin(angles)[:, None, :]
    first_half = operand[..., :half_width]
    second = operand[..., half_width:]
    return jnp.concatenate([first_half * cosine - second * sine_part, second * cosine + first_half * sine_part], axis=-1)

def block(tokens_in, lengths, params):
    query_w, key_matrix_local, value_matrix_local, out_w, gate_w, up_w, down_w, attn_g, ffn_g, query_g, key_g = params
    packed_length = tokens_in.shape[0]
    member, position = layout(lengths, packed_length)
    normed_inputs = reduced_precision(rms_scale(tokens_in, attn_g))
    query_raw = reduced_precision_backward(matrix_multiply(normed_inputs, query_w)).reshape(packed_length, QUERY_HEADS, HEAD_SIZE)
    key_unnormed = reduced_precision_backward(matrix_multiply(normed_inputs, key_matrix_local)).reshape(packed_length, KEY_VALUE_HEADS, HEAD_SIZE)
    value_unnormed = reduced_precision(reduced_precision_backward(matrix_multiply(normed_inputs, value_matrix_local))).reshape(packed_length, KEY_VALUE_HEADS, HEAD_SIZE)
    query_rows = reduced_precision(rotate(rms_scale(query_raw, query_g), position))
    keys = reduced_precision(rotate(rms_scale(key_unnormed, key_g), position))
    places = jnp.arange(packed_length, dtype=jnp.int32)
    allowed = (places[None, :] <= places[:, None]) & (member[None, :] == member[:, None])
    grouped_heads = query_rows.reshape(packed_length, KEY_VALUE_HEADS, QUERY_HEADS // KEY_VALUE_HEADS, HEAD_SIZE).transpose(1, 0, 2, 3)

    def one_head(head_inputs):
        head_q, head_k, head_v = head_inputs
        scores = jnp.einsum('igd,jd->gij', head_q, head_k, precision=lax.Precision.HIGHEST) * HEAD_SIZE ** (-0.5)
        scores = jnp.where(allowed[None], scores, NEGATIVE)
        log_total = jax.nn.logsumexp(scores, axis=-1, keepdims=True)
        softmax_low = reduced_precision(jnp.exp(scores - log_total))
        return jnp.einsum('gij,jd->igd', softmax_low, head_v, precision=lax.Precision.HIGHEST)
    attended_heads = lax.map(jax.checkpoint(one_head), (grouped_heads, keys.transpose(1, 0, 2), value_unnormed.transpose(1, 0, 2)))
    attended = reduced_precision(reduced_precision_backward(attended_heads.transpose(1, 0, 2, 3).reshape(packed_length, QUERY_HEADS * HEAD_SIZE)))
    branch = reduced_precision_backward(matrix_multiply(attended, out_w))
    middle = tokens_in + branch
    hidden = reduced_precision(rms_scale(middle, ffn_g))
    gate_pre = reduced_precision_backward(matrix_multiply(hidden, gate_w))
    upward = reduced_precision_backward(matrix_multiply(hidden, up_w))
    active = reduced_precision(jax.nn.silu(gate_pre) * upward)
    return middle + reduced_precision_backward(matrix_multiply(active, down_w))

def reference(tokens, seq_lengths, query_weight, key_matrix, value_matrix, out_weight, gate_weight, up_weight, down_weight, attn_gain, ffn_gain, query_gain, key_gain, cotangent):
    weights = tuple((record.astype(jnp.float32) for record in (query_weight, key_matrix, value_matrix, out_weight, gate_weight, up_weight, down_weight, attn_gain, ffn_gain, query_gain, key_gain)))
    inputs = tokens.astype(jnp.float32).reshape(GROUPS, TOK_DEV, MODEL_WIDTH)

    def forward(stacked, *params):

        def scan_step(carried, record):
            return (carried, jax.checkpoint(block)(record[0], record[1], params))
        _, outputs = lax.scan(scan_step, jnp.zeros((), jnp.float32), (stacked, seq_lengths))
        return outputs
    outputs, backward = jax.vjp(forward, inputs, *weights)
    gradients = backward(cotangent.astype(jnp.float32).reshape(GROUPS, TOK_DEV, MODEL_WIDTH))
    return (outputs.reshape(TOKENS, MODEL_WIDTH).astype(jnp.bfloat16), gradients[0].reshape(TOKENS, MODEL_WIDTH).astype(jnp.bfloat16), gradients[1], gradients[2], gradients[3], gradients[4], gradients[5], gradients[6], gradients[7], gradients[8], gradients[9], gradients[10], gradients[11])
```

```python
import math

import jax
import jax.numpy as jnp
from jax import lax
from jax.sharding import PartitionSpec as P

MODEL_WIDTH = 1024
HEAD_SIZE = 64


EPSILON = 1e-05
ROPE_BASE = 1000000.0
NEGATIVE = -1e30


def for_sending(x):

    def short(part):
        return part.astype(jnp.bfloat16) if part.dtype == jnp.float32 else part

    return jax.tree.map(short, x)


def layout(lengths, packed_length):
    numbers = jnp.arange(lengths.shape[0], dtype=jnp.int32)
    seq_ends = jnp.sum(jnp.where(numbers[None, :] <= numbers[:, None], lengths[None, :], 0), axis=1)
    starts = seq_ends - lengths
    places = jnp.arange(packed_length, dtype=jnp.int32)
    member = jnp.sum((places[:, None] >= seq_ends[None, :]).astype(jnp.int32), axis=1)
    picked = member[:, None] == jnp.arange(lengths.shape[0], dtype=jnp.int32)[None, :]
    offset = jnp.sum(jnp.where(picked, starts[None, :], 0), axis=1)
    return (member, places - offset)


def rotate(operand, position):
    half_width = operand.shape[-1] // 2
    freq_index = jnp.arange(half_width, dtype=jnp.float32)
    inverse = jnp.exp(freq_index * (-2.0 * math.log(ROPE_BASE) / operand.shape[-1]))
    angles = position.astype(jnp.float32)[:, None] * inverse[None, :]
    cosine = jnp.cos(angles)[:, None, :]
    sine_part = jnp.sin(angles)[:, None, :]
    first_half = operand[..., :half_width]
    second = operand[..., half_width:]
    return jnp.concatenate(
        [first_half * cosine - second * sine_part, second * cosine + first_half * sine_part],
        axis=-1,
    )


def head_prepare(raw_in, gain_in, position):
    head_rows = raw_in.reshape(raw_in.shape[0], -1, HEAD_SIZE)
    normed_inputs = (
        head_rows
        * lax.rsqrt(jnp.mean(head_rows * head_rows, axis=-1, keepdims=True) + EPSILON)
        * gain_in
    )
    return rotate(normed_inputs, position)


def feature_total(operand):
    return lax.psum(operand, "row")


def column_total(operand):
    return lax.psum(operand, "col")


def column_grads(operand):
    return lax.psum(operand, "col")


def scatter_back(operand):
    return lax.psum_scatter(operand, "row", scatter_dimension=1, tiled=True)


def gather_grads(operand):
    return jax.tree.map(
        lambda part, own: part.astype(own.dtype),
        lax.all_gather(for_sending(operand), "row", axis=1, tiled=True),
        operand,
    )


def contract_rows(left_side, right_side):
    return lax.dot_general(
        left_side, right_side, (((0,), (0,)), ((), ())), preferred_element_type=jnp.float32
    )


def times_transpose(left_side, right_side):
    return lax.dot_general(
        left_side, right_side, (((1,), (1,)), ((), ())), preferred_element_type=jnp.float32
    )


def block_scores(query_block, key_block):
    return jnp.einsum(
        "ikgd,jkd->kgij", query_block, key_block, preferred_element_type=jnp.float32
    ) * HEAD_SIZE ** (-0.5)


def block_mask(member, query_start, key_start, block_rows):
    offsets = jnp.arange(block_rows, dtype=jnp.int32)
    query_doc = lax.dynamic_slice_in_dim(member, query_start, block_rows)
    key_doc = lax.dynamic_slice_in_dim(member, key_start, block_rows)
    causal = (key_start + offsets)[None, :] <= (query_start + offsets)[:, None]
    return causal & (key_doc[None, :] == query_doc[:, None])


def guarded(query_index, key_index, update, loop_state):
    needed = key_index <= query_index
    return lax.cond(needed, update, lambda unchanged: unchanged, loop_state)


def add_block(buffer, addend, start_row):
    current = lax.dynamic_slice_in_dim(buffer, start_row, addend.shape[0])
    return lax.dynamic_update_slice_in_dim(buffer, current + addend, start_row, 0)


def attend(query_rows, keys, values, member, block_rows):
    packed_length = query_rows.shape[0]
    blocks = packed_length // block_rows
    kv_heads, group_size = (query_rows.shape[1], query_rows.shape[2])

    def query_step(query_index, carried):
        outputs, totals = carried
        query_start = query_index * block_rows
        query_block = lax.dynamic_slice_in_dim(query_rows, query_start, block_rows)

        def stats_step(key_index, loop_state):

            def update(running):
                run_peak, run_mass = running
                key_start = key_index * block_rows
                allowed = block_mask(member, query_start, key_start, block_rows)
                scores = jnp.where(
                    allowed,
                    block_scores(
                        query_block, lax.dynamic_slice_in_dim(keys, key_start, block_rows)
                    ),
                    NEGATIVE,
                )
                new_peak = jnp.maximum(run_peak, jnp.max(scores, axis=-1))
                new_mass = run_mass * jnp.exp(run_peak - new_peak) + jnp.sum(
                    jnp.where(allowed, jnp.exp(scores - new_peak[..., None]), 0.0), axis=-1
                )
                return (new_peak, new_mass)

            return guarded(query_index, key_index, update, loop_state)

        start_state = (
            jnp.full((kv_heads, group_size, block_rows), NEGATIVE, jnp.float32),
            jnp.zeros((kv_heads, group_size, block_rows), jnp.float32),
        )
        run_peak, run_mass = lax.fori_loop(0, blocks, stats_step, start_state)
        log_total = run_peak + jnp.log(run_mass)

        def value_step(key_index, loop_state):

            def update(running):
                key_start = key_index * block_rows
                allowed = block_mask(member, query_start, key_start, block_rows)
                scores = block_scores(
                    query_block, lax.dynamic_slice_in_dim(keys, key_start, block_rows)
                )
                probs_low = jnp.where(allowed, jnp.exp(scores - log_total[..., None]), 0.0).astype(
                    jnp.bfloat16
                )
                return running + jnp.einsum(
                    "kgij,jkd->ikgd",
                    probs_low,
                    lax.dynamic_slice_in_dim(values, key_start, block_rows),
                    preferred_element_type=jnp.float32,
                )

            return guarded(query_index, key_index, update, loop_state)

        block_out = lax.fori_loop(
            0,
            blocks,
            value_step,
            jnp.zeros((block_rows, kv_heads, group_size, HEAD_SIZE), jnp.float32),
        )
        outputs = lax.dynamic_update_slice_in_dim(outputs, block_out, query_start, 0)
        totals = lax.dynamic_update_slice_in_dim(totals, log_total, query_start, 2)
        return (outputs, totals)

    initial = (
        jnp.zeros((packed_length, kv_heads, group_size, HEAD_SIZE), jnp.float32),
        jnp.zeros((kv_heads, group_size, packed_length), jnp.float32),
    )
    return lax.fori_loop(0, blocks, query_step, initial)


def attend_back(query_rows, keys, values, outputs, totals, grad_out, member, block_rows):
    packed_length = query_rows.shape[0]
    blocks = packed_length // block_rows
    kv_heads, group_size = (query_rows.shape[1], query_rows.shape[2])
    balance = jnp.einsum("ikgd,ikgd->kgi", grad_out.astype(jnp.float32), outputs)

    def query_step(query_index, carried):
        grad_queries, grad_keys, grad_values = carried
        query_start = query_index * block_rows
        query_block = lax.dynamic_slice_in_dim(query_rows, query_start, block_rows)
        query_wide = query_block.astype(jnp.float32)
        grad_block = lax.dynamic_slice_in_dim(grad_out, query_start, block_rows)
        log_total = lax.dynamic_slice_in_dim(totals, query_start, block_rows, 2)
        balance_block = lax.dynamic_slice_in_dim(balance, query_start, block_rows, 2)

        def key_step(key_index, loop_state):

            def update(running):
                grad_query, grad_keys, grad_values = running
                key_start = key_index * block_rows
                key_block = lax.dynamic_slice_in_dim(keys, key_start, block_rows)
                value_block = lax.dynamic_slice_in_dim(values, key_start, block_rows)
                allowed = block_mask(member, query_start, key_start, block_rows)
                probs = jnp.where(
                    allowed,
                    jnp.exp(block_scores(query_block, key_block) - log_total[..., None]),
                    0.0,
                )
                probs_low = probs.astype(jnp.bfloat16)
                value_part = jnp.einsum(
                    "kgij,ikgd->jkd", probs_low, grad_block, preferred_element_type=jnp.float32
                )
                grad_probs = jnp.einsum(
                    "ikgd,jkd->kgij", grad_block, value_block, preferred_element_type=jnp.float32
                )
                grad_scores = probs * (grad_probs - balance_block[..., None])
                grad_query = grad_query + jnp.einsum(
                    "kgij,jkd->ikgd",
                    grad_scores,
                    key_block.astype(jnp.float32),
                    precision=lax.Precision.HIGHEST,
                    preferred_element_type=jnp.float32,
                ) * HEAD_SIZE ** (-0.5)
                key_part = jnp.einsum(
                    "kgij,ikgd->jkd",
                    grad_scores,
                    query_wide,
                    precision=lax.Precision.HIGHEST,
                    preferred_element_type=jnp.float32,
                ) * HEAD_SIZE ** (-0.5)
                return (
                    grad_query,
                    add_block(grad_keys, key_part, key_start),
                    add_block(grad_values, value_part, key_start),
                )

            return guarded(query_index, key_index, update, loop_state)

        start_state = (
            jnp.zeros((block_rows, kv_heads, group_size, HEAD_SIZE), jnp.float32),
            grad_keys,
            grad_values,
        )
        grad_query, grad_keys, grad_values = lax.fori_loop(0, blocks, key_step, start_state)
        grad_queries = lax.dynamic_update_slice_in_dim(grad_queries, grad_query, query_start, 0)
        return (grad_queries, grad_keys, grad_values)

    initial = (
        jnp.zeros((packed_length, kv_heads, group_size, HEAD_SIZE), jnp.float32),
        jnp.zeros((packed_length, kv_heads, HEAD_SIZE), jnp.float32),
        jnp.zeros((packed_length, kv_heads, HEAD_SIZE), jnp.float32),
    )
    return lax.fori_loop(0, blocks, query_step, initial)


def shards(
    tokens,
    seq_lengths,
    query_weight,
    key_matrix,
    value_matrix,
    out_weight,
    gate_weight,
    up_weight,
    down_weight,
    attn_gain,
    ffn_gain,
    query_gain,
    key_gain,
    cotangent,
):
    packed_length = tokens.shape[0]
    block_rows = min(512, packed_length)
    row_parts = lax.axis_size("row")
    member, position = layout(seq_lengths[0], packed_length)
    inputs = tokens.astype(jnp.float32)
    inverse_one = lax.rsqrt(feature_total(jnp.sum(inputs * inputs, axis=1)) / MODEL_WIDTH + EPSILON)
    normal_one = inputs * inverse_one[:, None]
    hidden_one = (normal_one * attn_gain).astype(jnp.bfloat16)
    query_part = jnp.dot(hidden_one, query_weight, preferred_element_type=jnp.float32).reshape(
        packed_length, row_parts, -1
    )
    key_part = jnp.dot(hidden_one, key_matrix, preferred_element_type=jnp.float32).reshape(
        packed_length, row_parts, -1
    )
    value_part = jnp.dot(hidden_one, value_matrix, preferred_element_type=jnp.float32).reshape(
        packed_length, row_parts, -1
    )
    query_raw, key_unnormed, value_unnormed = (
        lax.psum_scatter(query_part, "row", scatter_dimension=1, tiled=True),
        lax.psum_scatter(key_part, "row", scatter_dimension=1, tiled=True),
        lax.psum_scatter(value_part, "row", scatter_dimension=1, tiled=True),
    )
    query_raw = query_raw.reshape(packed_length, -1)
    key_unnormed = key_unnormed.reshape(packed_length, -1)
    value_unnormed = value_unnormed.reshape(packed_length, -1)
    kv_local = key_unnormed.shape[1] // HEAD_SIZE
    query_rows, query_back = jax.vjp(
        lambda raw_in, gain_in: head_prepare(raw_in, gain_in, position), query_raw, query_gain
    )
    keys, key_back = jax.vjp(
        lambda raw_in, gain_in: head_prepare(raw_in, gain_in, position), key_unnormed, key_gain
    )
    query_low = query_rows.astype(jnp.bfloat16).reshape(packed_length, kv_local, -1, HEAD_SIZE)
    key_low = keys.astype(jnp.bfloat16)
    value_low = value_unnormed.astype(jnp.bfloat16).reshape(packed_length, kv_local, HEAD_SIZE)
    outputs, totals = attend(query_low, key_low, value_low, member, block_rows)
    attended = outputs.reshape(packed_length, -1).astype(jnp.bfloat16)
    attended_all = lax.all_gather(attended, "row", axis=1, tiled=True)
    branch = column_total(jnp.dot(attended_all, out_weight, preferred_element_type=jnp.float32))
    middle = inputs + branch
    inverse_two = lax.rsqrt(feature_total(jnp.sum(middle * middle, axis=1)) / MODEL_WIDTH + EPSILON)
    normal_two = middle * inverse_two[:, None]
    hidden_two = (normal_two * ffn_gain).astype(jnp.bfloat16)
    gate_part = jnp.dot(hidden_two, gate_weight, preferred_element_type=jnp.float32).reshape(
        packed_length, row_parts, -1
    )
    up_part = jnp.dot(hidden_two, up_weight, preferred_element_type=jnp.float32).reshape(
        packed_length, row_parts, -1
    )
    gate_raw, up_raw = (
        lax.psum_scatter(gate_part, "row", scatter_dimension=1, tiled=True),
        lax.psum_scatter(up_part, "row", scatter_dimension=1, tiled=True),
    )
    gate_raw = gate_raw.reshape(packed_length, -1)
    up_raw = up_raw.reshape(packed_length, -1)
    active, active_back = jax.vjp(
        lambda gate_in, upward_in: jax.nn.silu(gate_in) * upward_in, gate_raw, up_raw
    )
    active_all = lax.all_gather(active.astype(jnp.bfloat16), "row", axis=1, tiled=True)
    result = middle + column_total(
        jnp.dot(active_all, down_weight, preferred_element_type=jnp.float32)
    )
    output = result.astype(jnp.bfloat16)
    grad_down = contract_rows(active_all, cotangent)
    grad_active = scatter_back(times_transpose(cotangent, down_weight))
    grad_gate, grad_up = active_back(grad_active)
    gate_all, up_all = gather_grads((grad_gate.astype(jnp.bfloat16), grad_up.astype(jnp.bfloat16)))
    grad_gate_w = contract_rows(hidden_two, gate_all)
    grad_up_w = contract_rows(hidden_two, up_all)
    grad_hidden_two = column_grads(
        times_transpose(gate_all, gate_weight) + times_transpose(up_all, up_weight)
    )
    grad_ffn_gain = jnp.sum(grad_hidden_two * normal_two, axis=0)
    grad_normal_two = grad_hidden_two * ffn_gain
    stat_two = feature_total(jnp.sum(grad_normal_two * normal_two, axis=1))
    grad_middle = inverse_two[:, None] * (
        grad_normal_two - normal_two * (stat_two / MODEL_WIDTH)[:, None]
    ) + cotangent.astype(jnp.float32)
    branch_low = grad_middle.astype(jnp.bfloat16)
    grad_out_w = contract_rows(attended_all, branch_low)
    attended_grad = scatter_back(times_transpose(branch_low, out_weight))
    grad_attended = attended_grad.astype(jnp.bfloat16).reshape(
        packed_length, kv_local, -1, HEAD_SIZE
    )
    grad_queries, grad_keys, grad_values = attend_back(
        query_low, key_low, value_low, outputs, totals, grad_attended, member, block_rows
    )
    grad_query_raw, grad_query_gain = query_back(grad_queries.reshape(packed_length, -1, HEAD_SIZE))
    grad_key_raw, grad_key_gain = key_back(grad_keys)
    query_all, key_all, value_all = gather_grads(
        (
            grad_query_raw.astype(jnp.bfloat16),
            grad_key_raw.astype(jnp.bfloat16),
            grad_values.reshape(packed_length, -1).astype(jnp.bfloat16),
        )
    )
    grad_query_w = contract_rows(hidden_one, query_all)
    grad_key_w = contract_rows(hidden_one, key_all)
    grad_value_w = contract_rows(hidden_one, value_all)
    hidden_sum = (
        times_transpose(query_all, query_weight)
        + times_transpose(key_all, key_matrix)
        + times_transpose(value_all, value_matrix)
    )
    grad_hidden_one, query_gain_col, key_gain_col = column_grads(
        (hidden_sum, grad_query_gain, grad_key_gain)
    )
    grad_attn_gain = jnp.sum(grad_hidden_one * normal_one, axis=0)
    grad_normal_one = grad_hidden_one * attn_gain
    stat_one, query_gain_row, key_gain_row = feature_total(
        (jnp.sum(grad_normal_one * normal_one, axis=1), query_gain_col, key_gain_col)
    )
    grad_inputs = (
        inverse_one[:, None] * (grad_normal_one - normal_one * (stat_one / MODEL_WIDTH)[:, None])
        + grad_middle
    )
    (
        grad_query_w,
        grad_key_w,
        grad_value_w,
        grad_out_w,
        grad_gate_w,
        grad_up_w,
        grad_down,
        grad_attn_gain,
        grad_ffn_gain,
        query_gain_row,
        key_gain_row,
    ) = lax.psum(
        (
            grad_query_w,
            grad_key_w,
            grad_value_w,
            grad_out_w,
            grad_gate_w,
            grad_up_w,
            grad_down,
            grad_attn_gain,
            grad_ffn_gain,
            query_gain_row,
            key_gain_row,
        ),
        "dp",
    )
    return (
        output,
        grad_inputs.astype(jnp.bfloat16),
        grad_query_w,
        grad_key_w,
        grad_value_w,
        grad_out_w,
        grad_gate_w,
        grad_up_w,
        grad_down,
        grad_attn_gain,
        grad_ffn_gain,
        query_gain_row,
        key_gain_row,
    )


def solution(mesh):
    return jax.shard_map(
        shards,
        mesh=mesh,
        in_specs=(
            P("dp", "row"),
            P("dp", None),
            P("row", "col"),
            P("row", "col"),
            P("row", "col"),
            P("col", "row"),
            P("row", "col"),
            P("row", "col"),
            P("col", "row"),
            P("row"),
            P("row"),
            P(),
            P(),
            P("dp", "row"),
        ),
        out_specs=(
            P("dp", "row"),
            P("dp", "row"),
            P("row", "col"),
            P("row", "col"),
            P("row", "col"),
            P("col", "row"),
            P("row", "col"),
            P("row", "col"),
            P("col", "row"),
            P("row"),
            P("row"),
            P(),
            P(),
        ),
        check_vma=False,
    )
```

```python
import functools
import math

import jax
import jax.numpy as jnp
from jax import lax
from jax.experimental import pallas as pl
from jax.experimental.pallas import tpu as pltpu
from jax.sharding import PartitionSpec as P

HEAD_SIZE = 64
EPSILON = 1e-05
ROPE_BASE = 1000000.0
F32, BF16 = jnp.float32, jnp.bfloat16


def dot(a, b, dims=(((1,), (0,)), ((), ()))):
    return lax.dot_general(a, b, dims, preferred_element_type=F32)


NT = (((1,), (1,)), ((), ()))

def stacked(x):
    first = lax.broadcasted_iota(jnp.int32, x.shape, 1) < 64
    zero = jnp.zeros_like(x)
    return jnp.concatenate([jnp.where(first, x, zero), jnp.where(first, zero, x)], axis=0)

def attend_kernel(bq, bk, first_ref, last_ref, q_ref, k_ref, v_ref, start_ref, low_ref, raw_ref, lse_ref, acc_ref, mass_ref):
    i = pl.program_id(1)
    qs = stacked(q_ref[...])
    starts = start_ref[...]
    starts = jnp.concatenate([starts, starts], axis=0)
    acc_ref[...] = jnp.zeros_like(acc_ref)
    mass_ref[...] = jnp.zeros_like(mass_ref)
    rows = i * bq + lax.rem(lax.broadcasted_iota(jnp.int32, (2 * bq, 1), 0), bq)

    def step(j, masked):
        k0 = pl.multiple_of(j * bk, bk)
        s = dot(qs, k_ref[pl.ds(k0, bk), :], NT)
        p = jnp.exp(s)
        if masked:
            cols = j * bk + lax.broadcasted_iota(jnp.int32, (1, bk), 1)
            p = jnp.where((cols <= rows) & (cols >= starts), p, 0.0)
        mass = p[:, :128]
        for n in range(1, bk // 128):
            mass = mass + p[:, n * 128:(n + 1) * 128]
        mass_ref[...] += mass
        acc_ref[...] += dot(p.astype(BF16), v_ref[pl.ds(k0, bk), :])

    low = first_ref[i] // bk
    clear = jnp.maximum((last_ref[i] + bk - 1) // bk, low)
    diagonal = (i * bq) // bk
    end = ((i + 1) * bq + bk - 1) // bk
    clear = jnp.minimum(clear, diagonal)

    @pl.loop(low, clear)
    def _(j):
        step(j, True)

    @pl.loop(clear, diagonal)
    def _(j):
        step(j, False)

    @pl.loop(diagonal, end)
    def _(j):
        step(j, True)

    mass = jnp.sum(mass_ref[...], axis=1, keepdims=True)
    out = acc_ref[...] / mass
    first = lax.broadcasted_iota(jnp.int32, (bq, 128), 1) < 64
    out = jnp.where(first, out[:bq], out[bq:])
    raw_ref[...] = out
    low_ref[...] = out.astype(BF16)
    total = jnp.log(jnp.sum(mass_ref[...].T, axis=0, keepdims=True))
    lse_ref[0, 0:1, :] = total[:, :bq]
    lse_ref[0, 1:2, :] = total[:, bq:]

def attend(q, k, v, starts, bq=512, bk=512):
    T, width = q.shape
    groups = width // 128
    first, last = starts[::bq], starts[bq - 1::bq]
    kern = functools.partial(attend_kernel, bq, bk)
    pairs = T * (T + bk) // 2
    return pl.pallas_call(
        kern,
        out_shape=(jax.ShapeDtypeStruct((T, width), BF16), jax.ShapeDtypeStruct((T, width), F32),
                   jax.ShapeDtypeStruct((groups, 2, T), F32)),
        grid_spec=pltpu.PrefetchScalarGridSpec(
            num_scalar_prefetch=2, grid=(groups, T // bq),
            in_specs=[
                pl.BlockSpec((bq, 128), lambda g, i, *_: (i, g)),
                pl.BlockSpec((T, 128), lambda g, i, *_: (0, g)),
                pl.BlockSpec((T, 128), lambda g, i, *_: (0, g)),
                pl.BlockSpec((bq, 1), lambda g, i, *_: (i, 0)),
            ],
            out_specs=[
                pl.BlockSpec((bq, 128), lambda g, i, *_: (i, g)),
                pl.BlockSpec((bq, 128), lambda g, i, *_: (i, g)),
                pl.BlockSpec((1, 2, bq), lambda g, i, *_: (g, 0, i)),
            ],
            scratch_shapes=[pltpu.VMEM((2 * bq, 128), F32), pltpu.VMEM((2 * bq, 128), F32)],
        ),
        compiler_params=pltpu.CompilerParams(vmem_limit_bytes=40 << 20),
        cost_estimate=pl.CostEstimate(flops=4 * groups * 2 * pairs * 256, transcendentals=2 * groups * pairs,
                                      bytes_accessed=10 * T * width),
        name="attend",
    )(first, last, q, k, v, starts[:, None])

def attend_back_kernel(b, T, first_ref, last_ref, q_ref, k_ref, v_ref, grad_ref, raw_ref, lse_ref, start_ref,
                       dq_ref, dk_ref, dv_ref, qs_ref, gs_ref, stat_ref, dqt_ref, dk_acc, dv_acc):
    j = pl.program_id(1)
    blocks = T // b

    @pl.when(j == 0)
    def _():
        dqt_ref[...] = jnp.zeros_like(dqt_ref)
        for i in range(blocks):
            rows = slice(i * b, (i + 1) * b)
            both = slice(i * 2 * b, (i + 1) * 2 * b)
            qs_ref[both, :] = stacked(q_ref[rows, :])
            grad = grad_ref[rows, :]
            gs_ref[both, :] = stacked(grad)
            prod = (grad.astype(F32) * raw_ref[rows, :]).T
            stat_ref[i, 0:1, 0:b] = lse_ref[0, 0:1, rows]
            stat_ref[i, 0:1, b:2 * b] = lse_ref[0, 1:2, rows]
            stat_ref[i, 1:2, 0:b] = jnp.sum(prod[:64], axis=0, keepdims=True)
            stat_ref[i, 1:2, b:2 * b] = jnp.sum(prod[64:], axis=0, keepdims=True)

    k = k_ref[...]
    v = v_ref[...]
    kt = k.T[:64]
    dk_acc[...] = jnp.zeros_like(dk_acc)
    dv_acc[...] = jnp.zeros_like(dv_acc)
    keys = j * b + lax.broadcasted_iota(jnp.int32, (b, 1), 0)

    def step(i, masked):
        at = pl.ds(pl.multiple_of(i * 2 * b, 2 * b), 2 * b)
        qs = qs_ref[at, :]
        gs = gs_ref[at, :]
        st = dot(k, qs, NT)
        pt = jnp.exp(st - stat_ref[i, 0:1, :])
        if masked:
            cols = i * b + lax.rem(lax.broadcasted_iota(jnp.int32, (1, 2 * b), 1), b)
            begin = start_ref[0:1, pl.ds(pl.multiple_of(i * b, b), b)]
            begin = jnp.concatenate([begin, begin], axis=1)
            pt = jnp.where((keys <= cols) & (keys >= begin), pt, 0.0)
        dv_acc[...] += dot(pt.astype(BF16), gs)
        dpt = dot(v, gs, NT)
        dst = (pt * (dpt - stat_ref[i, 1:2, :])).astype(BF16)
        dk_acc[...] += dot(dst, qs)
        part = dot(kt, dst)
        to = pl.ds(pl.multiple_of(i * b, b), b)
        dqt_ref[0:64, to] += part[:, :b]
        dqt_ref[64:128, to] += part[:, b:]

    step(j, True)

    @pl.loop(j + 1, blocks)
    def _(i):
        whole = last_ref[i] <= j * b
        none = first_ref[i] >= (j + 1) * b

        @pl.when(whole)
        def _():
            step(i, False)

        @pl.when(jnp.logical_not(whole | none))
        def _():
            step(i, True)

    dk = dk_acc[...]
    dv = dv_acc[...]
    dk_ref[...] = dk + pltpu.roll(dk, 64, 1)
    dv_ref[...] = dv + pltpu.roll(dv, 64, 1)
    dq_ref[...] = dqt_ref[:, pl.ds(pl.multiple_of(j * b, b), b)].T * 0.125

def attend_back(q, k, v, grad, raw, lse, starts, b=512):
    T, width = q.shape
    groups = width // 128
    first, last = starts[::b], starts[b - 1::b]
    blocks = T // b
    col = pl.BlockSpec((T, 128), lambda g, j, *_: (0, g))
    blk = pl.BlockSpec((b, 128), lambda g, j, *_: (j, g))
    out = jax.ShapeDtypeStruct((T, width), F32)
    pairs = T * (T + b) // 2
    return pl.pallas_call(
        functools.partial(attend_back_kernel, b, T),
        out_shape=(out, out, out),
        grid_spec=pltpu.PrefetchScalarGridSpec(
            num_scalar_prefetch=2, grid=(groups, blocks),
            in_specs=[col, blk, blk, col, col,
                      pl.BlockSpec((1, 2, T), lambda g, j, *_: (g, 0, 0)),
                      pl.BlockSpec((1, T), lambda g, j, *_: (0, 0))],
            out_specs=[blk, blk, blk],
            scratch_shapes=[pltpu.VMEM((2 * T, 128), BF16), pltpu.VMEM((2 * T, 128), BF16),
                            pltpu.VMEM((blocks, 2, 2 * b), F32), pltpu.VMEM((128, T), F32),
                            pltpu.VMEM((b, 128), F32), pltpu.VMEM((b, 128), F32)],
        ),
        compiler_params=pltpu.CompilerParams(vmem_limit_bytes=48 << 20),
        cost_estimate=pl.CostEstimate(flops=10 * groups * 2 * pairs * 256, transcendentals=2 * groups * pairs,
                                      bytes_accessed=20 * T * width),
        name="attend_back",
    )(first, last, q, k, v, grad, raw, lse, starts[None, :])


def head_sums(x):
    first = lax.broadcasted_iota(jnp.int32, x.shape, 1) < HEAD_SIZE
    one = jnp.sum(jnp.where(first, x, 0.0), axis=1, keepdims=True)
    two = jnp.sum(jnp.where(first, 0.0, x), axis=1, keepdims=True)
    return jnp.where(first, one, two)


def swapped(x):
    low = lax.rem(lax.broadcasted_iota(jnp.int32, x.shape, 1), HEAD_SIZE) < HEAD_SIZE // 2
    return jnp.where(low, pltpu.roll(x, 96, 1), pltpu.roll(x, 32, 1))


def doubled(x):
    first = lax.broadcasted_iota(jnp.int32, x.shape, 1) < HEAD_SIZE
    other = pltpu.roll(x, HEAD_SIZE, 1)
    return jnp.where(first, x, other), jnp.where(first, other, x)


def project_kernel(groups, near_ref, far_ref, gain_near_ref, gain_far_ref, w_near_ref, w_far_ref, q_gain_ref, k_gain_ref,
                   cos_ref, sin_ref, hid_near_ref, hid_far_ref, raw_ref, q_ref, k_ref, v_ref):
    near = near_ref[...].astype(F32)
    far = far_ref[...].astype(F32)
    width = near.shape[1] + far.shape[1]
    total = jnp.sum(near * near, axis=1, keepdims=True) + jnp.sum(far * far, axis=1, keepdims=True)
    inverse = lax.rsqrt(total / width + EPSILON)
    hid_near = (near * inverse * gain_near_ref[...]).astype(BF16)
    hid_far = (far * inverse * gain_far_ref[...]).astype(BF16)
    hid_near_ref[...] = hid_near
    hid_far_ref[...] = hid_far
    raw = dot(hid_near, w_near_ref[...]) + dot(hid_far, w_far_ref[...])
    cosine, sine = cos_ref[...], sin_ref[...]

    def prepared(x, gain):
        normed = x * lax.rsqrt(head_sums(x * x) / HEAD_SIZE + EPSILON) * gain
        return normed * cosine + swapped(normed) * sine

    lanes = 2 * HEAD_SIZE
    kv = groups * HEAD_SIZE
    raw_ref[...] = raw[:, :groups * lanes + kv]
    for n in range(groups):
        cut = slice(n * lanes, (n + 1) * lanes)
        q_ref[:, cut] = (prepared(raw[:, cut], q_gain_ref[...]).astype(BF16) * HEAD_SIZE ** (-0.5)).astype(BF16)
    for n in range(groups // 2):
        at = groups * lanes + n * lanes
        twice = doubled(prepared(raw[:, at:at + lanes], k_gain_ref[...]))
        for m in range(2):
            k_ref[:, (2 * n + m) * lanes:(2 * n + m + 1) * lanes] = twice[m].astype(BF16)
        at += kv
        twice = doubled(raw[:, at:at + lanes])
        for m in range(2):
            v_ref[:, (2 * n + m) * lanes:(2 * n + m + 1) * lanes] = twice[m].astype(BF16)


def project(near, far, gain_near, gain_far, w_near, w_far, q_gain, k_gain, cosine, sine, rows=512):
    packed, half = near.shape
    columns = w_near.shape[1]
    groups = columns // (4 * HEAD_SIZE)
    width = groups * 2 * HEAD_SIZE
    kv = groups * HEAD_SIZE
    rows = min(rows, packed)

    def tile(n):
        return pl.BlockSpec((rows, n), lambda i: (i, 0))

    def whole(x):
        return pl.BlockSpec(x.shape, lambda i: (0, 0))

    def out(n, dtype):
        return jax.ShapeDtypeStruct((packed, n), dtype)

    small = (gain_near, gain_far, w_near, w_far, q_gain, k_gain)
    return pl.pallas_call(
        functools.partial(project_kernel, groups),
        out_shape=(out(half, BF16), out(half, BF16), out(width + kv, F32), out(width, BF16), out(width, BF16), out(width, BF16)),
        grid=(packed // rows,),
        in_specs=[tile(half), tile(half), *map(whole, small), tile(2 * HEAD_SIZE), tile(2 * HEAD_SIZE)],
        out_specs=(tile(half), tile(half), tile(width + kv), tile(width), tile(width), tile(width)),
        compiler_params=pltpu.CompilerParams(vmem_limit_bytes=40 << 20),
        cost_estimate=pl.CostEstimate(flops=4 * packed * half * columns, transcendentals=packed * 8,
                                      bytes_accessed=packed * (8 * half + 10 * width)),
        name="project",
    )(near, far, *small, cosine, sine)


def project_back_kernel(groups, dq_ref, dk_ref, dv_ref, raw_ref, near_ref, far_ref, gain_near_ref, gain_far_ref,
                        w_near_ref, w_far_ref, q_gain_ref, k_gain_ref, cos_ref, sin_ref,
                        grads_ref, to_near_ref, to_far_ref, stat_ref, q_sum_ref, k_sum_ref, near_sum_ref, far_sum_ref):
    @pl.when(pl.program_id(0) == 0)
    def _():
        for ref in (q_sum_ref, k_sum_ref, near_sum_ref, far_sum_ref):
            ref[...] = jnp.zeros_like(ref)

    cosine, sine = cos_ref[...], sin_ref[...]
    lanes = 2 * HEAD_SIZE
    first = lax.broadcasted_iota(jnp.int32, cosine.shape, 1) < HEAD_SIZE

    def back(grad, x, gain):
        inverse = lax.rsqrt(head_sums(x * x) / HEAD_SIZE + EPSILON)
        normed = x * inverse
        turned = grad * cosine - swapped(grad) * sine
        inner = turned * gain
        part = inverse * (inner - normed * (head_sums(inner * normed) / HEAD_SIZE))
        return part, jnp.sum(turned * normed, axis=0, keepdims=True)

    grads = []
    for n in range(groups):
        cut = slice(n * lanes, (n + 1) * lanes)
        part, total = back(dq_ref[:, cut], raw_ref[:, cut], q_gain_ref[...])
        q_sum_ref[...] += total
        grads.append(part.astype(BF16))
    for n in range(groups // 2):
        one = slice(2 * n * lanes, (2 * n + 1) * lanes)
        two = slice((2 * n + 1) * lanes, (2 * n + 2) * lanes)
        at = groups * lanes + n * lanes
        part, total = back(jnp.where(first, dk_ref[:, one], dk_ref[:, two]), raw_ref[:, at:at + lanes], k_gain_ref[...])
        k_sum_ref[...] += total
        grads.append(part.astype(BF16))
    for n in range(groups // 2):
        one = slice(2 * n * lanes, (2 * n + 1) * lanes)
        two = slice((2 * n + 1) * lanes, (2 * n + 2) * lanes)
        grads.append(jnp.where(first, dv_ref[:, one], dv_ref[:, two]).astype(BF16))
    grads = jnp.concatenate(grads, axis=1)
    grads_ref[...] = grads
    to_near = dot(grads, w_near_ref[...], NT)
    to_far = dot(grads, w_far_ref[...], NT)
    to_near_ref[...] = to_near.astype(BF16)
    to_far_ref[...] = to_far.astype(BF16)
    near = near_ref[...].astype(F32)
    far = far_ref[...].astype(F32)
    width = near.shape[1] + far.shape[1]
    total = jnp.sum(near * near, axis=1, keepdims=True) + jnp.sum(far * far, axis=1, keepdims=True)
    inverse = lax.rsqrt(total / width + EPSILON)
    near = to_near * (near * inverse)
    far = to_far * (far * inverse)
    near_sum_ref[...] += jnp.sum(near, axis=0, keepdims=True)
    far_sum_ref[...] += jnp.sum(far, axis=0, keepdims=True)
    stat = jnp.sum(near * gain_near_ref[...], axis=1, keepdims=True) + jnp.sum(far * gain_far_ref[...], axis=1, keepdims=True)
    stat_ref[...] = jnp.broadcast_to(stat, stat_ref.shape)


def project_back(dq, dk, dv, raw, near, far, gain_near, gain_far, w_near, w_far, q_gain, k_gain, cosine, sine, rows=512):
    packed, half = near.shape
    columns = w_near.shape[1]
    groups = columns // (4 * HEAD_SIZE)
    width = groups * 2 * HEAD_SIZE
    rows = min(rows, packed)

    def tile(n):
        return pl.BlockSpec((rows, n), lambda i: (i, 0))

    def whole(x):
        return pl.BlockSpec(x.shape, lambda i: (0, 0))

    def kept(n):
        return pl.BlockSpec((1, n), lambda i: (0, 0))

    def out(n, dtype, many=packed):
        return jax.ShapeDtypeStruct((many, n), dtype)

    small = (gain_near, gain_far, w_near, w_far, q_gain, k_gain)
    lanes = 2 * HEAD_SIZE
    return pl.pallas_call(
        functools.partial(project_back_kernel, groups),
        out_shape=(out(columns, BF16), out(half, BF16), out(half, BF16), out(lanes, F32), out(lanes, F32, 1), out(lanes, F32, 1),
                   out(half, F32, 1), out(half, F32, 1)),
        grid=(packed // rows,),
        in_specs=[tile(width), tile(width), tile(width), tile(raw.shape[1]), tile(half), tile(half), *map(whole, small),
                  tile(lanes), tile(lanes)],
        out_specs=(tile(columns), tile(half), tile(half), tile(lanes), kept(lanes), kept(lanes), kept(half), kept(half)),
        compiler_params=pltpu.CompilerParams(vmem_limit_bytes=44 << 20),
        cost_estimate=pl.CostEstimate(flops=4 * packed * half * columns, transcendentals=packed * 8,
                                      bytes_accessed=packed * (8 * half + 18 * width)),
        name="project_back",
    )(dq, dk, dv, raw, near, far, *small, cosine, sine)


def layout(lengths, packed):
    count = lengths.shape[0]
    numbers = jnp.arange(count, dtype=jnp.int32)
    ends = jnp.sum(jnp.where(numbers[None, :] <= numbers[:, None], lengths[None, :], 0), axis=1)
    begins = ends - lengths
    places = jnp.arange(packed, dtype=jnp.int32)
    member = jnp.sum((places[:, None] >= ends[None, :]).astype(jnp.int32), axis=1)
    return jnp.sum(jnp.where(member[:, None] == numbers[None, :], begins[None, :], 0), axis=1)


def rope_tables(position):
    half = HEAD_SIZE // 2
    inverse = jnp.exp(jnp.arange(half, dtype=F32) * (-2.0 * math.log(ROPE_BASE) / HEAD_SIZE))
    angles = position.astype(F32)[:, None] * inverse[None, :]
    cosine, sine = jnp.cos(angles), jnp.sin(angles)
    return jnp.concatenate([cosine] * 4, axis=1), jnp.concatenate([-sine, sine] * 2, axis=1)


def swap(x, axis):
    return jax.tree.map(lambda part: lax.ppermute(part, axis, [(0, 1), (1, 0)]), x)


def ordered(own, other, index, axis=0):
    return jnp.where(index == 0, jnp.concatenate([own, other], axis), jnp.concatenate([other, own], axis))


def part_of(x, index, axis, parts=2):
    size = x.shape[axis] // parts
    return lax.dynamic_slice_in_dim(x, index * size, size, axis)


def over_t(left, right):
    return dot(left, right, (((0,), (0,)), ((), ())))


def shards(
    tokens,
    seq_lengths,
    query_weight,
    key_matrix,
    value_matrix,
    out_weight,
    gate_weight,
    up_weight,
    down_weight,
    attn_gain,
    ffn_gain,
    query_gain,
    key_gain,
    cotangent,
):
    packed, half = tokens.shape
    row, col, group = lax.axis_index("row"), lax.axis_index("col"), lax.axis_index("dp")
    parts = lax.axis_size("dp")
    width = 2 * half

    near_own = part_of(tokens, col, 0)
    far_own = swap(near_own, "row")
    qkv = jnp.concatenate(
        [part_of(w, row, 1) for w in (query_weight, key_matrix, value_matrix)], axis=1)
    qkv_sent = jnp.concatenate(
        [part_of(w, 1 - row, 1) for w in (query_weight, key_matrix, value_matrix)], axis=1)
    qkv_far = swap(qkv_sent, "row")
    gains = jnp.stack([attn_gain, ffn_gain])
    gains_far = swap(gains, "row")
    far_other = swap(far_own, "col")
    far = ordered(far_own, far_other, col)
    cot_own = part_of(cotangent, col, 0)

    def far_weight(sent):
        piece = swap(part_of(sent, group, 0, parts), "row")
        return lax.all_gather(piece, "dp", axis=0, tiled=True)

    gate_up_near = jnp.concatenate([part_of(gate_weight, row, 1), part_of(up_weight, row, 1)], axis=1)
    gate_up_far = far_weight(jnp.concatenate([part_of(gate_weight, 1 - row, 1), part_of(up_weight, 1 - row, 1)], axis=1))
    down_near = part_of(down_weight, row, 0)
    down_far = far_weight(part_of(down_weight, 1 - row, 0))
    units = down_near.shape[0]

    out_far = swap(out_weight, "row")
    out_c = jnp.concatenate([out_weight, out_far], axis=1)
    out_n = swap(out_c, "col")
    out_own = part_of(out_c, row, 0)
    out_all = jnp.concatenate(
        [out_own, part_of(out_n, row, 0), part_of(out_c, 1 - row, 0), part_of(out_n, 1 - row, 0)], axis=0)

    cot_far_own = swap(cot_own, "row")
    cot_o = swap(jnp.concatenate([cot_own, cot_far_own], axis=1), "col")
    cot_c = jnp.concatenate([cot_own, cot_far_own], axis=1)

    starts = layout(seq_lengths[0], packed)
    cosine, sine = rope_tables(jnp.arange(packed, dtype=jnp.int32) - starts)
    q_gain = jnp.tile(query_gain, 2)[None, :]
    k_gain = jnp.tile(key_gain, 2)[None, :]
    small = (attn_gain[None, :], gains_far[0][None, :], qkv, qkv_far, q_gain, k_gain)
    hid_near, hid_far, raw, q, k, v = project(tokens, far, *small, cosine, sine)
    low, attended_raw, totals = attend(q, k, v, starts)

    chip = jnp.concatenate([part_of(low, col, 0), swap(part_of(low, 1 - col, 0), "col")], axis=1)
    attended = jnp.concatenate([chip, swap(chip, "row")], axis=1)
    mine = jnp.concatenate([near_own, far_own], axis=1)
    middle = mine.astype(F32) + dot(attended, out_all)
    inverse_two = lax.rsqrt(jnp.sum(middle * middle, axis=1, keepdims=True) / width + EPSILON)
    normal_two = middle * inverse_two
    gain_two = jnp.concatenate([ffn_gain, gains_far[1]])[None, :]
    hidden_c = (normal_two * gain_two).astype(BF16)
    hidden_o = swap(hidden_c, "col")
    gate_up = jnp.concatenate([gate_up_near, gate_up_far], axis=0)
    down = jnp.concatenate([down_near, down_far], axis=1)

    def feed(hidden, cot):
        both = dot(hidden, gate_up)
        grad_active = dot(cot, down, NT)
        gate, upward = both[:, :units], both[:, units:]
        sig = 1.0 / (1.0 + jnp.exp(-gate))
        lifted = gate * sig
        active = (lifted * upward).astype(BF16)
        grad_gate = (grad_active * upward * (sig * (1.0 + gate * (1.0 - sig)))).astype(BF16)
        grad_up = (grad_active * lifted).astype(BF16)
        return active, jnp.concatenate([grad_gate, grad_up], axis=1)

    active_o, grads_o = feed(hidden_o, cot_o)
    active_c, grads_c = feed(hidden_c, cot_c)
    back_o = swap(dot(grads_o, gate_up, NT).astype(BF16), "col")
    back_c = dot(grads_c, gate_up, NT) + back_o.astype(F32)
    back_low = back_c.astype(BF16)
    grad_hidden = back_c + jnp.concatenate(swap((back_low[:, half:], back_low[:, :half]), "row"), axis=1).astype(F32)

    grad_down = over_t(active_c, cot_c) + over_t(active_o, cot_o)
    grad_gate_up = over_t(hidden_c, grads_c) + over_t(hidden_o, grads_o)

    result_o = swap(dot(active_o, down).astype(BF16), "col")
    result_c = dot(active_c, down) + result_o.astype(F32)
    result = middle[:, :half] + result_c[:, :half] + swap(result_c[:, half:].astype(BF16), "row").astype(F32)
    result = result.astype(BF16)
    output = ordered(result, swap(result, "col"), col)

    ffn_gain_sum = jnp.sum(grad_hidden * normal_two, axis=0)
    inner = grad_hidden * gain_two
    stat = jnp.sum(inner * normal_two, axis=1, keepdims=True) / width
    grad_middle = cot_c.astype(F32) + inverse_two * (inner - normal_two * stat)
    branch_c = grad_middle.astype(BF16)
    branch_o = swap(branch_c, "col")
    grad_attended = ordered(dot(branch_c, out_own, NT).astype(BF16), dot(branch_o, out_own, NT).astype(BF16), col)
    grad_out = over_t(attended, branch_c[:, :half])
    quarter = grad_out.shape[0] // 4
    kept = jnp.concatenate([grad_out[:quarter], grad_out[2 * quarter:3 * quarter]], axis=0)
    sent = jnp.concatenate([grad_out[quarter:2 * quarter], grad_out[3 * quarter:]], axis=0)
    grad_out = kept + swap(sent.astype(BF16), "col").astype(F32)
    grad_out = ordered(grad_out[:quarter], grad_out[quarter:], row).astype(BF16)

    dq, dk, dv = attend_back(q, k, v, grad_attended, attended_raw, totals, starts)
    grads, to_near, to_far, stat_one, q_sum, k_sum, near_sum, far_sum = project_back(
        dq, dk, dv, raw, tokens, far, *small, cosine, sine)
    grad_qkv = jnp.concatenate([over_t(hid_near, grads), over_t(hid_far, grads)], axis=0)

    to_all = jnp.concatenate([to_near, to_far], axis=1)
    stat_one = stat_one[:, 0]
    sent_o, sent_stat = swap((part_of(to_all, 1 - col, 0), part_of(stat_one, 1 - col, 0)), "col")
    chip_sum = part_of(to_all, col, 0).astype(F32) + sent_o.astype(F32)
    chip_stat = part_of(stat_one, col, 0) + sent_stat
    other_sum, other_stat = swap((chip_sum[:, half:].astype(BF16), chip_stat), "row")
    inner_one = (chip_sum[:, :half] + other_sum.astype(F32)) * attn_gain[None, :]
    mine = mine.astype(F32)
    inverse_one = lax.rsqrt(jnp.sum(mine * mine, axis=1, keepdims=True) / width + EPSILON)
    stat_one = (chip_stat + other_stat)[:, None] / width
    grad_inputs = inverse_one * (inner_one - mine[:, :half] * inverse_one * stat_one) + grad_middle[:, :half]
    grad_inputs = grad_inputs.astype(BF16)
    grad_tokens = ordered(grad_inputs, swap(grad_inputs, "col"), col)

    def reduced(x, axis):
        return lax.psum_scatter(x, "dp", scatter_dimension=axis, tiled=True)

    def gathered(x, axis):
        return lax.all_gather(x, "dp", axis=axis, tiled=True)

    def columns_split(grad):
        piece = reduced(grad.astype(BF16).reshape(2, half, -1), 1)
        other = swap(piece[1], "row")
        full = gathered(ordered(piece[0][None], other[None], row), 1)
        return full.astype(F32)

    def rows_split(grad):
        piece = reduced(grad.astype(BF16), 0)
        other = swap(piece[:, half:], "row")
        full = gathered(ordered(piece[:, :half][None], other[None], row), 1)
        return full.astype(F32).reshape(-1, half)

    def side(full, begin, end):
        return jnp.concatenate([full[0][:, begin:end], full[1][:, begin:end]], axis=1)

    down_full = rows_split(grad_down)
    gate_up_full = columns_split(grad_gate_up)
    qkv_full = columns_split(grad_qkv)
    out_full = lax.psum(grad_out, "dp").astype(F32)
    q_cols, k_cols = query_weight.shape[1] // 2, key_matrix.shape[1] // 2

    def slots(x_near, x_far):
        return ordered(x_near, x_far, row)

    def folded(x):
        return x[0, :HEAD_SIZE] + x[0, HEAD_SIZE:]

    ffn_slots = slots(ffn_gain_sum[:half], ffn_gain_sum[half:]) * 0.5
    sums = lax.psum(
        jnp.concatenate([slots(near_sum[0], far_sum[0]), ffn_slots, folded(q_sum), folded(k_sum)]), ("dp", "row", "col"))
    attn_sum = part_of(sums[:width], row, 0)
    ffn_sum = part_of(sums[width:2 * width], row, 0)
    return (
        output,
        grad_tokens,
        side(qkv_full, 0, q_cols),
        side(qkv_full, q_cols, q_cols + k_cols),
        side(qkv_full, q_cols + k_cols, q_cols + 2 * k_cols),
        out_full,
        side(gate_up_full, 0, units),
        side(gate_up_full, units, 2 * units),
        down_full,
        attn_sum,
        ffn_sum,
        sums[2 * width:2 * width + HEAD_SIZE],
        sums[2 * width + HEAD_SIZE:],
    )


def solution(mesh):
    return jax.shard_map(
        shards,
        mesh=mesh,
        in_specs=(
            P("dp", "row"),
            P("dp", None),
            P("row", "col"),
            P("row", "col"),
            P("row", "col"),
            P("col", "row"),
            P("row", "col"),
            P("row", "col"),
            P("col", "row"),
            P("row"),
            P("row"),
            P(),
            P(),
            P("dp", "row"),
        ),
        out_specs=(
            P("dp", "row"),
            P("dp", "row"),
            P("row", "col"),
            P("row", "col"),
            P("row", "col"),
            P("col", "row"),
            P("row", "col"),
            P("row", "col"),
            P("col", "row"),
            P("row"),
            P("row"),
            P(),
            P(),
        ),
        check_vma=False,
    )
```

```python
import functools
import math

import jax
import jax.numpy as jnp
from jax import lax
from jax.experimental import pallas as pl
from jax.experimental.pallas import tpu as pltpu
from jax.sharding import PartitionSpec as P

HEAD_SIZE = 64
EPSILON = 1e-05
ROPE_BASE = 1000000.0
F32, BF16 = jnp.float32, jnp.bfloat16
MESH = pl.DeviceIdType.MESH


def dot(a, b, dims=(((1,), (0,)), ((), ()))):
    return lax.dot_general(a, b, dims, preferred_element_type=F32)


NT = (((1,), (1,)), ((), ()))

def stacked(x):
    first = lax.broadcasted_iota(jnp.int32, x.shape, 1) < 64
    zero = jnp.zeros_like(x)
    return jnp.concatenate([jnp.where(first, x, zero), jnp.where(first, zero, x)], axis=0)

def attend_kernel(bq, bk, first_ref, last_ref, q_ref, k_ref, v_ref, start_ref, low_ref, raw_ref, lse_ref, acc_ref, mass_ref):
    i = pl.program_id(1)
    qs = stacked(q_ref[...])
    starts = start_ref[...]
    starts = jnp.concatenate([starts, starts], axis=0)
    acc_ref[...] = jnp.zeros_like(acc_ref)
    mass_ref[...] = jnp.zeros_like(mass_ref)
    rows = i * bq + lax.rem(lax.broadcasted_iota(jnp.int32, (2 * bq, 1), 0), bq)

    def step(j, masked):
        k0 = pl.multiple_of(j * bk, bk)
        s = dot(qs, k_ref[pl.ds(k0, bk), :], NT)
        p = jnp.exp(s)
        if masked:
            cols = j * bk + lax.broadcasted_iota(jnp.int32, (1, bk), 1)
            p = jnp.where((cols <= rows) & (cols >= starts), p, 0.0)
        mass = p[:, :128]
        for n in range(1, bk // 128):
            mass = mass + p[:, n * 128:(n + 1) * 128]
        mass_ref[...] += mass
        acc_ref[...] += dot(p.astype(BF16), v_ref[pl.ds(k0, bk), :])

    low = first_ref[i] // bk
    clear = jnp.maximum((last_ref[i] + bk - 1) // bk, low)
    diagonal = (i * bq) // bk
    end = ((i + 1) * bq + bk - 1) // bk
    clear = jnp.minimum(clear, diagonal)

    @pl.loop(low, clear)
    def _(j):
        step(j, True)

    @pl.loop(clear, diagonal)
    def _(j):
        step(j, False)

    @pl.loop(diagonal, end)
    def _(j):
        step(j, True)

    mass = jnp.sum(mass_ref[...], axis=1, keepdims=True)
    out = acc_ref[...] / mass
    first = lax.broadcasted_iota(jnp.int32, (bq, 128), 1) < 64
    out = jnp.where(first, out[:bq], out[bq:])
    raw_ref[...] = out
    low_ref[...] = out.astype(BF16)
    total = jnp.log(jnp.sum(mass_ref[...].T, axis=0, keepdims=True))
    lse_ref[0, 0:1, :] = total[:, :bq]
    lse_ref[0, 1:2, :] = total[:, bq:]

def attend(q, k, v, starts, group, bq=512, bk=512):
    T, width = q.shape[0], 128
    groups = 1
    first, last = starts[::bq], starts[bq - 1::bq]
    kern = functools.partial(attend_kernel, bq, bk)
    pairs = T * (T + bk) // 2
    return pl.pallas_call(
        kern,
        out_shape=(jax.ShapeDtypeStruct((T, width), BF16), jax.ShapeDtypeStruct((T, width), F32),
                   jax.ShapeDtypeStruct((groups, 2, T), F32)),
        grid_spec=pltpu.PrefetchScalarGridSpec(
            num_scalar_prefetch=2, grid=(groups, T // bq),
            in_specs=[
                pl.BlockSpec((bq, 128), lambda g, i, *_: (i, group)),
                pl.BlockSpec((T, 128), lambda g, i, *_: (0, group)),
                pl.BlockSpec((T, 128), lambda g, i, *_: (0, group)),
                pl.BlockSpec((bq, 1), lambda g, i, *_: (i, 0)),
            ],
            out_specs=[
                pl.BlockSpec((bq, 128), lambda g, i, *_: (i, g)),
                pl.BlockSpec((bq, 128), lambda g, i, *_: (i, g)),
                pl.BlockSpec((1, 2, bq), lambda g, i, *_: (g, 0, i)),
            ],
            scratch_shapes=[pltpu.VMEM((2 * bq, 128), F32), pltpu.VMEM((2 * bq, 128), F32)],
        ),
        compiler_params=pltpu.CompilerParams(vmem_limit_bytes=40 << 20),
        cost_estimate=pl.CostEstimate(flops=4 * groups * 2 * pairs * 256, transcendentals=2 * groups * pairs,
                                      bytes_accessed=10 * T * width),
        name="attend",
    )(first, last, q, k, v, starts[:, None])

def attend_back_kernel(b, T, first_ref, last_ref, q_ref, k_ref, v_ref, grad_ref, raw_ref, lse_ref, start_ref,
                       dq_ref, dk_ref, dv_ref, qs_ref, gs_ref, stat_ref, dqt_ref, dk_acc, dv_acc):
    j = pl.program_id(1)
    blocks = T // b

    @pl.when(j == 0)
    def _():
        dqt_ref[...] = jnp.zeros_like(dqt_ref)
        for i in range(blocks):
            rows = slice(i * b, (i + 1) * b)
            both = slice(i * 2 * b, (i + 1) * 2 * b)
            qs_ref[both, :] = stacked(q_ref[rows, :])
            grad = grad_ref[rows, :]
            gs_ref[both, :] = stacked(grad)
            prod = (grad.astype(F32) * raw_ref[rows, :]).T
            stat_ref[i, 0:1, 0:b] = lse_ref[0, 0:1, rows]
            stat_ref[i, 0:1, b:2 * b] = lse_ref[0, 1:2, rows]
            stat_ref[i, 1:2, 0:b] = jnp.sum(prod[:64], axis=0, keepdims=True)
            stat_ref[i, 1:2, b:2 * b] = jnp.sum(prod[64:], axis=0, keepdims=True)

    k = k_ref[...]
    v = v_ref[...]
    kt = k.T[:64]
    dk_acc[...] = jnp.zeros_like(dk_acc)
    dv_acc[...] = jnp.zeros_like(dv_acc)
    keys = j * b + lax.broadcasted_iota(jnp.int32, (b, 1), 0)

    def step(i, masked):
        at = pl.ds(pl.multiple_of(i * 2 * b, 2 * b), 2 * b)
        qs = qs_ref[at, :]
        gs = gs_ref[at, :]
        st = dot(k, qs, NT)
        pt = jnp.exp(st - stat_ref[i, 0:1, :])
        if masked:
            cols = i * b + lax.rem(lax.broadcasted_iota(jnp.int32, (1, 2 * b), 1), b)
            begin = start_ref[0:1, pl.ds(pl.multiple_of(i * b, b), b)]
            begin = jnp.concatenate([begin, begin], axis=1)
            pt = jnp.where((keys <= cols) & (keys >= begin), pt, 0.0)
        dv_acc[...] += dot(pt.astype(BF16), gs)
        dpt = dot(v, gs, NT)
        dst = (pt * (dpt - stat_ref[i, 1:2, :])).astype(BF16)
        dk_acc[...] += dot(dst, qs)
        part = dot(kt, dst)
        to = pl.ds(pl.multiple_of(i * b, b), b)
        dqt_ref[0:64, to] += part[:, :b]
        dqt_ref[64:128, to] += part[:, b:]

    step(j, True)

    @pl.loop(j + 1, blocks)
    def _(i):
        whole = last_ref[i] <= j * b
        none = first_ref[i] >= (j + 1) * b

        @pl.when(whole)
        def _():
            step(i, False)

        @pl.when(jnp.logical_not(whole | none))
        def _():
            step(i, True)

    dk = dk_acc[...]
    dv = dv_acc[...]
    dk_ref[...] = dk + pltpu.roll(dk, 64, 1)
    dv_ref[...] = dv + pltpu.roll(dv, 64, 1)
    dq_ref[...] = dqt_ref[:, pl.ds(pl.multiple_of(j * b, b), b)].T * 0.125

def attend_back(q, k, v, grad, raw, lse, starts, group, b=512):
    T, width = q.shape[0], 128
    groups = 1
    first, last = starts[::b], starts[b - 1::b]
    blocks = T // b
    own = pl.BlockSpec((T, 128), lambda g, j, *_: (0, 0))
    blk = pl.BlockSpec((b, 128), lambda g, j, *_: (j, 0))
    col = pl.BlockSpec((T, 128), lambda g, j, *_: (0, group))
    part = pl.BlockSpec((b, 128), lambda g, j, *_: (j, group))
    out = jax.ShapeDtypeStruct((T, width), F32)
    pairs = T * (T + b) // 2
    return pl.pallas_call(
        functools.partial(attend_back_kernel, b, T),
        out_shape=(out, out, out),
        grid_spec=pltpu.PrefetchScalarGridSpec(
            num_scalar_prefetch=2, grid=(groups, blocks),
            in_specs=[col, part, part, col, own,
                      pl.BlockSpec((1, 2, T), lambda g, j, *_: (g, 0, 0)),
                      pl.BlockSpec((1, T), lambda g, j, *_: (0, 0))],
            out_specs=[blk, blk, blk],
            scratch_shapes=[pltpu.VMEM((2 * T, 128), BF16), pltpu.VMEM((2 * T, 128), BF16),
                            pltpu.VMEM((blocks, 2, 2 * b), F32), pltpu.VMEM((128, T), F32),
                            pltpu.VMEM((b, 128), F32), pltpu.VMEM((b, 128), F32)],
        ),
        compiler_params=pltpu.CompilerParams(vmem_limit_bytes=48 << 20),
        cost_estimate=pl.CostEstimate(flops=10 * groups * 2 * pairs * 256, transcendentals=2 * groups * pairs,
                                      bytes_accessed=20 * T * width),
        name="attend_back",
    )(first, last, q, k, v, grad, raw, lse, starts[None, :])


def head_sums(x):
    first = lax.broadcasted_iota(jnp.int32, x.shape, 1) < HEAD_SIZE
    one = jnp.sum(jnp.where(first, x, 0.0), axis=1, keepdims=True)
    two = jnp.sum(jnp.where(first, 0.0, x), axis=1, keepdims=True)
    return jnp.where(first, one, two)


def swapped(x):
    low = lax.rem(lax.broadcasted_iota(jnp.int32, x.shape, 1), HEAD_SIZE) < HEAD_SIZE // 2
    return jnp.where(low, pltpu.roll(x, 96, 1), pltpu.roll(x, 32, 1))


def doubled(x):
    first = lax.broadcasted_iota(jnp.int32, x.shape, 1) < HEAD_SIZE
    other = pltpu.roll(x, HEAD_SIZE, 1)
    return jnp.where(first, x, other), jnp.where(first, other, x)


def project_kernel(groups, near_ref, far_ref, gain_near_ref, gain_far_ref, w_near_ref, w_far_ref, q_gain_ref, k_gain_ref,
                   cos_ref, sin_ref, hid_near_ref, hid_far_ref, raw_ref, q_ref, k_ref, v_ref):
    near = near_ref[...].astype(F32)
    far = far_ref[...].astype(F32)
    width = near.shape[1] + far.shape[1]
    total = jnp.sum(near * near, axis=1, keepdims=True) + jnp.sum(far * far, axis=1, keepdims=True)
    inverse = lax.rsqrt(total / width + EPSILON)
    hid_near = (near * inverse * gain_near_ref[...]).astype(BF16)
    hid_far = (far * inverse * gain_far_ref[...]).astype(BF16)
    hid_near_ref[...] = hid_near
    hid_far_ref[...] = hid_far
    raw = dot(hid_near, w_near_ref[...]) + dot(hid_far, w_far_ref[...])
    cosine, sine = cos_ref[...], sin_ref[...]

    def prepared(x, gain):
        normed = x * lax.rsqrt(head_sums(x * x) / HEAD_SIZE + EPSILON) * gain
        return normed * cosine + swapped(normed) * sine

    lanes = 2 * HEAD_SIZE
    kv = groups * HEAD_SIZE
    raw_ref[...] = raw[:, :groups * lanes + kv]
    for n in range(groups):
        cut = slice(n * lanes, (n + 1) * lanes)
        q_ref[:, cut] = (prepared(raw[:, cut], q_gain_ref[...]).astype(BF16) * HEAD_SIZE ** (-0.5)).astype(BF16)
    for n in range(groups // 2):
        at = groups * lanes + n * lanes
        twice = doubled(prepared(raw[:, at:at + lanes], k_gain_ref[...]))
        for m in range(2):
            k_ref[:, (2 * n + m) * lanes:(2 * n + m + 1) * lanes] = twice[m].astype(BF16)
        at += kv
        twice = doubled(raw[:, at:at + lanes])
        for m in range(2):
            v_ref[:, (2 * n + m) * lanes:(2 * n + m + 1) * lanes] = twice[m].astype(BF16)


def project(near, far, gain_near, gain_far, w_near, w_far, q_gain, k_gain, cosine, sine, rows=512):
    packed, half = near.shape
    columns = w_near.shape[1]
    groups = columns // (4 * HEAD_SIZE)
    width = groups * 2 * HEAD_SIZE
    kv = groups * HEAD_SIZE
    rows = min(rows, packed)

    def tile(n):
        return pl.BlockSpec((rows, n), lambda i: (i, 0))

    def whole(x):
        return pl.BlockSpec(x.shape, lambda i: (0, 0))

    def out(n, dtype):
        return jax.ShapeDtypeStruct((packed, n), dtype)

    small = (gain_near, gain_far, w_near, w_far, q_gain, k_gain)
    return pl.pallas_call(
        functools.partial(project_kernel, groups),
        out_shape=(out(half, BF16), out(half, BF16), out(width + kv, F32), out(width, BF16), out(width, BF16), out(width, BF16)),
        grid=(packed // rows,),
        in_specs=[tile(half), tile(half), *map(whole, small), tile(2 * HEAD_SIZE), tile(2 * HEAD_SIZE)],
        out_specs=(tile(half), tile(half), tile(width + kv), tile(width), tile(width), tile(width)),
        compiler_params=pltpu.CompilerParams(vmem_limit_bytes=40 << 20),
        cost_estimate=pl.CostEstimate(flops=4 * packed * half * columns, transcendentals=packed * 8,
                                      bytes_accessed=packed * (8 * half + 10 * width)),
        name="project",
    )(near, far, *small, cosine, sine)


def project_back_kernel(groups, *refs):
    dq, dk, dv = refs[:groups], refs[groups:2 * groups], refs[2 * groups:3 * groups]
    project_back_body(groups, dq, dk, dv, *refs[3 * groups:])


def project_back_body(groups, dq_refs, dk_refs, dv_refs, raw_ref, near_ref, far_ref, gain_near_ref, gain_far_ref,
                        w_near_ref, w_far_ref, q_gain_ref, k_gain_ref, cos_ref, sin_ref,
                        grads_ref, to_near_ref, to_far_ref, stat_ref, q_sum_ref, k_sum_ref, near_sum_ref, far_sum_ref):
    @pl.when(pl.program_id(0) == 0)
    def _():
        for ref in (q_sum_ref, k_sum_ref, near_sum_ref, far_sum_ref):
            ref[...] = jnp.zeros_like(ref)

    cosine, sine = cos_ref[...], sin_ref[...]
    lanes = 2 * HEAD_SIZE
    first = lax.broadcasted_iota(jnp.int32, cosine.shape, 1) < HEAD_SIZE

    def back(grad, x, gain):
        inverse = lax.rsqrt(head_sums(x * x) / HEAD_SIZE + EPSILON)
        normed = x * inverse
        turned = grad * cosine - swapped(grad) * sine
        inner = turned * gain
        part = inverse * (inner - normed * (head_sums(inner * normed) / HEAD_SIZE))
        return part, jnp.sum(turned * normed, axis=0, keepdims=True)

    grads = []
    for n in range(groups):
        cut = slice(n * lanes, (n + 1) * lanes)
        part, total = back(dq_refs[n][...], raw_ref[:, cut], q_gain_ref[...])
        q_sum_ref[...] += total
        grads.append(part.astype(BF16))
    for n in range(groups // 2):
        at = groups * lanes + n * lanes
        part, total = back(jnp.where(first, dk_refs[2 * n][...], dk_refs[2 * n + 1][...]), raw_ref[:, at:at + lanes], k_gain_ref[...])
        k_sum_ref[...] += total
        grads.append(part.astype(BF16))
    for n in range(groups // 2):
        grads.append(jnp.where(first, dv_refs[2 * n][...], dv_refs[2 * n + 1][...]).astype(BF16))
    grads = jnp.concatenate(grads, axis=1)
    grads_ref[...] = grads
    to_near = dot(grads, w_near_ref[...], NT)
    to_far = dot(grads, w_far_ref[...], NT)
    to_near_ref[...] = to_near.astype(BF16)
    to_far_ref[...] = to_far.astype(BF16)
    near = near_ref[...].astype(F32)
    far = far_ref[...].astype(F32)
    width = near.shape[1] + far.shape[1]
    total = jnp.sum(near * near, axis=1, keepdims=True) + jnp.sum(far * far, axis=1, keepdims=True)
    inverse = lax.rsqrt(total / width + EPSILON)
    near = to_near * (near * inverse)
    far = to_far * (far * inverse)
    near_sum_ref[...] += jnp.sum(near, axis=0, keepdims=True)
    far_sum_ref[...] += jnp.sum(far, axis=0, keepdims=True)
    stat = jnp.sum(near * gain_near_ref[...], axis=1, keepdims=True) + jnp.sum(far * gain_far_ref[...], axis=1, keepdims=True)
    stat_ref[...] = jnp.broadcast_to(stat, stat_ref.shape)


def project_back(dq, dk, dv, raw, near, far, gain_near, gain_far, w_near, w_far, q_gain, k_gain, cosine, sine, rows=512):
    packed, half = near.shape
    columns = w_near.shape[1]
    groups = columns // (4 * HEAD_SIZE)
    width = groups * 2 * HEAD_SIZE
    rows = min(rows, packed)

    def tile(n):
        return pl.BlockSpec((rows, n), lambda i: (i, 0))

    def whole(x):
        return pl.BlockSpec(x.shape, lambda i: (0, 0))

    def kept(n):
        return pl.BlockSpec((1, n), lambda i: (0, 0))

    def out(n, dtype, many=packed):
        return jax.ShapeDtypeStruct((many, n), dtype)

    small = (gain_near, gain_far, w_near, w_far, q_gain, k_gain)
    lanes = 2 * HEAD_SIZE
    return pl.pallas_call(
        functools.partial(project_back_kernel, groups),
        out_shape=(out(columns, BF16), out(half, BF16), out(half, BF16), out(lanes, F32), out(lanes, F32, 1), out(lanes, F32, 1),
                   out(half, F32, 1), out(half, F32, 1)),
        grid=(packed // rows,),
        in_specs=[tile(lanes)] * (3 * groups) + [tile(raw.shape[1]), tile(half), tile(half), *map(whole, small),
                  tile(lanes), tile(lanes)],
        out_specs=(tile(columns), tile(half), tile(half), tile(lanes), kept(lanes), kept(lanes), kept(half), kept(half)),
        compiler_params=pltpu.CompilerParams(vmem_limit_bytes=44 << 20),
        cost_estimate=pl.CostEstimate(flops=4 * packed * half * columns, transcendentals=packed * 8,
                                      bytes_accessed=packed * (8 * half + 18 * width)),
        name="project_back",
    )(*dq, *dk, *dv, raw, near, far, *small, cosine, sine)


def layout(lengths, packed):
    count = lengths.shape[0]
    numbers = jnp.arange(count, dtype=jnp.int32)
    ends = jnp.sum(jnp.where(numbers[None, :] <= numbers[:, None], lengths[None, :], 0), axis=1)
    begins = ends - lengths
    places = jnp.arange(packed, dtype=jnp.int32)
    member = jnp.sum((places[:, None] >= ends[None, :]).astype(jnp.int32), axis=1)
    return jnp.sum(jnp.where(member[:, None] == numbers[None, :], begins[None, :], 0), axis=1)


def rope_tables(position):
    half = HEAD_SIZE // 2
    inverse = jnp.exp(jnp.arange(half, dtype=F32) * (-2.0 * math.log(ROPE_BASE) / HEAD_SIZE))
    angles = position.astype(F32)[:, None] * inverse[None, :]
    cosine, sine = jnp.cos(angles), jnp.sin(angles)
    return jnp.concatenate([cosine] * 4, axis=1), jnp.concatenate([-sine, sine] * 2, axis=1)


def swap(x, axis):
    return jax.tree.map(lambda part: lax.ppermute(part, axis, [(0, 1), (1, 0)]), x)


def ordered(own, other, index, axis=0):
    return jnp.where(index == 0, jnp.concatenate([own, other], axis), jnp.concatenate([other, own], axis))


def part_of(x, index, axis, parts=2):
    size = x.shape[axis] // parts
    return lax.dynamic_slice_in_dim(x, index * size, size, axis)


def over_t(left, right):
    return dot(left, right, (((0,), (0,)), ((), ())))


def ring_kernel(n, names, plan, *refs):
    arrays = max(array for array, *_ in plan) + 1
    inputs, refs = refs[:arrays], refs[arrays:]
    gains_ref, give_ref, give_stat_ref, *refs = refs
    outs = max(out for _, _, _, out, _ in plan) + 1
    outputs, refs = refs[:outs], refs[outs:]
    (sums_ref, take_ref, take_stat_ref, *refs) = refs
    slots, refs = refs[:len(plan)], refs[len(plan):]
    (group_in, ring_in, mine, rs_send, rs_recv, ag_send, ag_recv, cross_send, cross_recv, group_send, group_recv,
     all_send, all_recv, give_send, give_recv) = refs
    dp, row, col = (lax.axis_index(name) for name in names)
    side = dp % 2
    place = (dp // 2) * (1 - side) + (n - 1 - dp // 2) * side

    def device(position):
        position = (position + 2 * n) % n
        back = position // (n // 2)
        return (position * (1 - back) + (n - 1 - position) * back) * 2 + back

    up, down = device(place + 1), device(place - 1)
    streams = range(len(plan))
    crossing = [s for s in streams if plan[s][4]]
    staying = [s for s in streams if not plan[s][4]]

    barrier = pltpu.get_barrier_semaphore()
    others = [((dp + k) % n, row, col) for k in range(1, n)]
    quad = [(dp, 1 - row, col), (dp, row, 1 - col), (dp, 1 - row, 1 - col)]
    for target in others + quad:
        pl.semaphore_signal(barrier, inc=1, device_id=target, device_id_type=MESH)
    pl.semaphore_wait(barrier, n + 2)

    def copy(src, dst, send, recv, target):
        return pltpu.make_async_remote_copy(
            src_ref=src, dst_ref=dst, send_sem=send, recv_sem=recv, device_id=target, device_id_type=MESH)

    def toward(s):
        return (up if s % 2 == 0 else down, row, col)

    def local(s, chunk):
        array, begin, columns, _, _ = plan[s]
        return inputs[array].at[chunk, :, pl.ds(begin, columns)]

    def result(s, chunk, quarter):
        _, begin, columns, out, _ = plan[s]
        if outputs[out].shape[0] == 1:
            quarter = 0
        return outputs[out].at[quarter, chunk, :, pl.ds(begin, columns)]

    def final(s, chunk):
        return result(s, chunk, 1 - row if plan[s][4] else row)

    def own(s):
        return (place + 1) % n if s % 2 == 0 else (place + n - 1) % n

    def reduce_copy(s, t, src):
        return copy(src, slots[s].at[t], rs_send.at[s, t], rs_recv.at[s, t], toward(s))

    for s in streams:
        reduce_copy(s, 0, local(s, place)).start()
    gathers = [copy(gains_ref, group_in.at[k], group_send.at[k], group_recv.at[k], quad[k]) for k in range(3)]
    for gather in gathers:
        gather.start()
    gives = [copy(give_ref, take_ref, give_send.at[0], give_recv.at[0], quad[0]),
             copy(give_stat_ref, take_stat_ref, give_send.at[1], give_recv.at[1], quad[0])]
    for give in gives:
        give.start()

    def reduce_step(t, carry):
        for s in streams:
            chunk = (place - t - 1 + 2 * n) % n if s % 2 == 0 else (place + t + 1) % n
            slot = slots[s].at[t]
            reduce_copy(s, t, slot).wait_recv()
            slot[...] = (slot[...].astype(F32) + local(s, chunk)[...].astype(F32)).astype(BF16)

            @pl.when(t < n - 2)
            def _():
                reduce_copy(s, t + 1, slot).start()
        return carry

    lax.fori_loop(0, n - 1, reduce_step, 0)

    crosses = [copy(slots[s].at[n - 2], result(s, own(s), row), cross_send.at[k], cross_recv.at[k], quad[0])
               for k, s in enumerate(crossing)]
    for cross in crosses:
        cross.start()

    def gather_copy(s, t, chunk):
        return copy(final(s, chunk), final(s, chunk), ag_send.at[s, t], ag_recv.at[s, t], toward(s))

    for s in staying:
        final(s, own(s))[...] = slots[s][n - 2]
        gather_copy(s, 0, own(s)).start()

    for gather in gathers:
        gather.wait()
    mine[...] = gains_ref[...] + group_in[0] + group_in[1] + group_in[2]
    spreads = [copy(mine, ring_in.at[k - 1], all_send.at[k - 1], all_recv.at[k - 1], others[k - 1]) for k in range(1, n)]
    for spread in spreads:
        spread.start()

    for k, s in enumerate(crossing):
        crosses[k].wait()
        gather_copy(s, 0, own(s)).start()

    def gather_step(t, carry):
        for s in staying + crossing:
            chunk = (place - t + 2 * n) % n if s % 2 == 0 else (place + t) % n
            gather_copy(s, t, chunk).wait_recv()

            @pl.when(t < n - 2)
            def _():
                gather_copy(s, t + 1, chunk).start()
        return carry

    lax.fori_loop(0, n - 1, gather_step, 0)

    total = mine[...]
    for spread in spreads:
        spread.wait()
    for k in range(n - 1):
        total = total + ring_in[k]
    sums_ref[...] = total
    for give in gives:
        give.wait()

    def finish(t, carry):
        for s in streams:
            reduce_copy(s, t, slots[s].at[t]).wait_send()
            gather_copy(s, t, 0).wait_send()
        return carry

    lax.fori_loop(0, n - 1, finish, 0)


def ring_sum(near, far, alone, gains, give, give_stat, names, n):
    inputs, plan, out_shape = [], [], []

    def lanes(k, x, out, crosses):
        columns = x.shape[2] // 2
        for begin in (0, columns):
            plan.append((k, begin, columns, out, crosses))

    for x in far:
        lanes(len(inputs), x, len(inputs), True)
        inputs.append(x)
    for out, x in enumerate(near):
        lanes(len(inputs), x, out, False)
        inputs.append(x)
        out_shape.append(jax.ShapeDtypeStruct((2, *x.shape), BF16))
    for x in alone:
        lanes(len(inputs), x, len(out_shape), False)
        inputs.append(x)
        out_shape.append(jax.ShapeDtypeStruct((1, *x.shape), BF16))
    out_shape += [jax.ShapeDtypeStruct(gains.shape, F32), jax.ShapeDtypeStruct(give.shape, give.dtype),
                  jax.ShapeDtypeStruct(give_stat.shape, F32)]
    vmem = pl.BlockSpec(memory_space=pltpu.VMEM)
    dma = pltpu.SemaphoreType.DMA
    many, crosses = len(plan), 2 * len(far)
    size = sum(x.size for x in inputs)
    slots = [pltpu.VMEM((n - 1, inputs[array].shape[1], columns), BF16) for array, _, columns, _, _ in plan]
    return pl.pallas_call(
        functools.partial(ring_kernel, n, names, tuple(plan)),
        out_shape=tuple(out_shape),
        in_specs=[vmem] * (len(inputs) + 3),
        out_specs=(vmem,) * len(out_shape),
        scratch_shapes=[
            *slots, pltpu.VMEM((3, *gains.shape), F32),
            pltpu.VMEM((n - 1, *gains.shape), F32), pltpu.VMEM(gains.shape, F32),
            dma((many, n - 1)), dma((many, n - 1)), dma((many, n - 1)), dma((many, n - 1)), dma((crosses,)), dma((crosses,)),
            dma((3,)), dma((3,)), dma((n - 1,)), dma((n - 1,)), dma((2,)), dma((2,)),
        ],
        compiler_params=pltpu.CompilerParams(collective_id=0, has_side_effects=True, vmem_limit_bytes=58 << 20),
        cost_estimate=pl.CostEstimate(flops=4 * size, transcendentals=0, bytes_accessed=60 * size),
        name="ring_sum",
    )(*inputs, gains, give, give_stat)


def gated(x, *deps):
    late = functools.reduce(jnp.logical_or, [dep != dep for dep in deps])
    return jnp.where(late, jnp.zeros_like(x), x)


def corner(x):
    return x[(0,) * x.ndim].astype(F32)


def shards(
    tokens,
    seq_lengths,
    query_weight,
    key_matrix,
    value_matrix,
    out_weight,
    gate_weight,
    up_weight,
    down_weight,
    attn_gain,
    ffn_gain,
    query_gain,
    key_gain,
    cotangent,
):
    packed, half = tokens.shape
    row, col, group = lax.axis_index("row"), lax.axis_index("col"), lax.axis_index("dp")
    parts = lax.axis_size("dp")
    width = 2 * half

    near_own = part_of(tokens, col, 0)
    far_own = swap(near_own, "row")
    qkv = jnp.concatenate(
        [part_of(w, row, 1) for w in (query_weight, key_matrix, value_matrix)], axis=1)
    qkv_sent = jnp.concatenate(
        [part_of(w, 1 - row, 1) for w in (query_weight, key_matrix, value_matrix)], axis=1)
    qkv_far = swap(qkv_sent, "row")
    gains = jnp.stack([attn_gain, ffn_gain])
    gains_far = swap(gains, "row")
    far = ordered(far_own, swap(far_own, "col"), col)

    def far_weight(sent):
        piece = swap(gated(part_of(sent, group, 0, parts), corner(far_own)), "row")
        return lax.all_gather(piece, "dp", axis=0, tiled=True), corner(piece)

    gate_up_near = jnp.concatenate([part_of(gate_weight, row, 1), part_of(up_weight, row, 1)], axis=1)
    gate_up_far, sign_one = far_weight(
        jnp.concatenate([part_of(gate_weight, 1 - row, 1), part_of(up_weight, 1 - row, 1)], axis=1))
    down_near = part_of(down_weight, row, 0)
    down_far, sign_two = far_weight(part_of(down_weight, 1 - row, 0))
    units = down_near.shape[0]

    out_far = swap(gated(out_weight, sign_one, sign_two), "row")
    out_c = jnp.concatenate([out_weight, out_far], axis=1)
    out_n = swap(out_c, "col")
    out_own = part_of(out_c, row, 0)
    out_all = jnp.concatenate(
        [out_own, part_of(out_n, row, 0), part_of(out_c, 1 - row, 0), part_of(out_n, 1 - row, 0)], axis=0)

    cot_own = part_of(cotangent, col, 0)
    cot_far_own = swap(gated(cot_own, corner(out_far)), "row")
    cot_c = jnp.concatenate([cot_own, cot_far_own], axis=1)
    cot_o = swap(cot_c, "col")

    starts = layout(seq_lengths[0], packed)
    cosine, sine = rope_tables(jnp.arange(packed, dtype=jnp.int32) - starts)
    q_gain = jnp.tile(query_gain, 2)[None, :]
    k_gain = jnp.tile(key_gain, 2)[None, :]
    small = (attn_gain[None, :], gains_far[0][None, :], qkv, qkv_far, q_gain, k_gain)
    hid_near, hid_far, raw, q, k, v = project(tokens, far, *small, cosine, sine)

    groups = q.shape[1] // (2 * HEAD_SIZE)
    attended, raws, totals = [], [], []
    for n in range(groups):
        low, attended_raw, total = attend(q, k, v, starts, n)
        raws.append(attended_raw)
        totals.append(total)
        chip = jnp.concatenate([part_of(low, col, 0), swap(part_of(low, 1 - col, 0), "col")], axis=1)
        attended.append(jnp.concatenate([chip, swap(chip, "row")], axis=1))
    size = out_own.shape[0] // groups

    def group_rows(n):
        quarter = out_own.shape[0]
        return jnp.concatenate([out_all[p * quarter + n * size:p * quarter + (n + 1) * size] for p in range(4)], axis=0)

    mine = jnp.concatenate([near_own, far_own], axis=1)
    middle = mine.astype(F32)
    for n in range(groups):
        middle = middle + dot(attended[n], group_rows(n))
    inverse_two = lax.rsqrt(jnp.sum(middle * middle, axis=1, keepdims=True) / width + EPSILON)
    normal_two = middle * inverse_two
    gain_two = jnp.concatenate([ffn_gain, gains_far[1]])[None, :]
    hidden_c = (normal_two * gain_two).astype(BF16)
    hidden_o = swap(hidden_c, "col")
    gate_up = jnp.concatenate([gate_up_near, gate_up_far], axis=0)
    down = jnp.concatenate([down_near, down_far], axis=1)

    def feed(hidden, cot):
        both = dot(hidden, gate_up)
        grad_active = dot(cot, down, NT)
        gate, upward = both[:, :units], both[:, units:]
        sig = 1.0 / (1.0 + jnp.exp(-gate))
        lifted = gate * sig
        active = (lifted * upward).astype(BF16)
        grad_gate = (grad_active * upward * (sig * (1.0 + gate * (1.0 - sig)))).astype(BF16)
        grad_up = (grad_active * lifted).astype(BF16)
        return active, jnp.concatenate([grad_gate, grad_up], axis=1)

    active_c, grads_c = feed(hidden_c, cot_c)
    active_o, grads_o = feed(hidden_o, cot_o)

    grad_down = (over_t(active_c, cot_c) + over_t(active_o, cot_o)).astype(BF16)
    grad_down = lax.psum(grad_down, "dp")

    back_o = swap(dot(grads_o, gate_up, NT).astype(BF16), "col")
    back_c = dot(grads_c, gate_up, NT) + back_o.astype(F32)
    back_low = back_c.astype(BF16)
    back_far = jnp.concatenate(swap((back_low[:, half:], back_low[:, :half]), "row"), axis=1)
    grad_hidden = back_c + back_far.astype(F32)

    grad_gate_up = (over_t(hidden_c, grads_c) + over_t(hidden_o, grads_o)).astype(BF16)

    result_o = swap(dot(active_o, down).astype(BF16), "col")
    result_c = dot(active_c, down) + result_o.astype(F32)
    result = middle[:, :half] + result_c[:, :half] + swap(result_c[:, half:].astype(BF16), "row").astype(F32)
    result = result.astype(BF16)
    output = ordered(result, swap(result, "col"), col)

    ffn_gain_sum = jnp.sum(grad_hidden * normal_two, axis=0)
    inner = grad_hidden * gain_two
    stat = jnp.sum(inner * normal_two, axis=1, keepdims=True) / width
    stat = gated(stat, corner(grad_gate_up), corner(result_c))
    grad_middle = cot_c.astype(F32) + inverse_two * (inner - normal_two * stat)
    branch_c = grad_middle.astype(BF16)
    branch_o = swap(branch_c, "col")
    grad_attended = ordered(dot(branch_c, out_own, NT).astype(BF16), dot(branch_o, out_own, NT).astype(BF16), col)

    grad_out = [over_t(attended[n], branch_c[:, :half]) for n in range(groups)]
    kept = jnp.concatenate([g[p * size:(p + 1) * size] for p in (0, 2) for g in grad_out], axis=0)
    sent = jnp.concatenate([g[p * size:(p + 1) * size] for p in (1, 3) for g in grad_out], axis=0)
    grad_out = kept + swap(sent.astype(BF16), "col").astype(F32)
    quarter = out_own.shape[0]
    grad_out = ordered(grad_out[:quarter], grad_out[quarter:], row).astype(BF16)

    dq, dk, dv = zip(*(attend_back(q, k, v, grad_attended, raws[n], totals[n], starts, n) for n in range(groups)))
    grads, to_near, to_far, stat_one, q_sum, k_sum, near_sum, far_sum = project_back(
        dq, dk, dv, raw, tokens, far, *small, cosine, sine)

    to_all = jnp.concatenate([to_near, to_far], axis=1)
    sent_o, sent_stat = swap((part_of(to_all, 1 - col, 0), part_of(stat_one, 1 - col, 0)), "col")
    chip_sum = part_of(to_all, col, 0).astype(F32) + sent_o.astype(F32)
    chip_stat = part_of(stat_one, col, 0) + sent_stat

    near_grads = jnp.concatenate([grad_gate_up[:half], over_t(hid_near, grads).astype(BF16)], axis=1)
    far_grads = jnp.concatenate([grad_gate_up[half:], over_t(hid_far, grads).astype(BF16)], axis=1)

    def folded(x):
        return x[0, :HEAD_SIZE] + x[0, HEAD_SIZE:]

    vector = jnp.concatenate([
        ordered(near_sum[0], far_sum[0], row),
        ordered(ffn_gain_sum[:half], ffn_gain_sum[half:], row) * 0.5,
        folded(q_sum), folded(k_sum)])
    length = vector.shape[0]
    lines = -(-length // 1024) * 8
    vector = jnp.concatenate([vector, jnp.zeros((lines * 128 - length,), F32)]).reshape(lines, 128)
    near_grads, far_grads, grad_out = (
        x.reshape(parts, half // parts, -1) for x in (near_grads, far_grads, grad_out))
    full, out_full, sums, other_sum, other_stat = ring_sum(
        [near_grads], [far_grads], [grad_out], vector, chip_sum[:, half:].astype(BF16), chip_stat,
        ("dp", "row", "col"), parts)
    full = full.reshape(2, half, -1)
    sums = sums.reshape(-1)

    def columns(begin, end):
        return jnp.concatenate([full[0][:, begin:end], full[1][:, begin:end]], axis=1).astype(F32)

    inner_one = (chip_sum[:, :half] + other_sum.astype(F32)) * attn_gain[None, :]
    mine = mine.astype(F32)
    inverse_one = lax.rsqrt(jnp.sum(mine * mine, axis=1, keepdims=True) / width + EPSILON)
    stat_one = (chip_stat + other_stat)[:, :1] / width
    grad_inputs = inverse_one * (inner_one - mine[:, :half] * inverse_one * stat_one) + grad_middle[:, :half]
    grad_inputs = grad_inputs.astype(BF16)
    grad_tokens = ordered(grad_inputs, swap(grad_inputs, "col"), col)

    grad_down = gated(grad_down, corner(q_sum))
    down_other = swap(grad_down[:, half:], "row")
    down_full = ordered(grad_down[:, :half], gated(down_other, sums[0]), row).astype(F32)
    q_cols, k_cols = query_weight.shape[1] // 2, key_matrix.shape[1] // 2
    at_q, at_k, at_v = 2 * units, 2 * units + q_cols, 2 * units + q_cols + k_cols
    return (
        output,
        grad_tokens,
        columns(at_q, at_k),
        columns(at_k, at_v),
        columns(at_v, at_v + k_cols),
        out_full.reshape(half, -1).astype(F32),
        columns(0, units),
        columns(units, 2 * units),
        down_full,
        part_of(sums[:width], row, 0),
        part_of(sums[width:2 * width], row, 0),
        sums[2 * width:2 * width + HEAD_SIZE],
        sums[2 * width + HEAD_SIZE:2 * width + 2 * HEAD_SIZE],
    )


def solution(mesh):
    return jax.shard_map(
        shards,
        mesh=mesh,
        in_specs=(
            P("dp", "row"),
            P("dp", None),
            P("row", "col"),
            P("row", "col"),
            P("row", "col"),
            P("col", "row"),
            P("row", "col"),
            P("row", "col"),
            P("col", "row"),
            P("row"),
            P("row"),
            P(),
            P(),
            P("dp", "row"),
        ),
        out_specs=(
            P("dp", "row"),
            P("dp", "row"),
            P("row", "col"),
            P("row", "col"),
            P("row", "col"),
            P("col", "row"),
            P("row", "col"),
            P("row", "col"),
            P("col", "row"),
            P("row"),
            P("row"),
            P(),
            P(),
        ),
        check_vma=False,
    )
```

```python
import functools
import math

import jax
import jax.numpy as jnp
from jax import lax
from jax.experimental import pallas as pl
from jax.experimental.pallas import tpu as pltpu
from jax.sharding import PartitionSpec as P

HEAD_SIZE = 64
EPSILON = 1e-05
ROPE_BASE = 1000000.0
F32, BF16 = jnp.float32, jnp.bfloat16
MESH = pl.DeviceIdType.MESH


def dot(a, b, dims=(((1,), (0,)), ((), ()))):
    return lax.dot_general(a, b, dims, preferred_element_type=F32)


NT = (((1,), (1,)), ((), ()))

def stacked(x):
    first = lax.broadcasted_iota(jnp.int32, x.shape, 1) < 64
    zero = jnp.zeros_like(x)
    return jnp.concatenate([jnp.where(first, x, zero), jnp.where(first, zero, x)], axis=0)

def attend_kernel(bq, bk, first_ref, last_ref, q_ref, k_ref, v_ref, start_ref, low_ref, raw_ref, lse_ref, acc_ref, mass_ref):
    i = pl.program_id(1)
    qs = stacked(q_ref[...])
    starts = start_ref[...]
    starts = jnp.concatenate([starts, starts], axis=0)
    acc_ref[...] = jnp.zeros_like(acc_ref)
    mass_ref[...] = jnp.zeros_like(mass_ref)
    rows = i * bq + lax.rem(lax.broadcasted_iota(jnp.int32, (2 * bq, 1), 0), bq)

    def step(j, masked):
        k0 = pl.multiple_of(j * bk, bk)
        s = dot(qs, k_ref[pl.ds(k0, bk), :], NT)
        p = jnp.exp(s)
        if masked:
            cols = j * bk + lax.broadcasted_iota(jnp.int32, (1, bk), 1)
            p = jnp.where((cols <= rows) & (cols >= starts), p, 0.0)
        mass = p[:, :128]
        for n in range(1, bk // 128):
            mass = mass + p[:, n * 128:(n + 1) * 128]
        mass_ref[...] += mass
        acc_ref[...] += dot(p.astype(BF16), v_ref[pl.ds(k0, bk), :])

    low = first_ref[i] // bk
    clear = jnp.maximum((last_ref[i] + bk - 1) // bk, low)
    diagonal = (i * bq) // bk
    end = ((i + 1) * bq + bk - 1) // bk
    clear = jnp.minimum(clear, diagonal)

    @pl.loop(low, clear)
    def _(j):
        step(j, True)

    @pl.loop(clear, diagonal)
    def _(j):
        step(j, False)

    @pl.loop(diagonal, end)
    def _(j):
        step(j, True)

    mass = jnp.sum(mass_ref[...], axis=1, keepdims=True)
    out = acc_ref[...] / mass
    first = lax.broadcasted_iota(jnp.int32, (bq, 128), 1) < 64
    out = jnp.where(first, out[:bq], out[bq:])
    raw_ref[...] = out
    low_ref[...] = out.astype(BF16)
    total = jnp.log(jnp.sum(mass_ref[...].T, axis=0, keepdims=True))
    lse_ref[0, 0:1, :] = total[:, :bq]
    lse_ref[0, 1:2, :] = total[:, bq:]

def attend(q, k, v, starts, bq=512, bk=512):
    T, width = q.shape
    groups = width // 128
    first, last = starts[::bq], starts[bq - 1::bq]
    kern = functools.partial(attend_kernel, bq, bk)
    pairs = T * (T + bk) // 2
    return pl.pallas_call(
        kern,
        out_shape=(jax.ShapeDtypeStruct((T, width), BF16), jax.ShapeDtypeStruct((T, width), F32),
                   jax.ShapeDtypeStruct((groups, 2, T), F32)),
        grid_spec=pltpu.PrefetchScalarGridSpec(
            num_scalar_prefetch=2, grid=(groups, T // bq),
            in_specs=[
                pl.BlockSpec((bq, 128), lambda g, i, *_: (i, g)),
                pl.BlockSpec((T, 128), lambda g, i, *_: (0, g)),
                pl.BlockSpec((T, 128), lambda g, i, *_: (0, g)),
                pl.BlockSpec((bq, 1), lambda g, i, *_: (i, 0)),
            ],
            out_specs=[
                pl.BlockSpec((bq, 128), lambda g, i, *_: (i, g)),
                pl.BlockSpec((bq, 128), lambda g, i, *_: (i, g)),
                pl.BlockSpec((1, 2, bq), lambda g, i, *_: (g, 0, i)),
            ],
            scratch_shapes=[pltpu.VMEM((2 * bq, 128), F32), pltpu.VMEM((2 * bq, 128), F32)],
        ),
        compiler_params=pltpu.CompilerParams(vmem_limit_bytes=40 << 20),
        cost_estimate=pl.CostEstimate(flops=4 * groups * 2 * pairs * 256, transcendentals=2 * groups * pairs,
                                      bytes_accessed=10 * T * width),
        name="attend",
    )(first, last, q, k, v, starts[:, None])


def head_sums(x):
    first = lax.broadcasted_iota(jnp.int32, x.shape, 1) < HEAD_SIZE
    one = jnp.sum(jnp.where(first, x, 0.0), axis=1, keepdims=True)
    two = jnp.sum(jnp.where(first, 0.0, x), axis=1, keepdims=True)
    return jnp.where(first, one, two)


def swapped(x):
    low = lax.rem(lax.broadcasted_iota(jnp.int32, x.shape, 1), HEAD_SIZE) < HEAD_SIZE // 2
    return jnp.where(low, pltpu.roll(x, 96, 1), pltpu.roll(x, 32, 1))


def doubled(x):
    first = lax.broadcasted_iota(jnp.int32, x.shape, 1) < HEAD_SIZE
    other = pltpu.roll(x, HEAD_SIZE, 1)
    return jnp.where(first, x, other), jnp.where(first, other, x)


def project_kernel(groups, near_ref, far_ref, gain_near_ref, gain_far_ref, w_near_ref, w_far_ref, q_gain_ref, k_gain_ref,
                   cos_ref, sin_ref, hid_near_ref, hid_far_ref, raw_ref, q_ref, k_ref, v_ref):
    near = near_ref[...].astype(F32)
    far = far_ref[...].astype(F32)
    width = near.shape[1] + far.shape[1]
    total = jnp.sum(near * near, axis=1, keepdims=True) + jnp.sum(far * far, axis=1, keepdims=True)
    inverse = lax.rsqrt(total / width + EPSILON)
    hid_near = (near * inverse * gain_near_ref[...]).astype(BF16)
    hid_far = (far * inverse * gain_far_ref[...]).astype(BF16)
    hid_near_ref[...] = hid_near
    hid_far_ref[...] = hid_far
    raw = dot(hid_near, w_near_ref[...]) + dot(hid_far, w_far_ref[...])
    cosine, sine = cos_ref[...], sin_ref[...]

    def prepared(x, gain):
        normed = x * lax.rsqrt(head_sums(x * x) / HEAD_SIZE + EPSILON) * gain
        return normed * cosine + swapped(normed) * sine

    lanes = 2 * HEAD_SIZE
    kv = groups * HEAD_SIZE
    raw_ref[...] = raw[:, :groups * lanes + kv]
    for n in range(groups):
        cut = slice(n * lanes, (n + 1) * lanes)
        q_ref[:, cut] = (prepared(raw[:, cut], q_gain_ref[...]).astype(BF16) * HEAD_SIZE ** (-0.5)).astype(BF16)
    for n in range(groups // 2):
        at = groups * lanes + n * lanes
        twice = doubled(prepared(raw[:, at:at + lanes], k_gain_ref[...]))
        for m in range(2):
            k_ref[:, (2 * n + m) * lanes:(2 * n + m + 1) * lanes] = twice[m].astype(BF16)
        at += kv
        twice = doubled(raw[:, at:at + lanes])
        for m in range(2):
            v_ref[:, (2 * n + m) * lanes:(2 * n + m + 1) * lanes] = twice[m].astype(BF16)


def project(near, far, gain_near, gain_far, w_near, w_far, q_gain, k_gain, cosine, sine, rows=512):
    packed, half = near.shape
    columns = w_near.shape[1]
    groups = columns // (4 * HEAD_SIZE)
    width = groups * 2 * HEAD_SIZE
    kv = groups * HEAD_SIZE
    rows = min(rows, packed)

    def tile(n):
        return pl.BlockSpec((rows, n), lambda i: (i, 0))

    def whole(x):
        return pl.BlockSpec(x.shape, lambda i: (0, 0))

    def out(n, dtype):
        return jax.ShapeDtypeStruct((packed, n), dtype)

    small = (gain_near, gain_far, w_near, w_far, q_gain, k_gain)
    return pl.pallas_call(
        functools.partial(project_kernel, groups),
        out_shape=(out(half, BF16), out(half, BF16), out(width + kv, F32), out(width, BF16), out(width, BF16), out(width, BF16)),
        grid=(packed // rows,),
        in_specs=[tile(half), tile(half), *map(whole, small), tile(2 * HEAD_SIZE), tile(2 * HEAD_SIZE)],
        out_specs=(tile(half), tile(half), tile(width + kv), tile(width), tile(width), tile(width)),
        compiler_params=pltpu.CompilerParams(vmem_limit_bytes=40 << 20),
        cost_estimate=pl.CostEstimate(flops=4 * packed * half * columns, transcendentals=packed * 8,
                                      bytes_accessed=packed * (8 * half + 10 * width)),
        name="project",
    )(near, far, *small, cosine, sine)


def project_back_kernel(groups, dq_ref, dk_ref, dv_ref, raw_ref, near_ref, far_ref, gain_near_ref, gain_far_ref,
                        w_near_ref, w_far_ref, q_gain_ref, k_gain_ref, cos_ref, sin_ref,
                        grads_ref, to_near_ref, to_far_ref, stat_ref, q_sum_ref, k_sum_ref, near_sum_ref, far_sum_ref):
    @pl.when(pl.program_id(0) == 0)
    def _():
        for ref in (q_sum_ref, k_sum_ref, near_sum_ref, far_sum_ref):
            ref[...] = jnp.zeros_like(ref)

    cosine, sine = cos_ref[...], sin_ref[...]
    lanes = 2 * HEAD_SIZE
    first = lax.broadcasted_iota(jnp.int32, cosine.shape, 1) < HEAD_SIZE

    def back(grad, x, gain):
        inverse = lax.rsqrt(head_sums(x * x) / HEAD_SIZE + EPSILON)
        normed = x * inverse
        turned = grad * cosine - swapped(grad) * sine
        inner = turned * gain
        part = inverse * (inner - normed * (head_sums(inner * normed) / HEAD_SIZE))
        return part, jnp.sum(turned * normed, axis=0, keepdims=True)

    grads = []
    for n in range(groups):
        cut = slice(n * lanes, (n + 1) * lanes)
        part, total = back(dq_ref[:, cut], raw_ref[:, cut], q_gain_ref[...])
        q_sum_ref[...] += total
        grads.append(part.astype(BF16))
    for n in range(groups // 2):
        at = groups * lanes + n * lanes
        part, total = back(jnp.where(first, dk_ref[:, 2 * n * lanes:(2 * n + 1) * lanes], dk_ref[:, (2 * n + 1) * lanes:(2 * n + 2) * lanes]), raw_ref[:, at:at + lanes], k_gain_ref[...])
        k_sum_ref[...] += total
        grads.append(part.astype(BF16))
    for n in range(groups // 2):
        grads.append(jnp.where(first, dv_ref[:, 2 * n * lanes:(2 * n + 1) * lanes], dv_ref[:, (2 * n + 1) * lanes:(2 * n + 2) * lanes]).astype(BF16))
    grads = jnp.concatenate(grads, axis=1)
    grads_ref[...] = grads
    to_near = dot(grads, w_near_ref[...], NT)
    to_far = dot(grads, w_far_ref[...], NT)
    to_near_ref[...] = to_near.astype(BF16)
    to_far_ref[...] = to_far.astype(BF16)
    near = near_ref[...].astype(F32)
    far = far_ref[...].astype(F32)
    width = near.shape[1] + far.shape[1]
    total = jnp.sum(near * near, axis=1, keepdims=True) + jnp.sum(far * far, axis=1, keepdims=True)
    inverse = lax.rsqrt(total / width + EPSILON)
    near = to_near * (near * inverse)
    far = to_far * (far * inverse)
    near_sum_ref[...] += jnp.sum(near, axis=0, keepdims=True)
    far_sum_ref[...] += jnp.sum(far, axis=0, keepdims=True)
    stat = jnp.sum(near * gain_near_ref[...], axis=1, keepdims=True) + jnp.sum(far * gain_far_ref[...], axis=1, keepdims=True)
    stat_ref[...] = jnp.where(first, stat, inverse)


def project_back(dq, dk, dv, raw, near, far, gain_near, gain_far, w_near, w_far, q_gain, k_gain, cosine, sine, rows=512):
    packed, half = near.shape
    columns = w_near.shape[1]
    groups = columns // (4 * HEAD_SIZE)
    width = groups * 2 * HEAD_SIZE
    rows = min(rows, packed)

    def tile(n):
        return pl.BlockSpec((rows, n), lambda i: (i, 0))

    def whole(x):
        return pl.BlockSpec(x.shape, lambda i: (0, 0))

    def kept(n):
        return pl.BlockSpec((1, n), lambda i: (0, 0))

    def out(n, dtype, many=packed):
        return jax.ShapeDtypeStruct((many, n), dtype)

    small = (gain_near, gain_far, w_near, w_far, q_gain, k_gain)
    lanes = 2 * HEAD_SIZE
    return pl.pallas_call(
        functools.partial(project_back_kernel, groups),
        out_shape=(out(columns, BF16), out(half, BF16), out(half, BF16), out(lanes, F32), out(lanes, F32, 1), out(lanes, F32, 1),
                   out(half, F32, 1), out(half, F32, 1)),
        grid=(packed // rows,),
        in_specs=[tile(width)] * 3 + [tile(raw.shape[1]), tile(half), tile(half), *map(whole, small),
                  tile(lanes), tile(lanes)],
        out_specs=(tile(columns), tile(half), tile(half), tile(lanes), kept(lanes), kept(lanes), kept(half), kept(half)),
        compiler_params=pltpu.CompilerParams(vmem_limit_bytes=44 << 20),
        cost_estimate=pl.CostEstimate(flops=4 * packed * half * columns, transcendentals=packed * 8,
                                      bytes_accessed=packed * (8 * half + 18 * width)),
        name="project_back",
    )(dq, dk, dv, raw, near, far, *small, cosine, sine)


def layout(lengths, packed):
    count = lengths.shape[0]
    numbers = jnp.arange(count, dtype=jnp.int32)
    ends = jnp.sum(jnp.where(numbers[None, :] <= numbers[:, None], lengths[None, :], 0), axis=1)
    begins = ends - lengths
    places = jnp.arange(packed, dtype=jnp.int32)
    member = jnp.sum((places[:, None] >= ends[None, :]).astype(jnp.int32), axis=1)
    return jnp.sum(jnp.where(member[:, None] == numbers[None, :], begins[None, :], 0), axis=1)


def rope_tables(position):
    half = HEAD_SIZE // 2
    inverse = jnp.exp(jnp.arange(half, dtype=F32) * (-2.0 * math.log(ROPE_BASE) / HEAD_SIZE))
    angles = position.astype(F32)[:, None] * inverse[None, :]
    cosine, sine = jnp.cos(angles), jnp.sin(angles)
    return jnp.concatenate([cosine] * 4, axis=1), jnp.concatenate([-sine, sine] * 2, axis=1)


def swap(x, axis):
    return jax.tree.map(lambda part: lax.ppermute(part, axis, [(0, 1), (1, 0)]), x)


def ordered(own, other, index, axis=0):
    return jnp.where(index == 0, jnp.concatenate([own, other], axis), jnp.concatenate([other, own], axis))


def part_of(x, index, axis, parts=2):
    size = x.shape[axis] // parts
    return lax.dynamic_slice_in_dim(x, index * size, size, axis)


def over_t(left, right):
    return dot(left, right, (((0,), (0,)), ((), ())))


def feed_kernel(units, hidden_ref, cot_near_ref, cot_far_ref, gate_up_ref, down_ref, active_ref, grads_ref, result_ref, back_ref):
    half = cot_near_ref.shape[1]
    hidden = hidden_ref[...]
    gate = dot(hidden, gate_up_ref[:, :units])
    upward = dot(hidden, gate_up_ref[:, units:])
    grad_active = dot(cot_near_ref[...], down_ref[:, :half], NT) + dot(cot_far_ref[...], down_ref[:, half:], NT)
    sig = 1.0 / (1.0 + jnp.exp(-gate))
    lifted = gate * sig
    active = (lifted * upward).astype(BF16)
    grad_gate = (grad_active * upward * (sig * (1.0 + gate * (1.0 - sig)))).astype(BF16)
    grad_up = (grad_active * lifted).astype(BF16)
    active_ref[...] = active
    grads_ref[:, :units] = grad_gate
    grads_ref[:, units:] = grad_up
    result_ref[...] = dot(active, down_ref[...]).astype(BF16)
    back = dot(grad_gate, gate_up_ref[:, :units], NT) + dot(grad_up, gate_up_ref[:, units:], NT)
    back_ref[...] = back.astype(BF16)


def feed(hidden, cot_near, cot_far, gate_up, down, rows=256):
    packed, width = hidden.shape
    units = down.shape[0]
    rows = min(rows, packed)

    def tile(n):
        return pl.BlockSpec((rows, n), lambda i: (i, 0))

    def whole(x):
        return pl.BlockSpec(x.shape, lambda i: (0, 0), pipeline_mode=pl.Buffered(1))

    def out(n):
        return jax.ShapeDtypeStruct((packed, n), BF16)

    return pl.pallas_call(
        functools.partial(feed_kernel, units),
        out_shape=(out(units), out(2 * units), out(width), out(width)),
        grid=(packed // rows,),
        in_specs=[tile(width), tile(width // 2), tile(width // 2), whole(gate_up), whole(down)],
        out_specs=(tile(units), tile(2 * units), tile(width), tile(width)),
        compiler_params=pltpu.CompilerParams(vmem_limit_bytes=56 << 20),
        cost_estimate=pl.CostEstimate(flops=12 * packed * width * units, transcendentals=packed * units,
                                      bytes_accessed=packed * (8 * width + 6 * units) + 6 * width * units),
        name="feed",
    )(hidden, cot_near, cot_far, gate_up, down)


class Group:
    def __init__(self, names, n):
        self.n = n
        self.dp, self.row, self.col = (lax.axis_index(name) for name in names)
        side = self.dp % 2
        self.place = (self.dp // 2) * (1 - side) + (n - 1 - self.dp // 2) * side
        self.across = (self.dp, 1 - self.row, self.col)
        self.beside = (self.dp, self.row, 1 - self.col)
        self.opposite = (self.dp, 1 - self.row, 1 - self.col)
        self.along = [((self.dp + k) % n, self.row, self.col) for k in range(1, n)]
        self.ring = [(self.at(self.place + 1), self.row, self.col), (self.at(self.place - 1), self.row, self.col)]

    def at(self, position):
        position = (position + 2 * self.n) % self.n
        back = position // (self.n // 2)
        return (position * (1 - back) + (self.n - 1 - position) * back) * 2 + back

    def arrive(self, targets):
        barrier = pltpu.get_barrier_semaphore()
        for target in targets:
            pl.semaphore_signal(barrier, inc=1, device_id=target, device_id_type=MESH)
        pl.semaphore_wait(barrier, len(targets))

    def reduced(self, way, t):
        return (self.place - t - 1 + 2 * self.n) % self.n if way == 0 else (self.place + t + 1) % self.n

    def spread(self, way, t):
        return (self.place - t + 2 * self.n) % self.n if way == 0 else (self.place + t) % self.n

    def own(self, way):
        return (self.place + 1) % self.n if way == 0 else (self.place + self.n - 1) % self.n


def remote(src, dst, send, recv, target):
    return pltpu.make_async_remote_copy(
        src_ref=src, dst_ref=dst, send_sem=send, recv_sem=recv, device_id=target, device_id_type=MESH)


class Reduce:
    def __init__(self, me, parts, slots, send, recv):
        self.me, self.parts, self.slots, self.send, self.recv = me, parts, slots, send, recv
        self.columns = parts[0].shape[2] // 2

    def local(self, s, chunk):
        return self.parts[s // 2].at[chunk, :, pl.ds((s % 2) * self.columns, self.columns)]

    def copy(self, s, t, src):
        return remote(src, self.slots.at[s, t], self.send.at[s, t], self.recv.at[s, t], self.me.ring[s % 2])

    def start(self):
        for s in range(2 * len(self.parts)):
            self.copy(s, 0, self.local(s, self.me.place)).start()

    def step(self, t):
        for s in range(2 * len(self.parts)):
            slot = self.slots.at[s, t]
            self.copy(s, t, slot).wait_recv()
            slot[...] = (slot[...].astype(F32) + self.local(s, self.me.reduced(s % 2, t))[...].astype(F32)).astype(BF16)

            @pl.when(t < self.me.n - 2)
            def _():
                self.copy(s, t + 1, slot).start()

    def last(self, s):
        return self.slots.at[s, self.me.n - 2]

    def finish(self, t):
        for s in range(2 * len(self.parts)):
            self.copy(s, t, self.slots.at[s, t]).wait_send()


class Spread:
    def __init__(self, me, full, send, recv):
        self.me, self.full, self.send, self.recv = me, full, send, recv
        self.lone = len(full.shape) == 3
        self.columns = full.shape[-1] // 2
        self.streams = (0, 1) if self.lone else (2, 3, 0, 1)

    def piece(self, s, chunk, quarter=None):
        lanes = pl.ds((s % 2) * self.columns, self.columns)
        if self.lone:
            return self.full.at[chunk, :, lanes]
        if quarter is None:
            quarter = 1 - self.me.row if s < 2 else self.me.row
        return self.full.at[quarter, chunk, :, lanes]

    def copy(self, s, t, chunk, src=None):
        piece = self.piece(s, chunk)
        return remote(piece if src is None else src, piece, self.send.at[s, t], self.recv.at[s, t], self.me.ring[s % 2])

    def start(self, s, src=None):
        self.copy(s, 0, self.me.own(s % 2), src).start()

    def step(self, t):
        for s in self.streams:
            chunk = self.me.spread(s % 2, t)
            self.copy(s, t, chunk).wait_recv()

            @pl.when(t < self.me.n - 2)
            def _():
                self.copy(s, t + 1, chunk).start()

    def finish(self, t):
        for s in self.streams:
            self.copy(s, t, 0).wait_send()


def steps(begin, end, *rings):
    def step(t, carry):
        for ring in rings:
            ring.step(t)
        return carry

    lax.fori_loop(begin, end, step, 0)


def finish(n, *rings):
    def each(t, carry):
        for ring in rings:
            ring.finish(t)
        return carry

    lax.fori_loop(0, n - 1, each, 0)


def turn_kernel(n, names, pieces, near_ref, far_ref, down_near_ref, down_far_ref, back_ref, middle_ref, cot_near_ref,
                cot_far_ref, gain_ref, branch_ref, keep_ref, gain_sum_ref, done_ref, down_done_ref,
                slots, down_slots, beside_in, across_out, across_in, rs_send, rs_recv, down_send, down_recv,
                cross_send, cross_recv, beside_send, beside_recv, across_send, across_recv, branch_send, branch_recv):
    me = Group(names, n)
    me.arrive([*me.ring, me.across, me.beside])
    half = cot_near_ref.shape[1]
    tokens = middle_ref.shape[0]
    rows = tokens // pieces
    wide = Reduce(me, (far_ref, near_ref), slots, rs_send, rs_recv)
    down = Reduce(me, (down_far_ref, down_near_ref), down_slots, down_send, down_recv)

    def place_of(core, k):
        return pl.ds(pl.multiple_of(core * tokens + k * rows, rows), rows)

    wide.start()
    down.start()
    besides = [remote(back_ref.at[place_of(1 - me.col, k), :], beside_in.at[k], beside_send.at[k], beside_recv.at[k], me.beside)
               for k in range(pieces)]
    for each in besides:
        each.start()
    acrosses = [remote(across_out.at[k], across_in.at[k], across_send.at[k], across_recv.at[k], me.across)
                for k in range(pieces)]
    for k in range(pieces):
        besides[k].wait()
        chip = (back_ref[place_of(me.col, k), :].astype(F32) + beside_in[k].astype(F32)).astype(BF16)
        across_out[k, :, :half] = chip[:, half:]
        across_out[k, :, half:] = chip[:, :half]
        acrosses[k].start()

    gain_sum_ref[...] = jnp.zeros_like(gain_sum_ref)
    branches = [remote(branch_ref.at[place_of(me.col, k), :], branch_ref.at[place_of(me.col, k), :],
                       branch_send.at[k], branch_recv.at[k], me.beside) for k in range(pieces)]
    for k in range(pieces):
        steps(k * (n - 1) // pieces, (k + 1) * (n - 1) // pieces, wide, down)
        acrosses[k].wait()
        mine = place_of(me.col, k)
        grad = back_ref[mine, :].astype(F32) + beside_in[k].astype(F32) + across_in[k].astype(F32)
        middle = middle_ref[k * rows:(k + 1) * rows, :]
        inverse = lax.rsqrt(jnp.sum(middle * middle, axis=1, keepdims=True) / (2 * half) + EPSILON)
        normal = middle * inverse
        weighed = grad * normal
        gain_sum_ref[...] += jnp.sum(weighed, axis=0, keepdims=True)
        stat = jnp.sum(weighed * gain_ref[...], axis=1, keepdims=True) / (2 * half)
        part = inverse * (grad * gain_ref[...] - normal * stat)
        near = cot_near_ref[mine, :].astype(F32) + part[:, :half]
        far = cot_far_ref[mine, :].astype(F32) + part[:, half:]
        keep_ref[k * rows:(k + 1) * rows, :] = near
        branch_ref[mine, :half] = near.astype(BF16)
        branch_ref[mine, half:] = far.astype(BF16)
        branches[k].start()

    crosses = [remote(ring.last(s), out.at[s], cross_send.at[2 * k + s], cross_recv.at[2 * k + s], me.across)
               for k, (ring, out) in enumerate(((wide, done_ref), (down, down_done_ref))) for s in range(2)]
    for cross in crosses:
        cross.start()
    for s in (2, 3):
        done_ref[s] = wide.last(s)[...]
        down_done_ref[s] = down.last(s)[...]
    for each in branches + crosses:
        each.wait()
    finish(n, wide, down)


def turn(near, far, down_near, down_far, back, middle, cot_near, cot_far, gain, names, n, pieces=4):
    packed, width = back.shape
    tokens = middle.shape[0]
    vmem = pl.BlockSpec(memory_space=pltpu.VMEM)
    dma = pltpu.SemaphoreType.DMA
    exchange = pltpu.VMEM((pieces, tokens // pieces, width), BF16)

    def streams(x):
        return x.shape[1], x.shape[2] // 2

    return pl.pallas_call(
        functools.partial(turn_kernel, n, names, pieces),
        out_shape=(jax.ShapeDtypeStruct((packed, width), BF16), jax.ShapeDtypeStruct((tokens, width // 2), F32),
                   jax.ShapeDtypeStruct((1, width), F32), jax.ShapeDtypeStruct((4, *streams(near)), BF16),
                   jax.ShapeDtypeStruct((4, *streams(down_near)), BF16)),
        in_specs=[vmem] * 9,
        out_specs=(vmem,) * 5,
        scratch_shapes=[
            pltpu.VMEM((4, n - 1, *streams(near)), BF16), pltpu.VMEM((4, n - 1, *streams(down_near)), BF16),
            exchange, exchange, exchange, *[dma((4, n - 1))] * 4, dma((4,)), dma((4,)), *[dma((pieces,))] * 6,
        ],
        compiler_params=pltpu.CompilerParams(collective_id=1, has_side_effects=True, vmem_limit_bytes=60 << 20),
        cost_estimate=pl.CostEstimate(flops=40 * back.size, transcendentals=tokens, bytes_accessed=150 << 20),
        name="turn",
    )(near, far, down_near, down_far, back, middle, cot_near, cot_far, gain)


def retreat_kernel(n, names, b, packed, q_ref, k_ref, v_ref, grad_ref, raw_ref, lse_ref, start_ref,
                   done_ref, down_done_ref, result_ref, middle_ref,
                   dq_ref, dk_ref, dv_ref, wide_ref, down_ref, output_ref,
                   qs_ref, gs_ref, stat_ref, dqt_ref, dk_acc, dv_acc,
                   sums, beside_in, across_out, across_in, wide_send, wide_recv, down_send, down_recv,
                   beside_send, beside_recv, across_send, across_recv, last_send, last_recv, load_sem, keep_sem):
    g, j = pl.program_id(0), pl.program_id(1)
    blocks = packed // b
    me = Group(names, n)
    half = output_ref.shape[1]
    count = packed // 2
    wide = Spread(me, wide_ref, wide_send, wide_recv)
    down = Spread(me, down_ref, down_send, down_recv)
    own_rows = pl.ds(pl.multiple_of(me.col * count, count), count)
    other_rows = pl.ds(pl.multiple_of((1 - me.col) * count, count), count)
    sides = (pl.ds(half, half), pl.ds(0, half))
    besides = [remote(result_ref.at[other_rows, side], beside_in.at[k], beside_send.at[k], beside_recv.at[k], me.beside)
               for k, side in enumerate(sides)]
    loads = [pltpu.make_async_copy(result_ref.at[own_rows, side], sums.at[k], load_sem.at[k]) for k, side in enumerate(sides)]
    across = remote(across_out, across_in, across_send, across_recv, me.across)
    last = remote(across_out, output_ref.at[own_rows, :], last_send, last_recv, me.beside)
    last_here = pltpu.make_async_copy(across_out, output_ref.at[own_rows, :], keep_sem.at[8])
    keeps = [pltpu.make_async_copy(src.at[s], ring.piece(s, me.own(s % 2)), keep_sem.at[4 * k + s])
             for k, (ring, src) in enumerate(((wide, done_ref), (down, down_done_ref))) for s in range(4)]

    @pl.when((g == 0) & (j == 0))
    def _():
        me.arrive([*me.ring, me.across, me.beside])
        for ring, src in ((wide, done_ref), (down, down_done_ref)):
            for s in range(4):
                ring.start(s, src.at[s])
        for each in besides + loads + keeps:
            each.start()

    @pl.when((g == 0) & (j == 1))
    def _():
        for each in besides + loads:
            each.wait()
        across_out[...] = (sums[0].astype(F32) + beside_in[0].astype(F32)).astype(BF16)
        across.start()

    @pl.when((g == 1) & (j == 1))
    def _():
        across.wait()
        total = middle_ref[...] + (sums[1].astype(F32) + beside_in[1].astype(F32) + across_in[...].astype(F32))
        across_out[...] = total.astype(BF16)
        last.start()
        last_here.start()

    @pl.when(j == 0)
    def _():
        dqt_ref[...] = jnp.zeros_like(dqt_ref)
        for i in range(blocks):
            rows = slice(i * b, (i + 1) * b)
            both = slice(i * 2 * b, (i + 1) * 2 * b)
            qs_ref[both, :] = stacked(q_ref[rows, :])
            grad = grad_ref[rows, :]
            gs_ref[both, :] = stacked(grad)
            prod = (grad.astype(F32) * raw_ref[rows, :]).T
            stat_ref[i, 0:1, 0:b] = lse_ref[0, 0:1, rows]
            stat_ref[i, 0:1, b:2 * b] = lse_ref[0, 1:2, rows]
            stat_ref[i, 1:2, 0:b] = jnp.sum(prod[:64], axis=0, keepdims=True)
            stat_ref[i, 1:2, b:2 * b] = jnp.sum(prod[64:], axis=0, keepdims=True)

    k = k_ref[...]
    v = v_ref[...]
    kt = k.T[:64]
    dk_acc[...] = jnp.zeros_like(dk_acc)
    dv_acc[...] = jnp.zeros_like(dv_acc)
    keys = j * b + lax.broadcasted_iota(jnp.int32, (b, 1), 0)
    every = blocks * (blocks + 1)
    before = g * (every // 2) + j * blocks - (j * (j - 1)) // 2

    def step(i, diagonal):
        at = pl.ds(pl.multiple_of(i * 2 * b, 2 * b), 2 * b)
        qs = qs_ref[at, :]
        gs = gs_ref[at, :]
        st = dot(k, qs, NT)
        pt = jnp.exp(st - stat_ref[i, 0:1, :])
        begin = start_ref[0:1, pl.ds(pl.multiple_of(i * b, b), b)]
        allowed = keys >= jnp.concatenate([begin, begin], axis=1)
        if diagonal:
            cols = i * b + lax.rem(lax.broadcasted_iota(jnp.int32, (1, 2 * b), 1), b)
            allowed = allowed & (keys <= cols)
        pt = jnp.where(allowed, pt, 0.0)
        dv_acc[...] += dot(pt.astype(BF16), gs)
        dpt = dot(v, gs, NT)
        dst = (pt * (dpt - stat_ref[i, 1:2, :])).astype(BF16)
        dk_acc[...] += dot(dst, qs)
        part = dot(kt, dst)
        to = pl.ds(pl.multiple_of(i * b, b), b)
        dqt_ref[0:64, to] += part[:, :b]
        dqt_ref[64:128, to] += part[:, b:]
        at = before + i - j
        steps((at * (n - 1)) // every, ((at + 1) * (n - 1)) // every, wide, down)

    step(j, True)

    @pl.loop(j + 1, blocks)
    def _(i):
        step(i, False)

    dk = dk_acc[...]
    dv = dv_acc[...]
    dk_ref[...] = dk + pltpu.roll(dk, 64, 1)
    dv_ref[...] = dv + pltpu.roll(dv, 64, 1)
    dq_ref[...] = dqt_ref[:, pl.ds(pl.multiple_of(j * b, b), b)].T * HEAD_SIZE ** (-0.5)

    @pl.when((g == 1) & (j == blocks - 1))
    def _():
        for each in keeps:
            each.wait()
        last_here.wait()
        last.wait()
        finish(n, wide, down)


def retreat(q, k, v, grad, raw, lse, starts, done, down_done, result, middle, names, n, b=512):
    packed, width = q.shape
    groups, lanes = width // 128, 128
    b = min(b, packed)
    blocks = packed // b
    half = middle.shape[1]
    col = pl.BlockSpec((packed, lanes), lambda g, j: (0, g))
    blk = pl.BlockSpec((b, lanes), lambda g, j: (j, g))
    some = pl.BlockSpec(memory_space=pl.ANY)
    out = jax.ShapeDtypeStruct((packed, width), F32)
    pairs = packed * (packed + b) // 2
    dma = pltpu.SemaphoreType.DMA

    def full(x):
        return jax.ShapeDtypeStruct((2, n, x.shape[1], 2 * x.shape[2]), BF16)

    exchange = pltpu.VMEM((packed // 2, half), BF16)
    two = pltpu.VMEM((2, packed // 2, half), BF16)
    return pl.pallas_call(
        functools.partial(retreat_kernel, n, names, b, packed),
        out_shape=(out, out, out, full(done), full(down_done), jax.ShapeDtypeStruct((packed, half), BF16)),
        grid=(groups, blocks),
        in_specs=[col, blk, blk, col, col, pl.BlockSpec((1, 2, packed), lambda g, j: (g, 0, 0)),
                  pl.BlockSpec((1, packed), lambda g, j: (0, 0)), some, some, some,
                  pl.BlockSpec(middle.shape, lambda g, j: (0, 0), pipeline_mode=pl.Buffered(1))],
        out_specs=(blk, blk, blk, some, some, some),
        scratch_shapes=[
            pltpu.VMEM((2 * packed, lanes), BF16), pltpu.VMEM((2 * packed, lanes), BF16),
            pltpu.VMEM((blocks, 2, 2 * b), F32), pltpu.VMEM((lanes, packed), F32),
            pltpu.VMEM((b, lanes), F32), pltpu.VMEM((b, lanes), F32),
            two, two, exchange, exchange, *[dma((4, n - 1))] * 4, dma((2,)), dma((2,)), *[dma] * 4, dma((2,)), dma((9,)),
        ],
        compiler_params=pltpu.CompilerParams(collective_id=3, has_side_effects=True, vmem_limit_bytes=60 << 20),
        cost_estimate=pl.CostEstimate(flops=10 * groups * 2 * pairs * 256, transcendentals=2 * groups * pairs,
                                      bytes_accessed=20 * packed * width),
        name="retreat",
    )(q, k, v, grad, raw, lse, starts[None, :], done, down_done, result, middle)


def close_kernel(n, names, near_ref, far_ref, out_ref, to_near_ref, to_far_ref, stat_ref, keep_ref, tokens_ref, gain_ref,
                 vector_ref, thin_ref, lone_ref, sums_ref, grad_ref,
                 slots, lone_slots, beside_in, beside_stat, across_out, across_in, stat_out, stat_in, group_in, ring_in, mine,
                 rs_send, rs_recv, ag_send, ag_recv, lone_send, lone_recv, lone_out_send, lone_out_recv, cross_send, cross_recv,
                 group_send, group_recv, all_send, all_recv, beside_send, beside_recv, across_send, across_recv,
                 last_send, last_recv):
    me = Group(names, n)
    me.arrive([*me.along, me.across, me.beside, me.opposite])
    half = tokens_ref.shape[1]
    count = keep_ref.shape[0]
    thin = Reduce(me, (far_ref, near_ref), slots, rs_send, rs_recv)
    lone = Reduce(me, (out_ref,), lone_slots, lone_send, lone_recv)
    thin_out = Spread(me, thin_ref, ag_send, ag_recv)
    lone_out = Spread(me, lone_ref, lone_out_send, lone_out_recv)

    own_rows = pl.ds(pl.multiple_of(me.col * count, count), count)
    other_rows = pl.ds(pl.multiple_of((1 - me.col) * count, count), count)
    besides = [remote(src.at[other_rows, :], dst, beside_send.at[k], beside_recv.at[k], me.beside)
               for k, (src, dst) in enumerate(((to_far_ref, beside_in.at[0]), (stat_ref, beside_stat), (to_near_ref, beside_in.at[1])))]
    for each in besides:
        each.start()
    thin.start()
    lone.start()
    gathers = [remote(vector_ref, group_in.at[k], group_send.at[k], group_recv.at[k], target)
               for k, target in enumerate((me.across, me.beside, me.opposite))]
    for gather in gathers:
        gather.start()

    acrosses = [remote(src, dst, across_send.at[k], across_recv.at[k], me.across)
                for k, (src, dst) in enumerate(((across_out, across_in), (stat_out, stat_in)))]
    besides[0].wait()
    across_out[...] = (to_far_ref[own_rows, :].astype(F32) + beside_in[0].astype(F32)).astype(BF16)
    acrosses[0].start()
    besides[1].wait()
    stat_out[...] = stat_ref[own_rows, :] + beside_stat[...]
    acrosses[1].start()

    for gather in gathers:
        gather.wait()
    mine[...] = vector_ref[...] + group_in[0] + group_in[1] + group_in[2]
    spreads = [remote(mine, ring_in.at[k], all_send.at[k], all_recv.at[k], target) for k, target in enumerate(me.along)]
    for spread in spreads:
        spread.start()
    steps(0, n - 1, thin, lone)

    crosses = [remote(thin.last(s), thin_out.piece(s, me.own(s % 2), me.row), cross_send.at[s], cross_recv.at[s], me.across)
               for s in range(2)]
    for cross in crosses:
        cross.start()
    for s in (2, 3):
        thin_out.piece(s, me.own(s % 2))[...] = thin.last(s)[...]
        thin_out.start(s)
    for s in range(2):
        lone_out.piece(s, me.own(s % 2))[...] = lone.last(s)[...]
        lone_out.start(s)
    for s in range(2):
        crosses[s].wait()
        thin_out.start(s)

    besides[2].wait()
    acrosses[0].wait()
    acrosses[1].wait()
    grad = to_near_ref[own_rows, :].astype(F32) + beside_in[1].astype(F32) + across_in[...].astype(F32)
    inverse = stat_ref[own_rows, pl.ds(HEAD_SIZE, 1)]
    stat = (stat_out[:, :1] + stat_in[:, :1]) / (2 * half)
    near = tokens_ref[own_rows, :].astype(F32) * inverse
    grad_ref[own_rows, :] = (inverse * (grad * gain_ref[...] - near * stat) + keep_ref[...]).astype(BF16)
    last = remote(grad_ref.at[own_rows, :], grad_ref.at[own_rows, :], last_send, last_recv, me.beside)
    last.start()

    steps(0, n - 1, thin_out, lone_out)

    total = mine[...]
    for spread in spreads:
        spread.wait()
    for k in range(n - 1):
        total = total + ring_in[k]
    sums_ref[...] = total
    last.wait()
    finish(n, thin, lone, thin_out, lone_out)


def close(near, far, out, to_near, to_far, stat, keep, tokens, gain, vector, names, n):
    packed, half = tokens.shape
    count = packed // 2
    rows, thin, lone = near.shape[1], near.shape[2] // 2, out.shape[2] // 2
    vmem = pl.BlockSpec(memory_space=pltpu.VMEM)
    dma = pltpu.SemaphoreType.DMA

    def shape(*dims, dtype=BF16):
        return jax.ShapeDtypeStruct(dims, dtype)

    exchange = pltpu.VMEM((count, half), BF16)
    stats = pltpu.VMEM((count, stat.shape[1]), F32)
    return pl.pallas_call(
        functools.partial(close_kernel, n, names),
        out_shape=(shape(2, n, rows, 2 * thin), shape(n, rows, 2 * lone), shape(*vector.shape, dtype=F32), shape(packed, half)),
        in_specs=[vmem] * 10,
        out_specs=(vmem,) * 4,
        scratch_shapes=[
            pltpu.VMEM((4, n - 1, rows, thin), BF16), pltpu.VMEM((2, n - 1, rows, lone), BF16),
            pltpu.VMEM((2, count, half), BF16), stats, exchange, exchange, stats, stats,
            pltpu.VMEM((3, *vector.shape), F32), pltpu.VMEM((n - 1, *vector.shape), F32), pltpu.VMEM(vector.shape, F32),
            *[dma((4, n - 1))] * 4, *[dma((2, n - 1))] * 4, dma((2,)), dma((2,)), dma((3,)), dma((3,)), dma((n - 1,)), dma((n - 1,)),
            dma((3,)), dma((3,)), dma((2,)), dma((2,)), dma, dma,
        ],
        compiler_params=pltpu.CompilerParams(collective_id=2, has_side_effects=True, vmem_limit_bytes=60 << 20),
        cost_estimate=pl.CostEstimate(flops=40 * packed * half, transcendentals=0, bytes_accessed=200 << 20),
        name="close",
    )(near, far, out, to_near, to_far, stat, keep, tokens, gain, vector)


def widen_kernel(widths, units, wide_ref, down_ref, thin_ref, lone_ref, gate_out, up_out, down_out, q_out, k_out, v_out, lone_out):
    for part in range(2):
        for out, begin in ((gate_out, 0), (up_out, units)):
            out[:, part * units:(part + 1) * units] = wide_ref[part, :, begin:begin + units].astype(F32)
        begin = 0
        for out, columns in zip((q_out, k_out, v_out), widths):
            out[:, part * columns:(part + 1) * columns] = thin_ref[part, :, begin:begin + columns].astype(F32)
            begin += columns
    down_out[...] = down_ref[...].astype(F32)
    lone_out[...] = lone_ref[...].astype(F32)


def widen(wide, down, thin, lone, widths, parts=8):
    half = lone.shape[0]
    units = wide.shape[2] // 2
    rows, down_rows = half // parts, down.shape[0] // parts

    def one(rows, columns):
        return pl.BlockSpec((rows, columns), lambda i: (i, 0))

    def two(columns):
        return pl.BlockSpec((2, rows, columns), lambda i: (0, i, 0))

    shapes = [(half, 2 * units)] * 2 + [down.shape] + [(half, 2 * columns) for columns in widths] + [lone.shape]
    return pl.pallas_call(
        functools.partial(widen_kernel, widths, units),
        out_shape=tuple(jax.ShapeDtypeStruct(shape, F32) for shape in shapes),
        grid=(parts,),
        in_specs=[two(2 * units), one(down_rows, down.shape[1]), two(thin.shape[2]), one(rows, lone.shape[1])],
        out_specs=tuple(one(down_rows if k == 2 else rows, shape[1]) for k, shape in enumerate(shapes)),
        compiler_params=pltpu.CompilerParams(vmem_limit_bytes=40 << 20),
        cost_estimate=pl.CostEstimate(flops=0, transcendentals=0, bytes_accessed=6 * (wide.size + down.size + thin.size + lone.size)),
        name="widen",
    )(wide, down, thin, lone)


def gated(x, *deps):
    late = functools.reduce(jnp.logical_or, [dep != dep for dep in deps])
    return jnp.where(late, jnp.zeros_like(x), x)


def corner(x):
    return x[(0,) * x.ndim].astype(F32)


def shards(
    tokens,
    seq_lengths,
    query_weight,
    key_matrix,
    value_matrix,
    out_weight,
    gate_weight,
    up_weight,
    down_weight,
    attn_gain,
    ffn_gain,
    query_gain,
    key_gain,
    cotangent,
):
    packed, half = tokens.shape
    row, col, group = lax.axis_index("row"), lax.axis_index("col"), lax.axis_index("dp")
    parts = lax.axis_size("dp")
    width = 2 * half

    near_own = part_of(tokens, col, 0)
    far_own = swap(near_own, "row")
    qkv = jnp.concatenate(
        [part_of(w, row, 1) for w in (query_weight, key_matrix, value_matrix)], axis=1)
    qkv_sent = jnp.concatenate(
        [part_of(w, 1 - row, 1) for w in (query_weight, key_matrix, value_matrix)], axis=1)
    qkv_far = swap(qkv_sent, "row")
    gains = jnp.stack([attn_gain, ffn_gain])
    gains_far = swap(gains, "row")
    far = ordered(far_own, swap(far_own, "col"), col)

    def far_weight(sent):
        piece = swap(gated(part_of(sent, group, 0, parts), corner(far_own)), "row")
        return lax.all_gather(piece, "dp", axis=0, tiled=True), corner(piece)

    gate_up_near = jnp.concatenate([part_of(gate_weight, row, 1), part_of(up_weight, row, 1)], axis=1)
    gate_up_far, sign_one = far_weight(
        jnp.concatenate([part_of(gate_weight, 1 - row, 1), part_of(up_weight, 1 - row, 1)], axis=1))
    down_near = part_of(down_weight, row, 0)
    down_far, sign_two = far_weight(part_of(down_weight, 1 - row, 0))
    units = down_near.shape[0]

    out_far = swap(gated(out_weight, sign_one, sign_two), "row")
    out_c = jnp.concatenate([out_weight, out_far], axis=1)
    out_n = swap(out_c, "col")
    out_own = part_of(out_c, row, 0)
    out_all = jnp.concatenate(
        [out_own, part_of(out_n, row, 0), part_of(out_c, 1 - row, 0), part_of(out_n, 1 - row, 0)], axis=0)

    cot_far_own = swap(gated(part_of(cotangent, col, 0), corner(out_far)), "row")
    cot_far = ordered(cot_far_own, swap(cot_far_own, "col"), col)

    starts = layout(seq_lengths[0], packed)
    cosine, sine = rope_tables(jnp.arange(packed, dtype=jnp.int32) - starts)
    q_gain = jnp.tile(query_gain, 2)[None, :]
    k_gain = jnp.tile(key_gain, 2)[None, :]
    small = (attn_gain[None, :], gains_far[0][None, :], qkv, qkv_far, q_gain, k_gain)
    hid_near, hid_far, raw, q, k, v = project(tokens, far, *small, cosine, sine)

    low, attended_raw, totals = attend(q, k, v, starts)

    chip = jnp.concatenate([part_of(low, col, 0), swap(part_of(low, 1 - col, 0), "col")], axis=1)
    attended = jnp.concatenate([chip, swap(chip, "row")], axis=1)
    mine = jnp.concatenate([near_own, far_own], axis=1)
    middle = mine.astype(F32) + dot(attended, out_all)
    inverse_two = lax.rsqrt(jnp.sum(middle * middle, axis=1, keepdims=True) / width + EPSILON)
    normal_two = middle * inverse_two
    gain_two = jnp.concatenate([ffn_gain, gains_far[1]])[None, :]
    hidden_c = (normal_two * gain_two).astype(BF16)
    hidden = ordered(hidden_c, swap(hidden_c, "col"), col)
    gate_up = jnp.concatenate([gate_up_near, gate_up_far], axis=0)
    down = jnp.concatenate([down_near, down_far], axis=1)
    active, feed_grads, result, back = feed(hidden, cotangent, cot_far, gate_up, down)

    grad_down_near, grad_down_far = (
        over_t(active, cot).astype(BF16).reshape(parts, units // parts, -1) for cot in (cotangent, cot_far))
    grad_gate_up = over_t(hidden, feed_grads).astype(BF16).reshape(2, parts, half // parts, -1)
    names = ("dp", "row", "col")
    branch, keep, ffn_sum, done, down_done = turn(
        grad_gate_up[0], grad_gate_up[1], grad_down_near, grad_down_far, back, middle, cotangent, cot_far, gain_two, names, parts)

    grad_attended = (dot(branch[:, :half], out_own[:, :half], NT) + dot(branch[:, half:], out_own[:, half:], NT)).astype(BF16)
    grad_out = over_t(attended, part_of(branch[:, :half], col, 0))
    quarter = out_own.shape[0]
    kept = jnp.concatenate([grad_out[:quarter], grad_out[2 * quarter:3 * quarter]], axis=0)
    sent = jnp.concatenate([grad_out[quarter:2 * quarter], grad_out[3 * quarter:]], axis=0)
    grad_out = kept + swap(sent.astype(BF16), "col").astype(F32)
    grad_out = ordered(grad_out[:quarter], grad_out[quarter:], row).astype(BF16).reshape(parts, half // parts, -1)

    dq, dk, dv, wide_full, down_full, output = retreat(
        q, k, v, grad_attended, attended_raw, totals, starts, done, down_done, result, middle[:, :half], names, parts)
    grads, to_near, to_far, stat_one, q_sum, k_sum, near_sum, far_sum = project_back(
        dq, dk, dv, raw, tokens, far, *small, cosine, sine)
    near_grads, far_grads = (
        over_t(hid, grads).astype(BF16).reshape(parts, half // parts, -1) for hid in (hid_near, hid_far))

    def folded(x):
        return x[0, :HEAD_SIZE] + x[0, HEAD_SIZE:]

    vector = jnp.concatenate([
        ordered(near_sum[0], far_sum[0], row), ordered(ffn_sum[0, :half], ffn_sum[0, half:], row) * 0.5,
        folded(q_sum), folded(k_sum)])
    length = vector.shape[0]
    lines = -(-length // 1024) * 8
    vector = jnp.concatenate([vector, jnp.zeros((lines * 128 - length,), F32)]).reshape(lines, 128)
    thin_full, out_full, sums, grad_tokens = close(
        near_grads, far_grads, grad_out, to_near, to_far, stat_one, keep, tokens, attn_gain[None, :], vector, names, parts)
    sums = sums.reshape(-1)
    widths = (query_weight.shape[1] // 2, key_matrix.shape[1] // 2, value_matrix.shape[1] // 2)
    gate_sum, up_sum, down_sum, q_weight_sum, k_weight_sum, v_weight_sum, out_sum = widen(
        wide_full.reshape(2, half, -1), down_full.reshape(2 * units, half), thin_full.reshape(2, half, -1),
        out_full.reshape(half, -1), widths)
    return (
        output,
        grad_tokens,
        q_weight_sum,
        k_weight_sum,
        v_weight_sum,
        out_sum,
        gate_sum,
        up_sum,
        down_sum,
        part_of(sums[:width], row, 0),
        part_of(sums[width:2 * width], row, 0),
        sums[2 * width:2 * width + HEAD_SIZE],
        sums[2 * width + HEAD_SIZE:2 * width + 2 * HEAD_SIZE],
    )


def solution(mesh):
    return jax.shard_map(
        shards,
        mesh=mesh,
        in_specs=(
            P("dp", "row"),
            P("dp", None),
            P("row", "col"),
            P("row", "col"),
            P("row", "col"),
            P("col", "row"),
            P("row", "col"),
            P("row", "col"),
            P("col", "row"),
            P("row"),
            P("row"),
            P(),
            P(),
            P("dp", "row"),
        ),
        out_specs=(
            P("dp", "row"),
            P("dp", "row"),
            P("row", "col"),
            P("row", "col"),
            P("row", "col"),
            P("col", "row"),
            P("row", "col"),
            P("row", "col"),
            P("col", "row"),
            P("row"),
            P("row"),
            P(),
            P(),
        ),
        check_vma=False,
    )
```

```python
import functools
import math

import jax
import jax.numpy as jnp
from jax import lax
from jax.experimental import pallas as pl
from jax.experimental.pallas import tpu as pltpu
from jax.sharding import PartitionSpec as P

HEAD_SIZE = 64
EPSILON = 1e-05
ROPE_BASE = 1000000.0
F32, BF16 = jnp.float32, jnp.bfloat16
MESH = pl.DeviceIdType.MESH


def dot(a, b, dims=(((1,), (0,)), ((), ()))):
    return lax.dot_general(a, b, dims, preferred_element_type=F32)


NT = (((1,), (1,)), ((), ()))

def stacked(x):
    first = lax.broadcasted_iota(jnp.int32, x.shape, 1) < 64
    zero = jnp.zeros_like(x)
    return jnp.concatenate([jnp.where(first, x, zero), jnp.where(first, zero, x)], axis=0)


def head_sums(x):
    first = lax.broadcasted_iota(jnp.int32, x.shape, 1) < HEAD_SIZE
    one = jnp.sum(jnp.where(first, x, 0.0), axis=1, keepdims=True)
    two = jnp.sum(jnp.where(first, 0.0, x), axis=1, keepdims=True)
    return jnp.where(first, one, two)


def swapped(x):
    low = lax.rem(lax.broadcasted_iota(jnp.int32, x.shape, 1), HEAD_SIZE) < HEAD_SIZE // 2
    return jnp.where(low, pltpu.roll(x, 96, 1), pltpu.roll(x, 32, 1))


def doubled(x):
    first = lax.broadcasted_iota(jnp.int32, x.shape, 1) < HEAD_SIZE
    other = pltpu.roll(x, HEAD_SIZE, 1)
    return jnp.where(first, x, other), jnp.where(first, other, x)


def project_back_kernel(groups, dq_ref, dk_ref, dv_ref, raw_ref, near_ref, far_ref, gain_near_ref, gain_far_ref,
                        w_near_ref, w_far_ref, q_gain_ref, k_gain_ref, table_ref,
                        grads_ref, to_near_ref, to_far_ref, stat_ref, q_sum_ref, k_sum_ref, near_sum_ref, far_sum_ref):
    @pl.when(pl.program_id(0) == 0)
    def _():
        for ref in (q_sum_ref, k_sum_ref, near_sum_ref, far_sum_ref):
            ref[...] = jnp.zeros_like(ref)

    cosine, sine = rope_block(table_ref, slice(None))
    lanes = 2 * HEAD_SIZE
    first = lax.broadcasted_iota(jnp.int32, cosine.shape, 1) < HEAD_SIZE

    def back(grad, x, gain):
        inverse = lax.rsqrt(head_sums(x * x) / HEAD_SIZE + EPSILON)
        normed = x * inverse
        turned = grad * cosine - swapped(grad) * sine
        inner = turned * gain
        part = inverse * (inner - normed * (head_sums(inner * normed) / HEAD_SIZE))
        return part, jnp.sum(turned * normed, axis=0, keepdims=True)

    grads = []
    for n in range(groups):
        cut = slice(n * lanes, (n + 1) * lanes)
        part, total = back(dq_ref[:, cut], raw_ref[:, cut], q_gain_ref[...])
        q_sum_ref[...] += total
        grads.append(part.astype(BF16))
    for n in range(groups // 2):
        at = groups * lanes + n * lanes
        part, total = back(jnp.where(first, dk_ref[:, 2 * n * lanes:(2 * n + 1) * lanes], dk_ref[:, (2 * n + 1) * lanes:(2 * n + 2) * lanes]), raw_ref[:, at:at + lanes], k_gain_ref[...])
        k_sum_ref[...] += total
        grads.append(part.astype(BF16))
    for n in range(groups // 2):
        grads.append(jnp.where(first, dv_ref[:, 2 * n * lanes:(2 * n + 1) * lanes], dv_ref[:, (2 * n + 1) * lanes:(2 * n + 2) * lanes]).astype(BF16))
    grads = jnp.concatenate(grads, axis=1)
    grads_ref[...] = grads
    to_near = dot(grads, w_near_ref[...], NT)
    to_far = dot(grads, w_far_ref[...], NT)
    to_near_ref[...] = to_near.astype(BF16)
    to_far_ref[...] = to_far.astype(BF16)
    near = near_ref[...].astype(F32)
    far = far_ref[...].astype(F32)
    width = near.shape[1] + far.shape[1]
    total = jnp.sum(near * near, axis=1, keepdims=True) + jnp.sum(far * far, axis=1, keepdims=True)
    inverse = lax.rsqrt(total / width + EPSILON)
    near = to_near * (near * inverse)
    far = to_far * (far * inverse)
    near_sum_ref[...] += jnp.sum(near, axis=0, keepdims=True)
    far_sum_ref[...] += jnp.sum(far, axis=0, keepdims=True)
    stat = jnp.sum(near * gain_near_ref[...], axis=1, keepdims=True) + jnp.sum(far * gain_far_ref[...], axis=1, keepdims=True)
    stat_ref[...] = jnp.where(first, stat, inverse)


def project_back(dq, dk, dv, raw, near, far, gain_near, gain_far, w_near, w_far, q_gain, k_gain, table, rows=512):
    packed, half = near.shape
    columns = w_near.shape[1]
    groups = columns // (4 * HEAD_SIZE)
    width = groups * 2 * HEAD_SIZE
    rows = min(rows, packed)

    def tile(n):
        return pl.BlockSpec((rows, n), lambda i: (i, 0))

    def whole(x):
        return pl.BlockSpec(x.shape, lambda i: (0, 0))

    def kept(n):
        return pl.BlockSpec((1, n), lambda i: (0, 0))

    def out(n, dtype, many=packed):
        return jax.ShapeDtypeStruct((many, n), dtype)

    small = (gain_near, gain_far, w_near, w_far, q_gain, k_gain)
    lanes = 2 * HEAD_SIZE
    return pl.pallas_call(
        functools.partial(project_back_kernel, groups),
        out_shape=(out(columns, BF16), out(half, BF16), out(half, BF16), out(lanes, F32), out(lanes, F32, 1), out(lanes, F32, 1),
                   out(half, F32, 1), out(half, F32, 1)),
        grid=(packed // rows,),
        in_specs=[tile(width)] * 3 + [tile(raw.shape[1]), tile(half), tile(half), *map(whole, small),
                  pl.BlockSpec((table.shape[0], rows), lambda i: (0, i))],
        out_specs=(tile(columns), tile(half), tile(half), tile(lanes), kept(lanes), kept(lanes), kept(half), kept(half)),
        compiler_params=pltpu.CompilerParams(vmem_limit_bytes=44 << 20),
        cost_estimate=pl.CostEstimate(flops=4 * packed * half * columns, transcendentals=packed * 8,
                                      bytes_accessed=packed * (8 * half + 18 * width)),
        name="project_back",
    )(dq, dk, dv, raw, near, far, *small, table)


def layout(lengths, packed):
    count = lengths.shape[0]
    numbers = jnp.arange(count, dtype=jnp.int32)
    ends = jnp.sum(jnp.where(numbers[None, :] <= numbers[:, None], lengths[None, :], 0), axis=1)
    begins = ends - lengths
    places = jnp.arange(packed, dtype=jnp.int32)
    member = jnp.sum((places[:, None] >= ends[None, :]).astype(jnp.int32), axis=1)
    return jnp.sum(jnp.where(member[:, None] == numbers[None, :], begins[None, :], 0), axis=1)


def rope_table(position):
    half = HEAD_SIZE // 2
    inverse = jnp.exp(jnp.arange(half, dtype=F32) * (-2.0 * math.log(ROPE_BASE) / HEAD_SIZE))
    angles = position.astype(F32)[None, :] * inverse[:, None]
    return jnp.concatenate([jnp.cos(angles), jnp.sin(angles)], axis=0)


def swap(x, axis):
    return jax.tree.map(lambda part: lax.ppermute(part, axis, [(0, 1), (1, 0)]), x)


def ordered(own, other, index, axis=0):
    return jnp.where(index == 0, jnp.concatenate([own, other], axis), jnp.concatenate([other, own], axis))


def part_of(x, index, axis, parts=2):
    size = x.shape[axis] // parts
    return lax.dynamic_slice_in_dim(x, index * size, size, axis)


def over_t(left, right):
    return dot(left, right, (((0,), (0,)), ((), ())))


def feed_kernel(units, row_ref, hidden_ref, cot_near_ref, cot_far_ref, gate_ref, up_ref, far_ref, down_near_ref, down_far_ref,
                active_ref, grads_ref, result_ref, back_ref):
    half = cot_near_ref.shape[1]
    near, far = hidden_ref[:, :half], hidden_ref[:, half:]
    gate = dot(near, gate_ref[...]) + dot(far, far_ref[:, :units])
    upward = dot(near, up_ref[...]) + dot(far, far_ref[:, units:])
    grad_active = dot(cot_near_ref[...], down_near_ref[...], NT) + dot(cot_far_ref[...], down_far_ref[...], NT)
    sig = 1.0 / (1.0 + jnp.exp(-gate))
    lifted = gate * sig
    active = (lifted * upward).astype(BF16)
    grad_gate = (grad_active * upward * (sig * (1.0 + gate * (1.0 - sig)))).astype(BF16)
    grad_up = (grad_active * lifted).astype(BF16)
    active_ref[...] = active
    grads_ref[:, :units] = grad_gate
    grads_ref[:, units:] = grad_up
    result_ref[:, :half] = dot(active, down_near_ref[...]).astype(BF16)
    result_ref[:, half:] = dot(active, down_far_ref[...]).astype(BF16)
    back_ref[:, :half] = (dot(grad_gate, gate_ref[...], NT) + dot(grad_up, up_ref[...], NT)).astype(BF16)
    back_ref[:, half:] = (dot(grad_gate, far_ref[:, :units], NT) + dot(grad_up, far_ref[:, units:], NT)).astype(BF16)


def feed(row, hidden, cot_near, cot_far, gate, up, far, down, down_far, rows=256):
    packed, width = hidden.shape
    units, half = down_far.shape
    rows = min(rows, packed)

    def tile(n):
        return pl.BlockSpec((rows, n), lambda i, row: (i, 0))

    def once(shape, place):
        return pl.BlockSpec(shape, place, pipeline_mode=pl.Buffered(1))

    def out(n):
        return jax.ShapeDtypeStruct((packed, n), BF16)

    columns = once((half, units), lambda i, row: (0, row[0]))
    return pl.pallas_call(
        functools.partial(feed_kernel, units),
        out_shape=(out(units), out(2 * units), out(width), out(width)),
        grid_spec=pltpu.PrefetchScalarGridSpec(
            num_scalar_prefetch=1, grid=(packed // rows,),
            in_specs=[tile(width), tile(half), tile(half), columns, columns, once(far.shape, lambda i, row: (0, 0)),
                      once((units, half), lambda i, row: (row[0], 0)), once(down_far.shape, lambda i, row: (0, 0))],
            out_specs=(tile(units), tile(2 * units), tile(width), tile(width)),
        ),
        compiler_params=pltpu.CompilerParams(vmem_limit_bytes=56 << 20),
        cost_estimate=pl.CostEstimate(flops=12 * packed * width * units, transcendentals=packed * units,
                                      bytes_accessed=packed * (8 * width + 6 * units) + 6 * width * units),
        name="feed",
    )(row, hidden, cot_near, cot_far, gate, up, far, down, down_far)


class Group:
    def __init__(self, names, total, n=None):
        n = total if n is None else n
        self.n = n
        self.dp, self.row, self.col = (lax.axis_index(name) for name in names)
        self.base, member = (self.dp // n) * n, self.dp % n
        side = member % 2
        self.place = (member // 2) * (1 - side) + (n - 1 - member // 2) * side
        self.across = (self.dp, 1 - self.row, self.col)
        self.beside = (self.dp, self.row, 1 - self.col)
        self.opposite = (self.dp, 1 - self.row, 1 - self.col)
        self.along = [((self.dp + k) % total, self.row, self.col) for k in range(1, total)]
        self.ring = [(self.at(self.place + 1), self.row, self.col), (self.at(self.place - 1), self.row, self.col)]

    def at(self, position):
        position = (position + 2 * self.n) % self.n
        back = position // (self.n // 2)
        return self.base + (position * (1 - back) + (self.n - 1 - position) * back) * 2 + back

    def arrive(self, targets):
        barrier = pltpu.get_barrier_semaphore()
        for target in targets:
            pl.semaphore_signal(barrier, inc=1, device_id=target, device_id_type=MESH)
        pl.semaphore_wait(barrier, len(targets))

    def reduced(self, way, t):
        return (self.place - t - 1 + 2 * self.n) % self.n if way == 0 else (self.place + t + 1) % self.n

    def spread(self, way, t):
        return (self.place - t + 2 * self.n) % self.n if way == 0 else (self.place + t) % self.n

    def own(self, way):
        return (self.place + 1) % self.n if way == 0 else (self.place + self.n - 1) % self.n


def remote(src, dst, send, recv, target):
    return pltpu.make_async_remote_copy(
        src_ref=src, dst_ref=dst, send_sem=send, recv_sem=recv, device_id=target, device_id_type=MESH)


class Reduce:
    def __init__(self, me, parts, slots, send, recv):
        self.me, self.parts, self.slots, self.send, self.recv = me, parts, slots, send, recv
        self.columns = parts[0].shape[2] // 2

    def local(self, s, chunk):
        return self.parts[s // 2].at[chunk, :, pl.ds((s % 2) * self.columns, self.columns)]

    def copy(self, s, t, src):
        return remote(src, self.slots.at[s, t], self.send.at[s, t], self.recv.at[s, t], self.me.ring[s % 2])

    def start(self):
        for s in range(2 * len(self.parts)):
            self.copy(s, 0, self.local(s, self.me.place)).start()

    def step(self, t):
        for s in range(2 * len(self.parts)):
            slot = self.slots.at[s, t]
            self.copy(s, t, slot).wait_recv()
            slot[...] = (slot[...].astype(F32) + self.local(s, self.me.reduced(s % 2, t))[...].astype(F32)).astype(BF16)

            @pl.when(t < self.me.n - 2)
            def _():
                self.copy(s, t + 1, slot).start()

    def last(self, s):
        return self.slots.at[s, self.me.n - 2]

    def finish(self, t):
        for s in range(2 * len(self.parts)):
            self.copy(s, t, self.slots.at[s, t]).wait_send()


class Spread:
    def __init__(self, me, full, send, recv):
        self.me, self.full, self.send, self.recv = me, full, send, recv
        self.lone = len(full.shape) == 3
        self.columns = full.shape[-1] // 2
        self.streams = (0, 1) if self.lone else (2, 3, 0, 1)

    def piece(self, s, chunk, quarter=None):
        lanes = pl.ds((s % 2) * self.columns, self.columns)
        if self.lone:
            return self.full.at[chunk, :, lanes]
        if quarter is None:
            quarter = 1 - self.me.row if s < 2 else self.me.row
        return self.full.at[quarter, chunk, :, lanes]

    def copy(self, s, t, chunk, src=None):
        piece = self.piece(s, chunk)
        return remote(piece if src is None else src, piece, self.send.at[s, t], self.recv.at[s, t], self.me.ring[s % 2])

    def start(self, s, src=None):
        self.copy(s, 0, self.me.own(s % 2), src).start()

    def step(self, t):
        for s in self.streams:
            chunk = self.me.spread(s % 2, t)
            self.copy(s, t, chunk).wait_recv()

            @pl.when(t < self.me.n - 2)
            def _():
                self.copy(s, t + 1, chunk).start()

    def finish(self, t):
        for s in self.streams:
            self.copy(s, t, 0).wait_send()


def steps(begin, end, *rings):
    def step(t, carry):
        for ring in rings:
            ring.step(t)
        return carry

    lax.fori_loop(begin, end, step, 0)


def finish(n, *rings):
    def each(t, carry):
        for ring in rings:
            ring.finish(t)
        return carry

    lax.fori_loop(0, n - 1, each, 0)


def begin_kernel(n, m, names, b, token_ref, cot_ref, wq_ref, wk_ref, wv_ref, gate_ref, up_ref, down_ref, wo_ref, gains_ref,
                 q_gain_ref, k_gain_ref, table_ref, starts_ref,
                 far_out, gate_up_out, down_out, cot_out, gains_out, hid_near_out, hid_far_out, raw_out, q_out, k_out, v_out,
                 heads_out, totals_out, attended_out, middle_out, hidden_out, wo_out, w_near_out, w_far_out,
                 near, far, w_near, w_far, wo_far, wo_all, hid_near, hid_far, raw, q_all, k_all, v_all, low, heads, attended,
                 middle, hidden, acc_ref, mass_ref,
                 local_sem, store_sem, token_send, token_recv, pass_send, pass_recv, piece_send, piece_recv, cot_send, cot_recv,
                 qkv_send, qkv_recv, wide_send, wide_recv, thin_send, thin_recv, out_send, out_recv, wo_send, wo_recv,
                 low_send, low_recv, hidden_send, hidden_recv):
    me = Group(names, n, m)
    packed, half = token_ref.shape
    count = packed // 2
    row, col = me.row, me.col
    lanes = 2 * HEAD_SIZE
    groups = q_all.shape[1] // lanes
    width = groups * lanes
    kv = groups * HEAD_SIZE
    units = gate_ref.shape[1] // 2
    chunk = half // m
    down_chunk = units // m
    pieces = 4
    rows = count // pieces
    me.arrive([*me.ring, me.across, me.beside, me.opposite])

    def at(begin, size):
        return pl.ds(pl.multiple_of(begin, size), size)

    def own_rows(k):
        return at(col * count + k * rows, rows)

    def other_rows(k):
        return at((1 - col) * count + k * rows, rows)

    def piece(k, src, dst):
        return remote(src, dst, piece_send.at[k], piece_recv.at[k], me.across)

    up_chunk, low_chunk = me.own(0), me.own(1)
    first_rows, second_rows = at(up_chunk * chunk, chunk), at(low_chunk * chunk, chunk)
    qkv_pieces = [
        piece(0, wq_ref.at[first_rows, at((1 - row) * width, width)], w_far.at[up_chunk, :, pl.ds(0, width)]),
        piece(1, wk_ref.at[second_rows, at((1 - row) * kv, kv)], w_far.at[low_chunk, :, pl.ds(width, kv)]),
        piece(2, wv_ref.at[second_rows, at((1 - row) * kv, kv)], w_far.at[low_chunk, :, pl.ds(width + kv, kv)]),
        piece(3, gains_ref, gains_out),
    ]
    down_first = at((1 - row) * units + up_chunk * down_chunk, down_chunk)
    down_second = at((1 - row) * units + low_chunk * down_chunk, down_chunk)
    late_pieces = [
        piece(4, wo_ref.at[first_rows, pl.ds(0, half // 2)], wo_far.at[up_chunk, :, pl.ds(0, half // 2)]),
        piece(5, wo_ref.at[second_rows, pl.ds(half // 2, half // 2)], wo_far.at[low_chunk, :, pl.ds(half // 2, half // 2)]),
        piece(6, gate_ref.at[first_rows, at((1 - row) * units, units)], gate_up_out.at[up_chunk, :, pl.ds(0, units)]),
        piece(7, up_ref.at[second_rows, at((1 - row) * units, units)], gate_up_out.at[low_chunk, :, pl.ds(units, units)]),
        piece(8, down_ref.at[down_first, pl.ds(0, half // 2)], down_out.at[up_chunk, :, pl.ds(0, half // 2)]),
        piece(9, down_ref.at[down_second, pl.ds(half // 2, half // 2)], down_out.at[low_chunk, :, pl.ds(half // 2, half // 2)]),
    ]
    token_copies = [remote(token_ref.at[own_rows(k), :], far.at[own_rows(k), :], token_send.at[k], token_recv.at[k], me.across)
                    for k in range(pieces)]
    passes = [remote(far.at[own_rows(k), :], far.at[own_rows(k), :], pass_send.at[k], pass_recv.at[k], me.beside)
              for k in range(pieces)]
    cots = [remote(cot_ref.at[own_rows(k), :], cot_out.at[own_rows(k), :], cot_send.at[0, k], cot_recv.at[0, k], me.across)
            for k in range(pieces)]
    cot_passes = [remote(cot_out.at[own_rows(k), :], cot_out.at[own_rows(k), :], cot_send.at[1, k], cot_recv.at[1, k], me.beside)
                  for k in range(pieces)]
    for each in qkv_pieces + token_copies:
        each.start()

    def fetch(k, src, dst):
        return pltpu.make_async_copy(src, dst, local_sem.at[k])

    quarter = half // 2
    mine_rows, other_quarter = at(row * quarter, quarter), at((1 - row) * quarter, quarter)
    fetches = [
        fetch(0, token_ref, near),
        fetch(1, wq_ref.at[:, at(row * width, width)], w_near.at[:, pl.ds(0, width)]),
        fetch(2, wk_ref.at[:, at(row * kv, kv)], w_near.at[:, pl.ds(width, kv)]),
        fetch(3, wv_ref.at[:, at(row * kv, kv)], w_near.at[:, pl.ds(width + kv, kv)]),
        fetch(4, wo_ref.at[mine_rows, :], wo_all.at[pl.ds(0, quarter), pl.ds(0, half)]),
        fetch(5, wo_ref.at[other_quarter, :], wo_all.at[pl.ds(2 * quarter, quarter), pl.ds(0, half)]),
    ]
    for each in fetches:
        each.start()

    def wo_copy(k, src, rows_at, side):
        return remote(src, wo_all.at[pl.ds(rows_at, quarter), pl.ds(side, half)], wo_send.at[k], wo_recv.at[k], me.beside)

    wo_copies = [wo_copy(0, wo_ref.at[mine_rows, :], quarter, 0), wo_copy(1, wo_ref.at[other_quarter, :], 3 * quarter, 0)]
    for each in wo_copies:
        each.start()

    qkv = Spread(me, w_far, qkv_send, qkv_recv)
    wide = Spread(me, gate_up_out, wide_send, wide_recv)
    thin = Spread(me, down_out, thin_send, thin_recv)
    wo = Spread(me, wo_far, out_send, out_recv)
    for each in qkv_pieces:
        each.wait()
    for s in range(2):
        qkv.start(s)
    for k in range(pieces):
        steps(k * (m - 1) // pieces, (k + 1) * (m - 1) // pieces, qkv)
        token_copies[k].wait()
        passes[k].start()
        if k == pieces // 2:
            for each in late_pieces:
                each.start()
    for each in cots:
        each.start()
    for each in fetches:
        each.wait()

    def prepared(x, gain, cosine, sine):
        normed = x * lax.rsqrt(head_sums(x * x) / HEAD_SIZE + EPSILON) * gain
        return normed * cosine + swapped(normed) * sine

    far_gains = gains_out

    def project_block(k):
        block = at(((col * pieces + 2 * k) % (2 * pieces)) * rows, 2 * rows)
        x_near = near[block, :].astype(F32)
        x_far = far[block, :].astype(F32)
        total = jnp.sum(x_near * x_near, axis=1, keepdims=True) + jnp.sum(x_far * x_far, axis=1, keepdims=True)
        inverse = lax.rsqrt(total / (2 * half) + EPSILON)
        h_near = (x_near * inverse * gains_ref[0:1, :]).astype(BF16)
        h_far = (x_far * inverse * far_gains[0:1, :]).astype(BF16)
        hid_near[block, :] = h_near
        hid_far[block, :] = h_far
        out = dot(h_near, w_near[...]) + dot(h_far, w_far[...].reshape(half, w_far.shape[2]))
        raw[block, :] = out[:, :width + kv]
        cosine, sine = rope_block(table_ref, block)
        for g in range(groups):
            cut = slice(g * lanes, (g + 1) * lanes)
            part = prepared(out[:, cut], q_gain_ref[...], cosine, sine).astype(BF16)
            q_all[block, cut] = (part * HEAD_SIZE ** (-0.5)).astype(BF16)
        for g in range(groups // 2):
            begin = width + g * lanes
            twice = doubled(prepared(out[:, begin:begin + lanes], k_gain_ref[...], cosine, sine))
            value = doubled(out[:, begin + kv:begin + kv + lanes])
            for h in range(2):
                cut = slice((2 * g + h) * lanes, (2 * g + h + 1) * lanes)
                k_all[block, cut] = twice[h].astype(BF16)
                v_all[block, cut] = value[h].astype(BF16)

    rings = (wide, thin, wo)
    slots = 3 + groups * (packed // b) * (packed // b + 1) // 2

    def tick(k):
        steps((k * (m - 1)) // slots, ((k + 1) * (m - 1)) // slots, *rings)

    project_block(0)
    for each in late_pieces:
        each.wait()
    for ring in rings:
        for s in range(2):
            ring.start(s)
    project_block(1)
    tick(0)
    for k in range(pieces):
        passes[k].wait()
        if k % 2 == 1:
            project_block(2 + k // 2)
            tick(1 + k // 2)

    def store(k, src, dst):
        return pltpu.make_async_copy(src, dst, store_sem.at[k])

    stores = [store(k, src, dst) for k, (src, dst) in enumerate((
        (far, far_out), (hid_near, hid_near_out), (hid_far, hid_far_out), (raw, raw_out), (q_all, q_out), (k_all, k_out),
        (v_all, v_out)))]
    for each in stores:
        each.start()

    blocks = packed // b
    per_half = blocks // 2

    def low_copy(kind, g, i, target):
        slot = (2, 1, 3)[kind] * width + g * lanes
        return remote(low.at[at(i * b, b), pl.ds(g * lanes, lanes)],
                      attended.at[at((i % per_half) * b, b), pl.ds(slot, lanes)],
                      low_send.at[kind, g, i % per_half], low_recv.at[kind, g, i % per_half], target)

    for g in range(groups):
        cut = slice(g * lanes, (g + 1) * lanes)

        def query_block(i, carry, g=g, cut=cut):
            place = at(i * b, b)
            qs = stacked(q_all[place, cut])
            begins = starts_ref[place, :]
            begins = jnp.concatenate([begins, begins], axis=0)
            acc_ref[...] = jnp.zeros_like(acc_ref)
            mass_ref[...] = jnp.zeros_like(mass_ref)
            base = 3 + g * (blocks * (blocks + 1) // 2) + (i * (i + 1)) // 2

            def key_block(j, diagonal):
                keys = at(j * b, b)
                s = dot(qs, k_all[keys, cut], NT)
                columns = j * b + lax.broadcasted_iota(jnp.int32, (1, b), 1)
                allowed = columns >= begins
                if diagonal:
                    lines = i * b + lax.rem(lax.broadcasted_iota(jnp.int32, (2 * b, 1), 0), b)
                    allowed = allowed & (columns <= lines)
                p = jnp.where(allowed, jnp.exp(s), 0.0)
                mass = p[:, :128]
                for part in range(1, b // 128):
                    mass = mass + p[:, part * 128:(part + 1) * 128]
                mass_ref[...] += mass
                acc_ref[...] += dot(p.astype(BF16), v_all[keys, cut])
                tick(base + j)

            @pl.loop(0, i)
            def _(j):
                key_block(j, False)

            key_block(i, True)
            mass = jnp.sum(mass_ref[...], axis=1, keepdims=True)
            out = acc_ref[...] / mass
            first = lax.broadcasted_iota(jnp.int32, (b, lanes), 1) < HEAD_SIZE
            out = jnp.where(first, out[:b], out[b:])
            heads[place, cut] = out
            low[place, cut] = out.astype(BF16)
            total = jnp.log(jnp.sum(mass_ref[...].T, axis=0, keepdims=True))
            totals_out[g, 0:1, place] = total[:, :b]
            totals_out[g, 1:2, place] = total[:, b:]

            @pl.when(i // per_half == col)
            def _():
                attended[at((i % per_half) * b, b), cut] = out.astype(BF16)
                low_copy(0, g, i, me.across).start()

            @pl.when(i // per_half != col)
            def _():
                low_copy(1, g, i, me.beside).start()
                low_copy(2, g, i, me.opposite).start()
            return carry

        lax.fori_loop(0, blocks, query_block, 0)
    heads_store = store(7, heads, heads_out)
    heads_store.start()
    w_stores = [store(8 + 3 * per_half, w_near, w_near_out), store(9 + 3 * per_half, w_far, w_far_out)]
    for each in w_stores:
        each.start()

    local_far = []
    per = quarter // chunk
    for p, begin in ((0, row), (2, 1 - row)):
        for k in range(per):
            local_far.append(pltpu.make_async_copy(
                wo_far.at[begin * per + k], wo_all.at[pl.ds(p * quarter + k * chunk, chunk), pl.ds(half, half)],
                local_sem.at[6 + len(local_far)]))
    remote_far = []
    for p, begin in ((1, row), (3, 1 - row)):
        for k in range(per):
            remote_far.append(remote(
                wo_far.at[begin * per + k], wo_all.at[pl.ds(p * quarter + k * chunk, chunk), pl.ds(half, half)],
                wo_send.at[2 + len(remote_far)], wo_recv.at[2 + len(remote_far)], me.beside))
    for each in local_far + remote_far:
        each.start()
    for k in range(pieces):
        cots[k].wait()
        cot_passes[k].start()
    for each in local_far + remote_far + wo_copies:
        each.wait()
    w_stores.append(store(10 + 3 * per_half, wo_all.at[pl.ds(0, quarter), :], wo_out))
    w_stores[-1].start()

    gain = jnp.concatenate([gains_ref[1:2, :], far_gains[1:2, :]], axis=1)
    hidden_stores = []
    for k in range(per_half):
        for g in range(groups):
            for kind in range(3):
                low_copy(kind, g, k, me.beside).wait()
        part = slice(k * b, (k + 1) * b)
        place = at(col * count + k * b, b)
        tokens = jnp.concatenate([near[place, :], far[place, :]], axis=1).astype(F32)
        total = tokens + dot(attended[part, :], wo_all[...])
        middle[part, :] = total
        inverse = lax.rsqrt(jnp.sum(total * total, axis=1, keepdims=True) / (2 * half) + EPSILON)
        hidden[part, :] = (total * inverse * gain).astype(BF16)
        hidden_stores += [
            remote(hidden.at[pl.ds(k * b, b), :], hidden_out.at[place, :], hidden_send.at[k], hidden_recv.at[k], me.beside),
            pltpu.make_async_copy(hidden.at[pl.ds(k * b, b), :], hidden_out.at[place, :], store_sem.at[8 + 3 * k]),
            pltpu.make_async_copy(middle.at[pl.ds(k * b, b), :], middle_out.at[pl.ds(k * b, b), :], store_sem.at[9 + 3 * k]),
            pltpu.make_async_copy(attended.at[pl.ds(k * b, b), :], attended_out.at[pl.ds(k * b, b), :], store_sem.at[10 + 3 * k]),
        ]
        for each in hidden_stores[-4:]:
            each.start()
    for each in stores + [heads_store] + w_stores + hidden_stores + cot_passes:
        each.wait()
    finish(m, qkv, *rings)


def rope_block(table_ref, block):
    half = HEAD_SIZE // 2
    cosine, sine = table_ref[:half, block], table_ref[half:, block]
    return jnp.concatenate([cosine] * 4, axis=0).T, jnp.concatenate([-sine, sine] * 2, axis=0).T


def begin(tokens, cot, wq, wk, wv, gate, up, down, wo, gains, q_gain, k_gain, table, starts, names, n, b=512):
    packed, half = tokens.shape
    b = min(b, packed // 2)
    m = math.gcd(n, 8)
    width, kv, units = wq.shape[1] // 2, wk.shape[1] // 2, gate.shape[1] // 2
    groups = width // (2 * HEAD_SIZE)
    count = packed // 2
    vmem = pl.BlockSpec(memory_space=pltpu.VMEM)
    some = pl.BlockSpec(memory_space=pl.ANY)
    dma = pltpu.SemaphoreType.DMA

    outs = [((packed, half), BF16, some), ((m, half // m, 2 * units), BF16, some), ((m, units // m, half), BF16, some),
            ((packed, half), BF16, some), (gains.shape, F32, vmem), ((packed, half), BF16, some), ((packed, half), BF16, some),
            ((packed, width + kv), F32, some), ((packed, width), BF16, some), ((packed, width), BF16, some),
            ((packed, width), BF16, some), ((packed, width), F32, some), ((groups, 2, packed), F32, vmem),
            ((count, 2 * half), BF16, some), ((count, 2 * half), F32, some), ((packed, 2 * half), BF16, some),
            ((half // 2, 2 * half), BF16, some), ((half, width + 2 * kv), BF16, some), ((m, half // m, width + 2 * kv), BF16, some)]
    scratch = [((packed, half), BF16), ((packed, half), BF16), ((half, width + 2 * kv), BF16), ((m, half // m, width + 2 * kv), BF16),
               ((m, half // m, half), BF16), ((2 * half, 2 * half), BF16), ((packed, half), BF16), ((packed, half), BF16),
               ((packed, width + kv), F32), ((packed, width), BF16), ((packed, width), BF16), ((packed, width), BF16),
               ((packed, width), BF16), ((packed, width), F32), ((count, 2 * half), BF16), ((count, 2 * half), F32),
               ((count, 2 * half), BF16), ((2 * b, 2 * HEAD_SIZE), F32), ((2 * b, 2 * HEAD_SIZE), F32)]
    per_half = count // b
    ring = [dma((2, m - 1))] * 8
    return pl.pallas_call(
        functools.partial(begin_kernel, n, m, names, b),
        out_shape=tuple(jax.ShapeDtypeStruct(shape, dtype) for shape, dtype, _ in outs),
        in_specs=[some] * 9 + [vmem] * 5,
        out_specs=tuple(spec for *_, spec in outs),
        scratch_shapes=[
            *[pltpu.VMEM(shape, dtype) for shape, dtype in scratch],
            dma((6 + m,)), dma((11 + 3 * per_half,)), dma((4,)), dma((4,)), dma((4,)), dma((4,)), dma((10,)), dma((10,)),
            dma((2, 4)), dma((2, 4)), *ring, dma((2 + m,)), dma((2 + m,)),
            dma((3, groups, per_half)), dma((3, groups, per_half)), dma((per_half,)), dma((per_half,)),
        ],
        compiler_params=pltpu.CompilerParams(collective_id=4, has_side_effects=True, vmem_limit_bytes=62 << 20),
        cost_estimate=pl.CostEstimate(flops=20 << 30, transcendentals=0, bytes_accessed=100 << 20),
        name="begin",
    )(tokens, cot, wq, wk, wv, gate, up, down, wo, gains, q_gain, k_gain, table, starts)


def turn_kernel(n, names, pieces, near_ref, far_ref, down_near_ref, down_far_ref, back_ref, middle_ref, cot_near_ref,
                cot_far_ref, gain_ref, branch_ref, keep_ref, gain_sum_ref, done_ref, down_done_ref,
                slots, down_slots, beside_in, across_out, across_in, rs_send, rs_recv, down_send, down_recv,
                cross_send, cross_recv, beside_send, beside_recv, across_send, across_recv, branch_send, branch_recv):
    me = Group(names, n)
    me.arrive([*me.ring, me.across, me.beside])
    half = cot_near_ref.shape[1]
    tokens = middle_ref.shape[0]
    rows = tokens // pieces
    wide = Reduce(me, (far_ref, near_ref), slots, rs_send, rs_recv)
    down = Reduce(me, (down_far_ref, down_near_ref), down_slots, down_send, down_recv)

    def place_of(core, k):
        return pl.ds(pl.multiple_of(core * tokens + k * rows, rows), rows)

    wide.start()
    down.start()
    besides = [remote(back_ref.at[place_of(1 - me.col, k), :], beside_in.at[k], beside_send.at[k], beside_recv.at[k], me.beside)
               for k in range(pieces)]
    for each in besides:
        each.start()
    acrosses = [remote(across_out.at[k], across_in.at[k], across_send.at[k], across_recv.at[k], me.across)
                for k in range(pieces)]
    for k in range(pieces):
        besides[k].wait()
        chip = (back_ref[place_of(me.col, k), :].astype(F32) + beside_in[k].astype(F32)).astype(BF16)
        across_out[k, :, :half] = chip[:, half:]
        across_out[k, :, half:] = chip[:, :half]
        acrosses[k].start()

    gain_sum_ref[...] = jnp.zeros_like(gain_sum_ref)
    branches = [remote(branch_ref.at[place_of(me.col, k), :], branch_ref.at[place_of(me.col, k), :],
                       branch_send.at[k], branch_recv.at[k], me.beside) for k in range(pieces)]
    for k in range(pieces):
        steps(k * (n - 1) // pieces, (k + 1) * (n - 1) // pieces, wide, down)
        acrosses[k].wait()
        mine = place_of(me.col, k)
        grad = back_ref[mine, :].astype(F32) + beside_in[k].astype(F32) + across_in[k].astype(F32)
        middle = middle_ref[k * rows:(k + 1) * rows, :]
        inverse = lax.rsqrt(jnp.sum(middle * middle, axis=1, keepdims=True) / (2 * half) + EPSILON)
        normal = middle * inverse
        weighed = grad * normal
        gain_sum_ref[...] += jnp.sum(weighed, axis=0, keepdims=True)
        stat = jnp.sum(weighed * gain_ref[...], axis=1, keepdims=True) / (2 * half)
        part = inverse * (grad * gain_ref[...] - normal * stat)
        near = cot_near_ref[mine, :].astype(F32) + part[:, :half]
        far = cot_far_ref[mine, :].astype(F32) + part[:, half:]
        keep_ref[k * rows:(k + 1) * rows, :] = near
        branch_ref[mine, :half] = near.astype(BF16)
        branch_ref[mine, half:] = far.astype(BF16)
        branches[k].start()

    crosses = [remote(ring.last(s), out.at[s], cross_send.at[2 * k + s], cross_recv.at[2 * k + s], me.across)
               for k, (ring, out) in enumerate(((wide, done_ref), (down, down_done_ref))) for s in range(2)]
    for cross in crosses:
        cross.start()
    for s in (2, 3):
        done_ref[s] = wide.last(s)[...]
        down_done_ref[s] = down.last(s)[...]
    for each in branches + crosses:
        each.wait()
    finish(n, wide, down)


def turn(near, far, down_near, down_far, back, middle, cot_near, cot_far, gain, names, n, pieces=4):
    packed, width = back.shape
    tokens = middle.shape[0]
    vmem = pl.BlockSpec(memory_space=pltpu.VMEM)
    dma = pltpu.SemaphoreType.DMA
    exchange = pltpu.VMEM((pieces, tokens // pieces, width), BF16)

    def streams(x):
        return x.shape[1], x.shape[2] // 2

    return pl.pallas_call(
        functools.partial(turn_kernel, n, names, pieces),
        out_shape=(jax.ShapeDtypeStruct((packed, width), BF16), jax.ShapeDtypeStruct((tokens, width // 2), F32),
                   jax.ShapeDtypeStruct((1, width), F32), jax.ShapeDtypeStruct((4, *streams(near)), BF16),
                   jax.ShapeDtypeStruct((4, *streams(down_near)), BF16)),
        in_specs=[vmem] * 9,
        out_specs=(vmem,) * 5,
        scratch_shapes=[
            pltpu.VMEM((4, n - 1, *streams(near)), BF16), pltpu.VMEM((4, n - 1, *streams(down_near)), BF16),
            exchange, exchange, exchange, *[dma((4, n - 1))] * 4, dma((4,)), dma((4,)), *[dma((pieces,))] * 6,
        ],
        compiler_params=pltpu.CompilerParams(collective_id=1, has_side_effects=True, vmem_limit_bytes=60 << 20),
        cost_estimate=pl.CostEstimate(flops=40 * back.size, transcendentals=tokens, bytes_accessed=150 << 20),
        name="turn",
    )(near, far, down_near, down_far, back, middle, cot_near, cot_far, gain)


def retreat_kernel(n, names, b, packed, q_ref, k_ref, v_ref, grad_ref, raw_ref, lse_ref, start_ref,
                   done_ref, down_done_ref, result_ref, middle_ref,
                   dq_ref, dk_ref, dv_ref, wide_ref, down_ref, output_ref,
                   qs_ref, gs_ref, stat_ref, dqt_ref, dk_acc, dv_acc,
                   sums, beside_in, across_out, across_in, wide_send, wide_recv, down_send, down_recv,
                   beside_send, beside_recv, across_send, across_recv, last_send, last_recv, load_sem, keep_sem):
    g, j = pl.program_id(0), pl.program_id(1)
    blocks = packed // b
    me = Group(names, n)
    half = output_ref.shape[1]
    count = packed // 2
    wide = Spread(me, wide_ref, wide_send, wide_recv)
    down = Spread(me, down_ref, down_send, down_recv)
    own_rows = pl.ds(pl.multiple_of(me.col * count, count), count)
    other_rows = pl.ds(pl.multiple_of((1 - me.col) * count, count), count)
    sides = (pl.ds(half, half), pl.ds(0, half))
    besides = [remote(result_ref.at[other_rows, side], beside_in.at[k], beside_send.at[k], beside_recv.at[k], me.beside)
               for k, side in enumerate(sides)]
    loads = [pltpu.make_async_copy(result_ref.at[own_rows, side], sums.at[k], load_sem.at[k]) for k, side in enumerate(sides)]
    across = remote(across_out, across_in, across_send, across_recv, me.across)
    last = remote(across_out, output_ref.at[own_rows, :], last_send, last_recv, me.beside)
    last_here = pltpu.make_async_copy(across_out, output_ref.at[own_rows, :], keep_sem.at[8])
    keeps = [pltpu.make_async_copy(src.at[s], ring.piece(s, me.own(s % 2)), keep_sem.at[4 * k + s])
             for k, (ring, src) in enumerate(((wide, done_ref), (down, down_done_ref))) for s in range(4)]

    @pl.when((g == 0) & (j == 0))
    def _():
        me.arrive([*me.ring, me.across, me.beside])
        for ring, src in ((wide, done_ref), (down, down_done_ref)):
            for s in range(4):
                ring.start(s, src.at[s])
        for each in besides + loads + keeps:
            each.start()

    @pl.when((g == 0) & (j == 1))
    def _():
        for each in besides + loads:
            each.wait()
        across_out[...] = (sums[0].astype(F32) + beside_in[0].astype(F32)).astype(BF16)
        across.start()

    @pl.when((g == 1) & (j == 1))
    def _():
        across.wait()
        total = middle_ref[...] + (sums[1].astype(F32) + beside_in[1].astype(F32) + across_in[...].astype(F32))
        across_out[...] = total.astype(BF16)
        last.start()
        last_here.start()

    @pl.when(j == 0)
    def _():
        dqt_ref[...] = jnp.zeros_like(dqt_ref)
        for i in range(blocks):
            rows = slice(i * b, (i + 1) * b)
            both = slice(i * 2 * b, (i + 1) * 2 * b)
            qs_ref[both, :] = stacked(q_ref[rows, :])
            grad = grad_ref[rows, :]
            gs_ref[both, :] = stacked(grad)
            prod = (grad.astype(F32) * raw_ref[rows, :]).T
            stat_ref[i, 0:1, 0:b] = lse_ref[0, 0:1, rows]
            stat_ref[i, 0:1, b:2 * b] = lse_ref[0, 1:2, rows]
            stat_ref[i, 1:2, 0:b] = jnp.sum(prod[:64], axis=0, keepdims=True)
            stat_ref[i, 1:2, b:2 * b] = jnp.sum(prod[64:], axis=0, keepdims=True)

    k = k_ref[...]
    v = v_ref[...]
    kt = k.T[:64]
    dk_acc[...] = jnp.zeros_like(dk_acc)
    dv_acc[...] = jnp.zeros_like(dv_acc)
    keys = j * b + lax.broadcasted_iota(jnp.int32, (b, 1), 0)
    every = blocks * (blocks + 1)
    before = g * (every // 2) + j * blocks - (j * (j - 1)) // 2

    def step(i, diagonal):
        at = pl.ds(pl.multiple_of(i * 2 * b, 2 * b), 2 * b)
        qs = qs_ref[at, :]
        gs = gs_ref[at, :]
        st = dot(k, qs, NT)
        pt = jnp.exp(st - stat_ref[i, 0:1, :])
        begin = start_ref[0:1, pl.ds(pl.multiple_of(i * b, b), b)]
        allowed = keys >= jnp.concatenate([begin, begin], axis=1)
        if diagonal:
            cols = i * b + lax.rem(lax.broadcasted_iota(jnp.int32, (1, 2 * b), 1), b)
            allowed = allowed & (keys <= cols)
        pt = jnp.where(allowed, pt, 0.0)
        dv_acc[...] += dot(pt.astype(BF16), gs)
        dpt = dot(v, gs, NT)
        dst = (pt * (dpt - stat_ref[i, 1:2, :])).astype(BF16)
        dk_acc[...] += dot(dst, qs)
        part = dot(kt, dst)
        to = pl.ds(pl.multiple_of(i * b, b), b)
        dqt_ref[0:64, to] += part[:, :b]
        dqt_ref[64:128, to] += part[:, b:]
        at = before + i - j
        steps((at * (n - 1)) // every, ((at + 1) * (n - 1)) // every, wide, down)

    step(j, True)

    @pl.loop(j + 1, blocks)
    def _(i):
        step(i, False)

    dk = dk_acc[...]
    dv = dv_acc[...]
    dk_ref[...] = dk + pltpu.roll(dk, 64, 1)
    dv_ref[...] = dv + pltpu.roll(dv, 64, 1)
    dq_ref[...] = dqt_ref[:, pl.ds(pl.multiple_of(j * b, b), b)].T * HEAD_SIZE ** (-0.5)

    @pl.when((g == 1) & (j == blocks - 1))
    def _():
        for each in keeps:
            each.wait()
        last_here.wait()
        last.wait()
        finish(n, wide, down)


def retreat(q, k, v, grad, raw, lse, starts, done, down_done, result, middle, names, n, b=512):
    packed, width = q.shape
    groups, lanes = width // 128, 128
    b = min(b, packed)
    blocks = packed // b
    half = middle.shape[1]
    col = pl.BlockSpec((packed, lanes), lambda g, j: (0, g))
    blk = pl.BlockSpec((b, lanes), lambda g, j: (j, g))
    some = pl.BlockSpec(memory_space=pl.ANY)
    out = jax.ShapeDtypeStruct((packed, width), F32)
    pairs = packed * (packed + b) // 2
    dma = pltpu.SemaphoreType.DMA

    def full(x):
        return jax.ShapeDtypeStruct((2, n, x.shape[1], 2 * x.shape[2]), BF16)

    exchange = pltpu.VMEM((packed // 2, half), BF16)
    two = pltpu.VMEM((2, packed // 2, half), BF16)
    return pl.pallas_call(
        functools.partial(retreat_kernel, n, names, b, packed),
        out_shape=(out, out, out, full(done), full(down_done), jax.ShapeDtypeStruct((packed, half), BF16)),
        grid=(groups, blocks),
        in_specs=[col, blk, blk, col, col, pl.BlockSpec((1, 2, packed), lambda g, j: (g, 0, 0)),
                  pl.BlockSpec((1, packed), lambda g, j: (0, 0)), some, some, some,
                  pl.BlockSpec(middle.shape, lambda g, j: (0, 0), pipeline_mode=pl.Buffered(1))],
        out_specs=(blk, blk, blk, some, some, some),
        scratch_shapes=[
            pltpu.VMEM((2 * packed, lanes), BF16), pltpu.VMEM((2 * packed, lanes), BF16),
            pltpu.VMEM((blocks, 2, 2 * b), F32), pltpu.VMEM((lanes, packed), F32),
            pltpu.VMEM((b, lanes), F32), pltpu.VMEM((b, lanes), F32),
            two, two, exchange, exchange, *[dma((4, n - 1))] * 4, dma((2,)), dma((2,)), *[dma] * 4, dma((2,)), dma((9,)),
        ],
        compiler_params=pltpu.CompilerParams(collective_id=3, has_side_effects=True, vmem_limit_bytes=60 << 20),
        cost_estimate=pl.CostEstimate(flops=10 * groups * 2 * pairs * 256, transcendentals=2 * groups * pairs,
                                      bytes_accessed=20 * packed * width),
        name="retreat",
    )(q, k, v, grad, raw, lse, starts[None, :], done, down_done, result, middle)


def close_kernel(n, names, near_ref, far_ref, out_ref, to_near_ref, to_far_ref, stat_ref, keep_ref, tokens_ref, gain_ref,
                 vector_ref, thin_ref, lone_ref, sums_ref, grad_ref,
                 slots, lone_slots, beside_in, beside_stat, across_out, across_in, stat_out, stat_in, group_in, ring_in, mine,
                 rs_send, rs_recv, ag_send, ag_recv, lone_send, lone_recv, lone_out_send, lone_out_recv, cross_send, cross_recv,
                 group_send, group_recv, all_send, all_recv, beside_send, beside_recv, across_send, across_recv,
                 last_send, last_recv):
    me = Group(names, n)
    me.arrive([*me.along, me.across, me.beside, me.opposite])
    half = tokens_ref.shape[1]
    count = keep_ref.shape[0]
    thin = Reduce(me, (far_ref, near_ref), slots, rs_send, rs_recv)
    lone = Reduce(me, (out_ref,), lone_slots, lone_send, lone_recv)
    thin_out = Spread(me, thin_ref, ag_send, ag_recv)
    lone_out = Spread(me, lone_ref, lone_out_send, lone_out_recv)

    own_rows = pl.ds(pl.multiple_of(me.col * count, count), count)
    other_rows = pl.ds(pl.multiple_of((1 - me.col) * count, count), count)
    besides = [remote(src.at[other_rows, :], dst, beside_send.at[k], beside_recv.at[k], me.beside)
               for k, (src, dst) in enumerate(((to_far_ref, beside_in.at[0]), (stat_ref, beside_stat), (to_near_ref, beside_in.at[1])))]
    for each in besides:
        each.start()
    thin.start()
    lone.start()
    gathers = [remote(vector_ref, group_in.at[k], group_send.at[k], group_recv.at[k], target)
               for k, target in enumerate((me.across, me.beside, me.opposite))]
    for gather in gathers:
        gather.start()

    acrosses = [remote(src, dst, across_send.at[k], across_recv.at[k], me.across)
                for k, (src, dst) in enumerate(((across_out, across_in), (stat_out, stat_in)))]
    besides[0].wait()
    across_out[...] = (to_far_ref[own_rows, :].astype(F32) + beside_in[0].astype(F32)).astype(BF16)
    acrosses[0].start()
    besides[1].wait()
    stat_out[...] = stat_ref[own_rows, :] + beside_stat[...]
    acrosses[1].start()

    for gather in gathers:
        gather.wait()
    mine[...] = vector_ref[...] + group_in[0] + group_in[1] + group_in[2]
    spreads = [remote(mine, ring_in.at[k], all_send.at[k], all_recv.at[k], target) for k, target in enumerate(me.along)]
    for spread in spreads:
        spread.start()
    steps(0, n - 1, thin, lone)

    crosses = [remote(thin.last(s), thin_out.piece(s, me.own(s % 2), me.row), cross_send.at[s], cross_recv.at[s], me.across)
               for s in range(2)]
    for cross in crosses:
        cross.start()
    for s in (2, 3):
        thin_out.piece(s, me.own(s % 2))[...] = thin.last(s)[...]
        thin_out.start(s)
    for s in range(2):
        lone_out.piece(s, me.own(s % 2))[...] = lone.last(s)[...]
        lone_out.start(s)
    for s in range(2):
        crosses[s].wait()
        thin_out.start(s)

    besides[2].wait()
    acrosses[0].wait()
    acrosses[1].wait()
    grad = to_near_ref[own_rows, :].astype(F32) + beside_in[1].astype(F32) + across_in[...].astype(F32)
    inverse = stat_ref[own_rows, pl.ds(HEAD_SIZE, 1)]
    stat = (stat_out[:, :1] + stat_in[:, :1]) / (2 * half)
    near = tokens_ref[own_rows, :].astype(F32) * inverse
    grad_ref[own_rows, :] = (inverse * (grad * gain_ref[...] - near * stat) + keep_ref[...]).astype(BF16)
    last = remote(grad_ref.at[own_rows, :], grad_ref.at[own_rows, :], last_send, last_recv, me.beside)
    last.start()

    steps(0, n - 1, thin_out, lone_out)

    total = mine[...]
    for spread in spreads:
        spread.wait()
    for k in range(n - 1):
        total = total + ring_in[k]
    sums_ref[...] = total
    last.wait()
    finish(n, thin, lone, thin_out, lone_out)


def close(near, far, out, to_near, to_far, stat, keep, tokens, gain, vector, names, n):
    packed, half = tokens.shape
    count = packed // 2
    rows, thin, lone = near.shape[1], near.shape[2] // 2, out.shape[2] // 2
    vmem = pl.BlockSpec(memory_space=pltpu.VMEM)
    dma = pltpu.SemaphoreType.DMA

    def shape(*dims, dtype=BF16):
        return jax.ShapeDtypeStruct(dims, dtype)

    exchange = pltpu.VMEM((count, half), BF16)
    stats = pltpu.VMEM((count, stat.shape[1]), F32)
    return pl.pallas_call(
        functools.partial(close_kernel, n, names),
        out_shape=(shape(2, n, rows, 2 * thin), shape(n, rows, 2 * lone), shape(*vector.shape, dtype=F32), shape(packed, half)),
        in_specs=[vmem] * 10,
        out_specs=(vmem,) * 4,
        scratch_shapes=[
            pltpu.VMEM((4, n - 1, rows, thin), BF16), pltpu.VMEM((2, n - 1, rows, lone), BF16),
            pltpu.VMEM((2, count, half), BF16), stats, exchange, exchange, stats, stats,
            pltpu.VMEM((3, *vector.shape), F32), pltpu.VMEM((n - 1, *vector.shape), F32), pltpu.VMEM(vector.shape, F32),
            *[dma((4, n - 1))] * 4, *[dma((2, n - 1))] * 4, dma((2,)), dma((2,)), dma((3,)), dma((3,)), dma((n - 1,)), dma((n - 1,)),
            dma((3,)), dma((3,)), dma((2,)), dma((2,)), dma, dma,
        ],
        compiler_params=pltpu.CompilerParams(collective_id=2, has_side_effects=True, vmem_limit_bytes=60 << 20),
        cost_estimate=pl.CostEstimate(flops=40 * packed * half, transcendentals=0, bytes_accessed=200 << 20),
        name="close",
    )(near, far, out, to_near, to_far, stat, keep, tokens, gain, vector)


def widen_kernel(widths, units, wide_ref, down_ref, thin_ref, lone_ref, gate_out, up_out, down_out, q_out, k_out, v_out, lone_out):
    for part in range(2):
        for out, begin in ((gate_out, 0), (up_out, units)):
            out[:, part * units:(part + 1) * units] = wide_ref[part, :, begin:begin + units].astype(F32)
        begin = 0
        for out, columns in zip((q_out, k_out, v_out), widths):
            out[:, part * columns:(part + 1) * columns] = thin_ref[part, :, begin:begin + columns].astype(F32)
            begin += columns
    down_out[...] = down_ref[...].astype(F32)
    lone_out[...] = lone_ref[...].astype(F32)


def widen(wide, down, thin, lone, widths, parts=8):
    half = lone.shape[0]
    units = wide.shape[2] // 2
    rows, down_rows = half // parts, down.shape[0] // parts

    def one(rows, columns):
        return pl.BlockSpec((rows, columns), lambda i: (i, 0))

    def two(columns):
        return pl.BlockSpec((2, rows, columns), lambda i: (0, i, 0))

    shapes = [(half, 2 * units)] * 2 + [down.shape] + [(half, 2 * columns) for columns in widths] + [lone.shape]
    return pl.pallas_call(
        functools.partial(widen_kernel, widths, units),
        out_shape=tuple(jax.ShapeDtypeStruct(shape, F32) for shape in shapes),
        grid=(parts,),
        in_specs=[two(2 * units), one(down_rows, down.shape[1]), two(thin.shape[2]), one(rows, lone.shape[1])],
        out_specs=tuple(one(down_rows if k == 2 else rows, shape[1]) for k, shape in enumerate(shapes)),
        compiler_params=pltpu.CompilerParams(vmem_limit_bytes=40 << 20),
        cost_estimate=pl.CostEstimate(flops=0, transcendentals=0, bytes_accessed=6 * (wide.size + down.size + thin.size + lone.size)),
        name="widen",
    )(wide, down, thin, lone)


def shards(
    tokens,
    seq_lengths,
    query_weight,
    key_matrix,
    value_matrix,
    out_weight,
    gate_weight,
    up_weight,
    down_weight,
    attn_gain,
    ffn_gain,
    query_gain,
    key_gain,
    cotangent,
):
    packed, half = tokens.shape
    row, col, group = lax.axis_index("row"), lax.axis_index("col"), lax.axis_index("dp")
    parts = lax.axis_size("dp")
    width = 2 * half

    names = ("dp", "row", "col")
    starts = layout(seq_lengths[0], packed)
    table = rope_table(jnp.arange(packed, dtype=jnp.int32) - starts)
    q_gain = jnp.tile(query_gain, 2)[None, :]
    k_gain = jnp.tile(key_gain, 2)[None, :]
    gains = jnp.stack([attn_gain, ffn_gain])
    (far, gate_up_far, down_far, cot_far, gains_far, hid_near, hid_far, raw, q, k, v, attended_raw, totals, attended, middle,
     hidden, out_own, qkv, qkv_far) = begin(
        tokens, cotangent, query_weight, key_matrix, value_matrix, gate_weight, up_weight, down_weight, out_weight, gains,
        q_gain, k_gain, table, starts[:, None], names, parts)
    gain_two = jnp.concatenate([ffn_gain, gains_far[1]])[None, :]
    units = down_weight.shape[0] // 2
    active, feed_grads, result, back = feed(
        row[None], hidden, cotangent, cot_far, gate_weight, up_weight, gate_up_far.reshape(half, -1), down_weight,
        down_far.reshape(units, half))

    grad_down_near, grad_down_far = (
        over_t(active, cot).astype(BF16).reshape(parts, units // parts, -1) for cot in (cotangent, cot_far))
    grad_gate_up = over_t(hidden, feed_grads).astype(BF16).reshape(2, parts, half // parts, -1)
    branch, keep, ffn_sum, done, down_done = turn(
        grad_gate_up[0], grad_gate_up[1], grad_down_near, grad_down_far, back, middle, cotangent, cot_far, gain_two, names, parts)

    grad_attended = (dot(branch[:, :half], out_own[:, :half], NT) + dot(branch[:, half:], out_own[:, half:], NT)).astype(BF16)
    grad_out = over_t(attended, part_of(branch[:, :half], col, 0))
    quarter = out_own.shape[0]
    kept = jnp.concatenate([grad_out[:quarter], grad_out[2 * quarter:3 * quarter]], axis=0)
    sent = jnp.concatenate([grad_out[quarter:2 * quarter], grad_out[3 * quarter:]], axis=0)
    grad_out = kept + swap(sent.astype(BF16), "col").astype(F32)
    grad_out = ordered(grad_out[:quarter], grad_out[quarter:], row).astype(BF16).reshape(parts, half // parts, -1)

    dq, dk, dv, wide_full, down_full, output = retreat(
        q, k, v, grad_attended, attended_raw, totals, starts, done, down_done, result, middle[:, :half], names, parts)
    grads, to_near, to_far, stat_one, q_sum, k_sum, near_sum, far_sum = project_back(
        dq, dk, dv, raw, tokens, far, attn_gain[None, :], gains_far[:1], qkv, qkv_far.reshape(half, -1), q_gain, k_gain, table)
    near_grads, far_grads = (
        over_t(hid, grads).astype(BF16).reshape(parts, half // parts, -1) for hid in (hid_near, hid_far))

    def folded(x):
        return x[0, :HEAD_SIZE] + x[0, HEAD_SIZE:]

    vector = jnp.concatenate([
        ordered(near_sum[0], far_sum[0], row), ordered(ffn_sum[0, :half], ffn_sum[0, half:], row) * 0.5,
        folded(q_sum), folded(k_sum)])
    length = vector.shape[0]
    lines = -(-length // 1024) * 8
    vector = jnp.concatenate([vector, jnp.zeros((lines * 128 - length,), F32)]).reshape(lines, 128)
    thin_full, out_full, sums, grad_tokens = close(
        near_grads, far_grads, grad_out, to_near, to_far, stat_one, keep, tokens, attn_gain[None, :], vector, names, parts)
    sums = sums.reshape(-1)
    widths = (query_weight.shape[1] // 2, key_matrix.shape[1] // 2, value_matrix.shape[1] // 2)
    gate_sum, up_sum, down_sum, q_weight_sum, k_weight_sum, v_weight_sum, out_sum = widen(
        wide_full.reshape(2, half, -1), down_full.reshape(2 * units, half), thin_full.reshape(2, half, -1),
        out_full.reshape(half, -1), widths)
    return (
        output,
        grad_tokens,
        q_weight_sum,
        k_weight_sum,
        v_weight_sum,
        out_sum,
        gate_sum,
        up_sum,
        down_sum,
        part_of(sums[:width], row, 0),
        part_of(sums[width:2 * width], row, 0),
        sums[2 * width:2 * width + HEAD_SIZE],
        sums[2 * width + HEAD_SIZE:2 * width + 2 * HEAD_SIZE],
    )


def solution(mesh):
    return jax.shard_map(
        shards,
        mesh=mesh,
        in_specs=(
            P("dp", "row"),
            P("dp", None),
            P("row", "col"),
            P("row", "col"),
            P("row", "col"),
            P("col", "row"),
            P("row", "col"),
            P("row", "col"),
            P("col", "row"),
            P("row"),
            P("row"),
            P(),
            P(),
            P("dp", "row"),
        ),
        out_specs=(
            P("dp", "row"),
            P("dp", "row"),
            P("row", "col"),
            P("row", "col"),
            P("row", "col"),
            P("col", "row"),
            P("row", "col"),
            P("row", "col"),
            P("col", "row"),
            P("row"),
            P("row"),
            P(),
            P(),
        ),
        check_vma=False,
    )
```

```python
import functools
import math

import jax
import jax.numpy as jnp
from jax import lax
from jax.experimental import pallas as pl
from jax.experimental.pallas import tpu as pltpu
from jax.sharding import PartitionSpec as P

HEAD_SIZE = 64
EPSILON = 1e-05
ROPE_BASE = 1000000.0
F32, BF16 = jnp.float32, jnp.bfloat16
MESH = pl.DeviceIdType.MESH


def dot(a, b, dims=(((1,), (0,)), ((), ()))):
    return lax.dot_general(a, b, dims, preferred_element_type=F32)


NT = (((1,), (1,)), ((), ()))

def stacked(x):
    first = lax.broadcasted_iota(jnp.int32, x.shape, 1) < 64
    zero = jnp.zeros_like(x)
    return jnp.concatenate([jnp.where(first, x, zero), jnp.where(first, zero, x)], axis=0)


def head_sums(x):
    first = lax.broadcasted_iota(jnp.int32, x.shape, 1) < HEAD_SIZE
    one = jnp.sum(jnp.where(first, x, 0.0), axis=1, keepdims=True)
    two = jnp.sum(jnp.where(first, 0.0, x), axis=1, keepdims=True)
    return jnp.where(first, one, two)


def swapped(x):
    low = lax.rem(lax.broadcasted_iota(jnp.int32, x.shape, 1), HEAD_SIZE) < HEAD_SIZE // 2
    return jnp.where(low, pltpu.roll(x, 96, 1), pltpu.roll(x, 32, 1))


def doubled(x):
    first = lax.broadcasted_iota(jnp.int32, x.shape, 1) < HEAD_SIZE
    other = pltpu.roll(x, HEAD_SIZE, 1)
    return jnp.where(first, x, other), jnp.where(first, other, x)


def layout(lengths, packed):
    count = lengths.shape[0]
    numbers = jnp.arange(count, dtype=jnp.int32)
    ends = jnp.sum(jnp.where(numbers[None, :] <= numbers[:, None], lengths[None, :], 0), axis=1)
    begins = ends - lengths
    places = jnp.arange(packed, dtype=jnp.int32)
    member = jnp.sum((places[:, None] >= ends[None, :]).astype(jnp.int32), axis=1)
    return jnp.sum(jnp.where(member[:, None] == numbers[None, :], begins[None, :], 0), axis=1)


def rope_table(position):
    half = HEAD_SIZE // 2
    inverse = jnp.exp(jnp.arange(half, dtype=F32) * (-2.0 * math.log(ROPE_BASE) / HEAD_SIZE))
    angles = position.astype(F32)[None, :] * inverse[:, None]
    return jnp.concatenate([jnp.cos(angles), jnp.sin(angles)], axis=0)


def swap(x, axis):
    return jax.tree.map(lambda part: lax.ppermute(part, axis, [(0, 1), (1, 0)]), x)


def ordered(own, other, index, axis=0):
    return jnp.where(index == 0, jnp.concatenate([own, other], axis), jnp.concatenate([other, own], axis))


def part_of(x, index, axis, parts=2):
    size = x.shape[axis] // parts
    return lax.dynamic_slice_in_dim(x, index * size, size, axis)


def over_t(left, right):
    return dot(left, right, (((0,), (0,)), ((), ())))


VMEM_LIMIT = 63 << 20


def feed_kernel(units, row_ref, hidden_ref, cot_near_ref, cot_far_ref, gate_ref, up_ref, far_ref, down_near_ref, down_far_ref,
                active_ref, grads_ref, result_ref, back_ref):
    half = cot_near_ref.shape[1]
    near, far = hidden_ref[:, :half], hidden_ref[:, half:]
    gate = dot(near, gate_ref[...]) + dot(far, far_ref[:, :units])
    upward = dot(near, up_ref[...]) + dot(far, far_ref[:, units:])
    grad_active = dot(cot_near_ref[...], down_near_ref[...], NT) + dot(cot_far_ref[...], down_far_ref[...], NT)
    sig = 1.0 / (1.0 + jnp.exp(-gate))
    lifted = gate * sig
    active = (lifted * upward).astype(BF16)
    grad_gate = (grad_active * upward * (sig * (1.0 + gate * (1.0 - sig)))).astype(BF16)
    grad_up = (grad_active * lifted).astype(BF16)
    active_ref[...] = active
    grads_ref[:, :units] = grad_gate
    grads_ref[:, units:] = grad_up
    result_ref[:, :half] = dot(active, down_near_ref[...]).astype(BF16)
    result_ref[:, half:] = dot(active, down_far_ref[...]).astype(BF16)
    back_ref[:, :half] = (dot(grad_gate, gate_ref[...], NT) + dot(grad_up, up_ref[...], NT)).astype(BF16)
    back_ref[:, half:] = (dot(grad_gate, far_ref[:, :units], NT) + dot(grad_up, far_ref[:, units:], NT)).astype(BF16)


def feed(row, hidden, cot_near, cot_far, gate, up, far, down, down_far, rows=256):
    packed, width = hidden.shape
    units, half = down_far.shape
    rows = min(rows, packed)

    def tile(n):
        return pl.BlockSpec((rows, n), lambda i, row: (i, 0))

    def once(shape, place):
        return pl.BlockSpec(shape, place, pipeline_mode=pl.Buffered(1))

    def out(n):
        return jax.ShapeDtypeStruct((packed, n), BF16)

    columns = once((half, units), lambda i, row: (0, row[0]))
    return pl.pallas_call(
        functools.partial(feed_kernel, units),
        out_shape=(out(units), out(2 * units), out(width), out(width)),
        grid_spec=pltpu.PrefetchScalarGridSpec(
            num_scalar_prefetch=1, grid=(packed // rows,),
            in_specs=[tile(width), tile(half), tile(half), columns, columns, once(far.shape, lambda i, row: (0, 0)),
                      once((units, half), lambda i, row: (row[0], 0)), once(down_far.shape, lambda i, row: (0, 0))],
            out_specs=(tile(units), tile(2 * units), tile(width), tile(width)),
        ),
        compiler_params=pltpu.CompilerParams(vmem_limit_bytes=56 << 20),
        cost_estimate=pl.CostEstimate(flops=12 * packed * width * units, transcendentals=packed * units,
                                      bytes_accessed=packed * (8 * width + 6 * units) + 6 * width * units),
        name="feed",
    )(row, hidden, cot_near, cot_far, gate, up, far, down, down_far)


class Group:
    def __init__(self, names, total, n=None):
        n = total if n is None else n
        self.n = n
        self.dp, self.row, self.col = (lax.axis_index(name) for name in names)
        self.base, member = (self.dp // n) * n, self.dp % n
        side = member % 2
        self.place = (member // 2) * (1 - side) + (n - 1 - member // 2) * side
        self.across = (self.dp, 1 - self.row, self.col)
        self.beside = (self.dp, self.row, 1 - self.col)
        self.opposite = (self.dp, 1 - self.row, 1 - self.col)
        self.along = [((self.dp + k) % total, self.row, self.col) for k in range(1, total)]
        self.ring = [(self.at(self.place + 1), self.row, self.col), (self.at(self.place - 1), self.row, self.col)]

    def at(self, position):
        position = (position + 2 * self.n) % self.n
        back = position // (self.n // 2)
        return self.base + (position * (1 - back) + (self.n - 1 - position) * back) * 2 + back

    def arrive(self, targets):
        barrier = pltpu.get_barrier_semaphore()
        for target in targets:
            pl.semaphore_signal(barrier, inc=1, device_id=target, device_id_type=MESH)
        pl.semaphore_wait(barrier, len(targets))

    def reduced(self, way, t):
        return (self.place - t - 1 + 2 * self.n) % self.n if way == 0 else (self.place + t + 1) % self.n

    def spread(self, way, t):
        return (self.place - t + 2 * self.n) % self.n if way == 0 else (self.place + t) % self.n

    def own(self, way):
        return (self.place + 1) % self.n if way == 0 else (self.place + self.n - 1) % self.n


def remote(src, dst, send, recv, target):
    return pltpu.make_async_remote_copy(
        src_ref=src, dst_ref=dst, send_sem=send, recv_sem=recv, device_id=target, device_id_type=MESH)


class Reduce:
    def __init__(self, me, parts, slots, send, recv):
        self.me, self.parts, self.slots, self.send, self.recv = me, parts, slots, send, recv
        self.columns = parts[0].shape[2] // 2

    def local(self, s, chunk):
        return self.parts[s // 2].at[chunk, :, pl.ds((s % 2) * self.columns, self.columns)]

    def copy(self, s, t, src):
        return remote(src, self.slots.at[s, t], self.send.at[s, t], self.recv.at[s, t], self.me.ring[s % 2])

    def start(self):
        for s in range(2 * len(self.parts)):
            self.copy(s, 0, self.local(s, self.me.place)).start()

    def step(self, t):
        for s in range(2 * len(self.parts)):
            slot = self.slots.at[s, t]
            self.copy(s, t, slot).wait_recv()
            slot[...] = (slot[...].astype(F32) + self.local(s, self.me.reduced(s % 2, t))[...].astype(F32)).astype(BF16)

            @pl.when(t < self.me.n - 2)
            def _():
                self.copy(s, t + 1, slot).start()

    def last(self, s):
        return self.slots.at[s, self.me.n - 2]

    def finish(self, t):
        for s in range(2 * len(self.parts)):
            self.copy(s, t, self.slots.at[s, t]).wait_send()


class Spread:
    def __init__(self, me, full, send, recv):
        self.me, self.full, self.send, self.recv = me, full, send, recv
        self.lone = len(full.shape) == 3
        self.columns = full.shape[-1] // 2
        self.streams = (0, 1) if self.lone else (2, 3, 0, 1)

    def piece(self, s, chunk, quarter=None):
        lanes = pl.ds((s % 2) * self.columns, self.columns)
        if self.lone:
            return self.full.at[chunk, :, lanes]
        if quarter is None:
            quarter = 1 - self.me.row if s < 2 else self.me.row
        return self.full.at[quarter, chunk, :, lanes]

    def copy(self, s, t, chunk, src=None):
        piece = self.piece(s, chunk)
        return remote(piece if src is None else src, piece, self.send.at[s, t], self.recv.at[s, t], self.me.ring[s % 2])

    def start(self, s, src=None):
        self.copy(s, 0, self.me.own(s % 2), src).start()

    def step(self, t):
        for s in self.streams:
            chunk = self.me.spread(s % 2, t)
            self.copy(s, t, chunk).wait_recv()

            @pl.when(t < self.me.n - 2)
            def _():
                self.copy(s, t + 1, chunk).start()

    def finish(self, t):
        for s in self.streams:
            self.copy(s, t, 0).wait_send()


class Meet:
    def __init__(self, me, parts, slots, send, recv):
        self.me, self.parts, self.slots, self.send, self.recv = me, parts, slots, send, recv
        self.hops = ((me.n - 1) // 2, me.n // 2)
        self.streams = [s for s in range(2 * len(parts)) if self.hops[s % 2]]

    def local(self, s, chunk):
        return self.parts[s // 2].at[(chunk + 2 * self.me.n) % self.me.n]

    def copy(self, s, t, src):
        return remote(src, self.slots.at[s, t], self.send.at[s, t], self.recv.at[s, t], self.me.ring[s % 2])

    def start(self):
        for s in self.streams:
            far = self.me.place + self.hops[0] if s % 2 == 0 else self.me.place - self.hops[1]
            self.copy(s, 0, self.local(s, far)).start()

    def step(self, t):
        for s in self.streams:
            hops = self.hops[s % 2]

            @pl.when(t < hops)
            def _(s=s, hops=hops):
                slot = self.slots.at[s, t]
                self.copy(s, t, slot).wait_recv()

                @pl.when(t < hops - 1)
                def _():
                    chunk = self.me.place + (hops - 1 - t if s % 2 == 0 else t + 1 - hops)
                    slot[...] = (slot[...].astype(F32) + self.local(s, chunk)[...].astype(F32)).astype(BF16)
                    self.copy(s, t + 1, slot).start()

    def total(self, part):
        out = self.local(2 * part, self.me.place)[...].astype(F32)
        for s in self.streams:
            if s // 2 == part:
                out = out + self.slots[s, self.hops[s % 2] - 1].astype(F32)
        return out.astype(BF16)

    def finish(self, t):
        for s in self.streams:
            @pl.when(t < self.hops[s % 2])
            def _(s=s):
                self.copy(s, t, self.slots.at[s, t]).wait_send()


class Fan:
    def __init__(self, me, full, send, recv):
        self.me, self.full, self.send, self.recv = me, full, send, recv
        self.lone = len(full.shape) == 3
        self.hops = (me.n // 2, (me.n - 1) // 2)
        self.streams = [s for s in ((0, 1) if self.lone else (2, 3, 0, 1)) if self.hops[s % 2]]

    def piece(self, part, chunk, quarter=None):
        chunk = (chunk + 2 * self.me.n) % self.me.n
        if self.lone:
            return self.full.at[chunk]
        if quarter is None:
            quarter = 1 - self.me.row if part == 0 else self.me.row
        return self.full.at[quarter, chunk]

    def copy(self, s, t, chunk):
        piece = self.piece(s // 2, chunk)
        return remote(piece, piece, self.send.at[s, t], self.recv.at[s, t], self.me.ring[s % 2])

    def start(self, part):
        for s in self.streams:
            if s // 2 == part:
                self.copy(s, 0, self.me.place).start()

    def step(self, t):
        for s in self.streams:
            hops = self.hops[s % 2]

            @pl.when(t < hops)
            def _(s=s, hops=hops):
                chunk = self.me.place + (-1 - t if s % 2 == 0 else 1 + t)
                self.copy(s, t, chunk).wait_recv()

                @pl.when(t < hops - 1)
                def _():
                    self.copy(s, t + 1, chunk).start()

    def finish(self, t):
        for s in self.streams:
            @pl.when(t < self.hops[s % 2])
            def _(s=s):
                self.copy(s, t, self.me.place).wait_send()


def steps(begin, end, *rings):
    def step(t, carry):
        for ring in rings:
            ring.step(t)
        return carry

    lax.fori_loop(begin, end, step, 0)


def by_rows(total, action, rows=64):
    rows = min(rows, total)

    def each(k, carry):
        action(pl.ds(pl.multiple_of(k * rows, rows), rows))
        return carry

    lax.fori_loop(0, total // rows, each, 0)


def finish(n, *rings):
    def each(t, carry):
        for ring in rings:
            ring.finish(t)
        return carry

    lax.fori_loop(0, n - 1, each, 0)


def begin_kernel(n, m, names, b, token_ref, cot_ref, wq_ref, wk_ref, wv_ref, gate_ref, up_ref, down_ref, wo_ref, gains_ref,
                 q_gain_ref, k_gain_ref, table_ref, starts_ref,
                 far_out, gate_up_out, down_out, cot_out, gains_out, hid_near_out, hid_far_out, raw_out, q_out, k_out, v_out,
                 heads_out, totals_out, attended_out, middle_out, hidden_out, wo_out, w_near_out, w_far_out,
                 near, far, w_near, w_far, wo_far, wo_all, hid_near, hid_far, raw, q_all, k_all, v_all, low, heads, attended,
                 middle, hidden, acc_ref, mass_ref,
                 local_sem, store_sem, token_send, token_recv, pass_send, pass_recv, piece_send, piece_recv, cot_send, cot_recv,
                 qkv_send, qkv_recv, wide_send, wide_recv, thin_send, thin_recv, out_send, out_recv, wo_send, wo_recv,
                 low_send, low_recv, hidden_send, hidden_recv):
    me = Group(names, n, m)
    packed, half = token_ref.shape
    count = packed // 2
    row, col = me.row, me.col
    lanes = 2 * HEAD_SIZE
    groups = q_all.shape[1] // lanes
    width = groups * lanes
    kv = groups * HEAD_SIZE
    units = gate_ref.shape[1] // 2
    chunk = half // m
    down_chunk = units // m
    pieces = 4
    rows = count // pieces
    me.arrive([*me.ring, me.across, me.beside, me.opposite])

    def at(begin, size):
        return pl.ds(pl.multiple_of(begin, size), size)

    def own_rows(k):
        return at(col * count + k * rows, rows)

    def other_rows(k):
        return at((1 - col) * count + k * rows, rows)

    def piece(k, src, dst):
        return remote(src, dst, piece_send.at[k], piece_recv.at[k], me.across)

    up_chunk, low_chunk = me.own(0), me.own(1)
    first_rows, second_rows = at(up_chunk * chunk, chunk), at(low_chunk * chunk, chunk)
    qkv_pieces = [
        piece(0, wq_ref.at[first_rows, at((1 - row) * width, width)], w_far.at[up_chunk, :, pl.ds(0, width)]),
        piece(1, wk_ref.at[second_rows, at((1 - row) * kv, kv)], w_far.at[low_chunk, :, pl.ds(width, kv)]),
        piece(2, wv_ref.at[second_rows, at((1 - row) * kv, kv)], w_far.at[low_chunk, :, pl.ds(width + kv, kv)]),
        piece(3, gains_ref, gains_out),
    ]
    down_first = at((1 - row) * units + up_chunk * down_chunk, down_chunk)
    down_second = at((1 - row) * units + low_chunk * down_chunk, down_chunk)
    late_pieces = [
        piece(4, wo_ref.at[first_rows, pl.ds(0, half // 2)], wo_far.at[up_chunk, :, pl.ds(0, half // 2)]),
        piece(5, wo_ref.at[second_rows, pl.ds(half // 2, half // 2)], wo_far.at[low_chunk, :, pl.ds(half // 2, half // 2)]),
        piece(6, gate_ref.at[first_rows, at((1 - row) * units, units)], gate_up_out.at[up_chunk, :, pl.ds(0, units)]),
        piece(7, up_ref.at[second_rows, at((1 - row) * units, units)], gate_up_out.at[low_chunk, :, pl.ds(units, units)]),
        piece(8, down_ref.at[down_first, pl.ds(0, half // 2)], down_out.at[up_chunk, :, pl.ds(0, half // 2)]),
        piece(9, down_ref.at[down_second, pl.ds(half // 2, half // 2)], down_out.at[low_chunk, :, pl.ds(half // 2, half // 2)]),
    ]
    token_copies = [remote(token_ref.at[own_rows(k), :], far.at[own_rows(k), :], token_send.at[k], token_recv.at[k], me.across)
                    for k in range(pieces)]
    passes = [remote(far.at[own_rows(k), :], far.at[own_rows(k), :], pass_send.at[k], pass_recv.at[k], me.beside)
              for k in range(pieces)]
    cots = [remote(cot_ref.at[own_rows(k), :], cot_out.at[own_rows(k), :], cot_send.at[0, k], cot_recv.at[0, k], me.across)
            for k in range(pieces)]
    cot_passes = [remote(cot_out.at[own_rows(k), :], cot_out.at[own_rows(k), :], cot_send.at[1, k], cot_recv.at[1, k], me.beside)
                  for k in range(pieces)]
    for each in qkv_pieces + token_copies:
        each.start()

    def fetch(k, src, dst):
        return pltpu.make_async_copy(src, dst, local_sem.at[k])

    quarter = half // 2
    mine_rows, other_quarter = at(row * quarter, quarter), at((1 - row) * quarter, quarter)
    fetches = [
        fetch(0, token_ref, near),
        fetch(1, wq_ref.at[:, at(row * width, width)], w_near.at[:, pl.ds(0, width)]),
        fetch(2, wk_ref.at[:, at(row * kv, kv)], w_near.at[:, pl.ds(width, kv)]),
        fetch(3, wv_ref.at[:, at(row * kv, kv)], w_near.at[:, pl.ds(width + kv, kv)]),
        fetch(4, wo_ref.at[mine_rows, :], wo_all.at[pl.ds(0, quarter), pl.ds(0, half)]),
        fetch(5, wo_ref.at[other_quarter, :], wo_all.at[pl.ds(2 * quarter, quarter), pl.ds(0, half)]),
    ]
    for each in fetches:
        each.start()

    def wo_copy(k, src, rows_at, side):
        return remote(src, wo_all.at[pl.ds(rows_at, quarter), pl.ds(side, half)], wo_send.at[k], wo_recv.at[k], me.beside)

    wo_copies = [wo_copy(0, wo_ref.at[mine_rows, :], quarter, 0), wo_copy(1, wo_ref.at[other_quarter, :], 3 * quarter, 0)]
    for each in wo_copies:
        each.start()

    qkv = Spread(me, w_far, qkv_send, qkv_recv)
    wide = Spread(me, gate_up_out, wide_send, wide_recv)
    thin = Spread(me, down_out, thin_send, thin_recv)
    wo = Spread(me, wo_far, out_send, out_recv)
    for each in qkv_pieces:
        each.wait()
    for s in range(2):
        qkv.start(s)
    for k in range(pieces):
        steps(k * (m - 1) // pieces, (k + 1) * (m - 1) // pieces, qkv)
        token_copies[k].wait()
        passes[k].start()
        if k == pieces // 2:
            for each in late_pieces:
                each.start()
    for each in cots:
        each.start()
    for each in fetches:
        each.wait()

    def prepared(x, gain, cosine, sine):
        normed = x * lax.rsqrt(head_sums(x * x) / HEAD_SIZE + EPSILON) * gain
        return normed * cosine + swapped(normed) * sine

    far_gains = gains_out

    def project_block(k):
        begin = ((col * pieces + 2 * k) % (2 * pieces)) * rows

        def part(k, carry):
            project_rows(at(begin + k * rows, rows))
            return carry

        lax.fori_loop(0, 2, part, 0)

    def project_rows(block):
        x_near = near[block, :].astype(F32)
        x_far = far[block, :].astype(F32)
        total = jnp.sum(x_near * x_near, axis=1, keepdims=True) + jnp.sum(x_far * x_far, axis=1, keepdims=True)
        inverse = lax.rsqrt(total / (2 * half) + EPSILON)
        h_near = (x_near * inverse * gains_ref[0:1, :]).astype(BF16)
        h_far = (x_far * inverse * far_gains[0:1, :]).astype(BF16)
        hid_near[block, :] = h_near
        hid_far[block, :] = h_far
        out = dot(h_near, w_near[...]) + dot(h_far, w_far[...].reshape(half, w_far.shape[2]))
        raw[block, :] = out[:, :width + kv]
        cosine, sine = rope_block(table_ref, block)
        for g in range(groups):
            cut = slice(g * lanes, (g + 1) * lanes)
            part = prepared(out[:, cut], q_gain_ref[...], cosine, sine).astype(BF16)
            q_all[block, cut] = (part * HEAD_SIZE ** (-0.5)).astype(BF16)
        for g in range(groups // 2):
            begin = width + g * lanes
            twice = doubled(prepared(out[:, begin:begin + lanes], k_gain_ref[...], cosine, sine))
            value = doubled(out[:, begin + kv:begin + kv + lanes])
            for h in range(2):
                cut = slice((2 * g + h) * lanes, (2 * g + h + 1) * lanes)
                k_all[block, cut] = twice[h].astype(BF16)
                v_all[block, cut] = value[h].astype(BF16)

    rings = (wide, thin, wo)
    slots = 3 + groups * (packed // b) * (packed // b + 1) // 2

    def tick(k):
        steps((k * (m - 1)) // slots, ((k + 1) * (m - 1)) // slots, *rings)

    project_block(0)
    for each in late_pieces:
        each.wait()
    for ring in rings:
        for s in range(2):
            ring.start(s)
    project_block(1)
    tick(0)
    for k in range(pieces):
        passes[k].wait()
        if k % 2 == 1:
            project_block(2 + k // 2)
            tick(1 + k // 2)

    def store(k, src, dst):
        return pltpu.make_async_copy(src, dst, store_sem.at[k])

    stores = [store(k, src, dst) for k, (src, dst) in enumerate((
        (far, far_out), (hid_near, hid_near_out), (hid_far, hid_far_out), (raw, raw_out), (q_all, q_out), (k_all, k_out),
        (v_all, v_out)))]
    for each in stores:
        each.start()

    blocks = packed // b
    per_half = blocks // 2

    def low_copy(kind, g, i, target):
        slot = (2, 1, 3)[kind] * width + g * lanes
        return remote(low.at[at(i * b, b), pl.ds(g * lanes, lanes)],
                      attended.at[at((i % per_half) * b, b), pl.ds(slot, lanes)],
                      low_send.at[kind, g, i % per_half], low_recv.at[kind, g, i % per_half], target)

    for g in range(groups):
        cut = slice(g * lanes, (g + 1) * lanes)

        def query_block(i, carry, g=g, cut=cut):
            place = at(i * b, b)
            qs = stacked(q_all[place, cut])
            begins = starts_ref[place, :]
            begins = jnp.concatenate([begins, begins], axis=0)
            acc_ref[...] = jnp.zeros_like(acc_ref)
            mass_ref[...] = jnp.zeros_like(mass_ref)
            base = 3 + g * (blocks * (blocks + 1) // 2) + (i * (i + 1)) // 2

            def key_block(j, diagonal):
                keys = at(j * b, b)
                s = dot(qs, k_all[keys, cut], NT)
                columns = j * b + lax.broadcasted_iota(jnp.int32, (1, b), 1)
                allowed = columns >= begins
                if diagonal:
                    lines = i * b + lax.rem(lax.broadcasted_iota(jnp.int32, (2 * b, 1), 0), b)
                    allowed = allowed & (columns <= lines)
                p = jnp.where(allowed, jnp.exp(s), 0.0)
                mass = p[:, :128]
                for part in range(1, b // 128):
                    mass = mass + p[:, part * 128:(part + 1) * 128]
                mass_ref[...] += mass
                acc_ref[...] += dot(p.astype(BF16), v_all[keys, cut])
                tick(base + j)

            @pl.loop(0, i)
            def _(j):
                key_block(j, False)

            key_block(i, True)
            mass = jnp.sum(mass_ref[...], axis=1, keepdims=True)
            out = acc_ref[...] / mass
            first = lax.broadcasted_iota(jnp.int32, (b, lanes), 1) < HEAD_SIZE
            out = jnp.where(first, out[:b], out[b:])
            heads[place, cut] = out
            low[place, cut] = out.astype(BF16)
            total = jnp.log(jnp.sum(mass_ref[...].T, axis=0, keepdims=True))
            totals_out[g, 0:1, place] = total[:, :b]
            totals_out[g, 1:2, place] = total[:, b:]

            @pl.when(i // per_half == col)
            def _():
                attended[at((i % per_half) * b, b), cut] = out.astype(BF16)
                low_copy(0, g, i, me.across).start()

            @pl.when(i // per_half != col)
            def _():
                low_copy(1, g, i, me.beside).start()
                low_copy(2, g, i, me.opposite).start()
            return carry

        lax.fori_loop(0, blocks, query_block, 0)
    heads_store = store(7, heads, heads_out)
    heads_store.start()
    w_stores = [store(8 + 3 * per_half, w_near, w_near_out), store(9 + 3 * per_half, w_far, w_far_out)]
    for each in w_stores:
        each.start()

    local_far = []
    per = quarter // chunk
    for p, begin in ((0, row), (2, 1 - row)):
        for k in range(per):
            local_far.append(pltpu.make_async_copy(
                wo_far.at[begin * per + k], wo_all.at[pl.ds(p * quarter + k * chunk, chunk), pl.ds(half, half)],
                local_sem.at[6 + len(local_far)]))
    remote_far = []
    for p, begin in ((1, row), (3, 1 - row)):
        for k in range(per):
            remote_far.append(remote(
                wo_far.at[begin * per + k], wo_all.at[pl.ds(p * quarter + k * chunk, chunk), pl.ds(half, half)],
                wo_send.at[2 + len(remote_far)], wo_recv.at[2 + len(remote_far)], me.beside))
    for each in local_far + remote_far:
        each.start()
    for k in range(pieces):
        cots[k].wait()
        cot_passes[k].start()
    for each in local_far + remote_far + wo_copies:
        each.wait()
    w_stores.append(store(10 + 3 * per_half, wo_all.at[pl.ds(0, quarter), :], wo_out))
    w_stores[-1].start()

    gain = jnp.concatenate([gains_ref[1:2, :], far_gains[1:2, :]], axis=1)
    hidden_stores = []
    for k in range(per_half):
        for g in range(groups):
            for kind in range(3):
                low_copy(kind, g, k, me.beside).wait()
        place = at(col * count + k * b, b)

        def merge(fine, k=k):
            part = at(k * b + fine.start, fine.size)
            mine = at(col * count + k * b + fine.start, fine.size)
            tokens = jnp.concatenate([near[mine, :], far[mine, :]], axis=1).astype(F32)
            total = tokens + dot(attended[part, :], wo_all[...])
            middle[part, :] = total
            inverse = lax.rsqrt(jnp.sum(total * total, axis=1, keepdims=True) / (2 * half) + EPSILON)
            hidden[part, :] = (total * inverse * gain).astype(BF16)

        by_rows(b, merge, 128)
        hidden_stores += [
            remote(hidden.at[pl.ds(k * b, b), :], hidden_out.at[place, :], hidden_send.at[k], hidden_recv.at[k], me.beside),
            pltpu.make_async_copy(hidden.at[pl.ds(k * b, b), :], hidden_out.at[place, :], store_sem.at[8 + 3 * k]),
            pltpu.make_async_copy(middle.at[pl.ds(k * b, b), :], middle_out.at[pl.ds(k * b, b), :], store_sem.at[9 + 3 * k]),
            pltpu.make_async_copy(attended.at[pl.ds(k * b, b), :], attended_out.at[pl.ds(k * b, b), :], store_sem.at[10 + 3 * k]),
        ]
        for each in hidden_stores[-4:]:
            each.start()
    for each in stores + [heads_store] + w_stores + hidden_stores + cot_passes:
        each.wait()
    finish(m, qkv, *rings)


def rope_block(table_ref, block):
    half = HEAD_SIZE // 2
    cosine, sine = table_ref[:half, block], table_ref[half:, block]
    return jnp.concatenate([cosine] * 4, axis=0).T, jnp.concatenate([-sine, sine] * 2, axis=0).T


def begin(tokens, cot, wq, wk, wv, gate, up, down, wo, gains, q_gain, k_gain, table, starts, names, n, b=512):
    packed, half = tokens.shape
    b = min(b, packed // 2)
    m = math.gcd(n, 8)
    width, kv, units = wq.shape[1] // 2, wk.shape[1] // 2, gate.shape[1] // 2
    groups = width // (2 * HEAD_SIZE)
    count = packed // 2
    vmem = pl.BlockSpec(memory_space=pltpu.VMEM)
    some = pl.BlockSpec(memory_space=pl.ANY)
    dma = pltpu.SemaphoreType.DMA

    outs = [((packed, half), BF16, some), ((m, half // m, 2 * units), BF16, some), ((m, units // m, half), BF16, some),
            ((packed, half), BF16, some), (gains.shape, F32, vmem), ((packed, half), BF16, some), ((packed, half), BF16, some),
            ((packed, width + kv), F32, some), ((packed, width), BF16, some), ((packed, width), BF16, some),
            ((packed, width), BF16, some), ((packed, width), F32, some), ((groups, 2, packed), F32, vmem),
            ((count, 2 * half), BF16, some), ((count, 2 * half), F32, some), ((packed, 2 * half), BF16, some),
            ((half // 2, 2 * half), BF16, some), ((half, width + 2 * kv), BF16, some), ((m, half // m, width + 2 * kv), BF16, some)]
    scratch = [((packed, half), BF16), ((packed, half), BF16), ((half, width + 2 * kv), BF16), ((m, half // m, width + 2 * kv), BF16),
               ((m, half // m, half), BF16), ((2 * half, 2 * half), BF16), ((packed, half), BF16), ((packed, half), BF16),
               ((packed, width + kv), F32), ((packed, width), BF16), ((packed, width), BF16), ((packed, width), BF16),
               ((packed, width), BF16), ((packed, width), F32), ((count, 2 * half), BF16), ((count, 2 * half), F32),
               ((count, 2 * half), BF16), ((2 * b, 2 * HEAD_SIZE), F32), ((2 * b, 2 * HEAD_SIZE), F32)]
    per_half = count // b
    ring = [dma((2, m - 1))] * 8
    return pl.pallas_call(
        functools.partial(begin_kernel, n, m, names, b),
        out_shape=tuple(jax.ShapeDtypeStruct(shape, dtype) for shape, dtype, _ in outs),
        in_specs=[some] * 9 + [vmem] * 5,
        out_specs=tuple(spec for *_, spec in outs),
        scratch_shapes=[
            *[pltpu.VMEM(shape, dtype) for shape, dtype in scratch],
            dma((6 + m,)), dma((11 + 3 * per_half,)), dma((4,)), dma((4,)), dma((4,)), dma((4,)), dma((10,)), dma((10,)),
            dma((2, 4)), dma((2, 4)), *ring, dma((2 + m,)), dma((2 + m,)),
            dma((3, groups, per_half)), dma((3, groups, per_half)), dma((per_half,)), dma((per_half,)),
        ],
        compiler_params=pltpu.CompilerParams(collective_id=4, has_side_effects=True, vmem_limit_bytes=62 << 20),
        cost_estimate=pl.CostEstimate(flops=20 << 30, transcendentals=0, bytes_accessed=100 << 20),
        name="begin",
    )(tokens, cot, wq, wk, wv, gate, up, down, wo, gains, q_gain, k_gain, table, starts)


def turn_kernel(n, names, pieces, hidden_ref, grads_ref, active_ref, cot_near_ref, cot_far_ref, back_ref, middle_ref,
                attended_ref, wo_ref, gain_ref, keep_ref, gain_sum_ref, done_ref, down_done_ref, heads_ref, wo_grad_ref,
                hidden, grads, active, cot_near, cot_far, back, middle, wo, near, far, down_near, down_far, branch, other_branch,
                slots, down_slots, beside_in, across_out, across_in, give_in, load_sem, rs_send, rs_recv, down_send, down_recv,
                cross_send, cross_recv, beside_send, beside_recv, across_send, across_recv, branch_send, branch_recv,
                give_send, give_recv):
    me = Group(names, n)
    half = cot_near_ref.shape[1]
    tokens = middle_ref.shape[0]
    rows = tokens // pieces
    units = active_ref.shape[1]
    row, col = me.row, me.col
    wide = Reduce(me, (far, near), slots, rs_send, rs_recv)
    down = Reduce(me, (down_far, down_near), down_slots, down_send, down_recv)

    def place_of(core, k):
        return pl.ds(pl.multiple_of(core * tokens + k * rows, rows), rows)

    def load(k, src, dst):
        return pltpu.make_async_copy(src, dst, load_sem.at[k])

    mine = pl.ds(pl.multiple_of(col * tokens, tokens), tokens)
    loads = [load(0, back_ref.at[mine, :], back), load(1, active_ref, active), load(2, cot_near_ref, cot_near),
             load(3, cot_far_ref, cot_far), load(4, hidden_ref, hidden), load(5, grads_ref, grads), load(6, middle_ref, middle),
             load(7, wo_ref, wo)]
    for each in loads:
        each.start()
    me.arrive([*me.ring, me.across, me.beside])
    besides = [remote(back_ref.at[place_of(1 - col, k), :], beside_in.at[k], beside_send.at[k], beside_recv.at[k], me.beside)
               for k in range(pieces)]
    for each in besides:
        each.start()
    acrosses = [remote(across_out.at[k], across_in.at[k], across_send.at[k], across_recv.at[k], me.across)
                for k in range(pieces)]
    loads[0].wait()
    for k in range(pieces):
        besides[k].wait()

        def add(part, k=k):
            mine = pl.ds(pl.multiple_of(k * rows + part.start, part.size), part.size)
            chip = (back[mine, :].astype(F32) + beside_in[k, part, :].astype(F32)).astype(BF16)
            across_out[k, part, :half] = chip[:, half:]
            across_out[k, part, half:] = chip[:, :half]

        by_rows(rows, add)
        acrosses[k].start()

    for each in loads[1:4]:
        each.wait()
    per = units // 3

    def down_tile(k, carry):
        left = active[:, pl.ds(pl.multiple_of(k * per, per), per)]
        for cot, out in ((cot_near, down_near), (cot_far, down_far)):
            part = over_t(left, cot[...]).astype(BF16)
            line = down_near.shape[1]
            if per % line == 0:
                for c in range(per // line):
                    out[k * (per // line) + c] = part[c * line:(c + 1) * line]
            else:
                for c in range(per // 16):
                    at = k * per + c * 16
                    out[at // line, pl.ds(at % line, 16), :] = part[c * 16:(c + 1) * 16]
        return carry

    if units // n % 16 == 0 and per % 16 == 0:
        lax.fori_loop(0, 3, down_tile, 0)
    else:
        for cot, out in ((cot_near, down_near), (cot_far, down_far)):
            part = over_t(active[...], cot[...]).astype(BF16)
            line = down_near.shape[1]
            for c in range(n):
                out[c] = part[c * line:(c + 1) * line]
    down.start()
    for each in loads[4:6]:
        each.wait()
    line = near.shape[1]
    tile = 256

    def wide_tiles(out, begin, count):
        def wide_tile(k, carry):
            left = hidden[:, pl.ds(pl.multiple_of(begin + k * tile, tile), tile)]
            for side in range(2):
                part = over_t(left, grads[:, side * units:(side + 1) * units]).astype(BF16)
                for c in range(tile // line):
                    out[k * (tile // line) + c, :, side * units:(side + 1) * units] = part[c * line:(c + 1) * line]
            return carry

        lax.fori_loop(0, count, wide_tile, 0)

    gain_sum_ref[...] = jnp.zeros_like(gain_sum_ref)

    def branch_copy(k):
        part = pl.ds(k * rows, rows)
        return remote(branch.at[part, :], other_branch.at[part, :], branch_send.at[k], branch_recv.at[k], me.beside)

    def norm_piece(k):
        acrosses[k].wait()

        def end(fine):
            part = pl.ds(pl.multiple_of(k * rows + fine.start, fine.size), fine.size)
            place = pl.ds(pl.multiple_of(col * tokens + k * rows + fine.start, fine.size), fine.size)
            grad = back[part, :].astype(F32) + beside_in[k, fine, :].astype(F32) + across_in[k, fine, :].astype(F32)
            x = middle[part, :]
            inverse = lax.rsqrt(jnp.sum(x * x, axis=1, keepdims=True) / (2 * half) + EPSILON)
            normal = x * inverse
            weighed = grad * normal
            gain_sum_ref[...] += jnp.sum(weighed, axis=0, keepdims=True)
            stat = jnp.sum(weighed * gain_ref[...], axis=1, keepdims=True) / (2 * half)
            change = inverse * (grad * gain_ref[...] - normal * stat)
            keep = cot_near[place, :].astype(F32) + change[:, :half]
            keep_ref[part, :] = keep
            branch[part, :half] = keep.astype(BF16)
            branch[part, half:] = (cot_far[place, :].astype(F32) + change[:, half:]).astype(BF16)

        by_rows(rows, end)
        branch_copy(k).start()

    wide_tiles(far, half, half // tile)
    steps(0, (n - 1) // 3, down)
    wide_tiles(near, 0, half // tile)
    wide.start()
    fetch_attended = load(8, attended_ref, hidden.at[pl.ds(0, tokens), :])
    fetch_attended.start()
    steps((n - 1) // 3, (2 * (n - 1)) // 3, down)
    loads[6].wait()
    for k in range(pieces):
        norm_piece(k)
        if k == pieces - 2:
            steps((2 * (n - 1)) // 3, n - 1, down)
        steps((k * (n - 1)) // (2 * pieces), ((k + 1) * (n - 1)) // (2 * pieces), wide)
    from_step = (n - 1) // 2

    def crosses_of(ring, out, base):
        return [remote(ring.last(s), out.at[s], cross_send.at[base + s], cross_recv.at[base + s], me.across) for s in range(2)]

    crosses = crosses_of(down, down_done_ref, 2)
    for cross in crosses:
        cross.start()
    for s in (2, 3):
        down_done_ref[s] = down.last(s)[...]

    fetch_attended.wait()
    loads[7].wait()
    quarter = half // 2
    gives = []
    for p in (1, 3, 0, 2):
        part = over_t(hidden[:tokens, p * quarter:(p + 1) * quarter], branch[:, :half])
        if p in (1, 3):
            across_out[p // 2, :quarter, :half] = part.astype(BF16)
            gives.append(remote(across_out.at[p // 2, pl.ds(0, quarter), pl.ds(0, half)],
                                give_in.at[p // 2],
                                give_send.at[p // 2], give_recv.at[p // 2], me.beside))
            gives[-1].start()
            steps(from_step, from_step + 1, wide) if p == 3 and n > 3 else None
        else:
            gives[p // 2].wait()
            place = row if p == 0 else 1 - row
            total = part + give_in[p // 2].astype(F32)
            wo_grad_ref[pl.ds(pl.multiple_of(place * quarter, quarter), quarter), :] = total.astype(BF16)

    def attended_grad(src, core):
        def each(part):
            heads_ref[pl.ds(pl.multiple_of(core * tokens + part.start, part.size), part.size), :] = dot(
                src[part, :], wo[...], NT).astype(BF16)

        by_rows(tokens, each, 256)

    attended_grad(branch, col)
    for k in range(pieces):
        branch_copy(k).wait()
    attended_grad(other_branch, 1 - col)
    steps(from_step + 1 if n > 3 else from_step, n - 1, wide)

    crosses += crosses_of(wide, done_ref, 0)
    for cross in crosses[2:]:
        cross.start()
    for s in (2, 3):
        done_ref[s] = wide.last(s)[...]
    for cross in crosses:
        cross.wait()
    finish(n, wide, down)


def turn(hidden, grads, active, cot_near, cot_far, back, middle, attended, wo, gain, names, n, pieces=4):
    packed, width = back.shape
    tokens, half, units = middle.shape[0], width // 2, active.shape[1]
    vmem = pl.BlockSpec(memory_space=pltpu.VMEM)
    some = pl.BlockSpec(memory_space=pl.ANY)
    dma = pltpu.SemaphoreType.DMA
    exchange = ((pieces, tokens // pieces, width), BF16)
    wide, down = (half // n, units), (units // n, half // 2)
    outs = [((tokens, half), F32), ((1, width), F32), ((4, *wide), BF16), ((4, *down), BF16), ((packed, wo.shape[0]), BF16),
            ((half, half), BF16)]
    scratch = [(x.shape, x.dtype) for x in (hidden, grads, active, cot_near, cot_far)]
    scratch += [((tokens, width), BF16), (middle.shape, F32), (wo.shape, BF16), ((n, half // n, 2 * units), BF16),
                ((n, half // n, 2 * units), BF16), ((n, units // n, half), BF16), ((n, units // n, half), BF16),
                ((tokens, width), BF16), ((tokens, width), BF16), ((4, n - 1, *wide), BF16), ((4, n - 1, *down), BF16),
                exchange, exchange, exchange, ((2, half // 2, half), BF16)]
    return pl.pallas_call(
        functools.partial(turn_kernel, n, names, pieces),
        out_shape=tuple(jax.ShapeDtypeStruct(shape, dtype) for shape, dtype in outs),
        in_specs=[some] * 9 + [vmem],
        out_specs=(vmem,) * len(outs),
        scratch_shapes=[
            *[pltpu.VMEM(shape, dtype) for shape, dtype in scratch], dma((9,)), *[dma((4, n - 1))] * 4, dma((4,)), dma((4,)),
            *[dma((pieces,))] * 6, dma((2,)), dma((2,)),
        ],
        compiler_params=pltpu.CompilerParams(collective_id=1, has_side_effects=True, vmem_limit_bytes=VMEM_LIMIT),
        cost_estimate=pl.CostEstimate(flops=6 * packed * width * units, transcendentals=tokens, bytes_accessed=150 << 20),
        name="turn",
    )(hidden, grads, active, cot_near, cot_far, back, middle, attended, wo, gain)


def finale_kernel(n, names, b, q_ref, k_ref, v_ref, grad_ref, heads_ref, totals_ref, start_ref, done_ref, down_done_ref,
                  result_ref, middle_ref, keep_ref, raw_ref, token_ref, far_ref, hid_near_ref, hid_far_ref, w_near_ref, w_far_ref,
                  wo_grad_ref, gain_near_ref, gain_far_ref, q_gain_ref, k_gain_ref, table_ref, ffn_sum_ref,
                  wide_ref, down_ref, output_ref, thin_ref, lone_ref, sums_ref, tokens_grad_ref,
                  q_all, k_all, v_all, grad_all, heads, raw, near, far, hid_near, hid_far, w_near, w_far, middle_near, sums,
                  qs_ref, gs_ref, stat_ref, dqt_ref, dk_acc, dv_acc, dq, dk, dv, grads, to_near, to_far, stat, near_grads, far_grads,
                  slots, lone_slots, result_in, result_out, result_back, beside_in, beside_stat, across_in,
                  stat_out, stat_in, far_total, vector, group_in, ring_in, mine, q_sum, k_sum, near_sum, far_sum,
                  load_sem, keep_sem, wide_send, wide_recv, down_send, down_recv, rs_send, rs_recv, ag_send, ag_recv,
                  lone_send, lone_recv, lone_out_send, lone_out_recv, cross_send, cross_recv, group_send, group_recv,
                  all_send, all_recv, result_send, result_recv, beside_send, beside_recv, across_send, across_recv,
                  last_send, last_recv):
    me = Group(names, n)
    row, col = me.row, me.col
    packed, half = token_ref.shape
    count = packed // 2
    lanes = 2 * HEAD_SIZE
    width = q_ref.shape[1]
    groups = width // lanes
    kv = groups * HEAD_SIZE
    blocks = packed // b
    per_half = blocks // 2
    wide = Spread(me, wide_ref, wide_send, wide_recv)
    down = Spread(me, down_ref, down_send, down_recv)
    lone = Meet(me, (wo_grad_ref,), lone_slots, lone_send, lone_recv)
    lone_out = Fan(me, lone_ref, lone_out_send, lone_out_recv)
    thin = Meet(me, (far_grads, near_grads), slots, rs_send, rs_recv)
    thin_out = Fan(me, thin_ref, ag_send, ag_recv)
    hops = n // 2

    def at(begin, size):
        return pl.ds(pl.multiple_of(begin, size), size)

    own_rows, other_rows = at(col * count, count), at((1 - col) * count, count)

    def load(k, src, dst):
        return pltpu.make_async_copy(src, dst, load_sem.at[k])

    first = [load(k, src, dst) for k, (src, dst) in enumerate((
        (q_ref, q_all), (k_ref, k_all), (v_ref, v_all), (grad_ref, grad_all), (heads_ref, heads)))]
    sides = (pl.ds(half, half), pl.ds(0, half))
    second = [load(5 + k, src, dst) for k, (src, dst) in enumerate((
        (result_ref.at[own_rows, sides[0]], sums.at[0]), (result_ref.at[own_rows, sides[1]], sums.at[1]),
        (middle_ref.at[:, pl.ds(0, half)], middle_near)))]
    third = [load(8 + k, src, dst) for k, (src, dst) in enumerate((
        (raw_ref, raw), (token_ref, near), (far_ref, far), (w_near_ref, w_near), (w_far_ref, w_far), (hid_near_ref, hid_near),
        (hid_far_ref, hid_far)))]
    keep, across_out = middle_near, sums.at[0]
    for each in first + second + third:
        each.start()

    me.arrive([*me.along, me.across, me.beside, me.opposite])
    for ring, src in ((wide, done_ref), (down, down_done_ref)):
        for s in range(4):
            ring.start(s, src.at[s])
    lone.start()
    keeps = [pltpu.make_async_copy(src.at[s], ring.piece(s, me.own(s % 2)), keep_sem.at[4 * k + s])
             for k, (ring, src) in enumerate(((wide, done_ref), (down, down_done_ref))) for s in range(4)]
    for each in keeps:
        each.start()
    results = [remote(result_ref.at[other_rows, side], result_in.at[k], result_send.at[k], result_recv.at[k], me.beside)
               for k, side in enumerate(sides)]
    for each in results:
        each.start()
    result_across = remote(result_out, result_back, result_send.at[2], result_recv.at[2], me.across)
    output_last = remote(result_out, output_ref.at[own_rows, :], last_send.at[0], last_recv.at[0], me.beside)
    output_here = pltpu.make_async_copy(result_out, output_ref.at[own_rows, :], keep_sem.at[8])
    for each in first:
        each.wait()

    every = groups * blocks * (blocks + 1) // 2
    slot_count = every + blocks

    early = max(n - 2, 1)

    def tick(k):
        steps((k * early) // slot_count, ((k + 1) * early) // slot_count, wide, down)
        steps((k * hops) // slot_count, ((k + 1) * hops) // slot_count, lone)

    def group_pass(g, carry):
        cut = at(g * lanes, lanes)
        dqt_ref[...] = jnp.zeros_like(dqt_ref)
        for i in range(blocks):
            rows = slice(i * b, (i + 1) * b)
            both = slice(i * 2 * b, (i + 1) * 2 * b)
            qs_ref[both, :] = stacked(q_all[rows, cut])
            grad = grad_all[rows, cut]
            gs_ref[both, :] = stacked(grad)
            prod = (grad.astype(F32) * heads[rows, cut]).T
            stat_ref[i, 0:1, 0:b] = totals_ref[g, 0:1, rows]
            stat_ref[i, 0:1, b:2 * b] = totals_ref[g, 1:2, rows]
            stat_ref[i, 1:2, 0:b] = jnp.sum(prod[:HEAD_SIZE], axis=0, keepdims=True)
            stat_ref[i, 1:2, b:2 * b] = jnp.sum(prod[HEAD_SIZE:], axis=0, keepdims=True)

        def key_pass(j, carry):
            place = at(j * b, b)
            k = k_all[place, cut]
            v = v_all[place, cut]
            kt = k.T[:HEAD_SIZE]
            dk_acc[...] = jnp.zeros_like(dk_acc)
            dv_acc[...] = jnp.zeros_like(dv_acc)
            keys = j * b + lax.broadcasted_iota(jnp.int32, (b, 1), 0)
            before = g * (every // groups) + j * blocks - (j * (j - 1)) // 2

            def step(i, diagonal):
                both = at(i * 2 * b, 2 * b)
                qs = qs_ref[both, :]
                gs = gs_ref[both, :]
                st = dot(k, qs, NT)
                pt = jnp.exp(st - stat_ref[i, 0:1, :])
                begin = start_ref[0:1, at(i * b, b)]
                allowed = keys >= jnp.concatenate([begin, begin], axis=1)
                if diagonal:
                    columns = i * b + lax.rem(lax.broadcasted_iota(jnp.int32, (1, 2 * b), 1), b)
                    allowed = allowed & (keys <= columns)
                pt = jnp.where(allowed, pt, 0.0)
                dv_acc[...] += dot(pt.astype(BF16), gs)
                dpt = dot(v, gs, NT)
                dst = (pt * (dpt - stat_ref[i, 1:2, :])).astype(BF16)
                dk_acc[...] += dot(dst, qs)
                part = dot(kt, dst)
                to = at(i * b, b)
                dqt_ref[:HEAD_SIZE, to] += part[:, :b]
                dqt_ref[HEAD_SIZE:, to] += part[:, b:]
                tick(before + i - j)

            step(j, True)

            @pl.loop(j + 1, blocks)
            def _(i):
                step(i, False)

            pair = at((g // 2) * lanes, lanes)
            keep_first = (lax.broadcasted_iota(jnp.int32, (b, lanes), 1) < HEAD_SIZE) & (g % 2 == 1)
            for acc, out in ((dk_acc, dk), (dv_acc, dv)):
                out[place, pair] = jnp.where(keep_first, out[place, pair], acc[...] + pltpu.roll(acc[...], HEAD_SIZE, 1))
            dq[place, cut] = dqt_ref[:, place].T * HEAD_SIZE ** (-0.5)

            @pl.when((g == 0) & (j == 0))
            def _():
                for each in results + second:
                    each.wait()

                def add(part):
                    result_out[part, :] = (sums[0, part, :].astype(F32) + result_in[0, part, :].astype(F32)).astype(BF16)

                by_rows(count, add)
                result_across.start()

            @pl.when((g == groups - 1) & (j == 0))
            def _():
                result_across.wait()

                def add(part):
                    total = sums[1, part, :].astype(F32) + result_in[1, part, :].astype(F32) + result_back[part, :].astype(F32)
                    result_out[part, :] = (middle_near[part, :] + total).astype(BF16)

                by_rows(count, add)
                output_last.start()
                output_here.start()
            return carry

        lax.fori_loop(0, blocks, key_pass, 0)
        return carry

    lax.fori_loop(0, groups, group_pass, 0)

    keep_load = load(15, keep_ref, keep)
    keep_load.start()
    for each in third:
        each.wait()
    for ref in (q_sum, k_sum, near_sum, far_sum):
        ref[...] = jnp.zeros_like(ref)

    def beside_copy(h, k):
        part = pl.ds(h * b, b)
        src = (to_far, stat, to_near)[k].at[at((1 - col) * count + h * b, b), :]
        dst = beside_stat.at[part, :] if k == 1 else beside_in.at[k // 2, part, :]
        return remote(src, dst, beside_send.at[h, k], beside_recv.at[h, k], me.beside)

    def across_copy(h, k):
        part = pl.ds(h * b, b)
        src, dst = ((across_out, across_in), (stat_out, stat_in))[k]
        return remote(src.at[part, :], dst.at[part, :], across_send.at[h, k], across_recv.at[h, k], me.across)

    fine = min(b, 256)

    def project_block(p):
        begin = (((1 - col) * per_half + p) % blocks) * b

        def part(k, carry):
            project_rows(at(begin + k * fine, fine))
            return carry

        lax.fori_loop(0, b // fine, part, 0)

    def project_rows(block):
        cosine, sine = rope_block(table_ref, block)
        head = lax.broadcasted_iota(jnp.int32, (fine, lanes), 1) < HEAD_SIZE

        def back(grad, x, gain):
            inverse = lax.rsqrt(head_sums(x * x) / HEAD_SIZE + EPSILON)
            normed = x * inverse
            turned = grad * cosine - swapped(grad) * sine
            inner = turned * gain
            part = inverse * (inner - normed * (head_sums(inner * normed) / HEAD_SIZE))
            return part, jnp.sum(turned * normed, axis=0, keepdims=True)

        for g in range(groups):
            cut = slice(g * lanes, (g + 1) * lanes)
            part, total = back(dq[block, cut], raw[block, cut], q_gain_ref[...])
            q_sum[...] += total
            grads[block, cut] = part.astype(BF16)
        for g in range(groups // 2):
            pair = slice(g * lanes, (g + 1) * lanes)
            cut = slice(width + g * lanes, width + (g + 1) * lanes)
            part, total = back(dk[block, pair], raw[block, cut], k_gain_ref[...])
            k_sum[...] += total
            grads[block, cut] = part.astype(BF16)
            cut = slice(width + kv + g * lanes, width + kv + (g + 1) * lanes)
            grads[block, cut] = dv[block, pair].astype(BF16)
        grad_near = dot(grads[block, :], w_near[...], NT)
        grad_far = dot(grads[block, :], w_far[...], NT)
        to_near[block, :] = grad_near.astype(BF16)
        to_far[block, :] = grad_far.astype(BF16)
        x_near = near[block, :].astype(F32)
        x_far = far[block, :].astype(F32)
        total = jnp.sum(x_near * x_near, axis=1, keepdims=True) + jnp.sum(x_far * x_far, axis=1, keepdims=True)
        inverse = lax.rsqrt(total / (2 * half) + EPSILON)
        x_near = grad_near * (x_near * inverse)
        x_far = grad_far * (x_far * inverse)
        near_sum[...] += jnp.sum(x_near, axis=0, keepdims=True)
        far_sum[...] += jnp.sum(x_far, axis=0, keepdims=True)
        total = (jnp.sum(x_near * gain_near_ref[...], axis=1, keepdims=True)
                 + jnp.sum(x_far * gain_far_ref[...], axis=1, keepdims=True))
        stat[block, :] = jnp.where(head, total, inverse)

    for p in range(blocks):
        project_block(p)
        h = p % per_half
        part = slice(h * b, (h + 1) * b)
        if p < per_half:
            for k in range(3):
                beside_copy(h, k).start()
        else:
            own = at(col * count + h * b, b)
            beside_copy(h, 0).wait()

            def add(fine, h=h):
                place = at(col * count + h * b + fine.start, fine.size)
                fine = at(h * b + fine.start, fine.size)
                across_out[fine, :] = (to_far[place, :].astype(F32) + beside_in[0, fine, :].astype(F32)).astype(BF16)

            by_rows(b, add)
            across_copy(h, 0).start()
            beside_copy(h, 1).wait()
            stat_out[part, :] = stat[own, :] + beside_stat[part, :]
            across_copy(h, 1).start()
        tick(every + p)

    line = half // n
    for hid, out in ((hid_far, far_grads), (hid_near, near_grads)):
        for k in range(2):
            part = over_t(hid[:, k * (half // 2):(k + 1) * (half // 2)], grads[...]).astype(BF16)
            for c in range(n // 2):
                out[k * (n // 2) + c] = part[c * line:(c + 1) * line]
    thin.start()
    lone_out.piece(0, me.place)[...] = lone.total(0)
    lone_out.start(0)

    vector[...] = jnp.zeros_like(vector)
    rows = half // 128
    for c in range(rows):
        cut = slice(c * 128, (c + 1) * 128)
        vector[pl.ds(row * rows + c, 1), :] = near_sum[:, cut]
        vector[pl.ds((1 - row) * rows + c, 1), :] = far_sum[:, cut]
        vector[pl.ds((2 + row) * rows + c, 1), :] = 0.5 * ffn_sum_ref[:, c * 128:(c + 1) * 128]
        vector[pl.ds((3 - row) * rows + c, 1), :] = 0.5 * ffn_sum_ref[:, half + c * 128:half + (c + 1) * 128]
    vector[4 * rows:4 * rows + 1, :] = q_sum[...]
    vector[4 * rows + 1:4 * rows + 2, :] = k_sum[...]
    gathers = [remote(vector, group_in.at[k], group_send.at[k], group_recv.at[k], target)
               for k, target in enumerate((me.across, me.beside, me.opposite))]
    for gather in gathers:
        gather.start()
    steps(0, hops // 2, thin, lone_out)
    steps(early, n - 1, wide, down)
    for gather in gathers:
        gather.wait()
    mine[...] = vector[...] + group_in[0] + group_in[1] + group_in[2]
    spreads = [remote(mine, ring_in.at[k], all_send.at[k], all_recv.at[k], target) for k, target in enumerate(me.along)]
    for spread in spreads:
        spread.start()
    steps(hops // 2, hops, thin, lone_out)

    far_total[...] = thin.total(0)
    cross = remote(far_total, thin_out.piece(0, me.place, row), cross_send, cross_recv, me.across)
    cross.start()
    thin_out.piece(1, me.place)[...] = thin.total(1)
    thin_out.start(1)
    cross.wait()
    thin_out.start(0)

    tails = []
    keep_load.wait()
    for h in range(per_half):
        part = slice(h * b, (h + 1) * b)
        own = at(col * count + h * b, b)
        beside_copy(h, 2).wait()
        for k in range(2):
            across_copy(h, k).wait()

        def end(fine, h=h):
            own = at(col * count + h * b + fine.start, fine.size)
            part = at(h * b + fine.start, fine.size)
            grad = to_near[own, :].astype(F32) + beside_in[1, part, :].astype(F32) + across_in[part, :].astype(F32)
            inverse = stat[own, HEAD_SIZE:HEAD_SIZE + 1]
            share = (stat_out[part, :1] + stat_in[part, :1]) / (2 * half)
            normal = near[own, :].astype(F32) * inverse
            across_out[part, :] = (inverse * (grad * gain_near_ref[...] - normal * share) + keep[part, :]).astype(BF16)

        by_rows(b, end)
        src = across_out.at[pl.ds(h * b, b), :]
        tails += [remote(src, tokens_grad_ref.at[own, :], last_send.at[1 + h], last_recv.at[1 + h], me.beside),
                  pltpu.make_async_copy(src, tokens_grad_ref.at[own, :], keep_sem.at[9 + h])]
        for each in tails[-2:]:
            each.start()
    steps(0, hops, thin_out)

    total = mine[...]
    for spread in spreads:
        spread.wait()
    for k in range(n - 1):
        total = total + ring_in[k]
    sums_ref[...] = total
    for each in tails + keeps + [output_here, output_last]:
        each.wait()
    finish(n, wide, down)
    finish(hops + 1, lone, lone_out, thin, thin_out)


def finale(q, k, v, grad, heads, totals, starts, done, down_done, result, middle, keep, raw, tokens, far, hid_near, hid_far,
           w_near, w_far, wo_grad, gain_near, gain_far, q_gain, k_gain, table, ffn_sum, names, n, b=512):
    packed, width = q.shape
    half = tokens.shape[1]
    b = min(b, packed // 2)
    count, blocks, lanes = packed // 2, packed // b, 2 * HEAD_SIZE
    per_half = blocks // 2
    line, columns = half // n, w_near.shape[1]
    vmem = pl.BlockSpec(memory_space=pltpu.VMEM)
    some = pl.BlockSpec(memory_space=pl.ANY)
    dma = pltpu.SemaphoreType.DMA
    rows = -(-(4 * (half // 128) + 2) // 8) * 8

    def full(x):
        return ((2, n, x.shape[1], 2 * x.shape[2]), BF16, some)

    outs = [full(done), full(down_done), ((packed, half), BF16, some), ((2, n, line, columns), BF16, vmem),
            ((n, line, half), BF16, vmem), ((rows, 128), F32, vmem), ((packed, half), BF16, some)]
    tall, short = ((packed, half), BF16), ((count, half), BF16)
    stats = ((count, lanes), F32)
    scratch = [*[((packed, width), BF16)] * 4, (heads.shape, F32), (raw.shape, F32), tall, tall, tall, tall,
               (w_near.shape, BF16), (w_far.shape, BF16), ((count, half), F32), ((2, count, half), BF16),
               ((2 * packed, lanes), BF16), ((2 * packed, lanes), BF16), ((blocks, 2, 2 * b), F32), ((lanes, packed), F32),
               ((b, lanes), F32), ((b, lanes), F32), ((packed, width), F32), ((packed, width // 2), F32), ((packed, width // 2), F32), ((packed, columns), BF16), tall, tall,
               ((packed, lanes), F32), ((n, line, columns), BF16), ((n, line, columns), BF16),
               ((4, n // 2, line, columns), BF16), ((2, n // 2, line, half), BF16),
               ((2, count, half), BF16), short, short, ((2, count, half), BF16), stats, short, stats, stats,
               ((line, columns), BF16), ((rows, 128), F32), ((3, rows, 128), F32), ((n - 1, rows, 128), F32), ((rows, 128), F32),
               ((1, lanes), F32), ((1, lanes), F32), ((1, half), F32), ((1, half), F32)]
    ring = [dma((4, n - 1))] * 4 + [dma((4, n // 2))] * 4 + [dma((2, n // 2))] * 4
    pairs = packed * (packed + b) // 2
    return pl.pallas_call(
        functools.partial(finale_kernel, n, names, b),
        out_shape=tuple(jax.ShapeDtypeStruct(shape, dtype) for shape, dtype, _ in outs),
        in_specs=[some] * 5 + [vmem] * 2 + [some] * 12 + [vmem] * 7,
        out_specs=tuple(spec for *_, spec in outs),
        scratch_shapes=[
            *[pltpu.VMEM(shape, dtype) for shape, dtype in scratch], dma((16,)), dma((9 + per_half,)), *ring,
            dma, dma, dma((3,)), dma((3,)), dma((n - 1,)), dma((n - 1,)), dma((3,)), dma((3,)),
            dma((per_half, 3)), dma((per_half, 3)), dma((per_half, 2)), dma((per_half, 2)), dma((1 + per_half,)), dma((1 + per_half,)),
        ],
        compiler_params=pltpu.CompilerParams(collective_id=3, has_side_effects=True, vmem_limit_bytes=VMEM_LIMIT),
        cost_estimate=pl.CostEstimate(flops=20 * 2 * pairs * 256, transcendentals=4 * pairs, bytes_accessed=100 << 20),
        name="finale",
    )(q, k, v, grad, heads, totals, starts[None, :], done, down_done, result, middle, keep, raw, tokens, far, hid_near, hid_far,
      w_near, w_far, wo_grad, gain_near, gain_far, q_gain, k_gain, table, ffn_sum)


def widen_kernel(widths, units, wide_ref, down_ref, thin_ref, lone_ref, gate_out, up_out, down_out, q_out, k_out, v_out, lone_out):
    for part in range(2):
        for out, begin in ((gate_out, 0), (up_out, units)):
            out[:, part * units:(part + 1) * units] = wide_ref[part, :, begin:begin + units].astype(F32)
        begin = 0
        for out, columns in zip((q_out, k_out, v_out), widths):
            out[:, part * columns:(part + 1) * columns] = thin_ref[part, :, begin:begin + columns].astype(F32)
            begin += columns
    down_out[...] = down_ref[...].astype(F32)
    lone_out[...] = lone_ref[...].astype(F32)


def widen(wide, down, thin, lone, widths, parts=8):
    half = lone.shape[0]
    units = wide.shape[2] // 2
    rows, down_rows = half // parts, down.shape[0] // parts

    def one(rows, columns):
        return pl.BlockSpec((rows, columns), lambda i: (i, 0))

    def two(columns):
        return pl.BlockSpec((2, rows, columns), lambda i: (0, i, 0))

    shapes = [(half, 2 * units)] * 2 + [down.shape] + [(half, 2 * columns) for columns in widths] + [lone.shape]
    return pl.pallas_call(
        functools.partial(widen_kernel, widths, units),
        out_shape=tuple(jax.ShapeDtypeStruct(shape, F32) for shape in shapes),
        grid=(parts,),
        in_specs=[two(2 * units), one(down_rows, down.shape[1]), two(thin.shape[2]), one(rows, lone.shape[1])],
        out_specs=tuple(one(down_rows if k == 2 else rows, shape[1]) for k, shape in enumerate(shapes)),
        compiler_params=pltpu.CompilerParams(vmem_limit_bytes=40 << 20),
        cost_estimate=pl.CostEstimate(flops=0, transcendentals=0, bytes_accessed=6 * (wide.size + down.size + thin.size + lone.size)),
        name="widen",
    )(wide, down, thin, lone)


def shards(
    tokens,
    seq_lengths,
    query_weight,
    key_matrix,
    value_matrix,
    out_weight,
    gate_weight,
    up_weight,
    down_weight,
    attn_gain,
    ffn_gain,
    query_gain,
    key_gain,
    cotangent,
):
    packed, half = tokens.shape
    row, col, group = lax.axis_index("row"), lax.axis_index("col"), lax.axis_index("dp")
    parts = lax.axis_size("dp")
    width = 2 * half

    names = ("dp", "row", "col")
    starts = layout(seq_lengths[0], packed)
    table = rope_table(jnp.arange(packed, dtype=jnp.int32) - starts)
    q_gain = jnp.tile(query_gain, 2)[None, :]
    k_gain = jnp.tile(key_gain, 2)[None, :]
    gains = jnp.stack([attn_gain, ffn_gain])
    (far, gate_up_far, down_far, cot_far, gains_far, hid_near, hid_far, raw, q, k, v, attended_raw, totals, attended, middle,
     hidden, out_own, qkv, qkv_far) = begin(
        tokens, cotangent, query_weight, key_matrix, value_matrix, gate_weight, up_weight, down_weight, out_weight, gains,
        q_gain, k_gain, table, starts[:, None], names, parts)
    gain_two = jnp.concatenate([ffn_gain, gains_far[1]])[None, :]
    units = down_weight.shape[0] // 2
    active, feed_grads, result, back = feed(
        row[None], hidden, cotangent, cot_far, gate_weight, up_weight, gate_up_far.reshape(half, -1), down_weight,
        down_far.reshape(units, half))

    keep, ffn_sum, done, down_done, grad_attended, grad_out = turn(
        hidden, feed_grads, active, cotangent, cot_far, back, middle, attended, out_own, gain_two, names, parts)
    grad_out = grad_out.reshape(parts, half // parts, -1)

    wide_full, down_full, output, thin_full, out_full, sums, grad_tokens = finale(
        q, k, v, grad_attended, attended_raw, totals, starts, done, down_done, result, middle, keep, raw, tokens, far,
        hid_near, hid_far, qkv, qkv_far.reshape(half, -1), grad_out, attn_gain[None, :], gains_far[:1], q_gain, k_gain, table,
        ffn_sum, names, parts)
    sums = sums.reshape(-1)

    def folded(x):
        return x[:HEAD_SIZE] + x[HEAD_SIZE:]

    widths = (query_weight.shape[1] // 2, key_matrix.shape[1] // 2, value_matrix.shape[1] // 2)
    gate_sum, up_sum, down_sum, q_weight_sum, k_weight_sum, v_weight_sum, out_sum = widen(
        wide_full.reshape(2, half, -1), down_full.reshape(2 * units, half), thin_full.reshape(2, half, -1),
        out_full.reshape(half, -1), widths)
    return (
        output,
        grad_tokens,
        q_weight_sum,
        k_weight_sum,
        v_weight_sum,
        out_sum,
        gate_sum,
        up_sum,
        down_sum,
        part_of(sums[:width], row, 0),
        part_of(sums[width:2 * width], row, 0),
        folded(sums[2 * width:2 * width + 2 * HEAD_SIZE]),
        folded(sums[2 * width + 2 * HEAD_SIZE:2 * width + 4 * HEAD_SIZE]),
    )


def solution(mesh):
    return jax.shard_map(
        shards,
        mesh=mesh,
        in_specs=(
            P("dp", "row"),
            P("dp", None),
            P("row", "col"),
            P("row", "col"),
            P("row", "col"),
            P("col", "row"),
            P("row", "col"),
            P("row", "col"),
            P("col", "row"),
            P("row"),
            P("row"),
            P(),
            P(),
            P("dp", "row"),
        ),
        out_specs=(
            P("dp", "row"),
            P("dp", "row"),
            P("row", "col"),
            P("row", "col"),
            P("row", "col"),
            P("col", "row"),
            P("row", "col"),
            P("row", "col"),
            P("col", "row"),
            P("row"),
            P("row"),
            P(),
            P(),
        ),
        check_vma=False,
    )
```

```python
import functools
import math

import jax
import jax.numpy as jnp
from jax import lax
from jax.experimental import pallas as pl
from jax.experimental.pallas import tpu as pltpu
from jax.sharding import PartitionSpec as P

HEAD_SIZE = 64
EPSILON = 1e-05
ROPE_BASE = 1000000.0
F32, BF16 = jnp.float32, jnp.bfloat16
MESH = pl.DeviceIdType.MESH


def dot(a, b, dims=(((1,), (0,)), ((), ()))):
    return lax.dot_general(a, b, dims, preferred_element_type=F32)


NT = (((1,), (1,)), ((), ()))

def stacked(x):
    first = lax.broadcasted_iota(jnp.int32, x.shape, 1) < 64
    zero = jnp.zeros_like(x)
    return jnp.concatenate([jnp.where(first, x, zero), jnp.where(first, zero, x)], axis=0)


def head_sums(x):
    first = lax.broadcasted_iota(jnp.int32, x.shape, 1) < HEAD_SIZE
    one = jnp.sum(jnp.where(first, x, 0.0), axis=1, keepdims=True)
    two = jnp.sum(jnp.where(first, 0.0, x), axis=1, keepdims=True)
    return jnp.where(first, one, two)


def swapped(x):
    low = lax.rem(lax.broadcasted_iota(jnp.int32, x.shape, 1), HEAD_SIZE) < HEAD_SIZE // 2
    return jnp.where(low, pltpu.roll(x, 96, 1), pltpu.roll(x, 32, 1))


def doubled(x):
    first = lax.broadcasted_iota(jnp.int32, x.shape, 1) < HEAD_SIZE
    other = pltpu.roll(x, HEAD_SIZE, 1)
    return jnp.where(first, x, other), jnp.where(first, other, x)


def layout(lengths, packed):
    count = lengths.shape[0]
    numbers = jnp.arange(count, dtype=jnp.int32)
    ends = jnp.sum(jnp.where(numbers[None, :] <= numbers[:, None], lengths[None, :], 0), axis=1)
    begins = ends - lengths
    places = jnp.arange(packed, dtype=jnp.int32)
    member = jnp.sum((places[:, None] >= ends[None, :]).astype(jnp.int32), axis=1)
    return jnp.sum(jnp.where(member[:, None] == numbers[None, :], begins[None, :], 0), axis=1)


def rope_table(position):
    half = HEAD_SIZE // 2
    inverse = jnp.exp(jnp.arange(half, dtype=F32) * (-2.0 * math.log(ROPE_BASE) / HEAD_SIZE))
    angles = position.astype(F32)[None, :] * inverse[:, None]
    return jnp.concatenate([jnp.cos(angles), jnp.sin(angles)], axis=0)


def swap(x, axis):
    return jax.tree.map(lambda part: lax.ppermute(part, axis, [(0, 1), (1, 0)]), x)


def ordered(own, other, index, axis=0):
    return jnp.where(index == 0, jnp.concatenate([own, other], axis), jnp.concatenate([other, own], axis))


def part_of(x, index, axis, parts=2):
    size = x.shape[axis] // parts
    return lax.dynamic_slice_in_dim(x, index * size, size, axis)


def over_t(left, right):
    return dot(left, right, (((0,), (0,)), ((), ())))


VMEM_LIMIT = 62 << 20


def feed_kernel(units, row_ref, hidden_ref, cot_near_ref, cot_far_ref, gate_ref, up_ref, far_ref, down_near_ref, down_far_ref,
                active_ref, grads_ref, result_ref):
    half = cot_near_ref.shape[1]
    near, far = hidden_ref[:, :half], hidden_ref[:, half:]
    gate = dot(near, gate_ref[...]) + dot(far, far_ref[:, :units])
    upward = dot(near, up_ref[...]) + dot(far, far_ref[:, units:])
    grad_active = dot(cot_near_ref[...], down_near_ref[...], NT) + dot(cot_far_ref[...], down_far_ref[...], NT)
    sig = 1.0 / (1.0 + jnp.exp(-gate))
    lifted = gate * sig
    active = (lifted * upward).astype(BF16)
    grad_gate = (grad_active * upward * (sig * (1.0 + gate * (1.0 - sig)))).astype(BF16)
    grad_up = (grad_active * lifted).astype(BF16)
    active_ref[...] = active
    grads_ref[:, :units] = grad_gate
    grads_ref[:, units:] = grad_up
    result_ref[:, :half] = dot(active, down_near_ref[...]).astype(BF16)
    result_ref[:, half:] = dot(active, down_far_ref[...]).astype(BF16)


def feed(row, hidden, cot_near, cot_far, gate, up, far, down, down_far, rows=256):
    packed, width = hidden.shape
    units, half = down_far.shape
    rows = min(rows, packed)

    def tile(n):
        return pl.BlockSpec((rows, n), lambda i, row: (i, 0))

    def once(shape, place):
        return pl.BlockSpec(shape, place, pipeline_mode=pl.Buffered(1))

    def out(n):
        return jax.ShapeDtypeStruct((packed, n), BF16)

    columns = once((half, units), lambda i, row: (0, row[0]))
    return pl.pallas_call(
        functools.partial(feed_kernel, units),
        out_shape=(out(units), out(2 * units), out(width)),
        grid_spec=pltpu.PrefetchScalarGridSpec(
            num_scalar_prefetch=1, grid=(packed // rows,),
            in_specs=[tile(width), tile(half), tile(half), columns, columns, once(far.shape, lambda i, row: (0, 0)),
                      once((units, half), lambda i, row: (row[0], 0)), once(down_far.shape, lambda i, row: (0, 0))],
            out_specs=(tile(units), tile(2 * units), tile(width)),
        ),
        compiler_params=pltpu.CompilerParams(vmem_limit_bytes=VMEM_LIMIT),
        cost_estimate=pl.CostEstimate(flops=8 * packed * width * units, transcendentals=packed * units,
                                      bytes_accessed=packed * (8 * width + 6 * units) + 6 * width * units),
        name="feed",
    )(row, hidden, cot_near, cot_far, gate, up, far, down, down_far)


class Group:
    def __init__(self, names, total, n=None):
        n = total if n is None else n
        self.n = n
        self.dp, self.row, self.col = (lax.axis_index(name) for name in names)
        self.base, member = (self.dp // n) * n, self.dp % n
        side = member % 2
        self.place = (member // 2) * (1 - side) + (n - 1 - member // 2) * side
        self.across = (self.dp, 1 - self.row, self.col)
        self.beside = (self.dp, self.row, 1 - self.col)
        self.opposite = (self.dp, 1 - self.row, 1 - self.col)
        self.along = [((self.dp + k) % total, self.row, self.col) for k in range(1, total)]
        self.ring = [(self.at(self.place + 1), self.row, self.col), (self.at(self.place - 1), self.row, self.col)]

    def at(self, position):
        position = (position + 2 * self.n) % self.n
        back = position // (self.n // 2)
        return self.base + (position * (1 - back) + (self.n - 1 - position) * back) * 2 + back

    def arrive(self, targets):
        barrier = pltpu.get_barrier_semaphore()
        for target in targets:
            pl.semaphore_signal(barrier, inc=1, device_id=target, device_id_type=MESH)
        pl.semaphore_wait(barrier, len(targets))

    def reduced(self, way, t):
        return (self.place - t - 1 + 2 * self.n) % self.n if way == 0 else (self.place + t + 1) % self.n

    def spread(self, way, t):
        return (self.place - t + 2 * self.n) % self.n if way == 0 else (self.place + t) % self.n

    def own(self, way):
        return (self.place + 1) % self.n if way == 0 else (self.place + self.n - 1) % self.n


def remote(src, dst, send, recv, target):
    return pltpu.make_async_remote_copy(
        src_ref=src, dst_ref=dst, send_sem=send, recv_sem=recv, device_id=target, device_id_type=MESH)


class Reduce:
    def __init__(self, me, parts, slots, send, recv):
        self.me, self.parts, self.slots, self.send, self.recv = me, parts, slots, send, recv
        self.columns = parts[0].shape[2] // 2

    def local(self, s, chunk):
        return self.parts[s // 2].at[chunk, :, pl.ds((s % 2) * self.columns, self.columns)]

    def copy(self, s, t, src):
        return remote(src, self.slots.at[s, t], self.send.at[s, t], self.recv.at[s, t], self.me.ring[s % 2])

    def start(self):
        for s in range(2 * len(self.parts)):
            self.copy(s, 0, self.local(s, self.me.place)).start()

    def step(self, t):
        for s in range(2 * len(self.parts)):
            slot = self.slots.at[s, t]
            self.copy(s, t, slot).wait_recv()
            slot[...] = (slot[...].astype(F32) + self.local(s, self.me.reduced(s % 2, t))[...].astype(F32)).astype(BF16)

            @pl.when(t < self.me.n - 2)
            def _():
                self.copy(s, t + 1, slot).start()

    def last(self, s):
        return self.slots.at[s, self.me.n - 2]

    def finish(self, t):
        for s in range(2 * len(self.parts)):
            self.copy(s, t, self.slots.at[s, t]).wait_send()


class Spread:
    def __init__(self, me, full, send, recv):
        self.me, self.full, self.send, self.recv = me, full, send, recv
        self.lone = len(full.shape) == 3
        self.columns = full.shape[-1] // 2
        self.streams = (0, 1) if self.lone else (2, 3, 0, 1)

    def piece(self, s, chunk, quarter=None):
        lanes = pl.ds((s % 2) * self.columns, self.columns)
        if self.lone:
            return self.full.at[chunk, :, lanes]
        if quarter is None:
            quarter = 1 - self.me.row if s < 2 else self.me.row
        return self.full.at[quarter, chunk, :, lanes]

    def copy(self, s, t, chunk, src=None):
        piece = self.piece(s, chunk)
        return remote(piece if src is None else src, piece, self.send.at[s, t], self.recv.at[s, t], self.me.ring[s % 2])

    def start(self, s, src=None):
        self.copy(s, 0, self.me.own(s % 2), src).start()

    def step(self, t):
        for s in self.streams:
            chunk = self.me.spread(s % 2, t)
            self.copy(s, t, chunk).wait_recv()

            @pl.when(t < self.me.n - 2)
            def _():
                self.copy(s, t + 1, chunk).start()

    def finish(self, t):
        for s in self.streams:
            self.copy(s, t, 0).wait_send()


class Meet:
    def __init__(self, me, parts, slots, send, recv):
        self.me, self.parts, self.slots, self.send, self.recv = me, parts, slots, send, recv
        self.hops = ((me.n - 1) // 2, me.n // 2)
        self.streams = [s for s in range(2 * len(parts)) if self.hops[s % 2]]

    def local(self, s, chunk):
        return self.parts[s // 2].at[(chunk + 2 * self.me.n) % self.me.n]

    def copy(self, s, t, src):
        return remote(src, self.slots.at[s, t], self.send.at[s, t], self.recv.at[s, t], self.me.ring[s % 2])

    def start(self):
        for s in self.streams:
            far = self.me.place + self.hops[0] if s % 2 == 0 else self.me.place - self.hops[1]
            self.copy(s, 0, self.local(s, far)).start()

    def step(self, t):
        for s in self.streams:
            hops = self.hops[s % 2]

            @pl.when(t < hops)
            def _(s=s, hops=hops):
                slot = self.slots.at[s, t]
                self.copy(s, t, slot).wait_recv()

                @pl.when(t < hops - 1)
                def _():
                    chunk = self.me.place + (hops - 1 - t if s % 2 == 0 else t + 1 - hops)
                    slot[...] = (slot[...].astype(F32) + self.local(s, chunk)[...].astype(F32)).astype(BF16)
                    self.copy(s, t + 1, slot).start()

    def total(self, part):
        out = self.local(2 * part, self.me.place)[...].astype(F32)
        for s in self.streams:
            if s // 2 == part:
                out = out + self.slots[s, self.hops[s % 2] - 1].astype(F32)
        return out.astype(BF16)

    def finish(self, t):
        for s in self.streams:
            @pl.when(t < self.hops[s % 2])
            def _(s=s):
                self.copy(s, t, self.slots.at[s, t]).wait_send()


class Fan:
    def __init__(self, me, full, send, recv):
        self.me, self.full, self.send, self.recv = me, full, send, recv
        self.lone = len(full.shape) == 3
        self.hops = (me.n // 2, (me.n - 1) // 2)
        self.streams = [s for s in ((0, 1) if self.lone else (2, 3, 0, 1)) if self.hops[s % 2]]

    def piece(self, part, chunk, quarter=None):
        chunk = (chunk + 2 * self.me.n) % self.me.n
        if self.lone:
            return self.full.at[chunk]
        if quarter is None:
            quarter = 1 - self.me.row if part == 0 else self.me.row
        return self.full.at[quarter, chunk]

    def copy(self, s, t, chunk):
        piece = self.piece(s // 2, chunk)
        return remote(piece, piece, self.send.at[s, t], self.recv.at[s, t], self.me.ring[s % 2])

    def start(self, part):
        for s in self.streams:
            if s // 2 == part:
                self.copy(s, 0, self.me.place).start()

    def step(self, t):
        for s in self.streams:
            hops = self.hops[s % 2]

            @pl.when(t < hops)
            def _(s=s, hops=hops):
                chunk = self.me.place + (-1 - t if s % 2 == 0 else 1 + t)
                self.copy(s, t, chunk).wait_recv()

                @pl.when(t < hops - 1)
                def _():
                    self.copy(s, t + 1, chunk).start()

    def finish(self, t):
        for s in self.streams:
            @pl.when(t < self.hops[s % 2])
            def _(s=s):
                self.copy(s, t, self.me.place).wait_send()


def steps(begin, end, *rings):
    def step(t, carry):
        for ring in rings:
            ring.step(t)
        return carry

    lax.fori_loop(begin, end, step, 0)


class Pace:
    def __init__(self, n):
        self.n, self.taken = n, {}

    def __call__(self, *rings):
        for ring in rings:
            at = self.taken.get(id(ring), 0)
            if at < self.n - 1 and self.n <= 16:
                ring.step(at)
                self.taken[id(ring)] = at + 1

    def rest(self, *rings):
        if self.n <= 16:
            while any(self.taken.get(id(ring), 0) < self.n - 1 for ring in rings):
                self(*rings)
            return
        for ring in rings:
            at = self.taken.get(id(ring), 0)
            if at < self.n - 1:
                steps(at, self.n - 1, ring)
                self.taken[id(ring)] = self.n - 1


def by_rows(total, action, rows=64):
    rows = min(rows, total)

    def each(k, carry):
        action(pl.ds(pl.multiple_of(k * rows, rows), rows))
        return carry

    lax.fori_loop(0, total // rows, each, 0)


def finish(n, *rings):
    def each(t, carry):
        for ring in rings:
            ring.finish(t)
        return carry

    lax.fori_loop(0, n - 1, each, 0)


def begin_kernel(n, m, names, b, token_ref, cot_ref, wq_ref, wk_ref, wv_ref, gate_ref, up_ref, down_ref, wo_ref, gains_ref,
                 q_gain_ref, k_gain_ref, table_ref, starts_ref,
                 far_out, gate_up_out, down_out, cot_out, gains_out, hid_near_out, hid_far_out, raw_out, q_out, k_out, v_out,
                 heads_out, totals_out, attended_out, middle_out, hidden_out, wo_out, w_near_out, w_far_out,
                 near, far, w_near, w_far, wo_far, wo_all, hid_near, hid_far, raw, q_all, k_all, v_all, low, heads, attended,
                 middle, hidden, acc_ref, mass_ref,
                 local_sem, store_sem, token_send, token_recv, pass_send, pass_recv, piece_send, piece_recv, cot_send, cot_recv,
                 qkv_send, qkv_recv, wide_send, wide_recv, thin_send, thin_recv, out_send, out_recv, wo_send, wo_recv,
                 low_send, low_recv, hidden_send, hidden_recv):
    me = Group(names, n, m)
    packed, half = token_ref.shape
    count = packed // 2
    row, col = me.row, me.col
    lanes = 2 * HEAD_SIZE
    groups = q_all.shape[1] // lanes
    width = groups * lanes
    kv = groups * HEAD_SIZE
    units = gate_ref.shape[1] // 2
    chunk = half // m
    down_chunk = units // m
    pieces = 4
    rows = count // pieces
    me.arrive([*me.ring, me.across, me.beside, me.opposite])

    def at(begin, size):
        return pl.ds(pl.multiple_of(begin, size), size)

    def own_rows(k):
        return at(col * count + k * rows, rows)

    def other_rows(k):
        return at((1 - col) * count + k * rows, rows)

    def piece(k, src, dst):
        return remote(src, dst, piece_send.at[k], piece_recv.at[k], me.across)

    up_chunk, low_chunk = me.own(0), me.own(1)
    first_rows, second_rows = at(up_chunk * chunk, chunk), at(low_chunk * chunk, chunk)
    qkv_pieces = [
        piece(0, wq_ref.at[first_rows, at((1 - row) * width, width)], w_far.at[up_chunk, :, pl.ds(0, width)]),
        piece(1, wk_ref.at[second_rows, at((1 - row) * kv, kv)], w_far.at[low_chunk, :, pl.ds(width, kv)]),
        piece(2, wv_ref.at[second_rows, at((1 - row) * kv, kv)], w_far.at[low_chunk, :, pl.ds(width + kv, kv)]),
        piece(3, gains_ref, gains_out),
    ]
    down_first = at((1 - row) * units + up_chunk * down_chunk, down_chunk)
    down_second = at((1 - row) * units + low_chunk * down_chunk, down_chunk)
    qkv_pieces += [
        piece(4, wo_ref.at[first_rows, pl.ds(0, half // 2)], wo_far.at[up_chunk, :, pl.ds(0, half // 2)]),
        piece(5, wo_ref.at[second_rows, pl.ds(half // 2, half // 2)], wo_far.at[low_chunk, :, pl.ds(half // 2, half // 2)]),
    ]
    late_pieces = [
        piece(6, gate_ref.at[first_rows, at((1 - row) * units, units)], gate_up_out.at[up_chunk, :, pl.ds(0, units)]),
        piece(7, up_ref.at[second_rows, at((1 - row) * units, units)], gate_up_out.at[low_chunk, :, pl.ds(units, units)]),
        piece(8, down_ref.at[down_first, pl.ds(0, half // 2)], down_out.at[up_chunk, :, pl.ds(0, half // 2)]),
        piece(9, down_ref.at[down_second, pl.ds(half // 2, half // 2)], down_out.at[low_chunk, :, pl.ds(half // 2, half // 2)]),
    ]
    token_copies = [remote(token_ref.at[own_rows(k), :], far.at[own_rows(k), :], token_send.at[k], token_recv.at[k], me.across)
                    for k in range(pieces)]
    passes = [remote(far.at[own_rows(k), :], far.at[own_rows(k), :], pass_send.at[k], pass_recv.at[k], me.beside)
              for k in range(pieces)]
    cots = [remote(cot_ref.at[own_rows(k), :], cot_out.at[own_rows(k), :], cot_send.at[0, k], cot_recv.at[0, k], me.across)
            for k in range(pieces)]
    cot_passes = [remote(cot_out.at[own_rows(k), :], cot_out.at[own_rows(k), :], cot_send.at[1, k], cot_recv.at[1, k], me.beside)
                  for k in range(pieces)]
    for each in qkv_pieces + late_pieces + token_copies:
        each.start()

    def fetch(k, src, dst):
        return pltpu.make_async_copy(src, dst, local_sem.at[k])

    quarter = half // 2
    mine_rows, other_quarter = at(row * quarter, quarter), at((1 - row) * quarter, quarter)
    fetches = [
        fetch(0, token_ref, near),
        fetch(1, wq_ref.at[:, at(row * width, width)], w_near.at[:, pl.ds(0, width)]),
        fetch(2, wk_ref.at[:, at(row * kv, kv)], w_near.at[:, pl.ds(width, kv)]),
        fetch(3, wv_ref.at[:, at(row * kv, kv)], w_near.at[:, pl.ds(width + kv, kv)]),
        fetch(4, wo_ref.at[mine_rows, :], wo_all.at[pl.ds(0, quarter), pl.ds(0, half)]),
        fetch(5, wo_ref.at[other_quarter, :], wo_all.at[pl.ds(2 * quarter, quarter), pl.ds(0, half)]),
    ]
    for each in fetches:
        each.start()

    def wo_copy(k, src, rows_at, side):
        return remote(src, wo_all.at[pl.ds(rows_at, quarter), pl.ds(side, half)], wo_send.at[k], wo_recv.at[k], me.beside)

    wo_copies = [wo_copy(0, wo_ref.at[mine_rows, :], quarter, 0), wo_copy(1, wo_ref.at[other_quarter, :], 3 * quarter, 0)]
    for each in wo_copies:
        each.start()

    qkv = Spread(me, w_far, qkv_send, qkv_recv)
    wide = Spread(me, gate_up_out, wide_send, wide_recv)
    thin = Spread(me, down_out, thin_send, thin_recv)
    wo = Spread(me, wo_far, out_send, out_recv)
    for each in qkv_pieces:
        each.wait()
    for ring in (qkv, wo):
        for s in range(2):
            ring.start(s)
    rings = (wide, thin)
    blocks = packed // b
    slots = 8 + groups * blocks * (blocks + 1) // 2

    def tick(k):
        steps((k * (m - 1)) // slots, ((k + 1) * (m - 1)) // slots, *rings)

    steps(0, (m - 1) // pieces, qkv, wo)
    for each in late_pieces:
        each.wait()
    for ring in rings:
        for s in range(2):
            ring.start(s)
    for k in range(pieces):
        if k:
            steps(k * (m - 1) // pieces, (k + 1) * (m - 1) // pieces, qkv, wo)
        token_copies[k].wait()
        passes[k].start()
        tick(k)
    for each in cots:
        each.start()
    for each in fetches:
        each.wait()

    def prepared(x, gain, cosine, sine):
        normed = x * lax.rsqrt(head_sums(x * x) / HEAD_SIZE + EPSILON) * gain
        return normed * cosine + swapped(normed) * sine

    far_gains = gains_out

    def project_block(k):
        begin = ((col * pieces + 2 * k) % (2 * pieces)) * rows

        def part(k, carry):
            project_rows(at(begin + k * rows, rows))
            return carry

        lax.fori_loop(0, 2, part, 0)

    def project_rows(block):
        x_near = near[block, :].astype(F32)
        x_far = far[block, :].astype(F32)
        total = jnp.sum(x_near * x_near, axis=1, keepdims=True) + jnp.sum(x_far * x_far, axis=1, keepdims=True)
        inverse = lax.rsqrt(total / (2 * half) + EPSILON)
        h_near = (x_near * inverse * gains_ref[0:1, :]).astype(BF16)
        h_far = (x_far * inverse * far_gains[0:1, :]).astype(BF16)
        hid_near[block, :] = h_near
        hid_far[block, :] = h_far
        out = dot(h_near, w_near[...]) + dot(h_far, w_far[...].reshape(half, w_far.shape[2]))
        raw[block, :] = out[:, :width + kv]
        cosine, sine = rope_block(table_ref, block)
        for g in range(groups):
            cut = slice(g * lanes, (g + 1) * lanes)
            part = prepared(out[:, cut], q_gain_ref[...], cosine, sine).astype(BF16)
            q_all[block, cut] = (part * HEAD_SIZE ** (-0.5)).astype(BF16)
        for g in range(groups // 2):
            begin = width + g * lanes
            twice = doubled(prepared(out[:, begin:begin + lanes], k_gain_ref[...], cosine, sine))
            value = doubled(out[:, begin + kv:begin + kv + lanes])
            for h in range(2):
                cut = slice((2 * g + h) * lanes, (2 * g + h + 1) * lanes)
                k_all[block, cut] = twice[h].astype(BF16)
                v_all[block, cut] = value[h].astype(BF16)

    project_block(0)
    tick(4)
    project_block(1)
    tick(5)
    for k in range(pieces):
        passes[k].wait()
        if k % 2 == 1:
            project_block(2 + k // 2)
            tick(6 + k // 2)

    def store(k, src, dst):
        return pltpu.make_async_copy(src, dst, store_sem.at[k])

    stores = [store(k, src, dst) for k, (src, dst) in enumerate((
        (far, far_out), (hid_near, hid_near_out), (hid_far, hid_far_out), (raw, raw_out), (q_all, q_out), (k_all, k_out),
        (v_all, v_out)))]
    for each in stores:
        each.start()

    per_half = blocks // 2

    def low_copy(kind, g, i, target):
        slot = (2, 1, 3)[kind] * width + g * lanes
        return remote(low.at[at(i * b, b), pl.ds(g * lanes, lanes)],
                      attended.at[at((i % per_half) * b, b), pl.ds(slot, lanes)],
                      low_send.at[kind, g, i % per_half], low_recv.at[kind, g, i % per_half], target)

    for g in range(groups):
        cut = slice(g * lanes, (g + 1) * lanes)

        def query_block(i, carry, g=g, cut=cut):
            place = at(i * b, b)
            qs = stacked(q_all[place, cut])
            begins = starts_ref[place, :]
            begins = jnp.concatenate([begins, begins], axis=0)
            acc_ref[...] = jnp.zeros_like(acc_ref)
            mass_ref[...] = jnp.zeros_like(mass_ref)
            base = 8 + g * (blocks * (blocks + 1) // 2) + (i * (i + 1)) // 2

            def key_block(j, diagonal):
                keys = at(j * b, b)
                s = dot(qs, k_all[keys, cut], NT)
                columns = j * b + lax.broadcasted_iota(jnp.int32, (1, b), 1)
                allowed = columns >= begins
                if diagonal:
                    lines = i * b + lax.rem(lax.broadcasted_iota(jnp.int32, (2 * b, 1), 0), b)
                    allowed = allowed & (columns <= lines)
                p = jnp.where(allowed, jnp.exp(s), 0.0)
                mass = p[:, :128]
                for part in range(1, b // 128):
                    mass = mass + p[:, part * 128:(part + 1) * 128]
                mass_ref[...] += mass
                acc_ref[...] += dot(p.astype(BF16), v_all[keys, cut])
                tick(base + j)

            @pl.loop(0, i)
            def _(j):
                key_block(j, False)

            key_block(i, True)
            mass = jnp.sum(mass_ref[...], axis=1, keepdims=True)
            out = acc_ref[...] / mass
            first = lax.broadcasted_iota(jnp.int32, (b, lanes), 1) < HEAD_SIZE
            out = jnp.where(first, out[:b], out[b:])
            heads[place, cut] = out
            low[place, cut] = out.astype(BF16)
            total = jnp.log(jnp.sum(mass_ref[...].T, axis=0, keepdims=True))
            totals_out[g, 0:1, place] = total[:, :b]
            totals_out[g, 1:2, place] = total[:, b:]

            @pl.when(i // per_half == col)
            def _():
                attended[at((i % per_half) * b, b), cut] = out.astype(BF16)
                low_copy(0, g, i, me.across).start()

            @pl.when(i // per_half != col)
            def _():
                low_copy(1, g, i, me.beside).start()
                low_copy(2, g, i, me.opposite).start()
            return carry

        lax.fori_loop(0, blocks, query_block, 0)
    heads_store = store(7, heads, heads_out)
    heads_store.start()
    w_stores = [store(8 + 3 * per_half, w_near, w_near_out), store(9 + 3 * per_half, w_far, w_far_out)]
    for each in w_stores:
        each.start()

    local_far = []
    per = quarter // chunk
    for p, begin in ((0, row), (2, 1 - row)):
        for k in range(per):
            local_far.append(pltpu.make_async_copy(
                wo_far.at[begin * per + k], wo_all.at[pl.ds(p * quarter + k * chunk, chunk), pl.ds(half, half)],
                local_sem.at[6 + len(local_far)]))
    remote_far = []
    for p, begin in ((1, row), (3, 1 - row)):
        for k in range(per):
            remote_far.append(remote(
                wo_far.at[begin * per + k], wo_all.at[pl.ds(p * quarter + k * chunk, chunk), pl.ds(half, half)],
                wo_send.at[2 + len(remote_far)], wo_recv.at[2 + len(remote_far)], me.beside))
    for each in local_far + remote_far:
        each.start()
    for k in range(pieces):
        cots[k].wait()
        cot_passes[k].start()
    for each in local_far + remote_far + wo_copies:
        each.wait()
    w_stores.append(store(10 + 3 * per_half, wo_all.at[pl.ds(0, quarter), :], wo_out))
    w_stores[-1].start()

    gain = jnp.concatenate([gains_ref[1:2, :], far_gains[1:2, :]], axis=1)
    hidden_stores = []
    for k in range(per_half):
        for g in range(groups):
            for kind in range(3):
                low_copy(kind, g, k, me.beside).wait()
        place = at(col * count + k * b, b)

        def merge(fine, k=k):
            part = at(k * b + fine.start, fine.size)
            mine = at(col * count + k * b + fine.start, fine.size)
            tokens = jnp.concatenate([near[mine, :], far[mine, :]], axis=1).astype(F32)
            total = tokens + dot(attended[part, :], wo_all[...])
            middle[part, :] = total
            inverse = lax.rsqrt(jnp.sum(total * total, axis=1, keepdims=True) / (2 * half) + EPSILON)
            hidden[part, :] = (total * inverse * gain).astype(BF16)

        by_rows(b, merge, 128)
        hidden_stores += [
            remote(hidden.at[pl.ds(k * b, b), :], hidden_out.at[place, :], hidden_send.at[k], hidden_recv.at[k], me.beside),
            pltpu.make_async_copy(hidden.at[pl.ds(k * b, b), :], hidden_out.at[place, :], store_sem.at[8 + 3 * k]),
            pltpu.make_async_copy(middle.at[pl.ds(k * b, b), :], middle_out.at[pl.ds(k * b, b), :], store_sem.at[9 + 3 * k]),
            pltpu.make_async_copy(attended.at[pl.ds(k * b, b), :], attended_out.at[pl.ds(k * b, b), :], store_sem.at[10 + 3 * k]),
        ]
        for each in hidden_stores[-4:]:
            each.start()
    for each in stores + [heads_store] + w_stores + hidden_stores + cot_passes:
        each.wait()
    finish(m, qkv, wo, *rings)


def rope_block(table_ref, block):
    half = HEAD_SIZE // 2
    cosine, sine = table_ref[:half, block], table_ref[half:, block]
    return jnp.concatenate([cosine] * 4, axis=0).T, jnp.concatenate([-sine, sine] * 2, axis=0).T


def begin(tokens, cot, wq, wk, wv, gate, up, down, wo, gains, q_gain, k_gain, table, starts, names, n, b=512):
    packed, half = tokens.shape
    b = min(b, packed // 2)
    m = math.gcd(n, 8)
    width, kv, units = wq.shape[1] // 2, wk.shape[1] // 2, gate.shape[1] // 2
    groups = width // (2 * HEAD_SIZE)
    count = packed // 2
    vmem = pl.BlockSpec(memory_space=pltpu.VMEM)
    some = pl.BlockSpec(memory_space=pl.ANY)
    dma = pltpu.SemaphoreType.DMA

    outs = [((packed, half), BF16, some), ((m, half // m, 2 * units), BF16, some), ((m, units // m, half), BF16, some),
            ((packed, half), BF16, some), (gains.shape, F32, vmem), ((packed, half), BF16, some), ((packed, half), BF16, some),
            ((packed, width + kv), F32, some), ((packed, width), BF16, some), ((packed, width), BF16, some),
            ((packed, width), BF16, some), ((packed, width), F32, some), ((groups, 2, packed), F32, vmem),
            ((count, 2 * half), BF16, some), ((count, 2 * half), F32, some), ((packed, 2 * half), BF16, some),
            ((half // 2, 2 * half), BF16, some), ((half, width + 2 * kv), BF16, some), ((m, half // m, width + 2 * kv), BF16, some)]
    scratch = [((packed, half), BF16), ((packed, half), BF16), ((half, width + 2 * kv), BF16), ((m, half // m, width + 2 * kv), BF16),
               ((m, half // m, half), BF16), ((2 * half, 2 * half), BF16), ((packed, half), BF16), ((packed, half), BF16),
               ((packed, width + kv), F32), ((packed, width), BF16), ((packed, width), BF16), ((packed, width), BF16),
               ((packed, width), BF16), ((packed, width), F32), ((count, 2 * half), BF16), ((count, 2 * half), F32),
               ((count, 2 * half), BF16), ((2 * b, 2 * HEAD_SIZE), F32), ((2 * b, 2 * HEAD_SIZE), F32)]
    per_half = count // b
    ring = [dma((2, m - 1))] * 8
    return pl.pallas_call(
        functools.partial(begin_kernel, n, m, names, b),
        out_shape=tuple(jax.ShapeDtypeStruct(shape, dtype) for shape, dtype, _ in outs),
        in_specs=[some] * 9 + [vmem] * 5,
        out_specs=tuple(spec for *_, spec in outs),
        scratch_shapes=[
            *[pltpu.VMEM(shape, dtype) for shape, dtype in scratch],
            dma((6 + m,)), dma((11 + 3 * per_half,)), dma((4,)), dma((4,)), dma((4,)), dma((4,)), dma((10,)), dma((10,)),
            dma((2, 4)), dma((2, 4)), *ring, dma((2 + m,)), dma((2 + m,)),
            dma((3, groups, per_half)), dma((3, groups, per_half)), dma((per_half,)), dma((per_half,)),
        ],
        compiler_params=pltpu.CompilerParams(collective_id=4, has_side_effects=True, vmem_limit_bytes=VMEM_LIMIT),
        cost_estimate=pl.CostEstimate(flops=20 << 30, transcendentals=0, bytes_accessed=100 << 20),
        name="begin",
    )(tokens, cot, wq, wk, wv, gate, up, down, wo, gains, q_gain, k_gain, table, starts)


def turn_kernel(n, names, pieces, hidden_ref, grads_ref, active_ref, cot_near_ref, cot_far_ref, gate_ref, up_ref, gate_up_ref,
                middle_ref, attended_ref, wo_ref, gain_ref, keep_ref, gain_sum_ref, done_ref, down_done_ref, heads_ref, wo_grad_ref,
                hidden, grads, active, cot_near, cot_far, back, middle, wo, near, far, down_near, down_far, branch, other_branch,
                far_slots, near_slots, down_slots, beside_in, across_out, across_in, give_in, load_sem,
                far_send, far_recv, near_send, near_recv, down_send, down_recv,
                cross_send, cross_recv, beside_send, beside_recv, across_send, across_recv, branch_send, branch_recv,
                give_send, give_recv):
    me = Group(names, n)
    half = cot_near_ref.shape[1]
    tokens = middle_ref.shape[0]
    rows = tokens // pieces
    units = active_ref.shape[1]
    row, col = me.row, me.col
    far_ring = Reduce(me, (far,), far_slots, far_send, far_recv)
    near_ring = Reduce(me, (near,), near_slots, near_send, near_recv)
    down = Reduce(me, (down_far, down_near), down_slots, down_send, down_recv)

    def load(k, src, dst):
        return pltpu.make_async_copy(src, dst, load_sem.at[k])

    loads = [load(1, active_ref, active), load(2, cot_near_ref, cot_near), load(3, cot_far_ref, cot_far),
             load(5, grads_ref, grads), load(4, hidden_ref, hidden), load(6, middle_ref, middle), load(7, wo_ref, wo)]
    for each in loads:
        each.start()
    me.arrive([*me.ring, me.across, me.beside])

    for each in loads[:3]:
        each.wait()
    per = units // 3

    def down_tile(k, carry):
        left = active[:, pl.ds(pl.multiple_of(k * per, per), per)]
        for cot, out in ((cot_near, down_near), (cot_far, down_far)):
            part = over_t(left, cot[...]).astype(BF16)
            line = down_near.shape[1]
            if per % line == 0:
                for c in range(per // line):
                    out[k * (per // line) + c] = part[c * line:(c + 1) * line]
            else:
                for c in range(per // 16):
                    at = k * per + c * 16
                    out[at // line, pl.ds(at % line, 16), :] = part[c * 16:(c + 1) * 16]
        return carry

    if units // n % 16 == 0 and per % 16 == 0:
        lax.fori_loop(0, 3, down_tile, 0)
    else:
        for cot, out in ((cot_near, down_near), (cot_far, down_far)):
            part = over_t(active[...], cot[...]).astype(BF16)
            line = down_near.shape[1]
            for c in range(n):
                out[c] = part[c * line:(c + 1) * line]
    down.start()

    columns = pl.ds(pl.multiple_of(row * units, units), units)
    weights = [load(9, gate_ref.at[:, columns], active.at[pl.ds(0, half), :]),
               load(10, up_ref.at[:, columns], active.at[pl.ds(half, half), :]),
               load(11, gate_up_ref.at[:, pl.ds(0, units)], active.at[pl.ds(2 * half, half), :]),
               load(12, gate_up_ref.at[:, pl.ds(units, units)], active.at[pl.ds(3 * half, half), :])]
    for each in weights:
        each.start()
    for each in weights + loads[3:4]:
        each.wait()
    acrosses = [remote(across_out.at[k], across_in.at[k], across_send.at[k], across_recv.at[k], me.across)
                for k in range(pieces)]

    def beside_copy(k):
        return remote(across_out.at[k], beside_in.at[k], beside_send.at[k], beside_recv.at[k], me.beside)

    def back_rows(place, side):
        first, second = 2 * side * half, (2 * side + 1) * half
        return (dot(grads[place, :units], active[first:first + half, :], NT)
                + dot(grads[place, units:], active[second:second + half, :], NT)).astype(BF16)

    pace = Pace(n)
    for k in range(pieces):
        place = pl.ds(pl.multiple_of((1 - col) * tokens + k * rows, rows), rows)
        for side in range(2):
            across_out[k, :, side * half:(side + 1) * half] = back_rows(place, side)
        beside_copy(k).start()
        if k % 2:
            pace(down)
    for k in range(pieces):
        place = pl.ds(pl.multiple_of(col * tokens + k * rows, rows), rows)
        for side in range(2):
            back[k * rows:(k + 1) * rows, side * half:(side + 1) * half] = back_rows(place, side)
        beside_copy(k).wait()

        def add(part, k=k):
            mine = pl.ds(pl.multiple_of(k * rows + part.start, part.size), part.size)
            chip = (back[mine, :].astype(F32) + beside_in[k, part, :].astype(F32)).astype(BF16)
            across_out[k, part, :half] = chip[:, half:]
            across_out[k, part, half:] = chip[:, :half]

        by_rows(rows, add)
        acrosses[k].start()
        if k % 2:
            pace(down)
    loads[4].wait()
    line = near.shape[1]
    tile = 256

    def wide_tiles(out, begin, *rings):
        for k in range(half // tile):
            for side in range(2):
                left = hidden[:, begin + k * tile:begin + (k + 1) * tile]
                part = over_t(left, grads[:, side * units:(side + 1) * units]).astype(BF16)
                for c in range(tile // line):
                    out[k * (tile // line) + c, :, side * units:(side + 1) * units] = part[c * line:(c + 1) * line]
            pace(*rings)

    gain_sum_ref[...] = jnp.zeros_like(gain_sum_ref)

    def branch_copy(k):
        part = pl.ds(k * rows, rows)
        return remote(branch.at[part, :], other_branch.at[part, :], branch_send.at[k], branch_recv.at[k], me.beside)

    def norm_piece(k):
        acrosses[k].wait()

        def end(fine):
            part = pl.ds(pl.multiple_of(k * rows + fine.start, fine.size), fine.size)
            place = pl.ds(pl.multiple_of(col * tokens + k * rows + fine.start, fine.size), fine.size)
            grad = back[part, :].astype(F32) + beside_in[k, fine, :].astype(F32) + across_in[k, fine, :].astype(F32)
            x = middle[part, :]
            inverse = lax.rsqrt(jnp.sum(x * x, axis=1, keepdims=True) / (2 * half) + EPSILON)
            normal = x * inverse
            weighed = grad * normal
            gain_sum_ref[...] += jnp.sum(weighed, axis=0, keepdims=True)
            stat = jnp.sum(weighed * gain_ref[...], axis=1, keepdims=True) / (2 * half)
            change = inverse * (grad * gain_ref[...] - normal * stat)
            keep = cot_near[place, :].astype(F32) + change[:, :half]
            keep_ref[part, :] = keep
            branch[part, :half] = keep.astype(BF16)
            branch[part, half:] = (cot_far[place, :].astype(F32) + change[:, half:]).astype(BF16)

        by_rows(rows, end)
        branch_copy(k).start()

    wide_tiles(far, half, down)
    far_ring.start()
    wide_tiles(near, 0, down, far_ring)
    near_ring.start()
    fetch_attended = load(8, attended_ref, hidden.at[pl.ds(0, tokens), :])
    fetch_attended.start()

    def crosses_of(ring, out, base):
        return [remote(ring.last(s), out.at[s], cross_send.at[base + s], cross_recv.at[base + s], me.across) for s in range(2)]

    loads[5].wait()
    pace(down, far_ring, near_ring)
    pace.rest(down)
    crosses = crosses_of(down, down_done_ref, 2)
    for cross in crosses:
        cross.start()
    for s in (2, 3):
        down_done_ref[s] = down.last(s)[...]
    for k in range(pieces):
        norm_piece(k)
        pace(far_ring, near_ring)
    pace.rest(far_ring)
    crosses += crosses_of(far_ring, done_ref, 0)
    for cross in crosses[2:]:
        cross.start()

    fetch_attended.wait()
    loads[6].wait()
    quarter = half // 2
    gives = []
    for p in (1, 3, 0, 2):
        part = over_t(hidden[:tokens, p * quarter:(p + 1) * quarter], branch[:, :half])
        if p in (1, 3):
            across_out[p // 2, :quarter, :half] = part.astype(BF16)
            gives.append(remote(across_out.at[p // 2, pl.ds(0, quarter), pl.ds(0, half)],
                                give_in.at[p // 2],
                                give_send.at[p // 2], give_recv.at[p // 2], me.beside))
            gives[-1].start()
            pace(near_ring)
        else:
            gives[p // 2].wait()
            place = row if p == 0 else 1 - row
            total = part + give_in[p // 2].astype(F32)
            wo_grad_ref[pl.ds(pl.multiple_of(place * quarter, quarter), quarter), :] = total.astype(BF16)

    def attended_grad(src, core):
        def each(part):
            heads_ref[pl.ds(pl.multiple_of(core * tokens + part.start, part.size), part.size), :] = dot(
                src[part, :], wo[...], NT).astype(BF16)

        by_rows(tokens, each, 256)

    attended_grad(branch, col)
    for k in range(pieces):
        branch_copy(k).wait()
    attended_grad(other_branch, 1 - col)
    pace.rest(near_ring)
    for s in range(2):
        done_ref[2 + s] = near_ring.last(s)[...]
    for cross in crosses:
        cross.wait()
    finish(n, far_ring, near_ring, down)


def turn(hidden, grads, active, cot_near, cot_far, gate, up, gate_up_far, middle, attended, wo, gain, names, n, pieces=4):
    packed, width = hidden.shape
    tokens, half, units = middle.shape[0], width // 2, active.shape[1]
    vmem = pl.BlockSpec(memory_space=pltpu.VMEM)
    some = pl.BlockSpec(memory_space=pl.ANY)
    dma = pltpu.SemaphoreType.DMA
    exchange = ((pieces, tokens // pieces, width), BF16)
    wide, down = (half // n, units), (units // n, half // 2)
    outs = [((tokens, half), F32), ((1, width), F32), ((4, *wide), BF16), ((4, *down), BF16), ((packed, wo.shape[0]), BF16),
            ((half, half), BF16)]
    scratch = [(x.shape, x.dtype) for x in (hidden, grads, active, cot_near, cot_far)]
    scratch += [((tokens, width), BF16), (middle.shape, F32), (wo.shape, BF16), ((n, half // n, 2 * units), BF16),
                ((n, half // n, 2 * units), BF16), ((n, units // n, half), BF16), ((n, units // n, half), BF16),
                ((tokens, width), BF16), ((tokens, width), BF16), ((2, n - 1, *wide), BF16), ((2, n - 1, *wide), BF16),
                ((4, n - 1, *down), BF16),
                exchange, exchange, exchange, ((2, half // 2, half), BF16)]
    return pl.pallas_call(
        functools.partial(turn_kernel, n, names, pieces),
        out_shape=tuple(jax.ShapeDtypeStruct(shape, dtype) for shape, dtype in outs),
        in_specs=[some] * 11 + [vmem],
        out_specs=(vmem,) * len(outs),
        scratch_shapes=[
            *[pltpu.VMEM(shape, dtype) for shape, dtype in scratch], dma((13,)), *[dma((2, n - 1))] * 4, *[dma((4, n - 1))] * 2,
            dma((4,)), dma((4,)),
            *[dma((pieces,))] * 6, dma((2,)), dma((2,)),
        ],
        compiler_params=pltpu.CompilerParams(collective_id=1, has_side_effects=True, vmem_limit_bytes=VMEM_LIMIT),
        cost_estimate=pl.CostEstimate(flops=6 * packed * width * units, transcendentals=tokens, bytes_accessed=150 << 20),
        name="turn",
    )(hidden, grads, active, cot_near, cot_far, gate, up, gate_up_far, middle, attended, wo, gain)


def finale_kernel(n, names, b, q_ref, k_ref, v_ref, grad_ref, heads_ref, totals_ref, start_ref, done_ref, down_done_ref,
                  result_ref, middle_ref, keep_ref, raw_ref, token_ref, far_ref, hid_near_ref, hid_far_ref, w_near_ref, w_far_ref,
                  wo_grad_ref, gain_near_ref, gain_far_ref, q_gain_ref, k_gain_ref, table_ref, ffn_sum_ref,
                  wide_ref, down_ref, output_ref, thin_ref, lone_ref, sums_ref, tokens_grad_ref,
                  q_all, k_all, v_all, grad_all, heads, raw, near, far, hid_near, hid_far, w_near, w_far, middle_near, sums,
                  qs_ref, gs_ref, stat_ref, dqt_ref, dk_acc, dv_acc, dq, dk, dv, grads, to_near, to_far, stat, near_grads, far_grads,
                  slots, lone_slots, result_in, result_out, result_back, beside_in, beside_stat, across_in,
                  stat_out, stat_in, far_total, vector, group_in, ring_in, mine, q_sum, k_sum, near_sum, far_sum,
                  load_sem, keep_sem, wide_send, wide_recv, down_send, down_recv, rs_send, rs_recv, ag_send, ag_recv,
                  lone_send, lone_recv, lone_out_send, lone_out_recv, cross_send, cross_recv, group_send, group_recv,
                  all_send, all_recv, result_send, result_recv, beside_send, beside_recv, across_send, across_recv,
                  last_send, last_recv):
    me = Group(names, n)
    row, col = me.row, me.col
    packed, half = token_ref.shape
    count = packed // 2
    lanes = 2 * HEAD_SIZE
    width = q_ref.shape[1]
    groups = width // lanes
    kv = groups * HEAD_SIZE
    blocks = packed // b
    per_half = blocks // 2
    wide = Spread(me, wide_ref, wide_send, wide_recv)
    down = Spread(me, down_ref, down_send, down_recv)
    lone = Meet(me, (wo_grad_ref,), lone_slots, lone_send, lone_recv)
    lone_out = Fan(me, lone_ref, lone_out_send, lone_out_recv)
    thin = Meet(me, (far_grads, near_grads), slots, rs_send, rs_recv)
    thin_out = Fan(me, thin_ref, ag_send, ag_recv)
    hops = n // 2

    def at(begin, size):
        return pl.ds(pl.multiple_of(begin, size), size)

    own_rows, other_rows = at(col * count, count), at((1 - col) * count, count)

    def load(k, src, dst):
        return pltpu.make_async_copy(src, dst, load_sem.at[k])

    first = [load(k, src, dst) for k, (src, dst) in enumerate((
        (q_ref, q_all), (k_ref, k_all), (v_ref, v_all), (grad_ref, grad_all), (heads_ref, heads)))]
    sides = (pl.ds(half, half), pl.ds(0, half))
    second = [load(5 + k, src, dst) for k, (src, dst) in enumerate((
        (result_ref.at[own_rows, sides[0]], sums.at[0]), (result_ref.at[own_rows, sides[1]], sums.at[1]),
        (middle_ref.at[:, pl.ds(0, half)], middle_near)))]
    third = [load(8 + k, src, dst) for k, (src, dst) in enumerate((
        (raw_ref, raw), (token_ref, near), (far_ref, far), (w_near_ref, w_near), (w_far_ref, w_far), (hid_near_ref, hid_near),
        (hid_far_ref, hid_far)))]
    keep, across_out = middle_near, sums.at[0]
    for each in first + second + third:
        each.start()

    me.arrive([*me.along, me.across, me.beside, me.opposite])
    for ring, src in ((wide, done_ref), (down, down_done_ref)):
        for s in range(4):
            ring.start(s, src.at[s])
    lone.start()
    keeps = [pltpu.make_async_copy(src.at[s], ring.piece(s, me.own(s % 2)), keep_sem.at[4 * k + s])
             for k, (ring, src) in enumerate(((wide, done_ref), (down, down_done_ref))) for s in range(4)]
    for each in keeps:
        each.start()
    results = [remote(result_ref.at[other_rows, side], result_in.at[k], result_send.at[k], result_recv.at[k], me.beside)
               for k, side in enumerate(sides)]
    for each in results:
        each.start()
    result_across = remote(result_out, result_back, result_send.at[2], result_recv.at[2], me.across)
    output_last = remote(result_out, output_ref.at[own_rows, :], last_send.at[0], last_recv.at[0], me.beside)
    output_here = pltpu.make_async_copy(result_out, output_ref.at[own_rows, :], keep_sem.at[8])
    for each in first:
        each.wait()

    every = groups * blocks * (blocks + 1) // 2
    slot_count = every + blocks

    early = max(n - 3, 0)

    def tick(k):
        steps((k * early) // slot_count, ((k + 1) * early) // slot_count, wide, down)
        steps((k * hops) // slot_count, ((k + 1) * hops) // slot_count, lone)

    def group_pass(g, carry):
        cut = at(g * lanes, lanes)
        dqt_ref[...] = jnp.zeros_like(dqt_ref)
        for i in range(blocks):
            rows = slice(i * b, (i + 1) * b)
            both = slice(i * 2 * b, (i + 1) * 2 * b)
            qs_ref[both, :] = stacked(q_all[rows, cut])
            grad = grad_all[rows, cut]
            gs_ref[both, :] = stacked(grad)
            prod = (grad.astype(F32) * heads[rows, cut]).T
            stat_ref[i, 0:1, 0:b] = totals_ref[g, 0:1, rows]
            stat_ref[i, 0:1, b:2 * b] = totals_ref[g, 1:2, rows]
            stat_ref[i, 1:2, 0:b] = jnp.sum(prod[:HEAD_SIZE], axis=0, keepdims=True)
            stat_ref[i, 1:2, b:2 * b] = jnp.sum(prod[HEAD_SIZE:], axis=0, keepdims=True)

        def key_pass(j, carry):
            place = at(j * b, b)
            k = k_all[place, cut]
            v = v_all[place, cut]
            kt = k.T[:HEAD_SIZE]
            dk_acc[...] = jnp.zeros_like(dk_acc)
            dv_acc[...] = jnp.zeros_like(dv_acc)
            keys = j * b + lax.broadcasted_iota(jnp.int32, (b, 1), 0)
            before = g * (every // groups) + j * blocks - (j * (j - 1)) // 2

            def step(i, diagonal):
                both = at(i * 2 * b, 2 * b)
                qs = qs_ref[both, :]
                gs = gs_ref[both, :]
                st = dot(k, qs, NT)
                pt = jnp.exp(st - stat_ref[i, 0:1, :])
                begin = start_ref[0:1, at(i * b, b)]
                allowed = keys >= jnp.concatenate([begin, begin], axis=1)
                if diagonal:
                    columns = i * b + lax.rem(lax.broadcasted_iota(jnp.int32, (1, 2 * b), 1), b)
                    allowed = allowed & (keys <= columns)
                pt = jnp.where(allowed, pt, 0.0)
                dv_acc[...] += dot(pt.astype(BF16), gs)
                dpt = dot(v, gs, NT)
                dst = (pt * (dpt - stat_ref[i, 1:2, :])).astype(BF16)
                dk_acc[...] += dot(dst, qs)
                part = dot(kt, dst)
                to = at(i * b, b)
                dqt_ref[:HEAD_SIZE, to] += part[:, :b]
                dqt_ref[HEAD_SIZE:, to] += part[:, b:]
                tick(before + i - j)

            step(j, True)

            @pl.loop(j + 1, blocks)
            def _(i):
                step(i, False)

            pair = at((g // 2) * lanes, lanes)
            keep_first = (lax.broadcasted_iota(jnp.int32, (b, lanes), 1) < HEAD_SIZE) & (g % 2 == 1)
            for acc, out in ((dk_acc, dk), (dv_acc, dv)):
                out[place, pair] = jnp.where(keep_first, out[place, pair], acc[...] + pltpu.roll(acc[...], HEAD_SIZE, 1))
            dq[place, cut] = dqt_ref[:, place].T * HEAD_SIZE ** (-0.5)

            @pl.when((g == 0) & (j == 0))
            def _():
                for each in results + second:
                    each.wait()

                def add(part):
                    result_out[part, :] = (sums[0, part, :].astype(F32) + result_in[0, part, :].astype(F32)).astype(BF16)

                by_rows(count, add)
                result_across.start()

            @pl.when((g == groups - 1) & (j == 0))
            def _():
                result_across.wait()

                def add(part):
                    total = sums[1, part, :].astype(F32) + result_in[1, part, :].astype(F32) + result_back[part, :].astype(F32)
                    result_out[part, :] = (middle_near[part, :] + total).astype(BF16)

                by_rows(count, add)
                output_last.start()
                output_here.start()
            return carry

        lax.fori_loop(0, blocks, key_pass, 0)
        return carry

    lax.fori_loop(0, groups, group_pass, 0)

    keep_load = load(15, keep_ref, keep)
    keep_load.start()
    for each in third:
        each.wait()
    for ref in (q_sum, k_sum, near_sum, far_sum):
        ref[...] = jnp.zeros_like(ref)

    def beside_copy(h, k):
        part = pl.ds(h * b, b)
        src = (to_far, stat, to_near)[k].at[at((1 - col) * count + h * b, b), :]
        dst = beside_stat.at[part, :] if k == 1 else beside_in.at[k // 2, part, :]
        return remote(src, dst, beside_send.at[h, k], beside_recv.at[h, k], me.beside)

    def across_copy(h, k):
        part = pl.ds(h * b, b)
        src, dst = ((across_out, across_in), (stat_out, stat_in))[k]
        return remote(src.at[part, :], dst.at[part, :], across_send.at[h, k], across_recv.at[h, k], me.across)

    fine = min(b, 256)

    def project_block(p):
        begin = (((1 - col) * per_half + p) % blocks) * b

        def part(k, carry):
            project_rows(at(begin + k * fine, fine))
            return carry

        lax.fori_loop(0, b // fine, part, 0)

    def project_rows(block):
        cosine, sine = rope_block(table_ref, block)
        head = lax.broadcasted_iota(jnp.int32, (fine, lanes), 1) < HEAD_SIZE

        def back(grad, x, gain):
            inverse = lax.rsqrt(head_sums(x * x) / HEAD_SIZE + EPSILON)
            normed = x * inverse
            turned = grad * cosine - swapped(grad) * sine
            inner = turned * gain
            part = inverse * (inner - normed * (head_sums(inner * normed) / HEAD_SIZE))
            return part, jnp.sum(turned * normed, axis=0, keepdims=True)

        for g in range(groups):
            cut = slice(g * lanes, (g + 1) * lanes)
            part, total = back(dq[block, cut], raw[block, cut], q_gain_ref[...])
            q_sum[...] += total
            grads[block, cut] = part.astype(BF16)
        for g in range(groups // 2):
            pair = slice(g * lanes, (g + 1) * lanes)
            cut = slice(width + g * lanes, width + (g + 1) * lanes)
            part, total = back(dk[block, pair], raw[block, cut], k_gain_ref[...])
            k_sum[...] += total
            grads[block, cut] = part.astype(BF16)
            cut = slice(width + kv + g * lanes, width + kv + (g + 1) * lanes)
            grads[block, cut] = dv[block, pair].astype(BF16)
        grad_near = dot(grads[block, :], w_near[...], NT)
        grad_far = dot(grads[block, :], w_far[...], NT)
        to_near[block, :] = grad_near.astype(BF16)
        to_far[block, :] = grad_far.astype(BF16)
        x_near = near[block, :].astype(F32)
        x_far = far[block, :].astype(F32)
        total = jnp.sum(x_near * x_near, axis=1, keepdims=True) + jnp.sum(x_far * x_far, axis=1, keepdims=True)
        inverse = lax.rsqrt(total / (2 * half) + EPSILON)
        x_near = grad_near * (x_near * inverse)
        x_far = grad_far * (x_far * inverse)
        near_sum[...] += jnp.sum(x_near, axis=0, keepdims=True)
        far_sum[...] += jnp.sum(x_far, axis=0, keepdims=True)
        total = (jnp.sum(x_near * gain_near_ref[...], axis=1, keepdims=True)
                 + jnp.sum(x_far * gain_far_ref[...], axis=1, keepdims=True))
        stat[block, :] = jnp.where(head, total, inverse)

    for p in range(blocks):
        project_block(p)
        h = p % per_half
        part = slice(h * b, (h + 1) * b)
        if p < per_half:
            for k in range(3):
                beside_copy(h, k).start()
        else:
            own = at(col * count + h * b, b)
            beside_copy(h, 0).wait()

            def add(fine, h=h):
                place = at(col * count + h * b + fine.start, fine.size)
                fine = at(h * b + fine.start, fine.size)
                across_out[fine, :] = (to_far[place, :].astype(F32) + beside_in[0, fine, :].astype(F32)).astype(BF16)

            by_rows(b, add)
            across_copy(h, 0).start()
            beside_copy(h, 1).wait()
            stat_out[part, :] = stat[own, :] + beside_stat[part, :]
            across_copy(h, 1).start()
        tick(every + p)

    line = half // n
    for hid, out in ((hid_far, far_grads), (hid_near, near_grads)):
        for k in range(2):
            part = over_t(hid[:, k * (half // 2):(k + 1) * (half // 2)], grads[...]).astype(BF16)
            for c in range(n // 2):
                out[k * (n // 2) + c] = part[c * line:(c + 1) * line]
    thin.start()
    lone_out.piece(0, me.place)[...] = lone.total(0)
    lone_out.start(0)

    vector[...] = jnp.zeros_like(vector)
    rows = half // 128
    for c in range(rows):
        cut = slice(c * 128, (c + 1) * 128)
        vector[pl.ds(row * rows + c, 1), :] = near_sum[:, cut]
        vector[pl.ds((1 - row) * rows + c, 1), :] = far_sum[:, cut]
        vector[pl.ds((2 + row) * rows + c, 1), :] = 0.5 * ffn_sum_ref[:, c * 128:(c + 1) * 128]
        vector[pl.ds((3 - row) * rows + c, 1), :] = 0.5 * ffn_sum_ref[:, half + c * 128:half + (c + 1) * 128]
    vector[4 * rows:4 * rows + 1, :] = q_sum[...]
    vector[4 * rows + 1:4 * rows + 2, :] = k_sum[...]
    gathers = [remote(vector, group_in.at[k], group_send.at[k], group_recv.at[k], target)
               for k, target in enumerate((me.across, me.beside, me.opposite))]
    for gather in gathers:
        gather.start()
    steps(0, hops // 2, thin, lone_out)
    steps(early, early + (n - 1 - early) // 2, wide, down)
    for gather in gathers:
        gather.wait()
    mine[...] = vector[...] + group_in[0] + group_in[1] + group_in[2]
    spreads = [remote(mine, ring_in.at[k], all_send.at[k], all_recv.at[k], target) for k, target in enumerate(me.along)]
    for spread in spreads:
        spread.start()
    steps(hops // 2, hops, thin, lone_out)

    far_total[...] = thin.total(0)
    cross = remote(far_total, thin_out.piece(0, me.place, row), cross_send, cross_recv, me.across)
    cross.start()
    thin_out.piece(1, me.place)[...] = thin.total(1)
    thin_out.start(1)
    cross.wait()
    thin_out.start(0)

    tails = []
    keep_load.wait()
    for h in range(per_half):
        part = slice(h * b, (h + 1) * b)
        own = at(col * count + h * b, b)
        beside_copy(h, 2).wait()
        for k in range(2):
            across_copy(h, k).wait()

        def end(fine, h=h):
            own = at(col * count + h * b + fine.start, fine.size)
            part = at(h * b + fine.start, fine.size)
            grad = to_near[own, :].astype(F32) + beside_in[1, part, :].astype(F32) + across_in[part, :].astype(F32)
            inverse = stat[own, HEAD_SIZE:HEAD_SIZE + 1]
            share = (stat_out[part, :1] + stat_in[part, :1]) / (2 * half)
            normal = near[own, :].astype(F32) * inverse
            across_out[part, :] = (inverse * (grad * gain_near_ref[...] - normal * share) + keep[part, :]).astype(BF16)

        by_rows(b, end)
        src = across_out.at[pl.ds(h * b, b), :]
        tails += [remote(src, tokens_grad_ref.at[own, :], last_send.at[1 + h], last_recv.at[1 + h], me.beside),
                  pltpu.make_async_copy(src, tokens_grad_ref.at[own, :], keep_sem.at[9 + h])]
        for each in tails[-2:]:
            each.start()
    steps(0, hops // 2, thin_out)
    steps(early + (n - 1 - early) // 2, n - 1, wide, down)
    steps(hops // 2, hops, thin_out)

    total = mine[...]
    for spread in spreads:
        spread.wait()
    for k in range(n - 1):
        total = total + ring_in[k]
    sums_ref[...] = total
    for each in tails + keeps + [output_here, output_last]:
        each.wait()
    finish(n, wide, down)
    finish(hops + 1, lone, lone_out, thin, thin_out)


def finale(q, k, v, grad, heads, totals, starts, done, down_done, result, middle, keep, raw, tokens, far, hid_near, hid_far,
           w_near, w_far, wo_grad, gain_near, gain_far, q_gain, k_gain, table, ffn_sum, names, n, b=512):
    packed, width = q.shape
    half = tokens.shape[1]
    b = min(b, packed // 2)
    count, blocks, lanes = packed // 2, packed // b, 2 * HEAD_SIZE
    per_half = blocks // 2
    line, columns = half // n, w_near.shape[1]
    vmem = pl.BlockSpec(memory_space=pltpu.VMEM)
    some = pl.BlockSpec(memory_space=pl.ANY)
    dma = pltpu.SemaphoreType.DMA
    rows = -(-(4 * (half // 128) + 2) // 8) * 8

    def full(x):
        return ((2, n, x.shape[1], 2 * x.shape[2]), BF16, some)

    outs = [full(done), full(down_done), ((packed, half), BF16, some), ((2, n, line, columns), BF16, vmem),
            ((n, line, half), BF16, vmem), ((rows, 128), F32, vmem), ((packed, half), BF16, some)]
    tall, short = ((packed, half), BF16), ((count, half), BF16)
    stats = ((count, lanes), F32)
    scratch = [*[((packed, width), BF16)] * 4, (heads.shape, F32), (raw.shape, F32), tall, tall, tall, tall,
               (w_near.shape, BF16), (w_far.shape, BF16), ((count, half), F32), ((2, count, half), BF16),
               ((2 * packed, lanes), BF16), ((2 * packed, lanes), BF16), ((blocks, 2, 2 * b), F32), ((lanes, packed), F32),
               ((b, lanes), F32), ((b, lanes), F32), ((packed, width), F32), ((packed, width // 2), F32), ((packed, width // 2), F32), ((packed, columns), BF16), tall, tall,
               ((packed, lanes), F32), ((n, line, columns), BF16), ((n, line, columns), BF16),
               ((4, n // 2, line, columns), BF16), ((2, n // 2, line, half), BF16),
               ((2, count, half), BF16), short, short, ((2, count, half), BF16), stats, short, stats, stats,
               ((line, columns), BF16), ((rows, 128), F32), ((3, rows, 128), F32), ((n - 1, rows, 128), F32), ((rows, 128), F32),
               ((1, lanes), F32), ((1, lanes), F32), ((1, half), F32), ((1, half), F32)]
    ring = [dma((4, n - 1))] * 4 + [dma((4, n // 2))] * 4 + [dma((2, n // 2))] * 4
    pairs = packed * (packed + b) // 2
    return pl.pallas_call(
        functools.partial(finale_kernel, n, names, b),
        out_shape=tuple(jax.ShapeDtypeStruct(shape, dtype) for shape, dtype, _ in outs),
        in_specs=[some] * 5 + [vmem] * 2 + [some] * 12 + [vmem] * 7,
        out_specs=tuple(spec for *_, spec in outs),
        scratch_shapes=[
            *[pltpu.VMEM(shape, dtype) for shape, dtype in scratch], dma((16,)), dma((9 + per_half,)), *ring,
            dma, dma, dma((3,)), dma((3,)), dma((n - 1,)), dma((n - 1,)), dma((3,)), dma((3,)),
            dma((per_half, 3)), dma((per_half, 3)), dma((per_half, 2)), dma((per_half, 2)), dma((1 + per_half,)), dma((1 + per_half,)),
        ],
        compiler_params=pltpu.CompilerParams(collective_id=3, has_side_effects=True, vmem_limit_bytes=VMEM_LIMIT),
        cost_estimate=pl.CostEstimate(flops=20 * 2 * pairs * 256, transcendentals=4 * pairs, bytes_accessed=100 << 20),
        name="finale",
    )(q, k, v, grad, heads, totals, starts[None, :], done, down_done, result, middle, keep, raw, tokens, far, hid_near, hid_far,
      w_near, w_far, wo_grad, gain_near, gain_far, q_gain, k_gain, table, ffn_sum)


def widen_kernel(widths, units, wide_ref, down_ref, thin_ref, lone_ref, gate_out, up_out, down_out, q_out, k_out, v_out, lone_out):
    for part in range(2):
        for out, begin in ((gate_out, 0), (up_out, units)):
            out[:, part * units:(part + 1) * units] = wide_ref[part, :, begin:begin + units].astype(F32)
        begin = 0
        for out, columns in zip((q_out, k_out, v_out), widths):
            out[:, part * columns:(part + 1) * columns] = thin_ref[part, :, begin:begin + columns].astype(F32)
            begin += columns
    down_out[...] = down_ref[...].astype(F32)
    lone_out[...] = lone_ref[...].astype(F32)


def widen(wide, down, thin, lone, widths, parts=8):
    half = lone.shape[0]
    units = wide.shape[2] // 2
    rows, down_rows = half // parts, down.shape[0] // parts

    def one(rows, columns):
        return pl.BlockSpec((rows, columns), lambda i: (i, 0))

    def two(columns):
        return pl.BlockSpec((2, rows, columns), lambda i: (0, i, 0))

    shapes = [(half, 2 * units)] * 2 + [down.shape] + [(half, 2 * columns) for columns in widths] + [lone.shape]
    return pl.pallas_call(
        functools.partial(widen_kernel, widths, units),
        out_shape=tuple(jax.ShapeDtypeStruct(shape, F32) for shape in shapes),
        grid=(parts,),
        in_specs=[two(2 * units), one(down_rows, down.shape[1]), two(thin.shape[2]), one(rows, lone.shape[1])],
        out_specs=tuple(one(down_rows if k == 2 else rows, shape[1]) for k, shape in enumerate(shapes)),
        compiler_params=pltpu.CompilerParams(vmem_limit_bytes=VMEM_LIMIT),
        cost_estimate=pl.CostEstimate(flops=0, transcendentals=0, bytes_accessed=6 * (wide.size + down.size + thin.size + lone.size)),
        name="widen",
    )(wide, down, thin, lone)


def shards(
    tokens,
    seq_lengths,
    query_weight,
    key_matrix,
    value_matrix,
    out_weight,
    gate_weight,
    up_weight,
    down_weight,
    attn_gain,
    ffn_gain,
    query_gain,
    key_gain,
    cotangent,
):
    packed, half = tokens.shape
    row, col, group = lax.axis_index("row"), lax.axis_index("col"), lax.axis_index("dp")
    parts = lax.axis_size("dp")
    width = 2 * half

    names = ("dp", "row", "col")
    starts = layout(seq_lengths[0], packed)
    table = rope_table(jnp.arange(packed, dtype=jnp.int32) - starts)
    q_gain = jnp.tile(query_gain, 2)[None, :]
    k_gain = jnp.tile(key_gain, 2)[None, :]
    gains = jnp.stack([attn_gain, ffn_gain])
    (far, gate_up_far, down_far, cot_far, gains_far, hid_near, hid_far, raw, q, k, v, attended_raw, totals, attended, middle,
     hidden, out_own, qkv, qkv_far) = begin(
        tokens, cotangent, query_weight, key_matrix, value_matrix, gate_weight, up_weight, down_weight, out_weight, gains,
        q_gain, k_gain, table, starts[:, None], names, parts)
    gain_two = jnp.concatenate([ffn_gain, gains_far[1]])[None, :]
    units = down_weight.shape[0] // 2
    gate_up_far = gate_up_far.reshape(half, -1)
    active, feed_grads, result = feed(
        row[None], hidden, cotangent, cot_far, gate_weight, up_weight, gate_up_far, down_weight,
        down_far.reshape(units, half))

    keep, ffn_sum, done, down_done, grad_attended, grad_out = turn(
        hidden, feed_grads, active, cotangent, cot_far, gate_weight, up_weight, gate_up_far, middle, attended, out_own, gain_two,
        names, parts)
    grad_out = grad_out.reshape(parts, half // parts, -1)

    wide_full, down_full, output, thin_full, out_full, sums, grad_tokens = finale(
        q, k, v, grad_attended, attended_raw, totals, starts, done, down_done, result, middle, keep, raw, tokens, far,
        hid_near, hid_far, qkv, qkv_far.reshape(half, -1), grad_out, attn_gain[None, :], gains_far[:1], q_gain, k_gain, table,
        ffn_sum, names, parts)
    sums = sums.reshape(-1)

    def folded(x):
        return x[:HEAD_SIZE] + x[HEAD_SIZE:]

    widths = (query_weight.shape[1] // 2, key_matrix.shape[1] // 2, value_matrix.shape[1] // 2)
    gate_sum, up_sum, down_sum, q_weight_sum, k_weight_sum, v_weight_sum, out_sum = widen(
        wide_full.reshape(2, half, -1), down_full.reshape(2 * units, half), thin_full.reshape(2, half, -1),
        out_full.reshape(half, -1), widths)
    return (
        output,
        grad_tokens,
        q_weight_sum,
        k_weight_sum,
        v_weight_sum,
        out_sum,
        gate_sum,
        up_sum,
        down_sum,
        part_of(sums[:width], row, 0),
        part_of(sums[width:2 * width], row, 0),
        folded(sums[2 * width:2 * width + 2 * HEAD_SIZE]),
        folded(sums[2 * width + 2 * HEAD_SIZE:2 * width + 4 * HEAD_SIZE]),
    )


def solution(mesh):
    return jax.shard_map(
        shards,
        mesh=mesh,
        in_specs=(
            P("dp", "row"),
            P("dp", None),
            P("row", "col"),
            P("row", "col"),
            P("row", "col"),
            P("col", "row"),
            P("row", "col"),
            P("row", "col"),
            P("col", "row"),
            P("row"),
            P("row"),
            P(),
            P(),
            P("dp", "row"),
        ),
        out_specs=(
            P("dp", "row"),
            P("dp", "row"),
            P("row", "col"),
            P("row", "col"),
            P("row", "col"),
            P("col", "row"),
            P("row", "col"),
            P("row", "col"),
            P("col", "row"),
            P("row"),
            P("row"),
            P(),
            P(),
        ),
        check_vma=False,
    )
```

```python
import functools
import math

import jax
import jax.numpy as jnp
from jax import lax
from jax.experimental import pallas as pl
from jax.experimental.pallas import tpu as pltpu
from jax.sharding import PartitionSpec as P

HEAD_SIZE = 64
EPSILON = 1e-05
ROPE_BASE = 1000000.0
F32, BF16 = jnp.float32, jnp.bfloat16
MESH = pl.DeviceIdType.MESH


def dot(a, b, dims=(((1,), (0,)), ((), ()))):
    return lax.dot_general(a, b, dims, preferred_element_type=F32)


NT = (((1,), (1,)), ((), ()))

def stacked(x):
    first = lax.broadcasted_iota(jnp.int32, x.shape, 1) < 64
    zero = jnp.zeros_like(x)
    return jnp.concatenate([jnp.where(first, x, zero), jnp.where(first, zero, x)], axis=0)


def head_sums(x):
    first = lax.broadcasted_iota(jnp.int32, x.shape, 1) < HEAD_SIZE
    one = jnp.sum(jnp.where(first, x, 0.0), axis=1, keepdims=True)
    two = jnp.sum(jnp.where(first, 0.0, x), axis=1, keepdims=True)
    return jnp.where(first, one, two)


def two_heads(ref):
    return jnp.concatenate([ref[...], ref[...]], axis=1)


def swapped(x):
    low = lax.rem(lax.broadcasted_iota(jnp.int32, x.shape, 1), HEAD_SIZE) < HEAD_SIZE // 2
    return jnp.where(low, pltpu.roll(x, 96, 1), pltpu.roll(x, 32, 1))


def doubled(x):
    first = lax.broadcasted_iota(jnp.int32, x.shape, 1) < HEAD_SIZE
    other = pltpu.roll(x, HEAD_SIZE, 1)
    return jnp.where(first, x, other), jnp.where(first, other, x)


def layout(lengths, packed):
    count = lengths.shape[0]
    numbers = jnp.arange(count, dtype=jnp.int32)
    ends = jnp.sum(jnp.where(numbers[None, :] <= numbers[:, None], lengths[None, :], 0), axis=1)
    begins = ends - lengths
    places = jnp.arange(packed, dtype=jnp.int32)
    member = jnp.sum((places[:, None] >= ends[None, :]).astype(jnp.int32), axis=1)
    return jnp.sum(jnp.where(member[:, None] == numbers[None, :], begins[None, :], 0), axis=1)


def rope_table(position):
    half = HEAD_SIZE // 2
    inverse = jnp.exp(jnp.arange(half, dtype=F32) * (-2.0 * math.log(ROPE_BASE) / HEAD_SIZE))
    angles = position.astype(F32)[None, :] * inverse[:, None]
    return jnp.concatenate([jnp.cos(angles), jnp.sin(angles)], axis=0)


def swap(x, axis):
    return jax.tree.map(lambda part: lax.ppermute(part, axis, [(0, 1), (1, 0)]), x)


def ordered(own, other, index, axis=0):
    return jnp.where(index == 0, jnp.concatenate([own, other], axis), jnp.concatenate([other, own], axis))


def part_of(x, index, axis, parts=2):
    size = x.shape[axis] // parts
    return lax.dynamic_slice_in_dim(x, index * size, size, axis)


def over_t(left, right):
    return dot(left, right, (((0,), (0,)), ((), ())))


VMEM_LIMIT = 62 << 20


def feed_kernel(units, row_ref, hidden_ref, cot_near_ref, cot_far_ref, gate_ref, up_ref, far_ref, down_near_ref, down_far_ref,
                active_ref, grads_ref, result_ref):
    half = cot_near_ref.shape[1]
    near, far = hidden_ref[:, :half], hidden_ref[:, half:]
    gate = dot(near, gate_ref[...]) + dot(far, far_ref[:, :units])
    upward = dot(near, up_ref[...]) + dot(far, far_ref[:, units:])
    grad_active = dot(cot_near_ref[...], down_near_ref[...], NT) + dot(cot_far_ref[...], down_far_ref[...], NT)
    sig = 1.0 / (1.0 + jnp.exp(-gate))
    lifted = gate * sig
    active = (lifted * upward).astype(BF16)
    grad_gate = (grad_active * upward * (sig * (1.0 + gate * (1.0 - sig)))).astype(BF16)
    grad_up = (grad_active * lifted).astype(BF16)
    active_ref[...] = active
    grads_ref[:, :units] = grad_gate
    grads_ref[:, units:] = grad_up
    result_ref[:, :half] = dot(active, down_near_ref[...]).astype(BF16)
    result_ref[:, half:] = dot(active, down_far_ref[...]).astype(BF16)


def feed(row, hidden, cot_near, cot_far, gate, up, far, down, down_far, rows=256):
    packed, width = hidden.shape
    units, half = down_far.shape
    rows = min(rows, packed)

    def tile(n):
        return pl.BlockSpec((rows, n), lambda i, row: (i, 0))

    def once(shape, place):
        return pl.BlockSpec(shape, place, pipeline_mode=pl.Buffered(1))

    def out(n):
        return jax.ShapeDtypeStruct((packed, n), BF16)

    columns = once((half, units), lambda i, row: (0, row[0]))
    return pl.pallas_call(
        functools.partial(feed_kernel, units),
        out_shape=(out(units), out(2 * units), out(width)),
        grid_spec=pltpu.PrefetchScalarGridSpec(
            num_scalar_prefetch=1, grid=(packed // rows,),
            in_specs=[tile(width), tile(half), tile(half), columns, columns, once(far.shape, lambda i, row: (0, 0)),
                      once((units, half), lambda i, row: (row[0], 0)), once(down_far.shape, lambda i, row: (0, 0))],
            out_specs=(tile(units), tile(2 * units), tile(width)),
        ),
        compiler_params=pltpu.CompilerParams(vmem_limit_bytes=VMEM_LIMIT),
        cost_estimate=pl.CostEstimate(flops=8 * packed * width * units, transcendentals=packed * units,
                                      bytes_accessed=packed * (8 * width + 6 * units) + 6 * width * units),
        name="feed",
    )(row, hidden, cot_near, cot_far, gate, up, far, down, down_far)


class Group:
    def __init__(self, names, total, n=None):
        n = total if n is None else n
        self.n = n
        self.dp, self.row, self.col = (lax.axis_index(name) for name in names)
        self.base, member = (self.dp // n) * n, self.dp % n
        side = member % 2
        self.place = (member // 2) * (1 - side) + (n - 1 - member // 2) * side
        self.across = (self.dp, 1 - self.row, self.col)
        self.beside = (self.dp, self.row, 1 - self.col)
        self.opposite = (self.dp, 1 - self.row, 1 - self.col)
        self.along = [((self.dp + k) % total, self.row, self.col) for k in range(1, total)]
        self.ring = [(self.at(self.place + 1), self.row, self.col), (self.at(self.place - 1), self.row, self.col)]

    def at(self, position):
        position = (position + 2 * self.n) % self.n
        back = position // (self.n // 2)
        return self.base + (position * (1 - back) + (self.n - 1 - position) * back) * 2 + back

    def arrive(self, targets):
        barrier = pltpu.get_barrier_semaphore()
        for target in targets:
            pl.semaphore_signal(barrier, inc=1, device_id=target, device_id_type=MESH)
        pl.semaphore_wait(barrier, len(targets))

    def reduced(self, way, t):
        return (self.place - t - 1 + 2 * self.n) % self.n if way == 0 else (self.place + t + 1) % self.n

    def spread(self, way, t):
        return (self.place - t + 2 * self.n) % self.n if way == 0 else (self.place + t) % self.n

    def own(self, way):
        return (self.place + 1) % self.n if way == 0 else (self.place + self.n - 1) % self.n


def remote(src, dst, send, recv, target):
    return pltpu.make_async_remote_copy(
        src_ref=src, dst_ref=dst, send_sem=send, recv_sem=recv, device_id=target, device_id_type=MESH)


class Reduce:
    def __init__(self, me, parts, slots, send, recv):
        self.me, self.parts, self.slots, self.send, self.recv = me, parts, slots, send, recv
        self.columns = parts[0].shape[2] // 2
        rows = parts[0].shape[1]
        first = (rows // 2 + 15) // 16 * 16
        self.cuts = [pl.ds(0, first), pl.ds(first, rows - first)] if rows % 16 == 0 and first < rows else [pl.ds(0, rows)]

    def each(self):
        return [(s, h) for h in range(len(self.cuts)) for s in range(2 * len(self.parts))]

    def local(self, s, h, chunk):
        return self.parts[s // 2].at[chunk, self.cuts[h], pl.ds((s % 2) * self.columns, self.columns)]

    def slot(self, s, h, t):
        return self.slots.at[s, t, self.cuts[h], :]

    def copy(self, s, h, t, src):
        return remote(src, self.slot(s, h, t), self.send.at[s, t, h], self.recv.at[s, t, h], self.me.ring[s % 2])

    def start(self):
        for s, h in self.each():
            self.copy(s, h, 0, self.local(s, h, self.me.place)).start()

    def step(self, t):
        for s, h in self.each():
            slot = self.slot(s, h, t)
            self.copy(s, h, t, slot).wait_recv()
            slot[...] = (slot[...].astype(F32) + self.local(s, h, self.me.reduced(s % 2, t))[...].astype(F32)).astype(BF16)

            @pl.when(t < self.me.n - 2)
            def _(s=s, h=h, slot=slot):
                self.copy(s, h, t + 1, slot).start()

    def last(self, s):
        return self.slots.at[s, self.me.n - 2]

    def finish(self, t):
        for s, h in self.each():
            self.copy(s, h, t, self.slot(s, h, t)).wait_send()


class Spread:
    def __init__(self, me, full, send, recv):
        self.me, self.full, self.send, self.recv = me, full, send, recv
        self.lone = len(full.shape) == 3
        self.columns = full.shape[-1] // 2
        self.streams = (0, 1) if self.lone else (2, 3, 0, 1)

    def piece(self, s, chunk, quarter=None):
        lanes = pl.ds((s % 2) * self.columns, self.columns)
        if self.lone:
            return self.full.at[chunk, :, lanes]
        if quarter is None:
            quarter = 1 - self.me.row if s < 2 else self.me.row
        return self.full.at[quarter, chunk, :, lanes]

    def copy(self, s, t, chunk, src=None):
        piece = self.piece(s, chunk)
        return remote(piece if src is None else src, piece, self.send.at[s, t], self.recv.at[s, t], self.me.ring[s % 2])

    def start(self, s, src=None):
        self.copy(s, 0, self.me.own(s % 2), src).start()

    def step(self, t):
        for s in self.streams:
            chunk = self.me.spread(s % 2, t)
            self.copy(s, t, chunk).wait_recv()

            @pl.when(t < self.me.n - 2)
            def _():
                self.copy(s, t + 1, chunk).start()

    def finish(self, t):
        for s in self.streams:
            self.copy(s, t, 0).wait_send()


class Meet:
    def __init__(self, me, parts, slots, send, recv):
        self.me, self.parts, self.slots, self.send, self.recv = me, parts, slots, send, recv
        self.hops = ((me.n - 1) // 2, me.n // 2)
        self.streams = [s for s in range(2 * len(parts)) if self.hops[s % 2]]

    def local(self, s, chunk):
        return self.parts[s // 2].at[(chunk + 2 * self.me.n) % self.me.n]

    def copy(self, s, t, src):
        return remote(src, self.slots.at[s, t], self.send.at[s, t], self.recv.at[s, t], self.me.ring[s % 2])

    def start(self):
        for s in self.streams:
            far = self.me.place + self.hops[0] if s % 2 == 0 else self.me.place - self.hops[1]
            self.copy(s, 0, self.local(s, far)).start()

    def step(self, t):
        for s in self.streams:
            hops = self.hops[s % 2]

            @pl.when(t < hops)
            def _(s=s, hops=hops):
                slot = self.slots.at[s, t]
                self.copy(s, t, slot).wait_recv()

                @pl.when(t < hops - 1)
                def _():
                    chunk = self.me.place + (hops - 1 - t if s % 2 == 0 else t + 1 - hops)
                    slot[...] = (slot[...].astype(F32) + self.local(s, chunk)[...].astype(F32)).astype(BF16)
                    self.copy(s, t + 1, slot).start()

    def total(self, part):
        out = self.local(2 * part, self.me.place)[...].astype(F32)
        for s in self.streams:
            if s // 2 == part:
                out = out + self.slots[s, self.hops[s % 2] - 1].astype(F32)
        return out.astype(BF16)

    def finish(self, t):
        for s in self.streams:
            @pl.when(t < self.hops[s % 2])
            def _(s=s):
                self.copy(s, t, self.slots.at[s, t]).wait_send()


class Fan:
    def __init__(self, me, full, send, recv):
        self.me, self.full, self.send, self.recv = me, full, send, recv
        self.lone = len(full.shape) == 3
        self.hops = (me.n // 2, (me.n - 1) // 2)
        self.streams = [s for s in ((0, 1) if self.lone else (2, 3, 0, 1)) if self.hops[s % 2]]

    def piece(self, part, chunk, quarter=None):
        chunk = (chunk + 2 * self.me.n) % self.me.n
        if self.lone:
            return self.full.at[chunk]
        if quarter is None:
            quarter = 1 - self.me.row if part == 0 else self.me.row
        return self.full.at[quarter, chunk]

    def copy(self, s, t, chunk):
        piece = self.piece(s // 2, chunk)
        return remote(piece, piece, self.send.at[s, t], self.recv.at[s, t], self.me.ring[s % 2])

    def start(self, part):
        for s in self.streams:
            if s // 2 == part:
                self.copy(s, 0, self.me.place).start()

    def step(self, t):
        for s in self.streams:
            hops = self.hops[s % 2]

            @pl.when(t < hops)
            def _(s=s, hops=hops):
                chunk = self.me.place + (-1 - t if s % 2 == 0 else 1 + t)
                self.copy(s, t, chunk).wait_recv()

                @pl.when(t < hops - 1)
                def _():
                    self.copy(s, t + 1, chunk).start()

    def finish(self, t):
        for s in self.streams:
            @pl.when(t < self.hops[s % 2])
            def _(s=s):
                self.copy(s, t, self.me.place).wait_send()


def steps(begin, end, *rings):
    def step(t, carry):
        for ring in rings:
            ring.step(t)
        return carry

    lax.fori_loop(begin, end, step, 0)


class Pace:
    def __init__(self, n):
        self.n, self.taken = n, {}

    def __call__(self, *rings):
        for ring in rings:
            at = self.taken.get(id(ring), 0)
            if at < self.n - 1 and self.n <= 16:
                ring.step(at)
                self.taken[id(ring)] = at + 1

    def rest(self, *rings):
        if self.n <= 16:
            while any(self.taken.get(id(ring), 0) < self.n - 1 for ring in rings):
                self(*rings)
            return
        for ring in rings:
            at = self.taken.get(id(ring), 0)
            if at < self.n - 1:
                steps(at, self.n - 1, ring)
                self.taken[id(ring)] = self.n - 1


def by_rows(total, action, rows=64):
    rows = min(rows, total)

    def each(k, carry):
        action(pl.ds(pl.multiple_of(k * rows, rows), rows))
        return carry

    lax.fori_loop(0, total // rows, each, 0)


def finish(n, *rings):
    def each(t, carry):
        for ring in rings:
            ring.finish(t)
        return carry

    lax.fori_loop(0, n - 1, each, 0)


def begin_kernel(n, m, names, b, token_ref, cot_ref, wq_ref, wk_ref, wv_ref, gate_ref, up_ref, down_ref, wo_ref, gains_ref,
                 q_gain_ref, k_gain_ref, table_ref, starts_ref,
                 far_out, gate_up_out, down_out, cot_out, gains_out, hid_near_out, hid_far_out, raw_out, q_out, k_out, v_out,
                 heads_out, totals_out, attended_out, middle_out, hidden_out, wo_out, w_near_out, w_far_out,
                 near, far, w_near, w_far, wo_far, wo_all, hid_near, hid_far, raw, q_all, k_all, v_all, low, heads, attended,
                 middle, hidden, acc_ref, mass_ref,
                 local_sem, store_sem, token_send, token_recv, pass_send, pass_recv, piece_send, piece_recv, cot_send, cot_recv,
                 qkv_send, qkv_recv, wide_send, wide_recv, thin_send, thin_recv, out_send, out_recv, wo_send, wo_recv,
                 low_send, low_recv, hidden_send, hidden_recv):
    me = Group(names, n, m)
    packed, half = token_ref.shape
    count = packed // 2
    row, col = me.row, me.col
    lanes = 2 * HEAD_SIZE
    groups = q_all.shape[1] // lanes
    width = groups * lanes
    kv = groups * HEAD_SIZE
    units = gate_ref.shape[1] // 2
    chunk = half // m
    down_chunk = units // m
    pieces = 4
    rows = count // pieces
    me.arrive([*me.ring, me.across, me.beside, me.opposite])

    def at(begin, size):
        return pl.ds(pl.multiple_of(begin, size), size)

    def own_rows(k):
        return at(col * count + k * rows, rows)

    def other_rows(k):
        return at((1 - col) * count + k * rows, rows)

    def piece(k, src, dst):
        return remote(src, dst, piece_send.at[k], piece_recv.at[k], me.across)

    up_chunk, low_chunk = me.own(0), me.own(1)
    first_rows, second_rows = at(up_chunk * chunk, chunk), at(low_chunk * chunk, chunk)
    qkv_pieces = [
        piece(0, wq_ref.at[first_rows, at((1 - row) * width, width)], w_far.at[up_chunk, :, pl.ds(0, width)]),
        piece(1, wk_ref.at[second_rows, at((1 - row) * kv, kv)], w_far.at[low_chunk, :, pl.ds(width, kv)]),
        piece(2, wv_ref.at[second_rows, at((1 - row) * kv, kv)], w_far.at[low_chunk, :, pl.ds(width + kv, kv)]),
        piece(3, gains_ref, gains_out),
    ]
    down_first = at((1 - row) * units + up_chunk * down_chunk, down_chunk)
    down_second = at((1 - row) * units + low_chunk * down_chunk, down_chunk)
    qkv_pieces += [
        piece(4, wo_ref.at[first_rows, pl.ds(0, half // 2)], wo_far.at[up_chunk, :, pl.ds(0, half // 2)]),
        piece(5, wo_ref.at[second_rows, pl.ds(half // 2, half // 2)], wo_far.at[low_chunk, :, pl.ds(half // 2, half // 2)]),
    ]
    late_pieces = [
        piece(6, gate_ref.at[first_rows, at((1 - row) * units, units)], gate_up_out.at[up_chunk, :, pl.ds(0, units)]),
        piece(7, up_ref.at[second_rows, at((1 - row) * units, units)], gate_up_out.at[low_chunk, :, pl.ds(units, units)]),
        piece(8, down_ref.at[down_first, pl.ds(0, half // 2)], down_out.at[up_chunk, :, pl.ds(0, half // 2)]),
        piece(9, down_ref.at[down_second, pl.ds(half // 2, half // 2)], down_out.at[low_chunk, :, pl.ds(half // 2, half // 2)]),
    ]
    token_copies = [remote(token_ref.at[own_rows(k), :], far.at[own_rows(k), :], token_send.at[k], token_recv.at[k], me.across)
                    for k in range(pieces)]
    passes = [remote(far.at[own_rows(k), :], far.at[own_rows(k), :], pass_send.at[k], pass_recv.at[k], me.beside)
              for k in range(pieces)]
    cots = [remote(cot_ref.at[own_rows(k), :], cot_out.at[own_rows(k), :], cot_send.at[0, k], cot_recv.at[0, k], me.across)
            for k in range(pieces)]
    cot_passes = [remote(cot_out.at[own_rows(k), :], cot_out.at[own_rows(k), :], cot_send.at[1, k], cot_recv.at[1, k], me.beside)
                  for k in range(pieces)]
    for each in qkv_pieces + late_pieces + token_copies:
        each.start()

    def fetch(k, src, dst):
        return pltpu.make_async_copy(src, dst, local_sem.at[k])

    quarter = half // 2
    mine_rows, other_quarter = at(row * quarter, quarter), at((1 - row) * quarter, quarter)
    fetches = [
        fetch(0, token_ref, near),
        fetch(1, wq_ref.at[:, at(row * width, width)], w_near.at[:, pl.ds(0, width)]),
        fetch(2, wk_ref.at[:, at(row * kv, kv)], w_near.at[:, pl.ds(width, kv)]),
        fetch(3, wv_ref.at[:, at(row * kv, kv)], w_near.at[:, pl.ds(width + kv, kv)]),
        fetch(4, wo_ref.at[mine_rows, :], wo_all.at[pl.ds(0, quarter), pl.ds(0, half)]),
        fetch(5, wo_ref.at[other_quarter, :], wo_all.at[pl.ds(2 * quarter, quarter), pl.ds(0, half)]),
    ]
    for each in fetches:
        each.start()

    def wo_copy(k, src, rows_at, side):
        return remote(src, wo_all.at[pl.ds(rows_at, quarter), pl.ds(side, half)], wo_send.at[k], wo_recv.at[k], me.beside)

    wo_copies = [wo_copy(0, wo_ref.at[mine_rows, :], quarter, 0), wo_copy(1, wo_ref.at[other_quarter, :], 3 * quarter, 0)]
    for each in wo_copies:
        each.start()

    qkv = Spread(me, w_far, qkv_send, qkv_recv)
    wide = Spread(me, gate_up_out, wide_send, wide_recv)
    thin = Spread(me, down_out, thin_send, thin_recv)
    wo = Spread(me, wo_far, out_send, out_recv)
    for each in qkv_pieces:
        each.wait()
    for ring in (qkv, wo):
        for s in range(2):
            ring.start(s)
    rings = (wide, thin)
    blocks = packed // b
    slots = 8 + groups * blocks * (blocks + 1) // 2

    def tick(k):
        steps((k * (m - 1)) // slots, ((k + 1) * (m - 1)) // slots, *rings)

    steps(0, (m - 1) // pieces, qkv, wo)
    for each in late_pieces:
        each.wait()
    for ring in rings:
        for s in range(2):
            ring.start(s)
    for k in range(pieces):
        if k:
            steps(k * (m - 1) // pieces, (k + 1) * (m - 1) // pieces, qkv, wo)
        token_copies[k].wait()
        passes[k].start()
        tick(k)
    for each in cots:
        each.start()
    for each in fetches:
        each.wait()

    def prepared(x, gain, cosine, sine):
        normed = x * lax.rsqrt(head_sums(x * x) / HEAD_SIZE + EPSILON) * gain
        return normed * cosine + swapped(normed) * sine

    far_gains = gains_out

    def project_block(k):
        begin = ((col * pieces + 2 * k) % (2 * pieces)) * rows

        def part(k, carry):
            project_rows(at(begin + k * rows, rows))
            return carry

        lax.fori_loop(0, 2, part, 0)

    def project_rows(block):
        x_near = near[block, :].astype(F32)
        x_far = far[block, :].astype(F32)
        total = jnp.sum(x_near * x_near, axis=1, keepdims=True) + jnp.sum(x_far * x_far, axis=1, keepdims=True)
        inverse = lax.rsqrt(total / (2 * half) + EPSILON)
        h_near = (x_near * inverse * gains_ref[0:1, :]).astype(BF16)
        h_far = (x_far * inverse * far_gains[0:1, :]).astype(BF16)
        hid_near[block, :] = h_near
        hid_far[block, :] = h_far
        out = dot(h_near, w_near[...]) + dot(h_far, w_far[...].reshape(half, w_far.shape[2]))
        raw[block, :] = out[:, :width + kv]
        cosine, sine = rope_block(table_ref, block)
        for g in range(groups):
            cut = slice(g * lanes, (g + 1) * lanes)
            part = prepared(out[:, cut], two_heads(q_gain_ref), cosine, sine).astype(BF16)
            q_all[block, cut] = (part * HEAD_SIZE ** (-0.5)).astype(BF16)
        for g in range(groups // 2):
            begin = width + g * lanes
            twice = doubled(prepared(out[:, begin:begin + lanes], two_heads(k_gain_ref), cosine, sine))
            value = doubled(out[:, begin + kv:begin + kv + lanes])
            for h in range(2):
                cut = slice((2 * g + h) * lanes, (2 * g + h + 1) * lanes)
                k_all[block, cut] = twice[h].astype(BF16)
                v_all[block, cut] = value[h].astype(BF16)

    project_block(0)
    tick(4)
    project_block(1)
    tick(5)
    for k in range(pieces):
        passes[k].wait()
        if k % 2 == 1:
            project_block(2 + k // 2)
            tick(6 + k // 2)

    def store(k, src, dst):
        return pltpu.make_async_copy(src, dst, store_sem.at[k])

    stores = [store(k, src, dst) for k, (src, dst) in enumerate((
        (far, far_out), (hid_near, hid_near_out), (hid_far, hid_far_out), (raw, raw_out), (q_all, q_out), (k_all, k_out),
        (v_all, v_out)))]
    for each in stores:
        each.start()

    per_half = blocks // 2

    def low_copy(kind, g, i, target):
        slot = (2, 1, 3)[kind] * width + g * lanes
        return remote(low.at[at(i * b, b), pl.ds(g * lanes, lanes)],
                      attended.at[at((i % per_half) * b, b), pl.ds(slot, lanes)],
                      low_send.at[kind, g, i % per_half], low_recv.at[kind, g, i % per_half], target)

    for g in range(groups):
        cut = slice(g * lanes, (g + 1) * lanes)

        def query_block(i, carry, g=g, cut=cut):
            place = at(i * b, b)
            qs = stacked(q_all[place, cut])
            begins = starts_ref[place, :]
            begins = jnp.concatenate([begins, begins], axis=0)
            acc_ref[...] = jnp.zeros_like(acc_ref)
            mass_ref[...] = jnp.zeros_like(mass_ref)
            base = 8 + g * (blocks * (blocks + 1) // 2) + (i * (i + 1)) // 2

            def key_block(j, diagonal):
                keys = at(j * b, b)
                s = dot(qs, k_all[keys, cut], NT)
                columns = j * b + lax.broadcasted_iota(jnp.int32, (1, b), 1)
                allowed = columns >= begins
                if diagonal:
                    lines = i * b + lax.rem(lax.broadcasted_iota(jnp.int32, (2 * b, 1), 0), b)
                    allowed = allowed & (columns <= lines)
                p = jnp.where(allowed, jnp.exp(s), 0.0)
                mass = p[:, :128]
                for part in range(1, b // 128):
                    mass = mass + p[:, part * 128:(part + 1) * 128]
                mass_ref[...] += mass
                acc_ref[...] += dot(p.astype(BF16), v_all[keys, cut])
                tick(base + j)

            @pl.loop(0, i)
            def _(j):
                key_block(j, False)

            key_block(i, True)
            mass = jnp.sum(mass_ref[...], axis=1, keepdims=True)
            out = acc_ref[...] / mass
            first = lax.broadcasted_iota(jnp.int32, (b, lanes), 1) < HEAD_SIZE
            out = jnp.where(first, out[:b], out[b:])
            heads[place, cut] = out
            low[place, cut] = out.astype(BF16)
            total = jnp.log(jnp.sum(mass_ref[...].T, axis=0, keepdims=True))
            totals_out[g, 0:1, place] = total[:, :b]
            totals_out[g, 1:2, place] = total[:, b:]

            @pl.when(i // per_half == col)
            def _():
                attended[at((i % per_half) * b, b), cut] = out.astype(BF16)
                low_copy(0, g, i, me.across).start()

            @pl.when(i // per_half != col)
            def _():
                low_copy(1, g, i, me.beside).start()
                low_copy(2, g, i, me.opposite).start()
            return carry

        lax.fori_loop(0, blocks, query_block, 0)
    heads_store = store(7, heads, heads_out)
    heads_store.start()
    w_stores = [store(8 + 3 * per_half, w_near, w_near_out), store(9 + 3 * per_half, w_far, w_far_out)]
    for each in w_stores:
        each.start()

    local_far = []
    per = quarter // chunk
    for p, begin in ((0, row), (2, 1 - row)):
        for k in range(per):
            local_far.append(pltpu.make_async_copy(
                wo_far.at[begin * per + k], wo_all.at[pl.ds(p * quarter + k * chunk, chunk), pl.ds(half, half)],
                local_sem.at[6 + len(local_far)]))
    remote_far = []
    for p, begin in ((1, row), (3, 1 - row)):
        for k in range(per):
            remote_far.append(remote(
                wo_far.at[begin * per + k], wo_all.at[pl.ds(p * quarter + k * chunk, chunk), pl.ds(half, half)],
                wo_send.at[2 + len(remote_far)], wo_recv.at[2 + len(remote_far)], me.beside))
    for each in local_far + remote_far:
        each.start()
    for k in range(pieces):
        cots[k].wait()
        cot_passes[k].start()
    for each in local_far + remote_far + wo_copies:
        each.wait()
    w_stores.append(store(10 + 3 * per_half, wo_all.at[pl.ds(0, quarter), :], wo_out))
    w_stores[-1].start()

    gain = jnp.concatenate([gains_ref[1:2, :], far_gains[1:2, :]], axis=1)
    hidden_stores = []
    for k in range(per_half):
        for g in range(groups):
            for kind in range(3):
                low_copy(kind, g, k, me.beside).wait()
        place = at(col * count + k * b, b)

        def merge(fine, k=k):
            part = at(k * b + fine.start, fine.size)
            mine = at(col * count + k * b + fine.start, fine.size)
            tokens = jnp.concatenate([near[mine, :], far[mine, :]], axis=1).astype(F32)
            total = tokens + dot(attended[part, :], wo_all[...])
            middle[part, :] = total
            inverse = lax.rsqrt(jnp.sum(total * total, axis=1, keepdims=True) / (2 * half) + EPSILON)
            hidden[part, :] = (total * inverse * gain).astype(BF16)

        by_rows(b, merge, 128)
        hidden_stores += [
            remote(hidden.at[pl.ds(k * b, b), :], hidden_out.at[place, :], hidden_send.at[k], hidden_recv.at[k], me.beside),
            pltpu.make_async_copy(hidden.at[pl.ds(k * b, b), :], hidden_out.at[place, :], store_sem.at[8 + 3 * k]),
            pltpu.make_async_copy(middle.at[pl.ds(k * b, b), :], middle_out.at[pl.ds(k * b, b), :], store_sem.at[9 + 3 * k]),
            pltpu.make_async_copy(attended.at[pl.ds(k * b, b), :], attended_out.at[pl.ds(k * b, b), :], store_sem.at[10 + 3 * k]),
        ]
        for each in hidden_stores[-4:]:
            each.start()
    for each in stores + [heads_store] + w_stores + hidden_stores + cot_passes:
        each.wait()
    finish(m, qkv, wo, *rings)


def rope_block(table_ref, block):
    half = HEAD_SIZE // 2
    cosine, sine = table_ref[:half, block], table_ref[half:, block]
    return jnp.concatenate([cosine] * 4, axis=0).T, jnp.concatenate([-sine, sine] * 2, axis=0).T


def begin(tokens, cot, wq, wk, wv, gate, up, down, wo, gains, q_gain, k_gain, table, starts, names, n, b=512):
    packed, half = tokens.shape
    b = min(b, packed // 2)
    m = math.gcd(n, 8)
    width, kv, units = wq.shape[1] // 2, wk.shape[1] // 2, gate.shape[1] // 2
    groups = width // (2 * HEAD_SIZE)
    count = packed // 2
    vmem = pl.BlockSpec(memory_space=pltpu.VMEM)
    some = pl.BlockSpec(memory_space=pl.ANY)
    dma = pltpu.SemaphoreType.DMA

    outs = [((packed, half), BF16, some), ((m, half // m, 2 * units), BF16, some), ((m, units // m, half), BF16, some),
            ((packed, half), BF16, some), (gains.shape, F32, vmem), ((packed, half), BF16, some), ((packed, half), BF16, some),
            ((packed, width + kv), F32, some), ((packed, width), BF16, some), ((packed, width), BF16, some),
            ((packed, width), BF16, some), ((packed, width), F32, some), ((groups, 2, packed), F32, vmem),
            ((count, 2 * half), BF16, some), ((count, 2 * half), F32, some), ((packed, 2 * half), BF16, some),
            ((half // 2, 2 * half), BF16, some), ((half, width + 2 * kv), BF16, some), ((m, half // m, width + 2 * kv), BF16, some)]
    scratch = [((packed, half), BF16), ((packed, half), BF16), ((half, width + 2 * kv), BF16), ((m, half // m, width + 2 * kv), BF16),
               ((m, half // m, half), BF16), ((2 * half, 2 * half), BF16), ((packed, half), BF16), ((packed, half), BF16),
               ((packed, width + kv), F32), ((packed, width), BF16), ((packed, width), BF16), ((packed, width), BF16),
               ((packed, width), BF16), ((packed, width), F32), ((count, 2 * half), BF16), ((count, 2 * half), F32),
               ((count, 2 * half), BF16), ((2 * b, 2 * HEAD_SIZE), F32), ((2 * b, 2 * HEAD_SIZE), F32)]
    per_half = count // b
    ring = [dma((2, m - 1))] * 8
    return pl.pallas_call(
        functools.partial(begin_kernel, n, m, names, b),
        out_shape=tuple(jax.ShapeDtypeStruct(shape, dtype) for shape, dtype, _ in outs),
        in_specs=[some] * 9 + [vmem] * 5,
        out_specs=tuple(spec for *_, spec in outs),
        scratch_shapes=[
            *[pltpu.VMEM(shape, dtype) for shape, dtype in scratch],
            dma((6 + m,)), dma((11 + 3 * per_half,)), dma((4,)), dma((4,)), dma((4,)), dma((4,)), dma((10,)), dma((10,)),
            dma((2, 4)), dma((2, 4)), *ring, dma((2 + m,)), dma((2 + m,)),
            dma((3, groups, per_half)), dma((3, groups, per_half)), dma((per_half,)), dma((per_half,)),
        ],
        compiler_params=pltpu.CompilerParams(collective_id=4, has_side_effects=True, vmem_limit_bytes=VMEM_LIMIT),
        cost_estimate=pl.CostEstimate(flops=20 << 30, transcendentals=0, bytes_accessed=100 << 20),
        name="begin",
    )(tokens, cot, wq, wk, wv, gate, up, down, wo, gains, q_gain, k_gain, table, starts)


def turn_kernel(n, names, pieces, hidden_ref, grads_ref, active_ref, cot_near_ref, cot_far_ref, gate_ref, up_ref, gate_up_ref,
                middle_ref, attended_ref, wo_ref, gain_ref, keep_ref, gain_sum_ref, done_ref, down_done_ref, heads_ref, wo_grad_ref,
                hidden, grads, active, cot_near, cot_far, back, middle, wo, near, far, down_near, down_far, branch, other_branch,
                far_slots, near_slots, down_slots, beside_in, across_out, across_in, give_in, load_sem,
                far_send, far_recv, near_send, near_recv, down_send, down_recv,
                cross_send, cross_recv, beside_send, beside_recv, across_send, across_recv, branch_send, branch_recv,
                give_send, give_recv):
    me = Group(names, n)
    half = cot_near_ref.shape[1]
    tokens = middle_ref.shape[0]
    rows = tokens // pieces
    units = active_ref.shape[1]
    row, col = me.row, me.col
    far_ring = Reduce(me, (far,), far_slots, far_send, far_recv)
    near_ring = Reduce(me, (near,), near_slots, near_send, near_recv)
    down = Reduce(me, (down_far, down_near), down_slots, down_send, down_recv)

    def load(k, src, dst):
        return pltpu.make_async_copy(src, dst, load_sem.at[k])

    loads = [load(1, active_ref, active), load(2, cot_near_ref, cot_near), load(3, cot_far_ref, cot_far),
             load(5, grads_ref, grads), load(4, hidden_ref, hidden), load(6, middle_ref, middle), load(7, wo_ref, wo)]
    for each in loads:
        each.start()
    me.arrive([*me.ring, me.across, me.beside])

    for each in loads[:3]:
        each.wait()
    per = units // 3

    def down_tile(k, carry):
        left = active[:, pl.ds(pl.multiple_of(k * per, per), per)]
        for cot, out in ((cot_near, down_near), (cot_far, down_far)):
            part = over_t(left, cot[...]).astype(BF16)
            line = down_near.shape[1]
            if per % line == 0:
                for c in range(per // line):
                    out[k * (per // line) + c] = part[c * line:(c + 1) * line]
            else:
                for c in range(per // 16):
                    at = k * per + c * 16
                    out[at // line, pl.ds(at % line, 16), :] = part[c * 16:(c + 1) * 16]
        return carry

    if units // n % 16 == 0 and per % 16 == 0:
        lax.fori_loop(0, 3, down_tile, 0)
    else:
        for cot, out in ((cot_near, down_near), (cot_far, down_far)):
            part = over_t(active[...], cot[...]).astype(BF16)
            line = down_near.shape[1]
            for c in range(n):
                out[c] = part[c * line:(c + 1) * line]
    down.start()

    columns = pl.ds(pl.multiple_of(row * units, units), units)
    weights = [load(9, gate_ref.at[:, columns], active.at[pl.ds(0, half), :]),
               load(10, up_ref.at[:, columns], active.at[pl.ds(half, half), :]),
               load(11, gate_up_ref.at[:, pl.ds(0, units)], active.at[pl.ds(2 * half, half), :]),
               load(12, gate_up_ref.at[:, pl.ds(units, units)], active.at[pl.ds(3 * half, half), :])]
    for each in weights:
        each.start()
    for each in weights + loads[3:4]:
        each.wait()
    acrosses = [remote(across_out.at[k], across_in.at[k], across_send.at[k], across_recv.at[k], me.across)
                for k in range(pieces)]

    def beside_copy(k):
        return remote(across_out.at[k], beside_in.at[k], beside_send.at[k], beside_recv.at[k], me.beside)

    def back_rows(place, side):
        first, second = 2 * side * half, (2 * side + 1) * half
        return (dot(grads[place, :units], active[first:first + half, :], NT)
                + dot(grads[place, units:], active[second:second + half, :], NT)).astype(BF16)

    pace = Pace(n)
    for k in range(pieces):
        place = pl.ds(pl.multiple_of((1 - col) * tokens + k * rows, rows), rows)
        for side in range(2):
            across_out[k, :, side * half:(side + 1) * half] = back_rows(place, side)
        beside_copy(k).start()
        if k % 2:
            pace(down)
    for k in range(pieces):
        place = pl.ds(pl.multiple_of(col * tokens + k * rows, rows), rows)
        for side in range(2):
            back[k * rows:(k + 1) * rows, side * half:(side + 1) * half] = back_rows(place, side)
        beside_copy(k).wait()

        def add(part, k=k):
            mine = pl.ds(pl.multiple_of(k * rows + part.start, part.size), part.size)
            chip = (back[mine, :].astype(F32) + beside_in[k, part, :].astype(F32)).astype(BF16)
            across_out[k, part, :half] = chip[:, half:]
            across_out[k, part, half:] = chip[:, :half]

        by_rows(rows, add)
        acrosses[k].start()
        if k % 2:
            pace(down)
    loads[4].wait()
    line = near.shape[1]
    tile = 256

    def wide_tiles(out, begin, *rings):
        for k in range(half // tile):
            for side in range(2):
                left = hidden[:, begin + k * tile:begin + (k + 1) * tile]
                part = over_t(left, grads[:, side * units:(side + 1) * units]).astype(BF16)
                for c in range(tile // line):
                    out[k * (tile // line) + c, :, side * units:(side + 1) * units] = part[c * line:(c + 1) * line]
            pace(*rings)

    gain_sum_ref[...] = jnp.zeros_like(gain_sum_ref)

    def branch_copy(k):
        part = pl.ds(k * rows, rows)
        return remote(branch.at[part, :], other_branch.at[part, :], branch_send.at[k], branch_recv.at[k], me.beside)

    def norm_piece(k):
        acrosses[k].wait()

        def end(fine):
            part = pl.ds(pl.multiple_of(k * rows + fine.start, fine.size), fine.size)
            place = pl.ds(pl.multiple_of(col * tokens + k * rows + fine.start, fine.size), fine.size)
            grad = back[part, :].astype(F32) + beside_in[k, fine, :].astype(F32) + across_in[k, fine, :].astype(F32)
            x = middle[part, :]
            inverse = lax.rsqrt(jnp.sum(x * x, axis=1, keepdims=True) / (2 * half) + EPSILON)
            normal = x * inverse
            weighed = grad * normal
            gain_sum_ref[...] += jnp.sum(weighed, axis=0, keepdims=True)
            stat = jnp.sum(weighed * gain_ref[...], axis=1, keepdims=True) / (2 * half)
            change = inverse * (grad * gain_ref[...] - normal * stat)
            keep = cot_near[place, :].astype(F32) + change[:, :half]
            keep_ref[part, :] = keep
            branch[part, :half] = keep.astype(BF16)
            branch[part, half:] = (cot_far[place, :].astype(F32) + change[:, half:]).astype(BF16)

        by_rows(rows, end)
        branch_copy(k).start()

    wide_tiles(far, half, down)
    far_ring.start()
    wide_tiles(near, 0, down, far_ring)
    near_ring.start()
    fetch_attended = load(8, attended_ref, hidden.at[pl.ds(0, tokens), :])
    fetch_attended.start()

    def crosses_of(ring, out, base):
        return [remote(ring.last(s), out.at[s], cross_send.at[base + s], cross_recv.at[base + s], me.across) for s in range(2)]

    loads[5].wait()
    pace(down, far_ring, near_ring)
    pace.rest(down)
    crosses = crosses_of(down, down_done_ref, 2)
    for cross in crosses:
        cross.start()
    for s in (2, 3):
        down_done_ref[s] = down.last(s)[...]
    for k in range(pieces):
        norm_piece(k)
        pace(far_ring, near_ring)
    pace.rest(far_ring)
    crosses += crosses_of(far_ring, done_ref, 0)
    for cross in crosses[2:]:
        cross.start()

    fetch_attended.wait()
    loads[6].wait()
    quarter = half // 2
    gives = []
    for p in (1, 3, 0, 2):
        part = over_t(hidden[:tokens, p * quarter:(p + 1) * quarter], branch[:, :half])
        if p in (1, 3):
            across_out[p // 2, :quarter, :half] = part.astype(BF16)
            gives.append(remote(across_out.at[p // 2, pl.ds(0, quarter), pl.ds(0, half)],
                                give_in.at[p // 2],
                                give_send.at[p // 2], give_recv.at[p // 2], me.beside))
            gives[-1].start()
            pace(near_ring)
        else:
            gives[p // 2].wait()
            place = row if p == 0 else 1 - row
            total = part + give_in[p // 2].astype(F32)
            wo_grad_ref[pl.ds(pl.multiple_of(place * quarter, quarter), quarter), :] = total.astype(BF16)

    def attended_grad(src, core):
        def each(part):
            heads_ref[pl.ds(pl.multiple_of(core * tokens + part.start, part.size), part.size), :] = dot(
                src[part, :], wo[...], NT).astype(BF16)

        by_rows(tokens, each, 256)

    attended_grad(branch, col)
    for k in range(pieces):
        branch_copy(k).wait()
    attended_grad(other_branch, 1 - col)
    pace.rest(near_ring)
    for s in range(2):
        done_ref[2 + s] = near_ring.last(s)[...]
    for cross in crosses:
        cross.wait()
    finish(n, far_ring, near_ring, down)


def turn(hidden, grads, active, cot_near, cot_far, gate, up, gate_up_far, middle, attended, wo, gain, names, n, pieces=4):
    packed, width = hidden.shape
    tokens, half, units = middle.shape[0], width // 2, active.shape[1]
    vmem = pl.BlockSpec(memory_space=pltpu.VMEM)
    some = pl.BlockSpec(memory_space=pl.ANY)
    dma = pltpu.SemaphoreType.DMA
    exchange = ((pieces, tokens // pieces, width), BF16)
    wide, down = (half // n, units), (units // n, half // 2)
    outs = [((tokens, half), F32), ((1, width), F32), ((4, *wide), BF16), ((4, *down), BF16), ((packed, wo.shape[0]), BF16),
            ((half, half), BF16)]
    scratch = [(x.shape, x.dtype) for x in (hidden, grads, active, cot_near, cot_far)]
    scratch += [((tokens, width), BF16), (middle.shape, F32), (wo.shape, BF16), ((n, half // n, 2 * units), BF16),
                ((n, half // n, 2 * units), BF16), ((n, units // n, half), BF16), ((n, units // n, half), BF16),
                ((tokens, width), BF16), ((tokens, width), BF16), ((2, n - 1, *wide), BF16), ((2, n - 1, *wide), BF16),
                ((4, n - 1, *down), BF16),
                exchange, exchange, exchange, ((2, half // 2, half), BF16)]
    return pl.pallas_call(
        functools.partial(turn_kernel, n, names, pieces),
        out_shape=tuple(jax.ShapeDtypeStruct(shape, dtype) for shape, dtype in outs),
        in_specs=[some] * 11 + [vmem],
        out_specs=(vmem,) * len(outs),
        scratch_shapes=[
            *[pltpu.VMEM(shape, dtype) for shape, dtype in scratch], dma((13,)), *[dma((2, n - 1, 2))] * 4, *[dma((4, n - 1, 2))] * 2,
            dma((4,)), dma((4,)),
            *[dma((pieces,))] * 6, dma((2,)), dma((2,)),
        ],
        compiler_params=pltpu.CompilerParams(collective_id=1, has_side_effects=True, vmem_limit_bytes=VMEM_LIMIT),
        cost_estimate=pl.CostEstimate(flops=6 * packed * width * units, transcendentals=tokens, bytes_accessed=150 << 20),
        name="turn",
    )(hidden, grads, active, cot_near, cot_far, gate, up, gate_up_far, middle, attended, wo, gain)


def finale_kernel(n, names, b, q_ref, k_ref, v_ref, grad_ref, heads_ref, totals_ref, start_ref, done_ref, down_done_ref,
                  result_ref, middle_ref, keep_ref, raw_ref, token_ref, far_ref, hid_near_ref, hid_far_ref, w_near_ref, w_far_ref,
                  wo_grad_ref, gain_near_ref, gain_far_ref, q_gain_ref, k_gain_ref, table_ref, ffn_sum_ref,
                  wide_ref, down_ref, output_ref, thin_ref, lone_ref, sums_ref, tokens_grad_ref,
                  q_all, k_all, v_all, grad_all, heads, raw, near, far, hid_near, hid_far, w_near, w_far, middle_near, sums,
                  qs_ref, gs_ref, stat_ref, dqt_ref, dk_acc, dv_acc, dq, dk, dv, grads, to_near, to_far, stat, near_grads, far_grads,
                  slots, lone_slots, result_in, result_out, result_back, beside_in, beside_stat, across_in,
                  stat_out, stat_in, far_total, vector, group_in, ring_in, mine, q_sum, k_sum, near_sum, far_sum,
                  load_sem, keep_sem, wide_send, wide_recv, down_send, down_recv, rs_send, rs_recv, ag_send, ag_recv,
                  lone_send, lone_recv, lone_out_send, lone_out_recv, cross_send, cross_recv, group_send, group_recv,
                  all_send, all_recv, result_send, result_recv, beside_send, beside_recv, across_send, across_recv,
                  last_send, last_recv):
    me = Group(names, n)
    row, col = me.row, me.col
    packed, half = token_ref.shape
    count = packed // 2
    lanes = 2 * HEAD_SIZE
    width = q_ref.shape[1]
    groups = width // lanes
    kv = groups * HEAD_SIZE
    blocks = packed // b
    per_half = blocks // 2
    wide = Spread(me, wide_ref, wide_send, wide_recv)
    down = Spread(me, down_ref, down_send, down_recv)
    lone = Meet(me, (wo_grad_ref,), lone_slots, lone_send, lone_recv)
    lone_out = Fan(me, lone_ref, lone_out_send, lone_out_recv)
    thin = Meet(me, (far_grads, near_grads), slots, rs_send, rs_recv)
    thin_out = Fan(me, thin_ref, ag_send, ag_recv)
    hops = n // 2

    def at(begin, size):
        return pl.ds(pl.multiple_of(begin, size), size)

    own_rows, other_rows = at(col * count, count), at((1 - col) * count, count)

    def load(k, src, dst):
        return pltpu.make_async_copy(src, dst, load_sem.at[k])

    first = [load(k, src, dst) for k, (src, dst) in enumerate((
        (q_ref, q_all), (k_ref, k_all), (v_ref, v_all), (grad_ref, grad_all), (heads_ref, heads)))]
    sides = (pl.ds(half, half), pl.ds(0, half))
    second = [load(5 + k, src, dst) for k, (src, dst) in enumerate((
        (result_ref.at[own_rows, sides[0]], sums.at[0]), (result_ref.at[own_rows, sides[1]], sums.at[1]),
        (middle_ref.at[:, pl.ds(0, half)], middle_near)))]
    third = [load(8 + k, src, dst) for k, (src, dst) in enumerate((
        (raw_ref, raw), (token_ref, near), (far_ref, far), (w_near_ref, w_near), (w_far_ref, w_far), (hid_near_ref, hid_near),
        (hid_far_ref, hid_far)))]
    keep, across_out = middle_near, sums.at[0]
    for each in first + second + third:
        each.start()

    me.arrive([*me.along, me.across, me.beside, me.opposite])
    for ring, src in ((wide, done_ref), (down, down_done_ref)):
        for s in range(4):
            ring.start(s, src.at[s])
    lone.start()
    keeps = [pltpu.make_async_copy(src.at[s], ring.piece(s, me.own(s % 2)), keep_sem.at[4 * k + s])
             for k, (ring, src) in enumerate(((wide, done_ref), (down, down_done_ref))) for s in range(4)]
    for each in keeps:
        each.start()
    results = [remote(result_ref.at[other_rows, side], result_in.at[k], result_send.at[k], result_recv.at[k], me.beside)
               for k, side in enumerate(sides)]
    for each in results:
        each.start()
    result_across = remote(result_out, result_back, result_send.at[2], result_recv.at[2], me.across)
    output_last = remote(result_out, output_ref.at[own_rows, :], last_send.at[0], last_recv.at[0], me.beside)
    output_here = pltpu.make_async_copy(result_out, output_ref.at[own_rows, :], keep_sem.at[8])
    for each in first:
        each.wait()

    every = groups * blocks * (blocks + 1) // 2
    slot_count = every + blocks

    early = max(n - 3, 0)

    def tick(k):
        steps((k * early) // slot_count, ((k + 1) * early) // slot_count, wide, down)
        steps((k * hops) // slot_count, ((k + 1) * hops) // slot_count, lone)

    def group_pass(g, carry):
        cut = at(g * lanes, lanes)
        dqt_ref[...] = jnp.zeros_like(dqt_ref)
        for i in range(blocks):
            rows = slice(i * b, (i + 1) * b)
            both = slice(i * 2 * b, (i + 1) * 2 * b)
            qs_ref[both, :] = stacked(q_all[rows, cut])
            grad = grad_all[rows, cut]
            gs_ref[both, :] = stacked(grad)
            prod = (grad.astype(F32) * heads[rows, cut]).T
            stat_ref[i, 0:1, 0:b] = totals_ref[g, 0:1, rows]
            stat_ref[i, 0:1, b:2 * b] = totals_ref[g, 1:2, rows]
            stat_ref[i, 1:2, 0:b] = jnp.sum(prod[:HEAD_SIZE], axis=0, keepdims=True)
            stat_ref[i, 1:2, b:2 * b] = jnp.sum(prod[HEAD_SIZE:], axis=0, keepdims=True)

        def key_pass(j, carry):
            place = at(j * b, b)
            k = k_all[place, cut]
            v = v_all[place, cut]
            kt = k.T[:HEAD_SIZE]
            dk_acc[...] = jnp.zeros_like(dk_acc)
            dv_acc[...] = jnp.zeros_like(dv_acc)
            keys = j * b + lax.broadcasted_iota(jnp.int32, (b, 1), 0)
            before = g * (every // groups) + j * blocks - (j * (j - 1)) // 2

            def step(i, diagonal):
                both = at(i * 2 * b, 2 * b)
                qs = qs_ref[both, :]
                gs = gs_ref[both, :]
                st = dot(k, qs, NT)
                pt = jnp.exp(st - stat_ref[i, 0:1, :])
                begin = start_ref[0:1, at(i * b, b)]
                allowed = keys >= jnp.concatenate([begin, begin], axis=1)
                if diagonal:
                    columns = i * b + lax.rem(lax.broadcasted_iota(jnp.int32, (1, 2 * b), 1), b)
                    allowed = allowed & (keys <= columns)
                pt = jnp.where(allowed, pt, 0.0)
                dv_acc[...] += dot(pt.astype(BF16), gs)
                dpt = dot(v, gs, NT)
                dst = (pt * (dpt - stat_ref[i, 1:2, :])).astype(BF16)
                dk_acc[...] += dot(dst, qs)
                part = dot(kt, dst)
                to = at(i * b, b)
                dqt_ref[:HEAD_SIZE, to] += part[:, :b]
                dqt_ref[HEAD_SIZE:, to] += part[:, b:]
                tick(before + i - j)

            step(j, True)

            @pl.loop(j + 1, blocks)
            def _(i):
                step(i, False)

            pair = at((g // 2) * lanes, lanes)
            keep_first = (lax.broadcasted_iota(jnp.int32, (b, lanes), 1) < HEAD_SIZE) & (g % 2 == 1)
            for acc, out in ((dk_acc, dk), (dv_acc, dv)):
                out[place, pair] = jnp.where(keep_first, out[place, pair], acc[...] + pltpu.roll(acc[...], HEAD_SIZE, 1))
            dq[place, cut] = dqt_ref[:, place].T * HEAD_SIZE ** (-0.5)

            @pl.when((g == 0) & (j == 0))
            def _():
                for each in results + second:
                    each.wait()

                def add(part):
                    result_out[part, :] = (sums[0, part, :].astype(F32) + result_in[0, part, :].astype(F32)).astype(BF16)

                by_rows(count, add)
                result_across.start()

            @pl.when((g == groups - 1) & (j == 0))
            def _():
                result_across.wait()

                def add(part):
                    total = sums[1, part, :].astype(F32) + result_in[1, part, :].astype(F32) + result_back[part, :].astype(F32)
                    result_out[part, :] = (middle_near[part, :] + total).astype(BF16)

                by_rows(count, add)
                output_last.start()
                output_here.start()
            return carry

        lax.fori_loop(0, blocks, key_pass, 0)
        return carry

    lax.fori_loop(0, groups, group_pass, 0)

    keep_load = load(15, keep_ref, keep)
    keep_load.start()
    for each in third:
        each.wait()
    for ref in (q_sum, k_sum, near_sum, far_sum):
        ref[...] = jnp.zeros_like(ref)

    def beside_copy(h, k):
        part = pl.ds(h * b, b)
        src = (to_far, stat, to_near)[k].at[at((1 - col) * count + h * b, b), :]
        dst = beside_stat.at[part, :] if k == 1 else beside_in.at[k // 2, part, :]
        return remote(src, dst, beside_send.at[h, k], beside_recv.at[h, k], me.beside)

    def across_copy(h, k):
        part = pl.ds(h * b, b)
        src, dst = ((across_out, across_in), (stat_out, stat_in))[k]
        return remote(src.at[part, :], dst.at[part, :], across_send.at[h, k], across_recv.at[h, k], me.across)

    fine = min(b, 256)

    def project_block(p):
        begin = (((1 - col) * per_half + p) % blocks) * b

        def part(k, carry):
            project_rows(at(begin + k * fine, fine))
            return carry

        lax.fori_loop(0, b // fine, part, 0)

    def project_rows(block):
        cosine, sine = rope_block(table_ref, block)
        head = lax.broadcasted_iota(jnp.int32, (fine, lanes), 1) < HEAD_SIZE

        def back(grad, x, gain):
            inverse = lax.rsqrt(head_sums(x * x) / HEAD_SIZE + EPSILON)
            normed = x * inverse
            turned = grad * cosine - swapped(grad) * sine
            inner = turned * gain
            part = inverse * (inner - normed * (head_sums(inner * normed) / HEAD_SIZE))
            return part, jnp.sum(turned * normed, axis=0, keepdims=True)

        for g in range(groups):
            cut = slice(g * lanes, (g + 1) * lanes)
            part, total = back(dq[block, cut], raw[block, cut], two_heads(q_gain_ref))
            q_sum[...] += total
            grads[block, cut] = part.astype(BF16)
        for g in range(groups // 2):
            pair = slice(g * lanes, (g + 1) * lanes)
            cut = slice(width + g * lanes, width + (g + 1) * lanes)
            part, total = back(dk[block, pair], raw[block, cut], two_heads(k_gain_ref))
            k_sum[...] += total
            grads[block, cut] = part.astype(BF16)
            cut = slice(width + kv + g * lanes, width + kv + (g + 1) * lanes)
            grads[block, cut] = dv[block, pair].astype(BF16)
        grad_near = dot(grads[block, :], w_near[...], NT)
        grad_far = dot(grads[block, :], w_far[...], NT)
        to_near[block, :] = grad_near.astype(BF16)
        to_far[block, :] = grad_far.astype(BF16)
        x_near = near[block, :].astype(F32)
        x_far = far[block, :].astype(F32)
        total = jnp.sum(x_near * x_near, axis=1, keepdims=True) + jnp.sum(x_far * x_far, axis=1, keepdims=True)
        inverse = lax.rsqrt(total / (2 * half) + EPSILON)
        x_near = grad_near * (x_near * inverse)
        x_far = grad_far * (x_far * inverse)
        near_sum[...] += jnp.sum(x_near, axis=0, keepdims=True)
        far_sum[...] += jnp.sum(x_far, axis=0, keepdims=True)
        total = (jnp.sum(x_near * gain_near_ref[...], axis=1, keepdims=True)
                 + jnp.sum(x_far * gain_far_ref[...], axis=1, keepdims=True))
        stat[block, :] = jnp.where(head, total, inverse)

    for p in range(blocks):
        project_block(p)
        h = p % per_half
        part = slice(h * b, (h + 1) * b)
        if p < per_half:
            for k in range(3):
                beside_copy(h, k).start()
        else:
            own = at(col * count + h * b, b)
            beside_copy(h, 0).wait()

            def add(fine, h=h):
                place = at(col * count + h * b + fine.start, fine.size)
                fine = at(h * b + fine.start, fine.size)
                across_out[fine, :] = (to_far[place, :].astype(F32) + beside_in[0, fine, :].astype(F32)).astype(BF16)

            by_rows(b, add)
            across_copy(h, 0).start()
            beside_copy(h, 1).wait()
            stat_out[part, :] = stat[own, :] + beside_stat[part, :]
            across_copy(h, 1).start()
        tick(every + p)

    line = half // n
    for hid, out in ((hid_far, far_grads), (hid_near, near_grads)):
        for k in range(2):
            part = over_t(hid[:, k * (half // 2):(k + 1) * (half // 2)], grads[...]).astype(BF16)
            for c in range(n // 2):
                out[k * (n // 2) + c] = part[c * line:(c + 1) * line]
    thin.start()
    lone_out.piece(0, me.place)[...] = lone.total(0)
    lone_out.start(0)

    vector[...] = jnp.zeros_like(vector)
    rows = half // 128
    for c in range(rows):
        cut = slice(c * 128, (c + 1) * 128)
        vector[pl.ds(row * rows + c, 1), :] = near_sum[:, cut]
        vector[pl.ds((1 - row) * rows + c, 1), :] = far_sum[:, cut]
        vector[pl.ds((2 + row) * rows + c, 1), :] = 0.5 * ffn_sum_ref[:, c * 128:(c + 1) * 128]
        vector[pl.ds((3 - row) * rows + c, 1), :] = 0.5 * ffn_sum_ref[:, half + c * 128:half + (c + 1) * 128]
    vector[4 * rows:4 * rows + 1, :] = q_sum[...]
    vector[4 * rows + 1:4 * rows + 2, :] = k_sum[...]
    gathers = [remote(vector, group_in.at[k], group_send.at[k], group_recv.at[k], target)
               for k, target in enumerate((me.across, me.beside, me.opposite))]
    for gather in gathers:
        gather.start()
    steps(0, hops // 2, thin, lone_out)
    steps(early, early + (n - 1 - early) // 2, wide, down)
    for gather in gathers:
        gather.wait()
    mine[...] = vector[...] + group_in[0] + group_in[1] + group_in[2]
    spreads = [remote(mine, ring_in.at[k], all_send.at[k], all_recv.at[k], target) for k, target in enumerate(me.along)]
    for spread in spreads:
        spread.start()
    steps(hops // 2, hops, thin, lone_out)

    far_total[...] = thin.total(0)
    cross = remote(far_total, thin_out.piece(0, me.place, row), cross_send, cross_recv, me.across)
    cross.start()
    thin_out.piece(1, me.place)[...] = thin.total(1)
    thin_out.start(1)
    cross.wait()
    thin_out.start(0)

    tails = []
    keep_load.wait()
    for h in range(per_half):
        part = slice(h * b, (h + 1) * b)
        own = at(col * count + h * b, b)
        beside_copy(h, 2).wait()
        for k in range(2):
            across_copy(h, k).wait()

        def end(fine, h=h):
            own = at(col * count + h * b + fine.start, fine.size)
            part = at(h * b + fine.start, fine.size)
            grad = to_near[own, :].astype(F32) + beside_in[1, part, :].astype(F32) + across_in[part, :].astype(F32)
            inverse = stat[own, HEAD_SIZE:HEAD_SIZE + 1]
            share = (stat_out[part, :1] + stat_in[part, :1]) / (2 * half)
            normal = near[own, :].astype(F32) * inverse
            across_out[part, :] = (inverse * (grad * gain_near_ref[...] - normal * share) + keep[part, :]).astype(BF16)

        by_rows(b, end)
        src = across_out.at[pl.ds(h * b, b), :]
        tails += [remote(src, tokens_grad_ref.at[own, :], last_send.at[1 + h], last_recv.at[1 + h], me.beside),
                  pltpu.make_async_copy(src, tokens_grad_ref.at[own, :], keep_sem.at[9 + h])]
        for each in tails[-2:]:
            each.start()
    steps(0, hops // 2, thin_out)
    steps(early + (n - 1 - early) // 2, n - 1, wide, down)
    steps(hops // 2, hops, thin_out)

    total = mine[...]
    for spread in spreads:
        spread.wait()
    for k in range(n - 1):
        total = total + ring_in[k]
    sums_ref[...] = total
    for each in tails + keeps + [output_here, output_last]:
        each.wait()
    finish(n, wide, down)
    finish(hops + 1, lone, lone_out, thin, thin_out)


def finale(q, k, v, grad, heads, totals, starts, done, down_done, result, middle, keep, raw, tokens, far, hid_near, hid_far,
           w_near, w_far, wo_grad, gain_near, gain_far, q_gain, k_gain, table, ffn_sum, names, n, b=512):
    packed, width = q.shape
    half = tokens.shape[1]
    b = min(b, packed // 2)
    count, blocks, lanes = packed // 2, packed // b, 2 * HEAD_SIZE
    per_half = blocks // 2
    line, columns = half // n, w_near.shape[1]
    vmem = pl.BlockSpec(memory_space=pltpu.VMEM)
    some = pl.BlockSpec(memory_space=pl.ANY)
    dma = pltpu.SemaphoreType.DMA
    rows = -(-(4 * (half // 128) + 2) // 8) * 8

    def full(x):
        return ((2, n, x.shape[1], 2 * x.shape[2]), BF16, some)

    outs = [full(done), full(down_done), ((packed, half), BF16, some), ((2, n, line, columns), BF16, vmem),
            ((n, line, half), BF16, vmem), ((rows, 128), F32, vmem), ((packed, half), BF16, some)]
    tall, short = ((packed, half), BF16), ((count, half), BF16)
    stats = ((count, lanes), F32)
    scratch = [*[((packed, width), BF16)] * 4, (heads.shape, F32), (raw.shape, F32), tall, tall, tall, tall,
               (w_near.shape, BF16), (w_far.shape, BF16), ((count, half), F32), ((2, count, half), BF16),
               ((2 * packed, lanes), BF16), ((2 * packed, lanes), BF16), ((blocks, 2, 2 * b), F32), ((lanes, packed), F32),
               ((b, lanes), F32), ((b, lanes), F32), ((packed, width), F32), ((packed, width // 2), F32), ((packed, width // 2), F32), ((packed, columns), BF16), tall, tall,
               ((packed, lanes), F32), ((n, line, columns), BF16), ((n, line, columns), BF16),
               ((4, n // 2, line, columns), BF16), ((2, n // 2, line, half), BF16),
               ((2, count, half), BF16), short, short, ((2, count, half), BF16), stats, short, stats, stats,
               ((line, columns), BF16), ((rows, 128), F32), ((3, rows, 128), F32), ((n - 1, rows, 128), F32), ((rows, 128), F32),
               ((1, lanes), F32), ((1, lanes), F32), ((1, half), F32), ((1, half), F32)]
    ring = [dma((4, n - 1))] * 4 + [dma((4, n // 2))] * 4 + [dma((2, n // 2))] * 4
    pairs = packed * (packed + b) // 2
    return pl.pallas_call(
        functools.partial(finale_kernel, n, names, b),
        out_shape=tuple(jax.ShapeDtypeStruct(shape, dtype) for shape, dtype, _ in outs),
        in_specs=[some] * 5 + [vmem] * 2 + [some] * 12 + [vmem] * 7,
        out_specs=tuple(spec for *_, spec in outs),
        scratch_shapes=[
            *[pltpu.VMEM(shape, dtype) for shape, dtype in scratch], dma((16,)), dma((9 + per_half,)), *ring,
            dma, dma, dma((3,)), dma((3,)), dma((n - 1,)), dma((n - 1,)), dma((3,)), dma((3,)),
            dma((per_half, 3)), dma((per_half, 3)), dma((per_half, 2)), dma((per_half, 2)), dma((1 + per_half,)), dma((1 + per_half,)),
        ],
        compiler_params=pltpu.CompilerParams(collective_id=3, has_side_effects=True, vmem_limit_bytes=VMEM_LIMIT),
        cost_estimate=pl.CostEstimate(flops=20 * 2 * pairs * 256, transcendentals=4 * pairs, bytes_accessed=100 << 20),
        name="finale",
    )(q, k, v, grad, heads, totals, starts[None, :], done, down_done, result, middle, keep, raw, tokens, far, hid_near, hid_far,
      w_near, w_far, wo_grad, gain_near, gain_far, q_gain, k_gain, table, ffn_sum)


def widen_kernel(widths, units, wide_ref, down_ref, thin_ref, lone_ref, gate_out, up_out, down_out, q_out, k_out, v_out, lone_out):
    for part in range(2):
        for out, begin in ((gate_out, 0), (up_out, units)):
            out[:, part * units:(part + 1) * units] = wide_ref[part, :, begin:begin + units].astype(F32)
        begin = 0
        for out, columns in zip((q_out, k_out, v_out), widths):
            out[:, part * columns:(part + 1) * columns] = thin_ref[part, :, begin:begin + columns].astype(F32)
            begin += columns
    down_out[...] = down_ref[...].astype(F32)
    lone_out[...] = lone_ref[...].astype(F32)


def widen(wide, down, thin, lone, widths, parts=8):
    half = lone.shape[0]
    units = wide.shape[2] // 2
    rows, down_rows = half // parts, down.shape[0] // parts

    def one(rows, columns):
        return pl.BlockSpec((rows, columns), lambda i: (i, 0))

    def two(columns):
        return pl.BlockSpec((2, rows, columns), lambda i: (0, i, 0))

    shapes = [(half, 2 * units)] * 2 + [down.shape] + [(half, 2 * columns) for columns in widths] + [lone.shape]
    return pl.pallas_call(
        functools.partial(widen_kernel, widths, units),
        out_shape=tuple(jax.ShapeDtypeStruct(shape, F32) for shape in shapes),
        grid=(parts,),
        in_specs=[two(2 * units), one(down_rows, down.shape[1]), two(thin.shape[2]), one(rows, lone.shape[1])],
        out_specs=tuple(one(down_rows if k == 2 else rows, shape[1]) for k, shape in enumerate(shapes)),
        compiler_params=pltpu.CompilerParams(vmem_limit_bytes=VMEM_LIMIT),
        cost_estimate=pl.CostEstimate(flops=0, transcendentals=0, bytes_accessed=6 * (wide.size + down.size + thin.size + lone.size)),
        name="widen",
    )(wide, down, thin, lone)


def shards(
    tokens,
    seq_lengths,
    query_weight,
    key_matrix,
    value_matrix,
    out_weight,
    gate_weight,
    up_weight,
    down_weight,
    attn_gain,
    ffn_gain,
    query_gain,
    key_gain,
    cotangent,
):
    packed, half = tokens.shape
    row, col, group = lax.axis_index("row"), lax.axis_index("col"), lax.axis_index("dp")
    parts = lax.axis_size("dp")
    width = 2 * half

    names = ("dp", "row", "col")
    starts = layout(seq_lengths[0], packed)
    table = rope_table(jnp.arange(packed, dtype=jnp.int32) - starts)
    q_gain, k_gain = query_gain[None, :], key_gain[None, :]
    gains = jnp.stack([attn_gain, ffn_gain])
    (far, gate_up_far, down_far, cot_far, gains_far, hid_near, hid_far, raw, q, k, v, attended_raw, totals, attended, middle,
     hidden, out_own, qkv, qkv_far) = begin(
        tokens, cotangent, query_weight, key_matrix, value_matrix, gate_weight, up_weight, down_weight, out_weight, gains,
        q_gain, k_gain, table, starts[:, None], names, parts)
    gain_two = jnp.concatenate([ffn_gain, gains_far[1]])[None, :]
    units = down_weight.shape[0] // 2
    gate_up_far = gate_up_far.reshape(half, -1)
    active, feed_grads, result = feed(
        row[None], hidden, cotangent, cot_far, gate_weight, up_weight, gate_up_far, down_weight,
        down_far.reshape(units, half))

    keep, ffn_sum, done, down_done, grad_attended, grad_out = turn(
        hidden, feed_grads, active, cotangent, cot_far, gate_weight, up_weight, gate_up_far, middle, attended, out_own, gain_two,
        names, parts)
    grad_out = grad_out.reshape(parts, half // parts, -1)

    wide_full, down_full, output, thin_full, out_full, sums, grad_tokens = finale(
        q, k, v, grad_attended, attended_raw, totals, starts, done, down_done, result, middle, keep, raw, tokens, far,
        hid_near, hid_far, qkv, qkv_far.reshape(half, -1), grad_out, attn_gain[None, :], gains_far[:1], q_gain, k_gain, table,
        ffn_sum, names, parts)
    sums = sums.reshape(-1)

    def folded(x):
        return x[:HEAD_SIZE] + x[HEAD_SIZE:]

    widths = (query_weight.shape[1] // 2, key_matrix.shape[1] // 2, value_matrix.shape[1] // 2)
    gate_sum, up_sum, down_sum, q_weight_sum, k_weight_sum, v_weight_sum, out_sum = widen(
        wide_full.reshape(2, half, -1), down_full.reshape(2 * units, half), thin_full.reshape(2, half, -1),
        out_full.reshape(half, -1), widths)
    return (
        output,
        grad_tokens,
        q_weight_sum,
        k_weight_sum,
        v_weight_sum,
        out_sum,
        gate_sum,
        up_sum,
        down_sum,
        part_of(sums[:width], row, 0),
        part_of(sums[width:2 * width], row, 0),
        folded(sums[2 * width:2 * width + 2 * HEAD_SIZE]),
        folded(sums[2 * width + 2 * HEAD_SIZE:2 * width + 4 * HEAD_SIZE]),
    )


def solution(mesh):
    return jax.shard_map(
        shards,
        mesh=mesh,
        in_specs=(
            P("dp", "row"),
            P("dp", None),
            P("row", "col"),
            P("row", "col"),
            P("row", "col"),
            P("col", "row"),
            P("row", "col"),
            P("row", "col"),
            P("col", "row"),
            P("row"),
            P("row"),
            P(),
            P(),
            P("dp", "row"),
        ),
        out_specs=(
            P("dp", "row"),
            P("dp", "row"),
            P("row", "col"),
            P("row", "col"),
            P("row", "col"),
            P("col", "row"),
            P("row", "col"),
            P("row", "col"),
            P("col", "row"),
            P("row"),
            P("row"),
            P(),
            P(),
        ),
        check_vma=False,
    )
```
